32 devices in a mesh: dp: 8 (over y, x, core), tensor: 4 (over z).
Axes of the slice: x: 2, y: 2, z: 4, core: 2. Of those that a mesh axis runs over, the one named last changes fastest.
Arguments:
- tokens: bfloat16 [2, 16, 320, 1024], P(None, 'dp', 'tensor'), may hold values from -6 to 6
- cotangent: bfloat16 [2, 16, 320, 1024], P(None, 'dp', 'tensor'), may hold values from -6 to 6
- keep_mask: int32 [2, 16, 320], P(None, 'dp'), may hold values 0 or 1
- intake: float32 [3072, 1024], P(('tensor', 'dp')), may hold values from -0.1875 to 0.1875
- outlet: float32 [1024, 1024], P(('tensor', 'dp')), may hold values from -1.5 to 1.5
- expand: float32 [4096, 1024], P(('tensor', 'dp')), may hold values from -0.1875 to 0.1875
- shrink: float32 [4096, 1024], P(('tensor', 'dp')), may hold values from -0.09375 to 0.09375
- intake_moment: float32 [3072, 1024], P(('tensor', 'dp')), may hold values from -320 to 320
- outlet_moment: float32 [1024, 1024], P(('tensor', 'dp')), may hold values from -320 to 320
- expand_moment: float32 [4096, 1024], P(('tensor', 'dp')), may hold values from -320 to 320
- shrink_moment: float32 [4096, 1024], P(('tensor', 'dp')), may hold values from -320 to 320
- head_bias: float32 [2, 1024], replicated, may hold values from -1.75 to 1.75
- expand_bias: float32 [4096], replicated, may hold values from -1.75 to 1.75
- norm_gain: float32 [2, 1024], replicated, may hold values from 0.5 to 1.5
- model_bias: float32 [4, 1024], replicated, may hold values from -1.25 to 1.25
- head_first: float32 [2, 1024], replicated, may hold values from -256 to 256
- head_second: float32 [2, 1024], replicated, may hold values from 1000 to 30000
- expand_first: float32 [4096], replicated, may hold values from -32 to 32
- expand_second: float32 [4096], replicated, may hold values from 20 to 600
- gain_first: float32 [2, 1024], replicated, may hold values from -256 to 256
- gain_second: float32 [2, 1024], replicated, may hold values from 1000 to 30000
- bias_first: float32 [4, 1024], replicated, may hold values from -256 to 256
- bias_second: float32 [4, 1024], replicated, may hold values from 1000 to 30000
Outputs:
- output: float32 [2, 16, 320, 1024], P(None, 'dp', 'tensor')
- token_grad: float32 [2, 16, 320, 1024], P(None, 'dp', 'tensor')
- intake_grad: float32 [3072, 1024], P(('tensor', 'dp'))
- outlet_grad: float32 [1024, 1024], P(('tensor', 'dp'))
- expand_grad: float32 [4096, 1024], P(('tensor', 'dp'))
- shrink_grad: float32 [4096, 1024], P(('tensor', 'dp'))
- head_bias_grad: float32 [2, 1024], replicated
- expand_bias_grad: float32 [4096], replicated
- norm_gain_grad: float32 [2, 1024], replicated
- model_bias_grad: float32 [4, 1024], replicated
- intake_moment_new: float32 [3072, 1024], P(('tensor', 'dp'))
- outlet_moment_new: float32 [1024, 1024], P(('tensor', 'dp'))
- expand_moment_new: float32 [4096, 1024], P(('tensor', 'dp'))
- shrink_moment_new: float32 [4096, 1024], P(('tensor', 'dp'))
- intake_new: float32 [3072, 1024], P(('tensor', 'dp'))
- outlet_new: float32 [1024, 1024], P(('tensor', 'dp'))
- expand_new: float32 [4096, 1024], P(('tensor', 'dp'))
- shrink_new: float32 [4096, 1024], P(('tensor', 'dp'))
- intake_copy: bfloat16 [3072, 1024], P(('tensor', 'dp'))
- outlet_copy: bfloat16 [1024, 1024], P(('tensor', 'dp'))
- expand_copy: bfloat16 [4096, 1024], P(('tensor', 'dp'))
- shrink_copy: bfloat16 [4096, 1024], P(('tensor', 'dp'))
- head_bias_change: float32 [2, 1024], replicated
- expand_bias_change: float32 [4096], replicated
- norm_gain_change: float32 [2, 1024], replicated
- model_bias_change: float32 [4, 1024], replicated
- head_first_new: float32 [2, 1024], replicated
- head_second_new: float32 [2, 1024], replicated
- expand_first_new: float32 [4096], replicated
- expand_second_new: float32 [4096], replicated
- gain_first_new: float32 [2, 1024], replicated
- gain_second_new: float32 [2, 1024], replicated
- bias_first_new: float32 [4, 1024], replicated
- bias_second_new: float32 [4, 1024], replicated
The draws below stay inside these ranges and needn't reach their ends.
All inputs are finite; a program needn't handle non-finite values. No bound on the sum of `keep_mask` on one device may be relied on, other than what follows from the above.
Results may differ from the reference program's by a relative error of at most 0.025.
Values may be sent and summed in bfloat16 or wider, within the bound.
A program may use at most 128 MiB of HBM per device.

```python
import math
import jax
import jax.numpy as jnp
from jax import lax

D = 1024
HEADS = 16
HEAD_DIM = 64
FF = 4096
SEQ = 320
BUF = 64
IMG = 2
MICRO = 2
NS_STEPS = 5
ADAM_STEP = 10
BATCH = 16
N_DP = 8


def touch_ends(values, rng, smallest, top_value):
    spot = [jax.random.randint(jax.random.fold_in(rng, axis), (), 0, length) for axis, length in enumerate(values.shape)]
    widest = values.shape.index(max(values.shape))
    beside = spot[:widest] + [(spot[widest] + 1) % values.shape[widest]] + spot[widest + 1:]
    return values.at[tuple(spot)].set(smallest).at[tuple(beside)].set(top_value)


def block_scale(key, dims, pieces, smallest, high):
    def one(axis_at, shards_of):
        heights = jax.random.uniform(jax.random.fold_in(jax.random.fold_in(key, 6), axis_at), (shards_of,), jnp.float32, smallest / len(pieces), high / len(pieces))
        return jnp.repeat(jnp.exp(heights), dims[axis_at] // shards_of).reshape((-1,) + (1,) * (len(dims) - axis_at - 1))

    gain = one(*pieces[0])
    for cut in pieces[1:]:
        gain = gain * one(*cut)
    return gain


def scatter_about(rng, extent, deviation, reach, split=(), dtype=jnp.bfloat16):
    loudness = block_scale(rng, extent, split, -0.22, 0.18) if split else 1.0
    array = jax.random.normal(rng, extent, jnp.float32) * deviation * loudness
    return jnp.minimum(jnp.maximum(array, -reach), reach).astype(dtype)


def setup_inputs(seed: int = 0) -> dict:
    key_list = jax.random.split(jax.random.key(seed), 24)
    return {
        "tokens": scatter_about(key_list[0], (MICRO, BATCH, SEQ, D), 1.0, 6.0, ((1, 8), (2, 4))),
        "cotangent": scatter_about(key_list[1], (MICRO, BATCH, SEQ, D), 1.0, 6.0, ((1, 8), (2, 4))),
        "keep_mask": touch_ends((jax.random.randint(key_list[2], (MICRO, BATCH, SEQ), 0, 20) < 17).astype(jnp.int32), jax.random.fold_in(key_list[2], 1), 0, 1),
        "intake": scatter_about(key_list[3], (3 * D, D), D ** -0.5, 0.1875, ((0, 32),), jnp.float32),
        "outlet": scatter_about(key_list[4], (D, D), (D // 64) ** -0.5, 1.5, ((0, 32),), jnp.float32),
        "expand": scatter_about(key_list[5], (FF, D), D ** -0.5, 0.1875, ((0, 32),), jnp.float32),
        "shrink": scatter_about(key_list[6], (FF, D), FF ** -0.5, 0.09375, ((0, 32),), jnp.float32),
        "intake_moment": scatter_about(key_list[7], (3 * D, D), 50.0, 320.0, ((0, 32),), jnp.float32),
        "outlet_moment": scatter_about(key_list[8], (D, D), 50.0, 320.0, ((0, 32),), jnp.float32),
        "expand_moment": scatter_about(key_list[9], (FF, D), 50.0, 320.0, ((0, 32),), jnp.float32),
        "shrink_moment": scatter_about(key_list[10], (FF, D), 50.0, 320.0, ((0, 32),), jnp.float32),
        "head_bias": scatter_about(key_list[11], (2, D), 0.3, 1.75, (), jnp.float32),
        "expand_bias": scatter_about(key_list[12], (FF,), 0.3, 1.75, (), jnp.float32),
        "norm_gain": jnp.clip(1.0 + 0.1 * jax.random.normal(key_list[13], (2, D), jnp.float32), 0.5, 1.5),
        "model_bias": scatter_about(key_list[14], (4, D), 0.2, 1.25, (), jnp.float32),
        "head_first": scatter_about(key_list[15], (2, D), 40.0, 256.0, (), jnp.float32),
        "head_second": jnp.clip(jnp.exp(jax.random.uniform(key_list[16], (2, D), jnp.float32, math.log(1000.0), math.log(30000.0))), 1000.0, 30000.0),
        "expand_first": scatter_about(key_list[17], (FF,), 5.0, 32.0, (), jnp.float32),
        "expand_second": jnp.clip(jnp.exp(jax.random.uniform(key_list[18], (FF,), jnp.float32, math.log(20.0), math.log(600.0))), 20.0, 600.0),
        "gain_first": scatter_about(key_list[19], (2, D), 40.0, 256.0, (), jnp.float32),
        "gain_second": jnp.clip(jnp.exp(jax.random.uniform(key_list[20], (2, D), jnp.float32, math.log(1000.0), math.log(30000.0))), 1000.0, 30000.0),
        "bias_first": scatter_about(key_list[21], (4, D), 40.0, 256.0, (), jnp.float32),
        "bias_second": jnp.clip(jnp.exp(jax.random.uniform(key_list[22], (4, D), jnp.float32, math.log(1000.0), math.log(30000.0))), 1000.0, 30000.0),
    }


norm_eps = 1e-06
first_decay = 0.9
second_decay = 0.95
adam_rate = 0.05
adam_eps = 1e-08
muon_decay = 0.5
muon_rates = (1.0, 4.0, 1.0, 1.0)
frob_eps = 1e-07
coef_a = 3.4445
coef_b = -4.775
coef_c = 2.0315
masked_score = -1000000000.0

@jax.custom_vjp
def low(v):
    return lax.optimization_barrier(v.astype(jnp.bfloat16)).astype(jnp.float32)

@jax.custom_vjp
def low_back(v):
    return v

def low_keep(v):
    return (low(v), None)

def low_pass(kept, grad):
    return (grad,)

def back_keep(v):
    return (v, None)

def back_low(kept, grad):
    return (low(grad),)
low.defvjp(low_keep, low_pass)
low_back.defvjp(back_keep, back_low)

def precise(form, left, right):
    return jnp.einsum(form, left, right, precision=lax.Precision.HIGHEST)

def layer_norm(inputs_row, gain_row, shift_row):
    center = inputs_row - lax.optimization_barrier(jnp.mean(inputs_row, axis=-1, keepdims=True))
    spread = lax.optimization_barrier(jnp.mean(center * center, axis=-1, keepdims=True))
    return center * lax.rsqrt(spread + norm_eps) * gain_row + shift_row

def softmax_rows(scores):
    largest = lax.optimization_barrier(jnp.max(scores, axis=-1, keepdims=True))
    powers = jnp.exp(scores - largest)
    return powers / lax.optimization_barrier(jnp.sum(powers, axis=-1, keepdims=True))

def group_forward(params, tokens_f, keep):
    intake, outlet, expand, shrink, head_bias, expand_bias, norm_gain, model_bias = params
    images = tokens_f.shape[0]
    first_norm = low(layer_norm(tokens_f, norm_gain[0], model_bias[0]))
    zero_part = jnp.zeros((HEADS, HEAD_DIM), jnp.float32)
    mixed_bias = jnp.stack([head_bias[0].reshape(HEADS, HEAD_DIM), zero_part, head_bias[1].reshape(HEADS, HEAD_DIM)], axis=1).reshape(3 * D)
    mixed_rows = precise('isd,rd->isr', first_norm, low(intake)) + mixed_bias
    mixed_rows = low(low_back(mixed_rows)).reshape(images, SEQ, HEADS, 3, HEAD_DIM)
    queries = mixed_rows[:, :, :, 0]
    keys_all = mixed_rows[:, :, :, 1]
    values = mixed_rows[:, :, :, 2]
    scores = low_back(precise('iqhe,ikhe->ihqk', queries, keys_all) * HEAD_DIM ** (-0.5))
    position = jnp.arange(SEQ)
    live_keys = jnp.logical_or(keep > 0, position[None, :] < BUF)
    scores = jnp.where(live_keys[:, None, None, :], scores, masked_score)
    attention = low(softmax_rows(scores))
    attended = precise('ihqk,ikhe->iqhe', attention, values).reshape(images, SEQ, D)
    attended = low(low_back(attended))
    branch = low_back(precise('isc,cd->isd', attended, low(outlet)) + model_bias[2])
    middle = tokens_f + branch
    second_norm = low(layer_norm(middle, norm_gain[1], model_bias[1]))
    hidden = low_back(precise('isd,fd->isf', second_norm, low(expand)) + expand_bias)
    active = low(jax.nn.gelu(hidden, approximate=False))
    branch_two = low_back(precise('isf,fd->isd', active, low(shrink)) + model_bias[3])
    return middle + branch_two

def muon_step(weight, gradient, moment, rate):
    moment_new = muon_decay * moment + gradient
    update = gradient + muon_decay * moment_new
    scaled = update / (jnp.sqrt(jnp.sum(update * update)) + frob_eps)
    for step in range(NS_STEPS):
        gram = precise('rm,rn->mn', scaled, scaled)
        poly = coef_b * gram + coef_c * precise('mk,kn->mn', gram, gram)
        scaled = coef_a * scaled + precise('rk,kn->rn', scaled, poly)
    factor = math.sqrt(weight.shape[0] / weight.shape[1])
    weight_new = weight - rate * factor * scaled
    return (moment_new, weight_new)

def adam_step(gradient, first, second):
    first_new = first_decay * first + (1.0 - first_decay) * gradient
    second_new = second_decay * second + (1.0 - second_decay) * gradient * gradient
    first_hat = first_new / (1.0 - first_decay ** ADAM_STEP)
    second_hat = second_new / (1.0 - second_decay ** ADAM_STEP)
    change = -adam_rate * first_hat / (jnp.sqrt(second_hat) + adam_eps)
    return (change, first_new, second_new)

def reference(tokens, cotangent, keep_mask, intake, outlet, expand, shrink, intake_moment, outlet_moment, expand_moment, shrink_moment, head_bias, expand_bias, norm_gain, model_bias, head_first, head_second, expand_first, expand_second, gain_first, gain_second, bias_first, bias_second):
    groups = MICRO * N_DP
    tokens_f = tokens.astype(jnp.float32).reshape(groups, IMG, SEQ, D)
    keep_groups = keep_mask.reshape(groups, IMG, SEQ)
    params = (intake, outlet, expand, shrink, head_bias, expand_bias, norm_gain, model_bias)

    def forward_all(params_in, tokens_in):

        def run_group(group_pair):
            return group_forward(params_in, group_pair[0], group_pair[1])
        return lax.map(jax.checkpoint(run_group), (tokens_in, keep_groups))
    output, pullback = jax.vjp(forward_all, params, tokens_f)
    param_grads, token_grad = pullback(cotangent.astype(jnp.float32).reshape(groups, IMG, SEQ, D))
    full_shape = (MICRO, IMG * N_DP, SEQ, D)
    output = output.reshape(full_shape)
    token_grad = token_grad.reshape(full_shape)
    intake_grad, outlet_grad, expand_grad, shrink_grad, head_bias_grad, expand_bias_grad, norm_gain_grad, model_bias_grad = param_grads
    intake_moment_new, intake_new = muon_step(intake, intake_grad, intake_moment, muon_rates[0])
    outlet_moment_new, outlet_new = muon_step(outlet, outlet_grad, outlet_moment, muon_rates[1])
    expand_moment_new, expand_new = muon_step(expand, expand_grad, expand_moment, muon_rates[2])
    shrink_moment_new, shrink_new = muon_step(shrink, shrink_grad, shrink_moment, muon_rates[3])
    head_bias_change, head_first_new, head_second_new = adam_step(head_bias_grad, head_first, head_second)
    expand_bias_change, expand_first_new, expand_second_new = adam_step(expand_bias_grad, expand_first, expand_second)
    norm_gain_change, gain_first_new, gain_second_new = adam_step(norm_gain_grad, gain_first, gain_second)
    model_bias_change, bias_first_new, bias_second_new = adam_step(model_bias_grad, bias_first, bias_second)
    return (output, token_grad, intake_grad, outlet_grad, expand_grad, shrink_grad, head_bias_grad, expand_bias_grad, norm_gain_grad, model_bias_grad, intake_moment_new, outlet_moment_new, expand_moment_new, shrink_moment_new, intake_new, outlet_new, expand_new, shrink_new, intake_new.astype(jnp.bfloat16), outlet_new.astype(jnp.bfloat16), expand_new.astype(jnp.bfloat16), shrink_new.astype(jnp.bfloat16), head_bias_change, expand_bias_change, norm_gain_change, model_bias_change, head_first_new, head_second_new, expand_first_new, expand_second_new, gain_first_new, gain_second_new, bias_first_new, bias_second_new)
```

```python
import functools

import jax
import jax.numpy as jnp
from jax import lax
from jax.experimental import pallas as pl
from jax.experimental.pallas import tpu as pltpu
from jax.sharding import PartitionSpec as P

HEAD_DIM = 64
BUF = 64
NS_STEPS = 5
ADAM_STEP = 10


norm_eps = 1e-06
first_decay = 0.9
second_decay = 0.95
adam_rate = 0.05
adam_eps = 1e-08
muon_decay = 0.5
muon_rates = (1.0, 4.0, 1.0, 1.0)
frob_eps = 1e-07
coef_a = 3.4445
coef_b = -4.775
coef_c = 2.0315
masked_score = -1000000000.0


def precise(form, left, right):
    return jnp.einsum(form, left, right, precision=lax.Precision.HIGHEST)


def layer_norm(inputs_row, gain_row, shift_row):
    center = inputs_row - jnp.mean(inputs_row, axis=-1, keepdims=True)
    spread = jnp.mean(center * center, axis=-1, keepdims=True)
    return center * lax.rsqrt(spread + norm_eps) * gain_row + shift_row


def softmax_rows(scores):
    largest = jnp.max(scores, axis=-1, keepdims=True)
    powers = jnp.exp(scores - largest)
    return powers / jnp.sum(powers, axis=-1, keepdims=True)


def exact_gelu(inputs_row):
    return jax.nn.gelu(inputs_row, approximate=False)


def attend_weights(queries, keys_all, live_keys):
    scores = jnp.einsum(
        "iqhe,ikhe->ihqk", queries, keys_all, preferred_element_type=jnp.float32
    ) * HEAD_DIM ** (-0.5)
    scores = jnp.where(live_keys[:, None, None, :], scores, masked_score)
    return softmax_rows(scores)


def reduce_blocks(blocks):
    return (
        lax.psum_scatter(blocks[0], "dp", scatter_dimension=0, tiled=True),
        lax.psum_scatter(blocks[1], "dp", scatter_dimension=0, tiled=True),
        lax.psum_scatter(blocks[2], "dp", scatter_dimension=0, tiled=True),
        lax.psum_scatter(blocks[3], "dp", scatter_dimension=0, tiled=True),
    )


def gram_whole(matrix):
    model_width = matrix.shape[1]
    own_rows = model_width // lax.axis_size("dp")
    shard_rows = lax.psum_scatter(
        precise(
            "rm,rn->mn", lax.slice_in_dim(matrix, 0, own_rows * lax.axis_size("dp"), axis=1), matrix
        ),
        "dp",
        scatter_dimension=0,
        tiled=True,
    )
    return lax.all_gather(shard_rows, "dp", axis=0, tiled=True)


def newton_step(scaled, gram):
    product = precise("rk,kn->rn", scaled, gram)
    return coef_a * scaled + coef_b * product + coef_c * precise("rk,kn->rn", product, gram)


def adam_step(gradient, first, second):
    first_new = first_decay * first + (1.0 - first_decay) * gradient
    second_new = second_decay * second + (1.0 - second_decay) * gradient * gradient
    first_hat = first_new / (1.0 - first_decay**ADAM_STEP)
    second_hat = second_new / (1.0 - second_decay**ADAM_STEP)
    change = -adam_rate * first_hat / (jnp.sqrt(second_hat) + adam_eps)
    return (change, first_new, second_new)


def per_device(
    tokens,
    cotangent,
    keep_mask,
    intake,
    outlet,
    expand,
    shrink,
    intake_moment,
    outlet_moment,
    expand_moment,
    shrink_moment,
    head_bias,
    expand_bias,
    norm_gain,
    model_bias,
    head_first,
    head_second,
    expand_first,
    expand_second,
    gain_first,
    gain_second,
    bias_first,
    bias_second,
):
    micro_count, images, local_seq, model_width = tokens.shape
    seq_len = keep_mask.shape[2]
    tensor_size = lax.axis_size("tensor")
    tensor_index = lax.axis_index("tensor")
    head_cols = model_width // tensor_size
    local_heads = head_cols // HEAD_DIM
    hidden_cols = expand_bias.shape[0] // tensor_size
    head_start = tensor_index * head_cols
    hidden_start = tensor_index * hidden_cols
    query_bias = lax.dynamic_slice_in_dim(head_bias[0], head_start, head_cols, 0).reshape(
        local_heads, HEAD_DIM
    )
    value_bias = lax.dynamic_slice_in_dim(head_bias[1], head_start, head_cols, 0).reshape(
        local_heads, HEAD_DIM
    )
    mixed_bias = jnp.stack([query_bias, jnp.zeros_like(query_bias), value_bias], axis=1).reshape(
        3 * head_cols
    )
    hidden_bias = lax.dynamic_slice_in_dim(expand_bias, hidden_start, hidden_cols, 0)
    position = jnp.arange(seq_len)
    masters = (intake, outlet, expand, shrink)
    block_shapes = (
        (3 * head_cols, model_width),
        (head_cols, model_width),
        (hidden_cols, model_width),
        (hidden_cols, model_width),
    )
    totals = tuple((jnp.zeros(shape_one, jnp.float32) for shape_one in block_shapes))
    gain_grad = jnp.zeros((2, model_width), jnp.float32)
    bias_grad = jnp.zeros((4, model_width), jnp.float32)
    mixed_bias_grad = jnp.zeros((2, head_cols), jnp.float32)
    hidden_bias_grad = jnp.zeros((hidden_cols,), jnp.float32)
    outputs = []
    token_grads = []
    for micro_index in range(micro_count):
        intake_block, outlet_block, expand_block, shrink_block = (
            lax.all_gather(intake.astype(jnp.bfloat16), "dp", axis=0, tiled=True),
            lax.all_gather(outlet.astype(jnp.bfloat16), "dp", axis=0, tiled=True),
            lax.all_gather(expand.astype(jnp.bfloat16), "dp", axis=0, tiled=True),
            lax.all_gather(shrink.astype(jnp.bfloat16), "dp", axis=0, tiled=True),
        )
        token_rows = tokens[micro_index].astype(jnp.float32)
        live_keys = jnp.logical_or(keep_mask[micro_index] > 0, position[None, :] < BUF)
        first_local = layer_norm(token_rows, norm_gain[0], model_bias[0]).astype(jnp.bfloat16)
        first_norm = lax.all_gather(first_local, "tensor", axis=1, tiled=True)
        mixed_rows = (
            jnp.einsum("isd,rd->isr", first_norm, intake_block, preferred_element_type=jnp.float32)
            + mixed_bias
        )
        mixed_rows = mixed_rows.astype(jnp.bfloat16).reshape(
            images, seq_len, local_heads, 3, HEAD_DIM
        )
        queries = mixed_rows[:, :, :, 0]
        keys_all = mixed_rows[:, :, :, 1]
        values = mixed_rows[:, :, :, 2]
        attention = attend_weights(queries, keys_all, live_keys)
        attention_low = attention.astype(jnp.bfloat16)
        attended = jnp.einsum(
            "ihqk,ikhe->iqhe", attention_low, values, preferred_element_type=jnp.float32
        )
        attended = attended.reshape(images, seq_len, head_cols).astype(jnp.bfloat16)
        part_sum = jnp.einsum(
            "isc,cd->isd", attended, outlet_block, preferred_element_type=jnp.float32
        )
        middle = (
            token_rows
            + lax.psum_scatter(part_sum, "tensor", scatter_dimension=1, tiled=True)
            + model_bias[2]
        )
        second_local = layer_norm(middle, norm_gain[1], model_bias[1]).astype(jnp.bfloat16)
        second_norm = lax.all_gather(second_local, "tensor", axis=1, tiled=True)
        hidden = (
            jnp.einsum("isd,fd->isf", second_norm, expand_block, preferred_element_type=jnp.float32)
            + hidden_bias
        )
        active = exact_gelu(hidden).astype(jnp.bfloat16)
        part_two = jnp.einsum(
            "isf,fd->isd", active, shrink_block, preferred_element_type=jnp.float32
        )
        outputs.append(
            middle
            + lax.psum_scatter(part_two, "tensor", scatter_dimension=1, tiled=True)
            + model_bias[3]
        )
        cot_local = cotangent[micro_index]
        cot_rows = lax.all_gather(cot_local, "tensor", axis=1, tiled=True)
        shrink_block_grad = jnp.einsum(
            "isf,isd->fd", active, cot_rows, preferred_element_type=jnp.float32
        )
        active_grad = jnp.einsum(
            "isd,fd->isf", cot_rows, shrink_block, preferred_element_type=jnp.float32
        )
        gelu_value, gelu_back = jax.vjp(exact_gelu, hidden)
        hidden_grad = gelu_back(active_grad)[0].astype(jnp.bfloat16)
        hidden_bias_grad = hidden_bias_grad + jnp.sum(hidden_grad.astype(jnp.float32), axis=(0, 1))
        expand_block_grad = jnp.einsum(
            "isf,isd->fd", hidden_grad, second_norm, preferred_element_type=jnp.float32
        )
        second_part = jnp.einsum(
            "isf,fd->isd", hidden_grad, expand_block, preferred_element_type=jnp.float32
        )
        second_grad = lax.psum_scatter(second_part, "tensor", scatter_dimension=1, tiled=True)
        norm_value, norm_back = jax.vjp(layer_norm, middle, norm_gain[1], model_bias[1])
        middle_from_norm, gain_two_grad, shift_two_grad = norm_back(second_grad)
        cot_float = cot_local.astype(jnp.float32)
        middle_grad = cot_float + middle_from_norm
        branch_grad = middle_grad.astype(jnp.bfloat16)
        branch_rows = lax.all_gather(branch_grad, "tensor", axis=1, tiled=True)
        outlet_block_grad = jnp.einsum(
            "isc,isd->cd", attended, branch_rows, preferred_element_type=jnp.float32
        )
        attended_grad = jnp.einsum(
            "isd,cd->isc", branch_rows, outlet_block, preferred_element_type=jnp.float32
        )
        attended_grad = attended_grad.astype(jnp.bfloat16).reshape(
            images, seq_len, local_heads, HEAD_DIM
        )
        attention = attend_weights(queries, keys_all, live_keys)
        attention_low = attention.astype(jnp.bfloat16)
        values_grad = jnp.einsum(
            "ihqk,iqhe->ikhe", attention_low, attended_grad, preferred_element_type=jnp.float32
        )
        attention_grad = jnp.einsum(
            "iqhe,ikhe->ihqk", attended_grad, values, preferred_element_type=jnp.float32
        )
        score_grad = attention * (
            attention_grad - jnp.sum(attention_grad * attention, axis=-1, keepdims=True)
        )
        score_grad = score_grad.astype(jnp.bfloat16)
        queries_grad = jnp.einsum(
            "ihqk,ikhe->iqhe", score_grad, keys_all, preferred_element_type=jnp.float32
        ) * HEAD_DIM ** (-0.5)
        keys_grad = jnp.einsum(
            "ihqk,iqhe->ikhe", score_grad, queries, preferred_element_type=jnp.float32
        ) * HEAD_DIM ** (-0.5)
        mixed_grad = jnp.stack([queries_grad, keys_grad, values_grad], axis=3).astype(jnp.bfloat16)
        mixed_sums = jnp.sum(mixed_grad.astype(jnp.float32), axis=(0, 1))
        mixed_bias_grad = mixed_bias_grad + jnp.stack(
            [mixed_sums[:, 0].reshape(head_cols), mixed_sums[:, 2].reshape(head_cols)]
        )
        mixed_grad = mixed_grad.reshape(images, seq_len, 3 * head_cols)
        intake_block_grad = jnp.einsum(
            "isr,isd->rd", mixed_grad, first_norm, preferred_element_type=jnp.float32
        )
        first_part = jnp.einsum(
            "isr,rd->isd", mixed_grad, intake_block, preferred_element_type=jnp.float32
        )
        first_grad = lax.psum_scatter(first_part, "tensor", scatter_dimension=1, tiled=True)
        first_value, first_back = jax.vjp(layer_norm, token_rows, norm_gain[0], model_bias[0])
        token_from_norm, gain_one_grad, shift_one_grad = first_back(first_grad)
        token_grads.append(middle_grad + token_from_norm)
        gain_grad = gain_grad + jnp.stack([gain_one_grad, gain_two_grad])
        bias_grad = bias_grad + jnp.stack(
            [
                shift_one_grad,
                shift_two_grad,
                jnp.sum(branch_grad.astype(jnp.float32), axis=(0, 1)),
                jnp.sum(cot_float, axis=(0, 1)),
            ]
        )
        block_grads = (intake_block_grad, outlet_block_grad, expand_block_grad, shrink_block_grad)
        totals = tuple((total + block_one for total, block_one in zip(totals, block_grads)))
    shards = reduce_blocks(totals)
    head_full = lax.dynamic_update_slice_in_dim(
        jnp.zeros((2, model_width), jnp.float32), mixed_bias_grad, head_start, 1
    )
    hidden_full = lax.dynamic_update_slice_in_dim(
        jnp.zeros(expand_bias.shape, jnp.float32), hidden_bias_grad, hidden_start, 0
    )
    gain_total, bias_total, head_total, hidden_total = lax.psum(
        (gain_grad, bias_grad, head_full, hidden_full), ("dp", "tensor")
    )
    moments = (intake_moment, outlet_moment, expand_moment, shrink_moment)
    moments_new = [muon_decay * moment + gradient for gradient, moment in zip(shards, moments)]
    updates = [gradient + muon_decay * moment for gradient, moment in zip(shards, moments_new)]
    rows_max = max((update.shape[0] for update in updates))
    padded = jnp.stack(
        [jnp.pad(update, ((0, rows_max - update.shape[0]), (0, 0))) for update in updates]
    )
    spread = lax.all_to_all(padded, "tensor", split_axis=0, concat_axis=0, tiled=True)
    own_matrix = spread.reshape(tensor_size * rows_max, model_width)
    raw_gram = gram_whole(own_matrix)
    measure = jnp.sqrt(jnp.trace(raw_gram)) + frob_eps
    scaled = own_matrix / measure
    gram = raw_gram / (measure * measure)
    for step in range(NS_STEPS):
        if step > 0:
            gram = gram_whole(scaled)
        scaled = newton_step(scaled, gram)
    returned = lax.all_to_all(
        scaled.reshape(tensor_size, rows_max, model_width),
        "tensor",
        split_axis=0,
        concat_axis=0,
        tiled=True,
    )
    rows_scale = lax.axis_size("dp") * tensor_size
    masters_new = [
        weight
        - muon_rates[position_one]
        * (weight.shape[0] * rows_scale / weight.shape[1]) ** 0.5
        * returned[position_one, : weight.shape[0]]
        for position_one, weight in enumerate(masters)
    ]
    head_bias_change, head_first_new, head_second_new = adam_step(
        head_total, head_first, head_second
    )
    expand_bias_change, expand_first_new, expand_second_new = adam_step(
        hidden_total, expand_first, expand_second
    )
    norm_gain_change, gain_first_new, gain_second_new = adam_step(
        gain_total, gain_first, gain_second
    )
    model_bias_change, bias_first_new, bias_second_new = adam_step(
        bias_total, bias_first, bias_second
    )
    output = jnp.stack(outputs)
    token_grad = jnp.stack(token_grads)
    return (
        output,
        token_grad,
        shards[0],
        shards[1],
        shards[2],
        shards[3],
        head_total,
        hidden_total,
        gain_total,
        bias_total,
        moments_new[0],
        moments_new[1],
        moments_new[2],
        moments_new[3],
        masters_new[0],
        masters_new[1],
        masters_new[2],
        masters_new[3],
        masters_new[0].astype(jnp.bfloat16),
        masters_new[1].astype(jnp.bfloat16),
        masters_new[2].astype(jnp.bfloat16),
        masters_new[3].astype(jnp.bfloat16),
        head_bias_change,
        expand_bias_change,
        norm_gain_change,
        model_bias_change,
        head_first_new,
        head_second_new,
        expand_first_new,
        expand_second_new,
        gain_first_new,
        gain_second_new,
        bias_first_new,
        bias_second_new,
    )


MESH = pl.DeviceIdType.MESH
BF = jnp.bfloat16
F32 = jnp.float32
VMEM_LIMIT = 60 * 1024 * 1024


def place():
    d = lax.axis_index("dp")
    z = lax.axis_index("tensor")
    y, x, c = d // 4, (d // 2) % 2, d % 2
    return d, z, y, x, c


def partners(d, z, y, x, c):
    core = (d + 1 - 2 * c, z)
    xn = (d + 2 - 4 * x, z)
    yn = (d + 4 - 8 * y, z)
    zn = [(d, (z + k) % 4) for k in range(1, 4)]
    return core, xn, yn, zn


def greet(others):
    barrier = pltpu.get_barrier_semaphore()
    for other in others:
        pl.semaphore_signal(barrier, inc=1, device_id=other, device_id_type=MESH)
    pl.semaphore_wait(barrier, len(others))


def push(src, dst, sems, to):
    return pltpu.make_async_remote_copy(
        src_ref=src, dst_ref=dst, send_sem=sems[0], recv_sem=sems[1], device_id=to, device_id_type=MESH
    )


def gather_kernel(sizes, order, *refs):
    n = len(sizes)
    w = refs[:n]
    tok, cot = refs[n : n + 2]
    mom = refs[n + 2 : 2 * n + 2]
    full = refs[2 * n + 2 : 3 * n + 2]
    tok_all, cot_all, mom_all = refs[3 * n + 2 : 3 * n + 5]
    z_s, z_r, loc, t_s, t_r, m_s, m_r, p_s, p_r = refs[3 * n + 5 :]
    d, z, y, x, c = place()
    core, xn, yn, zn = partners(d, z, y, x, c)
    greet([core, xn, yn] + zn)
    held = []

    def start(copy):
        copy.start()
        held.append(copy)
        return copy

    def z_push(m):
        for k in range(1, 4):
            start(push(w[m], full[m].at[z, y, x, c], (z_s.at[m, k - 1], z_r.at[m, k - 1]), zn[k - 1]))

    def z_wait(m, k):
        slot = full[m].at[(z + 4 - k) % 4, y, x, c]
        push(slot, slot, (z_s.at[m, k - 1], z_r.at[m, k - 1]), zn[k - 1]).wait_recv()

    locals_ = []
    for m in range(n):
        copy = pltpu.make_async_copy(w[m], full[m].at[z, y, x, c], loc.at[m])
        copy.start()
        locals_.append(copy)
    for i, (a, b) in enumerate(((tok, tok_all), (cot, cot_all))):
        copy = pltpu.make_async_copy(a.at[z], b.at[z], loc.at[n + i])
        copy.start()
        locals_.append(copy)
    z_push(0)

    def rows_push(i, a, b):
        for k in range(1, 4):
            start(push(a.at[(z + k) % 4], b.at[z], (t_s.at[i, k - 1], t_r.at[i, k - 1]), zn[k - 1]))

    def mom_push():
        for t in range(n):
            here = mom_all.at[z, pl.ds(0, sizes[t])]

            @pl.when(z == t)
            def _(t=t, here=here):
                pltpu.make_async_copy(mom[t], here, loc.at[n + 2]).start()

            @pl.when(z != t)
            def _(t=t, here=here):
                push(mom[t], here, (m_s.at[t], m_r.at[z]), (d, t)).start()

    def mom_wait():
        for t in range(n):
            here = mom_all.at[z, pl.ds(0, sizes[t])]

            @pl.when(z == t)
            def _(t=t, here=here):
                pltpu.make_async_copy(mom[t], here, loc.at[n + 2]).wait()
                for k in range(1, 4):
                    s = (t + k) % 4
                    there = mom_all.at[s, pl.ds(0, sizes[t])]
                    push(mom[t], there, (m_s.at[t], m_r.at[s]), (d, s)).wait_recv()

            @pl.when(z != t)
            def _(t=t, here=here):
                push(mom[t], here, (m_s.at[t], m_r.at[z]), (d, t)).wait_send()

    def sem(i, stage):
        return (p_s.at[stage, i], p_r.at[stage, i])

    def one(i):
        m, k = order[i]
        h = sizes[m] // 2
        if k > 0:
            z_wait(m, k)
        else:
            locals_[m].wait()
        s = (z + 4 - k) % 4
        a = full[m].at[s, y, x, c, pl.ds(0, h)]
        b = full[m].at[s, y, x, c, pl.ds(h, h)]
        start(push(a, a, sem(i, 0), xn))
        start(push(b, b, sem(i, 1), yn))

    def two(i):
        m, k = order[i]
        h = sizes[m] // 2
        s = (z + 4 - k) % 4
        a = full[m].at[s, y, 1 - x, c, pl.ds(0, h)]
        push(a, a, sem(i, 0), xn).wait_recv()
        a = full[m].at[s, y, :, c, pl.ds(0, h)]
        start(push(a, a, sem(i, 2), yn))
        b = full[m].at[s, 1 - y, x, c, pl.ds(h, h)]
        push(b, b, sem(i, 1), yn).wait_recv()
        b = full[m].at[s, :, x, c, pl.ds(h, h)]
        start(push(b, b, sem(i, 3), xn))

    def three(i):
        m, k = order[i]
        h = sizes[m] // 2
        s = (z + 4 - k) % 4
        a = full[m].at[s, 1 - y, :, c, pl.ds(0, h)]
        push(a, a, sem(i, 2), yn).wait_recv()
        b = full[m].at[s, :, 1 - x, c, pl.ds(h, h)]
        push(b, b, sem(i, 3), xn).wait_recv()
        e = full[m].at[s, :, :, c]
        start(push(e, e, sem(i, 4), core))

    count = len(order)
    for i in range(count + 2):
        if i < count:
            one(i)
        if i == 0:
            z_push(1)
            rows_push(0, tok, tok_all)
            z_push(2)
        if i == 5:
            z_push(3)
            rows_push(1, cot, cot_all)
            mom_push()
        if 1 <= i <= count:
            two(i - 1)
        if i >= 2:
            three(i - 2)
    for i in range(count):
        m, k = order[i]
        e = full[m].at[(z + 4 - k) % 4, :, :, 1 - c]
        push(e, e, sem(i, 4), core).wait_recv()
    for i, b in enumerate((tok_all, cot_all)):
        locals_[n + i].wait()
        for k in range(1, 4):
            slot = b.at[(z + 4 - k) % 4]
            push(slot, slot, (t_s.at[i, k - 1], t_r.at[i, k - 1]), zn[k - 1]).wait_recv()
    mom_wait()
    for copy in held:
        copy.wait_send()


def gather_all(weights, tok, cot, moms):
    sizes = tuple(v.shape[0] for v in weights)
    width = weights[0].shape[1]
    order = [(0, 0), (1, 0), (2, 0), (0, 1), (0, 2), (0, 3), (1, 1), (1, 2), (1, 3)]
    order += [(2, 1), (2, 2), (2, 3), (3, 0), (3, 1), (3, 2), (3, 3)]
    count = len(order)
    anyspace = pl.BlockSpec(memory_space=pl.ANY)
    dma = pltpu.SemaphoreType.DMA
    return pl.pallas_call(
        functools.partial(gather_kernel, sizes, order),
        out_shape=[jax.ShapeDtypeStruct((4, 2, 2, 2, s, width), BF) for s in sizes]
        + [jax.ShapeDtypeStruct(tok.shape, BF), jax.ShapeDtypeStruct(cot.shape, BF)]
        + [jax.ShapeDtypeStruct((4, max(sizes), width), BF)],
        in_specs=[anyspace] * (2 * len(sizes) + 2),
        out_specs=[anyspace] * (len(sizes) + 3),
        scratch_shapes=[
            dma((4, 3)),
            dma((4, 3)),
            dma((7,)),
            dma((2, 3)),
            dma((2, 3)),
            dma((4,)),
            dma((4,)),
            dma((5, count)),
            dma((5, count)),
        ],
        compiler_params=pltpu.CompilerParams(collective_id=1, has_side_effects=True, vmem_limit_bytes=8 << 20),
    )(*weights, tok, cot, *moms)


def add_rows(dst, src, lead, rows):
    step = 16

    def body(i, carry):
        j, r = i // (rows // step), (i % (rows // step)) * step
        at = pl.ds(pl.multiple_of(r, step), step)
        dst[j, at] = dst[j, at] + src[j, at]
        return carry

    lax.fori_loop(0, lead * (rows // step), body, 0)


def reduce_kernel(sizes, order, *refs):
    n = len(sizes)
    part = refs[:n]
    small = refs[n]
    total, small_out = refs[n + 1 : n + 3]
    own = refs[n + 3 : 2 * n + 3]
    got = refs[2 * n + 3 : 3 * n + 3]
    mid = refs[3 * n + 3 : 4 * n + 3]
    end = refs[4 * n + 3 : 5 * n + 3]
    far, s_got, s_acc, s_z, loc, p_s, p_r, f_s, f_r, q_s, q_r = refs[5 * n + 3 :]
    d, z, y, x, c = place()
    core, xn, yn, zn = partners(d, z, y, x, c)
    greet([core, xn, yn] + zn)
    held = []

    def start(copy):
        copy.start()
        held.append(copy)

    def sem(i, stage):
        return (p_s.at[stage, i], p_r.at[stage, i])

    def zero(i):
        m, k = order[i]
        start(push(part[m].at[k, :, :, 1 - c], got[m].at[k], sem(i, 0), core))
        pltpu.make_async_copy(part[m].at[k, :, :, c], own[m].at[k], loc.at[i]).start()

    def one(i):
        m, k = order[i]
        s, h = sizes[m], sizes[m] // 2
        pltpu.make_async_copy(part[m].at[k, :, :, c], own[m].at[k], loc.at[i]).wait()
        push(part[m].at[k, :, :, 1 - c], got[m].at[k], sem(i, 0), core).wait_recv()
        for j in range(2):
            add_rows(own[m].at[k, j], got[m].at[k, j], 2, s)
        start(push(own[m].at[k, 1 - y, :, pl.ds(0, h)], mid[m].at[k, 0], sem(i, 1), yn))
        start(push(own[m].at[k, :, 1 - x, pl.ds(h, h)], mid[m].at[k, 1], sem(i, 2), xn))

    def two(i):
        m, k = order[i]
        h = sizes[m] // 2
        push(mid[m].at[k, 0], mid[m].at[k, 0], sem(i, 1), yn).wait_recv()
        add_rows(own[m].at[k, y, :, pl.ds(0, h)], mid[m].at[k, 0], 2, h)
        start(push(own[m].at[k, y, 1 - x, pl.ds(0, h)], end[m].at[k, pl.ds(0, h)], sem(i, 3), xn))
        push(mid[m].at[k, 1], mid[m].at[k, 1], sem(i, 2), xn).wait_recv()
        add_rows(own[m].at[k, :, x, pl.ds(h, h)], mid[m].at[k, 1], 2, h)
        start(push(own[m].at[k, 1 - y, x, pl.ds(h, h)], end[m].at[k, pl.ds(h, h)], sem(i, 4), yn))

    def three(i):
        m, k = order[i]
        s, h = sizes[m], sizes[m] // 2
        push(end[m].at[k, pl.ds(0, h)], end[m].at[k, pl.ds(0, h)], sem(i, 3), xn).wait_recv()
        push(end[m].at[k, pl.ds(h, h)], end[m].at[k, pl.ds(h, h)], sem(i, 4), yn).wait_recv()
        add_rows(own[m].at[k, pl.ds(y, 1), x], end[m].at[pl.ds(k, 1)], 1, s)

        @pl.when(z != m)
        def _():
            push(own[m].at[k, y, x], far.at[z, k, pl.ds(0, s)], (f_s.at[m, k], f_r.at[z, k]), (d, m)).start()

    def four(i):
        m, k = order[i]
        s = sizes[m]

        @pl.when(z == m)
        def _():
            for j in range(1, 4):
                v = (m + j) % 4
                slot = far.at[v, k, pl.ds(0, s)]
                push(slot, slot, (f_s.at[m, k], f_r.at[v, k]), (d, v)).wait_recv()

            def body(r, carry):
                at = pl.ds(pl.multiple_of(r * 16, 16), 16)
                acc = own[m][k, y, x, at].astype(F32)
                for j in range(1, 4):
                    acc = acc + far[(m + j) % 4, k, at].astype(F32)
                total[k, at] = acc
                return carry

            lax.fori_loop(0, s // 16, body, 0)
            if s < total.shape[1]:
                total[k, pl.ds(s, total.shape[1] - s)] = jnp.zeros((total.shape[1] - s, total.shape[2]), F32)

    def small_step(stage):
        to = (core, xn, yn)
        if stage > 0:
            here = s_got.at[stage - 1]
            push(here, here, (q_s.at[stage - 1], q_r.at[stage - 1]), to[stage - 1]).wait_recv()
            s_acc[stage] = s_acc[stage - 1] + s_got[stage - 1]
        else:
            s_acc[0] = small[...]
        if stage < 3:
            start(push(s_acc.at[stage], s_got.at[stage], (q_s.at[stage], q_r.at[stage]), to[stage]))
        else:
            s_z[z] = s_acc[3]
            for k in range(1, 4):
                start(push(s_acc.at[3], s_z.at[z], (q_s.at[2 + k], q_r.at[2 + k]), zn[k - 1]))

    count = len(order)
    lead = 4
    for i in range(lead):
        zero(i)
    small_step(0)
    for i in range(count + 4):
        if i + lead < count:
            zero(i + lead)
        if i < count:
            one(i)
        if 1 <= i <= count:
            two(i - 1)
        if 2 <= i <= count + 1:
            three(i - 2)
        if 4 <= i:
            four(i - 4)
        if i in (2, 4, 6):
            small_step(i // 2)
    for k in range(1, 4):
        slot = s_z.at[(z + 4 - k) % 4]
        push(slot, slot, (q_s.at[2 + k], q_r.at[2 + k]), zn[k - 1]).wait_recv()
    small_out[...] = s_z[0] + s_z[1] + s_z[2] + s_z[3]
    for copy in held:
        copy.wait_send()
    for m, k in order:

        @pl.when(z != m)
        def _(m=m, k=k):
            slot = own[m].at[k, y, x]
            push(slot, slot, (f_s.at[m, k], f_r.at[z, k]), (d, m)).wait_send()


def reduce_all(parts, small):
    sizes = tuple(v.shape[4] for v in parts)
    width = parts[0].shape[5]
    top = max(sizes)
    order = [(m, k) for m in (3, 2, 1, 0) for k in range(4)]
    count = len(order)
    anyspace = pl.BlockSpec(memory_space=pl.ANY)
    vmem = pl.BlockSpec(memory_space=pltpu.VMEM)
    dma = pltpu.SemaphoreType.DMA
    return pl.pallas_call(
        functools.partial(reduce_kernel, sizes, order),
        out_shape=[jax.ShapeDtypeStruct((4, top, width), F32), jax.ShapeDtypeStruct(small.shape, F32)],
        in_specs=[anyspace] * len(sizes) + [vmem],
        out_specs=[vmem, vmem],
        scratch_shapes=[pltpu.VMEM((4, 2, 2, s, width), BF) for s in sizes]
        + [pltpu.VMEM((4, 2, 2, s, width), BF) for s in sizes]
        + [pltpu.VMEM((4, 2, 2, s // 2, width), BF) for s in sizes]
        + [pltpu.VMEM((4, s, width), BF) for s in sizes]
        + [
            pltpu.VMEM((4, 4, top, width), BF),
            pltpu.VMEM((3,) + small.shape, F32),
            pltpu.VMEM((4,) + small.shape, F32),
            pltpu.VMEM((4,) + small.shape, F32),
            dma((count,)),
            dma((5, count)),
            dma((5, count)),
            dma((4, 4)),
            dma((4, 4)),
            dma((6,)),
            dma((6,)),
        ],
        compiler_params=pltpu.CompilerParams(collective_id=2, has_side_effects=True, vmem_limit_bytes=VMEM_LIMIT),
    )(*parts, small)


def gram_kernel(sizes, *refs):
    n = len(sizes)
    total, mom, outp, tokg = refs[:4]
    gram, upd, upl = refs[4:7]
    grads = refs[7 : 7 + n]
    outp_all, tokg_all = refs[7 + n : 9 + n]
    low_g, part, r_core, r_one, r_two, g_s, g_r, a_s, a_r, o_s, o_r, loc = refs[9 + n :]
    d, z, y, x, c = place()
    core, xn, yn, zn = partners(d, z, y, x, c)
    greet([core, xn, yn] + zn)
    held = []

    def start(copy):
        copy.start()
        held.append(copy)

    width = total.shape[2]
    top = total.shape[1]
    def cast(i, carry):
        at = pl.ds(pl.multiple_of((i % (top // 16)) * 16, 16), 16)
        low_g[i // (top // 16), at] = total[i // (top // 16), at].astype(BF)
        return carry

    lax.fori_loop(0, 4 * (top // 16), cast, 0)
    for t in range(n):

        @pl.when(z == t)
        def _(t=t):
            s = sizes[t]
            for k in range(1, 4):
                v = (t + k) % 4
                push(low_g.at[v, pl.ds(0, s)], grads[t], (g_s.at[v], g_r.at[t]), (d, v)).start()
            pltpu.make_async_copy(low_g.at[t, pl.ds(0, s)], grads[t], loc.at[0]).start()

    height = jnp.where(z == 0, sizes[0], jnp.where(z == 1, sizes[1], jnp.where(z == 2, sizes[2], sizes[3])))

    def make(i, carry):
        k, r = i // (top // 16), (i % (top // 16)) * 16
        at = pl.ds(pl.multiple_of(r, 16), 16)
        g = total[k, at]
        u = g + muon_decay * (muon_decay * mom[k, at].astype(F32) + g)
        row = lax.broadcasted_iota(jnp.int32, u.shape, 0) + r
        u = jnp.where(row < height, u, 0.0)
        hi = u.astype(BF)
        to = pl.ds(pl.multiple_of(i * 16, 16), 16)
        upd[to] = hi
        upl[to] = (u - hi.astype(F32)).astype(BF)
        return carry

    lax.fori_loop(0, 4 * (top // 16), make, 0)
    tile = 256
    dims = (((0,), (0,)), ((), ()))

    def mul(i, carry):
        at = pl.ds(pl.multiple_of(i * tile, tile), tile)
        hi, lo = upd[:, at], upl[:, at]
        acc = lax.dot_general(upd[...], hi, dims, preferred_element_type=F32)
        acc = acc + lax.dot_general(upd[...], lo, dims, preferred_element_type=F32)
        part[:, at] = acc + lax.dot_general(upl[...], hi, dims, preferred_element_type=F32)
        return carry

    lax.fori_loop(0, width // tile, mul, 0)

    def add(dst, r0, src, rows, into=None, r1=None):
        def body(i, carry):
            at = pl.ds(pl.multiple_of(r0 + i * 8, 8), 8)
            v = dst[at] + src[pl.ds(pl.multiple_of(i * 8, 8), 8)]
            if into is None:
                dst[at] = v
            else:
                into[at] = v
            return carry

        lax.fori_loop(0, rows // 8, body, 0)

    half, quarter, eighth = width // 2, width // 8, width // 16

    def sem(i):
        return (a_s.at[i], a_r.at[i])

    def rows(ref, r, count):
        return ref.at[pl.ds(pl.multiple_of(r, 64), count)]

    start(push(rows(part, (1 - c) * half, half), r_core, sem(0), core))
    push(r_core, r_core, sem(0), core).wait_recv()
    base_a = c * half
    base_b = c * half + half // 2
    add(part, base_a, r_core, half)
    start(push(rows(part, base_a + (1 - y) * quarter, quarter), r_one.at[0], sem(1), yn))
    start(push(rows(part, base_b + (1 - x) * quarter, quarter), r_one.at[1], sem(2), xn))
    for i, (a, b) in enumerate(((outp, outp_all), (tokg, tokg_all))):
        pltpu.make_async_copy(a.at[z], b.at[z], loc.at[1 + i]).start()
        for k in range(1, 4):
            start(push(a.at[(z + k) % 4], b.at[z], (o_s.at[i, k - 1], o_r.at[i, k - 1]), zn[k - 1]))
    push(r_one.at[0], r_one.at[0], sem(1), yn).wait_recv()
    mine_a = base_a + y * quarter
    add(part, mine_a, r_one.at[0], quarter)
    start(push(rows(part, mine_a + (1 - x) * eighth, eighth), r_two.at[0], sem(3), xn))
    push(r_one.at[1], r_one.at[1], sem(2), xn).wait_recv()
    mine_b = base_b + x * quarter
    add(part, mine_b, r_one.at[1], quarter)
    start(push(rows(part, mine_b + (1 - y) * eighth, eighth), r_two.at[1], sem(4), yn))
    push(r_two.at[0], r_two.at[0], sem(3), xn).wait_recv()
    own_a = mine_a + x * eighth
    add(part, own_a, r_two.at[0], eighth, gram)
    start(push(rows(gram, own_a, eighth), rows(gram, own_a, eighth), sem(5), xn))
    push(r_two.at[1], r_two.at[1], sem(4), yn).wait_recv()
    own_b = mine_b + y * eighth
    add(part, own_b, r_two.at[1], eighth, gram)
    start(push(rows(gram, own_b, eighth), rows(gram, own_b, eighth), sem(6), yn))
    got_a = rows(gram, mine_a + (1 - x) * eighth, eighth)
    push(got_a, got_a, sem(5), xn).wait_recv()
    start(push(rows(gram, mine_a, quarter), rows(gram, mine_a, quarter), sem(7), yn))
    got_b = rows(gram, mine_b + (1 - y) * eighth, eighth)
    push(got_b, got_b, sem(6), yn).wait_recv()
    start(push(rows(gram, mine_b, quarter), rows(gram, mine_b, quarter), sem(8), xn))
    got_a = rows(gram, base_a + (1 - y) * quarter, quarter)
    push(got_a, got_a, sem(7), yn).wait_recv()
    start(push(rows(gram, base_a, half // 2), rows(gram, base_a, half // 2), sem(9), core))
    got_b = rows(gram, base_b + (1 - x) * quarter, quarter)
    push(got_b, got_b, sem(8), xn).wait_recv()
    start(push(rows(gram, base_b, half // 2), rows(gram, base_b, half // 2), sem(10), core))
    got_a = rows(gram, (1 - c) * half, half // 2)
    push(got_a, got_a, sem(9), core).wait_recv()
    got_b = rows(gram, (1 - c) * half + half // 2, half // 2)
    push(got_b, got_b, sem(10), core).wait_recv()

    for i, (a, b) in enumerate(((outp, outp_all), (tokg, tokg_all))):
        pltpu.make_async_copy(a.at[z], b.at[z], loc.at[1 + i]).wait()
        for k in range(1, 4):
            slot = b.at[(z + 4 - k) % 4]
            push(slot, slot, (o_s.at[i, k - 1], o_r.at[i, k - 1]), zn[k - 1]).wait_recv()
    for t in range(n):
        s = sizes[t]

        @pl.when(z == t)
        def _(t=t, s=s):
            pltpu.make_async_copy(low_g.at[t, pl.ds(0, s)], grads[t], loc.at[0]).wait()
            for k in range(1, 4):
                v = (t + k) % 4
                push(low_g.at[v, pl.ds(0, s)], grads[t], (g_s.at[v], g_r.at[t]), (d, v)).wait_send()

        @pl.when(z != t)
        def _(t=t):
            push(grads[t], grads[t], (g_s.at[t], g_r.at[t]), (d, t)).wait_recv()
    for copy in held:
        copy.wait_send()


def gram_all(total, mom, outp, tokg, sizes):
    top, width = total.shape[1:]
    anyspace = pl.BlockSpec(memory_space=pl.ANY)
    vmem = pl.BlockSpec(memory_space=pltpu.VMEM)
    dma = pltpu.SemaphoreType.DMA
    return pl.pallas_call(
        functools.partial(gram_kernel, sizes),
        out_shape=[jax.ShapeDtypeStruct((width, width), F32)]
        + [jax.ShapeDtypeStruct((4 * top, width), BF)] * 2
        + [jax.ShapeDtypeStruct((s, width), BF) for s in sizes]
        + [jax.ShapeDtypeStruct(outp.shape, outp.dtype), jax.ShapeDtypeStruct(tokg.shape, tokg.dtype)],
        in_specs=[vmem, vmem, anyspace, anyspace],
        out_specs=[vmem] * 3 + [anyspace] * (len(sizes) + 2),
        scratch_shapes=[
            pltpu.VMEM((4, top, width), BF),
            pltpu.VMEM((width, width), F32),
            pltpu.VMEM((width // 2, width), F32),
            pltpu.VMEM((2, width // 8, width), F32),
            pltpu.VMEM((2, width // 16, width), F32),
            dma((4,)),
            dma((4,)),
            dma((11,)),
            dma((11,)),
            dma((2, 3)),
            dma((2, 3)),
            dma((3,)),
        ],
        compiler_params=pltpu.CompilerParams(collective_id=3, has_side_effects=True, vmem_limit_bytes=VMEM_LIMIT),
    )(total, mom, outp, tokg)


def split(v):
    hi = v.astype(BF)
    return hi, (v - hi.astype(F32)).astype(BF)


def dot(a, b):
    return jnp.dot(a, b, preferred_element_type=F32)


def polish_kernel(gram, hi, lo, out, gf, gh, gl, low, b, xf, xh, xl):
    width = gram.shape[0]
    rows = hi.shape[0]
    tile = 256
    step = 64
    eye = jnp.where(
        lax.broadcasted_iota(jnp.int32, (128, 128), 0) == lax.broadcasted_iota(jnp.int32, (128, 128), 1), 1.0, 0.0
    ).astype(F32)
    trace = jnp.zeros((1, 1), F32)
    for i in range(width // 128):
        block = gram[i * 128 : (i + 1) * 128, i * 128 : (i + 1) * 128] * eye
        trace = trace + jnp.sum(jnp.sum(block, axis=1, keepdims=True), axis=0, keepdims=True)
    inverse = 1.0 / (jnp.sqrt(trace) + frob_eps)
    squared = inverse * inverse

    def scale_gram(i, carry):
        at = pl.ds(pl.multiple_of(i * step, step), step)
        v = gram[at] * squared
        gf[at] = v
        gh[at], gl[at] = split(v)
        return carry

    lax.fori_loop(0, width // step, scale_gram, 0)

    def scale_x(i, carry):
        at = pl.ds(pl.multiple_of(i * step, step), step)
        v = (hi[at].astype(F32) + lo[at].astype(F32)) * inverse
        xf[at] = v
        xh[at], xl[at] = split(v)
        return carry

    lax.fori_loop(0, rows // step, scale_x, 0)

    def columns(i):
        return pl.ds(pl.multiple_of(i * tile, tile), tile)

    def iterate(shift, double, last):
        level = coef_a + coef_b * shift + coef_c * shift * shift
        slope = coef_b + 2.0 * coef_c * shift
        left = low if last else gh

        def poly(i, carry):
            at = columns(i)
            g = gf[:, at]
            if last:
                row = lax.broadcasted_iota(jnp.int32, g.shape, 0)
                col = lax.broadcasted_iota(jnp.int32, g.shape, 1) + i * tile
                g = g - jnp.where(row == col, shift, 0.0)
            b[:, at] = (slope * g + coef_c * dot(left[...], left[:, at])).astype(BF)
            return carry

        if last:

            def lower(i, carry):
                at = pl.ds(pl.multiple_of(i * step, step), step)
                g = gf[at]
                row = lax.broadcasted_iota(jnp.int32, g.shape, 0) + i * step
                col = lax.broadcasted_iota(jnp.int32, g.shape, 1)
                low[at] = (g - jnp.where(row == col, shift, 0.0)).astype(BF)
                return carry

            lax.fori_loop(0, width // step, lower, 0)
        lax.fori_loop(0, width // tile, poly, 0)

        def apply(i, carry):
            at = columns(i)
            right = b[:, at]
            v = level * xf[:, at] + dot(xh[...], right)
            if double:
                v = v + dot(xl[...], right)
            if last:
                out[:, at] = v.astype(BF)
                return carry
            xf[:, at] = v
            t = level * gf[:, at] + dot(gh[...], right)
            if double:
                t = t + dot(gl[...], right)
                th, tl = split(t)
                gf[:, at] = level * t + dot(b[...], th) + dot(b[...], tl)
            else:
                gf[:, at] = level * t + dot(b[...], t.astype(BF))
            return carry

        lax.fori_loop(0, width // tile, apply, 0)
        if not last:

            def lower_g(i, carry):
                at = pl.ds(pl.multiple_of(i * step, step), step)
                gh[at] = gf[at].astype(BF)
                return carry

            lax.fori_loop(0, width // step, lower_g, 0)

            def lower_x(i, carry):
                at = pl.ds(pl.multiple_of(i * step, step), step)
                xh[at] = xf[at].astype(BF)
                return carry

            lax.fori_loop(0, rows // step, lower_x, 0)

    iterate(0.0, True, False)

    def middle(i, carry):
        iterate(0.0, False, False)
        return carry

    lax.fori_loop(0, NS_STEPS - 2, middle, 0)
    iterate(0.8, False, True)


def polish(gram, hi, lo):
    rows, width = hi.shape
    vmem = pl.BlockSpec(memory_space=pltpu.VMEM)
    return pl.pallas_call(
        polish_kernel,
        out_shape=jax.ShapeDtypeStruct((rows, width), BF),
        in_specs=[vmem] * 3,
        out_specs=vmem,
        scratch_shapes=[pltpu.VMEM((width, width), F32)]
        + [pltpu.VMEM((width, width), BF)] * 4
        + [pltpu.VMEM((rows, width), F32)]
        + [pltpu.VMEM((rows, width), BF)] * 2,
        compiler_params=pltpu.CompilerParams(vmem_limit_bytes=VMEM_LIMIT),
        cost_estimate=pl.CostEstimate(flops=39 * 10**9, bytes_accessed=8 * 10**6, transcendentals=0),
    )(gram, hi, lo)


def return_kernel(sizes, *refs):
    n = len(sizes)
    done = refs[0]
    rows = refs[1 : 1 + n]
    s_s, s_r, loc = refs[1 + n :]
    d, z, y, x, c = place()
    core, xn, yn, zn = partners(d, z, y, x, c)
    greet(zn)
    for t in range(n):
        s = sizes[t]

        @pl.when(z == t)
        def _(t=t, s=s):
            for k in range(1, 4):
                v = (t + k) % 4
                push(done.at[v, pl.ds(0, s)], rows[t], (s_s.at[v], s_r.at[t]), (d, v)).start()
            pltpu.make_async_copy(done.at[t, pl.ds(0, s)], rows[t], loc.at[0]).start()

    for t in range(n):
        s = sizes[t]

        @pl.when(z == t)
        def _(t=t, s=s):
            pltpu.make_async_copy(done.at[t, pl.ds(0, s)], rows[t], loc.at[0]).wait()
            for k in range(1, 4):
                v = (t + k) % 4
                push(done.at[v, pl.ds(0, s)], rows[t], (s_s.at[v], s_r.at[t]), (d, v)).wait_send()

        @pl.when(z != t)
        def _(t=t):
            push(rows[t], rows[t], (s_s.at[t], s_r.at[t]), (d, t)).wait_recv()


def return_all(done, sizes):
    anyspace = pl.BlockSpec(memory_space=pl.ANY)
    dma = pltpu.SemaphoreType.DMA
    return pl.pallas_call(
        functools.partial(return_kernel, sizes),
        out_shape=[jax.ShapeDtypeStruct((s, done.shape[2]), BF) for s in sizes],
        in_specs=[anyspace],
        out_specs=[anyspace] * len(sizes),
        scratch_shapes=[dma((4,)), dma((4,)), dma((1,))],
        compiler_params=pltpu.CompilerParams(collective_id=4, has_side_effects=True, vmem_limit_bytes=8 << 20),
    )(done)


def whole_image(x, cot, live, weights, head_bias, expand_bias, norm_gain, model_bias):
    intake, outlet, expand, shrink = weights
    seq, width = x.shape
    heads = width // HEAD_DIM
    scale = HEAD_DIM ** (-0.5)
    query_bias = head_bias[0].reshape(heads, HEAD_DIM)
    value_bias = head_bias[1].reshape(heads, HEAD_DIM)
    mixed_bias = jnp.stack([query_bias, jnp.zeros_like(query_bias), value_bias], axis=1).reshape(3 * width)

    def ein(form, a, b):
        return jnp.einsum(form, a, b, preferred_element_type=F32)

    def norm(v, g, s):
        center = v - jnp.mean(v, axis=-1, keepdims=True)
        r = lax.rsqrt(jnp.mean(center * center, axis=-1, keepdims=True) + norm_eps)
        n = center * r
        return n * g + s, n, r

    def norm_back(n, r, g, w):
        u = w * g
        down = r * (u - jnp.mean(u, axis=-1, keepdims=True) - n * jnp.mean(u * n, axis=-1, keepdims=True))
        return down, jnp.sum(w * n, axis=0), jnp.sum(w, axis=0)

    rows = x.astype(F32)
    first, n1, r1 = norm(rows, norm_gain[0], model_bias[0])
    first = first.astype(BF)
    mixed = (ein("sd,rd->sr", first, intake) + mixed_bias).astype(BF).reshape(seq, heads, 3, HEAD_DIM)
    q, k, v = mixed[:, :, 0], mixed[:, :, 1], mixed[:, :, 2]
    scores = ein("qhe,khe->hqk", q, k) * scale
    scores = jnp.where(live[None, None, :], scores, masked_score)
    attention = softmax_rows(scores)
    attention16 = attention.astype(BF)
    attended = ein("hqk,khe->qhe", attention16, v).reshape(seq, width).astype(BF)
    middle = rows + ein("sc,cd->sd", attended, outlet) + model_bias[2]
    second, n2, r2 = norm(middle, norm_gain[1], model_bias[1])
    second = second.astype(BF)
    hidden = ein("sd,fd->sf", second, expand) + expand_bias
    bell = 0.5 * (1.0 + lax.erf(hidden * (0.5**0.5)))
    active = (hidden * bell).astype(BF)
    output = middle + ein("sf,fd->sd", active, shrink) + model_bias[3]
    shrink_grad = ein("sf,sd->fd", active, cot)
    active_grad = ein("sd,fd->sf", cot, shrink)
    slope = bell + hidden * jnp.exp(-0.5 * hidden * hidden) * (0.5 / jnp.pi) ** 0.5
    hidden_grad = (active_grad * slope).astype(BF)
    hidden_bias_grad = jnp.sum(hidden_grad.astype(F32), axis=0)
    expand_grad = ein("sf,sd->fd", hidden_grad, second)
    second_grad = ein("sf,fd->sd", hidden_grad, expand)
    down, gain_two, shift_two = norm_back(n2, r2, norm_gain[1], second_grad)
    cot_float = cot.astype(F32)
    middle_grad = cot_float + down
    branch = middle_grad.astype(BF)
    outlet_grad = ein("sc,sd->cd", attended, branch)
    attended_grad = ein("sd,cd->sc", branch, outlet).astype(BF).reshape(seq, heads, HEAD_DIM)
    values_grad = ein("hqk,qhe->khe", attention16, attended_grad)
    attention_grad = ein("qhe,khe->hqk", attended_grad, v)
    score_grad = attention * (attention_grad - jnp.sum(attention_grad * attention, axis=-1, keepdims=True))
    score_grad = score_grad.astype(BF)
    queries_grad = ein("hqk,khe->qhe", score_grad, k) * scale
    keys_grad = ein("hqk,qhe->khe", score_grad, q) * scale
    mixed_grad = jnp.stack([queries_grad, keys_grad, values_grad], axis=2).astype(BF)
    sums = jnp.sum(mixed_grad.astype(F32), axis=0)
    mixed_grad = mixed_grad.reshape(seq, 3 * width)
    intake_grad = ein("sr,sd->rd", mixed_grad, first)
    first_grad = ein("sr,rd->sd", mixed_grad, intake)
    down, gain_one, shift_one = norm_back(n1, r1, norm_gain[0], first_grad)
    token_grad = middle_grad + down
    small = jnp.concatenate(
        [
            sums[:, 0].reshape(1, width),
            sums[:, 2].reshape(1, width),
            hidden_bias_grad.reshape(-1, width),
            gain_one[None],
            gain_two[None],
            shift_one[None],
            shift_two[None],
            jnp.sum(branch.astype(F32), axis=0)[None],
            jnp.sum(cot_float, axis=0)[None],
        ]
    )
    grads = tuple(g.astype(BF) for g in (intake_grad, outlet_grad, expand_grad, shrink_grad))
    return output.astype(BF), token_grad.astype(BF), grads, small


def per_device_fast(
    tokens,
    cotangent,
    keep_mask,
    intake,
    outlet,
    expand,
    shrink,
    intake_moment,
    outlet_moment,
    expand_moment,
    shrink_moment,
    head_bias,
    expand_bias,
    norm_gain,
    model_bias,
    head_first,
    head_second,
    expand_first,
    expand_second,
    gain_first,
    gain_second,
    bias_first,
    bias_second,
):
    shape = tokens.shape
    local, width = shape[2:]
    z = lax.axis_index("tensor")
    masters = (intake, outlet, expand, shrink)
    moments = (intake_moment, outlet_moment, expand_moment, shrink_moment)
    sizes = tuple(v.shape[0] for v in masters)
    gathered = gather_all(
        [v.astype(BF) for v in masters],
        tokens.reshape(-1, local, width),
        cotangent.reshape(-1, local, width),
        [v.astype(BF) for v in moments],
    )
    whole = [v.reshape(-1, width) for v in gathered[:4]]
    x, cot = (v.reshape(-1, width) for v in gathered[4:6])
    seq = x.shape[0]
    keep = lax.dynamic_index_in_dim(keep_mask.reshape(-1, seq), z, 0, keepdims=False)
    live = jnp.logical_or(keep != 0, jnp.arange(seq) < BUF)
    out, token_grad, grads, small = whole_image(
        x, cot, live, whole, head_bias, expand_bias, norm_gain, model_bias
    )
    count = small.shape[0]
    small = jnp.pad(small, ((0, -count % 8), (0, 0)))
    parts = [g.reshape(4, 2, 2, 2, s, width) for g, s in zip(grads, sizes)]
    total, small = reduce_all(parts, small)
    made = gram_all(total, gathered[6], out.reshape(-1, local, width), token_grad.reshape(-1, local, width), sizes)
    gram, hi, lo = made[:3]
    shards = [g.astype(F32) for g in made[3:7]]
    output = made[7].reshape(shape).astype(F32)
    token_grad = made[8].reshape(shape).astype(F32)
    done = polish(gram, hi, lo).reshape(4, -1, width)
    returned = return_all(done, sizes)
    head_total = small[0:2]
    units = expand_bias.shape[0] // width
    hidden_total = small[2 : 2 + units].reshape(expand_bias.shape)
    gain_total = small[2 + units : 4 + units]
    bias_total = small[4 + units : 8 + units]
    moments_new = [muon_decay * moment + gradient for gradient, moment in zip(shards, moments)]
    rows_scale = lax.axis_size("dp") * lax.axis_size("tensor")
    masters_new = [
        weight - rate * (weight.shape[0] * rows_scale / width) ** 0.5 * rows.astype(F32)
        for weight, rate, rows in zip(masters, muon_rates, returned)
    ]
    head = adam_step(head_total, head_first, head_second)
    hidden = adam_step(hidden_total, expand_first, expand_second)
    gain = adam_step(gain_total, gain_first, gain_second)
    bias = adam_step(bias_total, bias_first, bias_second)
    return (
        (output, token_grad)
        + tuple(shards)
        + (head_total, hidden_total, gain_total, bias_total)
        + tuple(moments_new)
        + tuple(masters_new)
        + tuple(v.astype(BF) for v in masters_new)
        + (head[0], hidden[0], gain[0], bias[0])
        + head[1:]
        + hidden[1:]
        + gain[1:]
        + bias[1:]
    )


def solution(mesh):
    placed = (
        P(None, "dp", "tensor", None),
        P(None, "dp", "tensor", None),
        P(None, "dp", None),
        P(("tensor", "dp"), None),
        P(("tensor", "dp"), None),
        P(("tensor", "dp"), None),
        P(("tensor", "dp"), None),
        P(("tensor", "dp"), None),
        P(("tensor", "dp"), None),
        P(("tensor", "dp"), None),
        P(("tensor", "dp"), None),
        P(),
        P(),
        P(),
        P(),
        P(),
        P(),
        P(),
        P(),
        P(),
        P(),
        P(),
        P(),
    )
    fast = mesh.shape["dp"] == 8 and mesh.shape["tensor"] == 4
    return jax.shard_map(
        per_device_fast if fast else per_device,
        mesh=mesh,
        in_specs=placed,
        out_specs=(
            P(None, "dp", "tensor", None),
            P(None, "dp", "tensor", None),
            P(("tensor", "dp"), None),
            P(("tensor", "dp"), None),
            P(("tensor", "dp"), None),
            P(("tensor", "dp"), None),
            P(),
            P(),
            P(),
            P(),
            P(("tensor", "dp"), None),
            P(("tensor", "dp"), None),
            P(("tensor", "dp"), None),
            P(("tensor", "dp"), None),
            P(("tensor", "dp"), None),
            P(("tensor", "dp"), None),
            P(("tensor", "dp"), None),
            P(("tensor", "dp"), None),
            P(("tensor", "dp"), None),
            P(("tensor", "dp"), None),
            P(("tensor", "dp"), None),
            P(("tensor", "dp"), None),
            P(),
            P(),
            P(),
            P(),
            P(),
            P(),
            P(),
            P(),
            P(),
            P(),
            P(),
            P(),
        ),
        check_vma=False,
    )
```

```python
import functools

import jax
import jax.numpy as jnp
from jax import lax
from jax.experimental import pallas as pl
from jax.experimental.pallas import tpu as pltpu
from jax.sharding import PartitionSpec as P

HEAD_DIM = 64
BUF = 64
NS_STEPS = 5
ADAM_STEP = 10


norm_eps = 1e-06
first_decay = 0.9
second_decay = 0.95
adam_rate = 0.05
adam_eps = 1e-08
muon_decay = 0.5
muon_rates = (1.0, 4.0, 1.0, 1.0)
frob_eps = 1e-07
coef_a = 3.4445
coef_b = -4.775
coef_c = 2.0315
masked_score = -1000000000.0


def precise(form, left, right):
    return jnp.einsum(form, left, right, precision=lax.Precision.HIGHEST)


def layer_norm(inputs_row, gain_row, shift_row):
    center = inputs_row - jnp.mean(inputs_row, axis=-1, keepdims=True)
    spread = jnp.mean(center * center, axis=-1, keepdims=True)
    return center * lax.rsqrt(spread + norm_eps) * gain_row + shift_row


def softmax_rows(scores):
    largest = jnp.max(scores, axis=-1, keepdims=True)
    powers = jnp.exp(scores - largest)
    return powers / jnp.sum(powers, axis=-1, keepdims=True)


def exact_gelu(inputs_row):
    return jax.nn.gelu(inputs_row, approximate=False)


def attend_weights(queries, keys_all, live_keys):
    scores = jnp.einsum(
        "iqhe,ikhe->ihqk", queries, keys_all, preferred_element_type=jnp.float32
    ) * HEAD_DIM ** (-0.5)
    scores = jnp.where(live_keys[:, None, None, :], scores, masked_score)
    return softmax_rows(scores)


def reduce_blocks(blocks):
    return (
        lax.psum_scatter(blocks[0], "dp", scatter_dimension=0, tiled=True),
        lax.psum_scatter(blocks[1], "dp", scatter_dimension=0, tiled=True),
        lax.psum_scatter(blocks[2], "dp", scatter_dimension=0, tiled=True),
        lax.psum_scatter(blocks[3], "dp", scatter_dimension=0, tiled=True),
    )


def gram_whole(matrix):
    model_width = matrix.shape[1]
    own_rows = model_width // lax.axis_size("dp")
    shard_rows = lax.psum_scatter(
        precise(
            "rm,rn->mn", lax.slice_in_dim(matrix, 0, own_rows * lax.axis_size("dp"), axis=1), matrix
        ),
        "dp",
        scatter_dimension=0,
        tiled=True,
    )
    return lax.all_gather(shard_rows, "dp", axis=0, tiled=True)


def newton_step(scaled, gram):
    product = precise("rk,kn->rn", scaled, gram)
    return coef_a * scaled + coef_b * product + coef_c * precise("rk,kn->rn", product, gram)


def adam_step(gradient, first, second):
    first_new = first_decay * first + (1.0 - first_decay) * gradient
    second_new = second_decay * second + (1.0 - second_decay) * gradient * gradient
    first_hat = first_new / (1.0 - first_decay**ADAM_STEP)
    second_hat = second_new / (1.0 - second_decay**ADAM_STEP)
    change = -adam_rate * first_hat / (jnp.sqrt(second_hat) + adam_eps)
    return (change, first_new, second_new)


def per_device(
    tokens,
    cotangent,
    keep_mask,
    intake,
    outlet,
    expand,
    shrink,
    intake_moment,
    outlet_moment,
    expand_moment,
    shrink_moment,
    head_bias,
    expand_bias,
    norm_gain,
    model_bias,
    head_first,
    head_second,
    expand_first,
    expand_second,
    gain_first,
    gain_second,
    bias_first,
    bias_second,
):
    micro_count, images, local_seq, model_width = tokens.shape
    seq_len = keep_mask.shape[2]
    tensor_size = lax.axis_size("tensor")
    tensor_index = lax.axis_index("tensor")
    head_cols = model_width // tensor_size
    local_heads = head_cols // HEAD_DIM
    hidden_cols = expand_bias.shape[0] // tensor_size
    head_start = tensor_index * head_cols
    hidden_start = tensor_index * hidden_cols
    query_bias = lax.dynamic_slice_in_dim(head_bias[0], head_start, head_cols, 0).reshape(
        local_heads, HEAD_DIM
    )
    value_bias = lax.dynamic_slice_in_dim(head_bias[1], head_start, head_cols, 0).reshape(
        local_heads, HEAD_DIM
    )
    mixed_bias = jnp.stack([query_bias, jnp.zeros_like(query_bias), value_bias], axis=1).reshape(
        3 * head_cols
    )
    hidden_bias = lax.dynamic_slice_in_dim(expand_bias, hidden_start, hidden_cols, 0)
    position = jnp.arange(seq_len)
    masters = (intake, outlet, expand, shrink)
    block_shapes = (
        (3 * head_cols, model_width),
        (head_cols, model_width),
        (hidden_cols, model_width),
        (hidden_cols, model_width),
    )
    totals = tuple((jnp.zeros(shape_one, jnp.float32) for shape_one in block_shapes))
    gain_grad = jnp.zeros((2, model_width), jnp.float32)
    bias_grad = jnp.zeros((4, model_width), jnp.float32)
    mixed_bias_grad = jnp.zeros((2, head_cols), jnp.float32)
    hidden_bias_grad = jnp.zeros((hidden_cols,), jnp.float32)
    outputs = []
    token_grads = []
    for micro_index in range(micro_count):
        intake_block, outlet_block, expand_block, shrink_block = (
            lax.all_gather(intake.astype(jnp.bfloat16), "dp", axis=0, tiled=True),
            lax.all_gather(outlet.astype(jnp.bfloat16), "dp", axis=0, tiled=True),
            lax.all_gather(expand.astype(jnp.bfloat16), "dp", axis=0, tiled=True),
            lax.all_gather(shrink.astype(jnp.bfloat16), "dp", axis=0, tiled=True),
        )
        token_rows = tokens[micro_index].astype(jnp.float32)
        live_keys = jnp.logical_or(keep_mask[micro_index] > 0, position[None, :] < BUF)
        first_local = layer_norm(token_rows, norm_gain[0], model_bias[0]).astype(jnp.bfloat16)
        first_norm = lax.all_gather(first_local, "tensor", axis=1, tiled=True)
        mixed_rows = (
            jnp.einsum("isd,rd->isr", first_norm, intake_block, preferred_element_type=jnp.float32)
            + mixed_bias
        )
        mixed_rows = mixed_rows.astype(jnp.bfloat16).reshape(
            images, seq_len, local_heads, 3, HEAD_DIM
        )
        queries = mixed_rows[:, :, :, 0]
        keys_all = mixed_rows[:, :, :, 1]
        values = mixed_rows[:, :, :, 2]
        attention = attend_weights(queries, keys_all, live_keys)
        attention_low = attention.astype(jnp.bfloat16)
        attended = jnp.einsum(
            "ihqk,ikhe->iqhe", attention_low, values, preferred_element_type=jnp.float32
        )
        attended = attended.reshape(images, seq_len, head_cols).astype(jnp.bfloat16)
        part_sum = jnp.einsum(
            "isc,cd->isd", attended, outlet_block, preferred_element_type=jnp.float32
        )
        middle = (
            token_rows
            + lax.psum_scatter(part_sum, "tensor", scatter_dimension=1, tiled=True)
            + model_bias[2]
        )
        second_local = layer_norm(middle, norm_gain[1], model_bias[1]).astype(jnp.bfloat16)
        second_norm = lax.all_gather(second_local, "tensor", axis=1, tiled=True)
        hidden = (
            jnp.einsum("isd,fd->isf", second_norm, expand_block, preferred_element_type=jnp.float32)
            + hidden_bias
        )
        active = exact_gelu(hidden).astype(jnp.bfloat16)
        part_two = jnp.einsum(
            "isf,fd->isd", active, shrink_block, preferred_element_type=jnp.float32
        )
        outputs.append(
            middle
            + lax.psum_scatter(part_two, "tensor", scatter_dimension=1, tiled=True)
            + model_bias[3]
        )
        cot_local = cotangent[micro_index]
        cot_rows = lax.all_gather(cot_local, "tensor", axis=1, tiled=True)
        shrink_block_grad = jnp.einsum(
            "isf,isd->fd", active, cot_rows, preferred_element_type=jnp.float32
        )
        active_grad = jnp.einsum(
            "isd,fd->isf", cot_rows, shrink_block, preferred_element_type=jnp.float32
        )
        gelu_value, gelu_back = jax.vjp(exact_gelu, hidden)
        hidden_grad = gelu_back(active_grad)[0].astype(jnp.bfloat16)
        hidden_bias_grad = hidden_bias_grad + jnp.sum(hidden_grad.astype(jnp.float32), axis=(0, 1))
        expand_block_grad = jnp.einsum(
            "isf,isd->fd", hidden_grad, second_norm, preferred_element_type=jnp.float32
        )
        second_part = jnp.einsum(
            "isf,fd->isd", hidden_grad, expand_block, preferred_element_type=jnp.float32
        )
        second_grad = lax.psum_scatter(second_part, "tensor", scatter_dimension=1, tiled=True)
        norm_value, norm_back = jax.vjp(layer_norm, middle, norm_gain[1], model_bias[1])
        middle_from_norm, gain_two_grad, shift_two_grad = norm_back(second_grad)
        cot_float = cot_local.astype(jnp.float32)
        middle_grad = cot_float + middle_from_norm
        branch_grad = middle_grad.astype(jnp.bfloat16)
        branch_rows = lax.all_gather(branch_grad, "tensor", axis=1, tiled=True)
        outlet_block_grad = jnp.einsum(
            "isc,isd->cd", attended, branch_rows, preferred_element_type=jnp.float32
        )
        attended_grad = jnp.einsum(
            "isd,cd->isc", branch_rows, outlet_block, preferred_element_type=jnp.float32
        )
        attended_grad = attended_grad.astype(jnp.bfloat16).reshape(
            images, seq_len, local_heads, HEAD_DIM
        )
        attention = attend_weights(queries, keys_all, live_keys)
        attention_low = attention.astype(jnp.bfloat16)
        values_grad = jnp.einsum(
            "ihqk,iqhe->ikhe", attention_low, attended_grad, preferred_element_type=jnp.float32
        )
        attention_grad = jnp.einsum(
            "iqhe,ikhe->ihqk", attended_grad, values, preferred_element_type=jnp.float32
        )
        score_grad = attention * (
            attention_grad - jnp.sum(attention_grad * attention, axis=-1, keepdims=True)
        )
        score_grad = score_grad.astype(jnp.bfloat16)
        queries_grad = jnp.einsum(
            "ihqk,ikhe->iqhe", score_grad, keys_all, preferred_element_type=jnp.float32
        ) * HEAD_DIM ** (-0.5)
        keys_grad = jnp.einsum(
            "ihqk,iqhe->ikhe", score_grad, queries, preferred_element_type=jnp.float32
        ) * HEAD_DIM ** (-0.5)
        mixed_grad = jnp.stack([queries_grad, keys_grad, values_grad], axis=3).astype(jnp.bfloat16)
        mixed_sums = jnp.sum(mixed_grad.astype(jnp.float32), axis=(0, 1))
        mixed_bias_grad = mixed_bias_grad + jnp.stack(
            [mixed_sums[:, 0].reshape(head_cols), mixed_sums[:, 2].reshape(head_cols)]
        )
        mixed_grad = mixed_grad.reshape(images, seq_len, 3 * head_cols)
        intake_block_grad = jnp.einsum(
            "isr,isd->rd", mixed_grad, first_norm, preferred_element_type=jnp.float32
        )
        first_part = jnp.einsum(
            "isr,rd->isd", mixed_grad, intake_block, preferred_element_type=jnp.float32
        )
        first_grad = lax.psum_scatter(first_part, "tensor", scatter_dimension=1, tiled=True)
        first_value, first_back = jax.vjp(layer_norm, token_rows, norm_gain[0], model_bias[0])
        token_from_norm, gain_one_grad, shift_one_grad = first_back(first_grad)
        token_grads.append(middle_grad + token_from_norm)
        gain_grad = gain_grad + jnp.stack([gain_one_grad, gain_two_grad])
        bias_grad = bias_grad + jnp.stack(
            [
                shift_one_grad,
                shift_two_grad,
                jnp.sum(branch_grad.astype(jnp.float32), axis=(0, 1)),
                jnp.sum(cot_float, axis=(0, 1)),
            ]
        )
        block_grads = (intake_block_grad, outlet_block_grad, expand_block_grad, shrink_block_grad)
        totals = tuple((total + block_one for total, block_one in zip(totals, block_grads)))
    shards = reduce_blocks(totals)
    head_full = lax.dynamic_update_slice_in_dim(
        jnp.zeros((2, model_width), jnp.float32), mixed_bias_grad, head_start, 1
    )
    hidden_full = lax.dynamic_update_slice_in_dim(
        jnp.zeros(expand_bias.shape, jnp.float32), hidden_bias_grad, hidden_start, 0
    )
    gain_total, bias_total, head_total, hidden_total = lax.psum(
        (gain_grad, bias_grad, head_full, hidden_full), ("dp", "tensor")
    )
    moments = (intake_moment, outlet_moment, expand_moment, shrink_moment)
    moments_new = [muon_decay * moment + gradient for gradient, moment in zip(shards, moments)]
    updates = [gradient + muon_decay * moment for gradient, moment in zip(shards, moments_new)]
    rows_max = max((update.shape[0] for update in updates))
    padded = jnp.stack(
        [jnp.pad(update, ((0, rows_max - update.shape[0]), (0, 0))) for update in updates]
    )
    spread = lax.all_to_all(padded, "tensor", split_axis=0, concat_axis=0, tiled=True)
    own_matrix = spread.reshape(tensor_size * rows_max, model_width)
    raw_gram = gram_whole(own_matrix)
    measure = jnp.sqrt(jnp.trace(raw_gram)) + frob_eps
    scaled = own_matrix / measure
    gram = raw_gram / (measure * measure)
    for step in range(NS_STEPS):
        if step > 0:
            gram = gram_whole(scaled)
        scaled = newton_step(scaled, gram)
    returned = lax.all_to_all(
        scaled.reshape(tensor_size, rows_max, model_width),
        "tensor",
        split_axis=0,
        concat_axis=0,
        tiled=True,
    )
    rows_scale = lax.axis_size("dp") * tensor_size
    masters_new = [
        weight
        - muon_rates[position_one]
        * (weight.shape[0] * rows_scale / weight.shape[1]) ** 0.5
        * returned[position_one, : weight.shape[0]]
        for position_one, weight in enumerate(masters)
    ]
    head_bias_change, head_first_new, head_second_new = adam_step(
        head_total, head_first, head_second
    )
    expand_bias_change, expand_first_new, expand_second_new = adam_step(
        hidden_total, expand_first, expand_second
    )
    norm_gain_change, gain_first_new, gain_second_new = adam_step(
        gain_total, gain_first, gain_second
    )
    model_bias_change, bias_first_new, bias_second_new = adam_step(
        bias_total, bias_first, bias_second
    )
    output = jnp.stack(outputs)
    token_grad = jnp.stack(token_grads)
    return (
        output,
        token_grad,
        shards[0],
        shards[1],
        shards[2],
        shards[3],
        head_total,
        hidden_total,
        gain_total,
        bias_total,
        moments_new[0],
        moments_new[1],
        moments_new[2],
        moments_new[3],
        masters_new[0],
        masters_new[1],
        masters_new[2],
        masters_new[3],
        masters_new[0].astype(jnp.bfloat16),
        masters_new[1].astype(jnp.bfloat16),
        masters_new[2].astype(jnp.bfloat16),
        masters_new[3].astype(jnp.bfloat16),
        head_bias_change,
        expand_bias_change,
        norm_gain_change,
        model_bias_change,
        head_first_new,
        head_second_new,
        expand_first_new,
        expand_second_new,
        gain_first_new,
        gain_second_new,
        bias_first_new,
        bias_second_new,
    )


MESH = pl.DeviceIdType.MESH
BF = jnp.bfloat16
F32 = jnp.float32
VMEM_LIMIT = 60 * 1024 * 1024


def place():
    d = lax.axis_index("dp")
    z = lax.axis_index("tensor")
    y, x, c = d // 4, (d // 2) % 2, d % 2
    return d, z, y, x, c


def partners(d, z, y, x, c):
    core = (d + 1 - 2 * c, z)
    xn = (d + 2 - 4 * x, z)
    yn = (d + 4 - 8 * y, z)
    zn = [(d, (z + k) % 4) for k in range(1, 4)]
    return core, xn, yn, zn


def greet(others):
    barrier = pltpu.get_barrier_semaphore()
    for other in others:
        pl.semaphore_signal(barrier, inc=1, device_id=other, device_id_type=MESH)
    pl.semaphore_wait(barrier, len(others))


def push(src, dst, sems, to):
    return pltpu.make_async_remote_copy(
        src_ref=src, dst_ref=dst, send_sem=sems[0], recv_sem=sems[1], device_id=to, device_id_type=MESH
    )


def gather_kernel(sizes, order, *refs):
    n = len(sizes)
    w = refs[:n]
    tok, cot = refs[n : n + 2]
    full = refs[n + 2 : 2 * n + 2]
    tok_all, cot_all = refs[2 * n + 2 : 2 * n + 4]
    z_s, z_r, loc, t_s, t_r, p_s, p_r = refs[2 * n + 4 :]
    d, z, y, x, c = place()
    core, xn, yn, zn = partners(d, z, y, x, c)
    greet([core, xn, yn] + zn)
    held = []
    inner = z * (3 - z) > 0

    def start(copy):
        copy.start()
        held.append(copy)
        return copy

    def source(j):
        return (z, z + 1 - 2 * (z % 2), 2 - z // 2, 3 - 3 * (z // 2))[j]

    def along(m, j, go):
        slot = full[m].at[source(j), y, x, c]
        if j == 0:

            @pl.when(z < 3)
            def _():
                go(push(w[m], slot, (z_s.at[m, 0], z_r.at[m, z]), (d, z + 1)))

            @pl.when(z > 0)
            def _():
                go(push(w[m], slot, (z_s.at[m, 1], z_r.at[m, z]), (d, z - 1)))

        else:
            beyond = 3 - z if j == 1 else 3 * (z - 1)

            @pl.when(inner)
            def _():
                go(push(slot, slot, (z_s.at[m, 1 + j], z_r.at[m, source(j)]), (d, beyond)))

    locals_ = []
    for m in range(n):
        copy = pltpu.make_async_copy(w[m], full[m].at[z, y, x, c], loc.at[m])
        copy.start()
        locals_.append(copy)
    for i, (a, b) in enumerate(((tok, tok_all), (cot, cot_all))):
        copy = pltpu.make_async_copy(a.at[z], b.at[z], loc.at[n + i])
        copy.start()
        locals_.append(copy)

    def rows_push(i, a, b):
        for k in range(1, 4):
            start(push(a.at[(z + k) % 4], b.at[z], (t_s.at[i, k - 1], t_r.at[i, k - 1]), zn[k - 1]))

    def sem(i, stage):
        return (p_s.at[stage, i], p_r.at[stage, i])

    def one(i):
        m, k = order[i]
        h = sizes[m] // 2
        s = source(k)
        if k > 0:
            slot = full[m].at[s, y, x, c]
            push(slot, slot, (z_s.at[m, 1 + k], z_r.at[m, s]), core).wait_recv()
            along(m, k, lambda copy: copy.start())
        else:
            locals_[m].wait()
        a = full[m].at[s, y, x, c, pl.ds(0, h)]
        b = full[m].at[s, y, x, c, pl.ds(h, h)]
        start(push(a, a, sem(i, 0), xn))
        start(push(b, b, sem(i, 1), yn))

    def two(i):
        m, k = order[i]
        h = sizes[m] // 2
        s = source(k)
        a = full[m].at[s, y, 1 - x, c, pl.ds(0, h)]
        push(a, a, sem(i, 0), xn).wait_recv()
        a = full[m].at[s, y, :, c, pl.ds(0, h)]
        start(push(a, a, sem(i, 2), yn))
        b = full[m].at[s, 1 - y, x, c, pl.ds(h, h)]
        push(b, b, sem(i, 1), yn).wait_recv()
        b = full[m].at[s, :, x, c, pl.ds(h, h)]
        start(push(b, b, sem(i, 3), xn))

    def three(i):
        m, k = order[i]
        h = sizes[m] // 2
        s = source(k)
        a = full[m].at[s, 1 - y, :, c, pl.ds(0, h)]
        push(a, a, sem(i, 2), yn).wait_recv()
        b = full[m].at[s, :, 1 - x, c, pl.ds(h, h)]
        push(b, b, sem(i, 3), xn).wait_recv()
        e = full[m].at[s, :, :, c]
        start(push(e, e, sem(i, 4), core))

    count = len(order)
    go = lambda copy: copy.start()
    along(0, 0, go)
    along(1, 0, go)
    for i in range(count + 2):
        if i < count:
            one(i)
        if i == 0:
            rows_push(0, tok, tok_all)
            along(2, 0, go)
        if i == 4:
            along(3, 0, go)
        if i == 6:
            rows_push(1, cot, cot_all)
        if 1 <= i <= count:
            two(i - 1)
        if i >= 2:
            three(i - 2)
    for i in range(count):
        m, k = order[i]
        e = full[m].at[source(k), :, :, 1 - c]
        push(e, e, sem(i, 4), core).wait_recv()
    for i, b in enumerate((tok_all, cot_all)):
        locals_[n + i].wait()
        for k in range(1, 4):
            slot = b.at[(z + 4 - k) % 4]
            push(slot, slot, (t_s.at[i, k - 1], t_r.at[i, k - 1]), zn[k - 1]).wait_recv()
    for copy in held:
        copy.wait_send()
    for m in range(n):
        for j in range(4):
            along(m, j, lambda copy: copy.wait_send())


def gather_all(weights, tok, cot):
    sizes = tuple(v.shape[0] for v in weights)
    width = weights[0].shape[1]
    order = [(m, 0) for m in range(4)] + [(m, k) for m in range(4) for k in (1, 2, 3)]
    count = len(order)
    anyspace = pl.BlockSpec(memory_space=pl.ANY)
    dma = pltpu.SemaphoreType.DMA
    return pl.pallas_call(
        functools.partial(gather_kernel, sizes, order),
        out_shape=[jax.ShapeDtypeStruct((4, 2, 2, 2, s, width), BF) for s in sizes]
        + [jax.ShapeDtypeStruct(tok.shape, BF), jax.ShapeDtypeStruct(cot.shape, BF)],
        in_specs=[anyspace] * (len(sizes) + 2),
        out_specs=[anyspace] * (len(sizes) + 2),
        scratch_shapes=[
            dma((4, 5)),
            dma((4, 4)),
            dma((6,)),
            dma((2, 3)),
            dma((2, 3)),
            dma((5, count)),
            dma((5, count)),
        ],
        compiler_params=pltpu.CompilerParams(collective_id=1, has_side_effects=True, vmem_limit_bytes=8 << 20),
    )(*weights, tok, cot)


def add_rows(dst, src, lead, rows):
    step = 16

    def body(i, carry):
        j, r = i // (rows // step), (i % (rows // step)) * step
        at = pl.ds(pl.multiple_of(r, step), step)
        dst[j, at] = dst[j, at] + src[j, at]
        return carry

    lax.fori_loop(0, lead * (rows // step), body, 0)


PLANES = (1, 0, 2, 3)


LINK = 93.5e3


def plan(blocks, sizes, order, free_after, width):
    todo = list(blocks)
    done = []
    events = []
    link = {"x": 0.0, "y": 0.0, "z": 0.0}
    now = 0.0
    finished = set()

    def carry(lane, start, rows):
        begin = max(start, link[lane])
        link[lane] = begin + rows * width * 2 * 2 / LINK
        return link[lane] + 1.5

    def emit(step):
        nonlocal now
        kind, i = step[0], step[1]
        done.append(step)
        finished.add(step)
        s = sizes[order[i][0]]
        if kind == "one":
            now += s / 128 * 1.0
            ready = max(carry("y", now, s), carry("x", now, s))
            events.append((ready, ("two", i)))
        elif kind == "two":
            now += s / 128 * 0.6
            ready = max(carry("x", now, s / 2), carry("y", now, s / 2))
            events.append((ready, ("three", i)))
        elif kind == "three":
            now += s / 128 * 0.3
            ready = carry("z", now, s)
            events.append((ready, ("four", i)))
            events.append((ready + 0.001, ("fourb", i)))
        elif kind == "four":
            finished.discard(step)
            now += 0.2
        elif kind == "fourb":
            now += 0.2

    while todo or events:
        events.sort()
        if events and events[0][0] <= now:
            at, step = events.pop(0)
            if step[0] == "fourb":
                events.append((now + 3.0, ("fourc", step[1])))
                events.sort()
                continue
            emit(step)
            continue
        if todo:
            name, us, piece = todo[0]
            blocked = piece is not None and piece >= free_after and ("one", piece - free_after) not in finished
            if not blocked:
                todo.pop(0)
                done.append(("block", name))
                now += us
                if piece is not None:
                    done.append(("push", piece))
                    events.append((now + 3.0, ("one", piece)))
                continue
        now = max(now, events[0][0])
    return done


def backward_kernel(sizes, order, *refs):
    n = 4
    small_count = 16
    (shrink, expand, outlet, intake, active, slope, middle, mixed, attended, second, first, x_in, cot) = refs[:13]
    norm_gain, live = refs[13:15]
    mom = refs[15:19]
    total, small_out, mom_all, token_grad = refs[19:23]
    refs = refs[23:]
    own, mid, end, far = (refs[i * n : i * n + n] for i in range(4))
    refs = refs[4 * n :]
    (made, act, slo, wbuf, obuf, hgrad, wide, mgrad, branch, agrad) = refs[:10]
    small, s_got, s_acc, s_z = refs[10:14]
    loc, c_s, c_r, p_s, p_r, f_s, f_r, q_s, q_r, m_s, m_r, w_l = refs[14:]
    d, z, y, x, c = place()
    core, xn, yn, zn = partners(d, z, y, x, c)
    greet([core, xn, yn] + zn)
    seq, width = cot.shape
    held = []
    top = max(sizes)

    def start(copy):
        copy.start()
        held.append(copy)

    def sem(i, stage):
        return (p_s.at[stage, i], p_r.at[stage, i])

    slots = made.shape[0]

    def core_push(i):
        m, k = order[i]
        return push(
            made.at[i % slots, :, :, 1 - c, pl.ds(0, sizes[m])], own[m].at[k], (c_s.at[i], c_r.at[i]), core
        )

    def one(i):
        m, k = order[i]
        s, h = sizes[m], sizes[m] // 2
        core_push(i).wait_recv()
        for j in range(2):
            for l in range(2):
                add_rows(own[m].at[k, j, pl.ds(l, 1)], made.at[i % slots, j, l, pl.ds(c, 1)], 1, s)
        start(push(own[m].at[k, 1 - y, :, pl.ds(0, h)], mid[m].at[k, 0], sem(i, 0), yn))
        start(push(own[m].at[k, :, 1 - x, pl.ds(h, h)], mid[m].at[k, 1], sem(i, 1), xn))

    def two(i):
        m, k = order[i]
        h = sizes[m] // 2
        push(mid[m].at[k, 0], mid[m].at[k, 0], sem(i, 0), yn).wait_recv()
        add_rows(own[m].at[k, y, :, pl.ds(0, h)], mid[m].at[k, 0], 2, h)
        start(push(own[m].at[k, y, 1 - x, pl.ds(0, h)], end[m].at[k, pl.ds(0, h)], sem(i, 2), xn))
        push(mid[m].at[k, 1], mid[m].at[k, 1], sem(i, 1), xn).wait_recv()
        add_rows(own[m].at[k, :, x, pl.ds(h, h)], mid[m].at[k, 1], 2, h)
        start(push(own[m].at[k, 1 - y, x, pl.ds(h, h)], end[m].at[k, pl.ds(h, h)], sem(i, 3), yn))

    def hop(i, p, go):
        m, k = order[i]
        side, to = (0, p + 1) if p < PLANES[m] else (1, p - 1)
        at = side if PLANES[m] in (1, 2) else 0
        go(push(own[m].at[k, y, x], far[m].at[at, k], (f_s.at[m, k], f_r.at[m, k, side]), (d, to)))

    def came(m, k, side):
        slot = far[m].at[side if PLANES[m] in (1, 2) else 0, k]
        push(slot, slot, (f_s.at[m, k], f_r.at[m, k, side]), core).wait_recv()

    def three(i):
        m, k = order[i]
        s, h = sizes[m], sizes[m] // 2
        push(end[m].at[k, pl.ds(0, h)], end[m].at[k, pl.ds(0, h)], sem(i, 2), xn).wait_recv()
        push(end[m].at[k, pl.ds(h, h)], end[m].at[k, pl.ds(h, h)], sem(i, 3), yn).wait_recv()
        add_rows(own[m].at[k, pl.ds(y, 1), x], end[m].at[pl.ds(k, 1)], 1, s)
        for p in (0, 3):
            if p != PLANES[m]:

                @pl.when(z == p)
                def _(p=p):
                    hop(i, p, lambda copy: copy.start())

    def four(i, far_hop):
        m, k = order[i]
        for p in (1, 2):
            below = p < PLANES[m]
            if p == PLANES[m] or far_hop != (p if below else 3 - p):
                continue

            @pl.when(z == p)
            def _(p=p, below=below):
                side = 0 if below else 1
                came(m, k, side)
                at = side if PLANES[m] in (1, 2) else 0
                add_rows(own[m].at[k, pl.ds(y, 1), x], far[m].at[at, pl.ds(k, 1)], 1, sizes[m])
                hop(i, p, lambda copy: copy.start())

    def five(i):
        m, k = order[i]
        s, p = sizes[m], PLANES[m]
        sides = [v for v in (0, 1) if p != 3 * v]

        @pl.when(z == p)
        def _():
            for side in sides:
                came(m, k, side)

            def body(r, carry):
                at = pl.ds(pl.multiple_of(r * 16, 16), 16)
                acc = own[m][k, y, x, at].astype(F32)
                for side in range(len(sides)):
                    acc = acc + far[m][side, k, at].astype(F32)
                total[k, at] = acc
                return carry

            lax.fori_loop(0, s // 16, body, 0)
            if s < total.shape[1]:
                total[k, pl.ds(s, total.shape[1] - s)] = jnp.zeros((total.shape[1] - s, width), F32)

    def small_step(stage):
        to = (core, xn, yn)
        if stage > 0:
            here = s_got.at[stage - 1]
            push(here, here, (q_s.at[stage - 1], q_r.at[stage - 1]), to[stage - 1]).wait_recv()
            s_acc[stage] = s_acc[stage - 1] + s_got[stage - 1]
        else:
            s_acc[0] = small[...]
        if stage < 3:
            start(push(s_acc.at[stage], s_got.at[stage], (q_s.at[stage], q_r.at[stage]), to[stage]))
        else:
            s_z[z] = s_acc[3]
            for k in range(1, 4):
                start(push(s_acc.at[3], s_z.at[z], (q_s.at[2 + k], q_r.at[2 + k]), zn[k - 1]))

    def moments(first):
        for t in range(n):
            p = PLANES[t]
            here = mom_all.at[z, pl.ds(0, sizes[t])]

            @pl.when(z == p)
            def _(t=t, p=p, here=here):
                copy = pltpu.make_async_copy(mom[t], here, loc.at[0])
                if first:
                    copy.start()
                else:
                    copy.wait()
                    for k in range(1, 4):
                        s = (p + k) % 4
                        there = mom_all.at[s, pl.ds(0, sizes[t])]
                        push(mom[t], there, (m_s.at[t], m_r.at[s]), (d, s)).wait_recv()

            @pl.when(z != p)
            def _(t=t, p=p, here=here):
                copy = push(mom[t], here, (m_s.at[t], m_r.at[z]), (d, p))
                if first:
                    copy.start()
                else:
                    copy.wait_send()

    unit = wbuf.shape[1]
    count_units = shrink.shape[0] // unit

    def load(u):
        at = pl.ds(u * unit, unit)
        return [
            pltpu.make_async_copy(shrink.at[at], wbuf.at[u % 2], w_l.at[0, u % 2]),
            pltpu.make_async_copy(expand.at[at], wbuf.at[2 + u % 2], w_l.at[1, u % 2]),
            pltpu.make_async_copy(active.at[:, at], act.at[u % 2], w_l.at[2, u % 2]),
            pltpu.make_async_copy(slope.at[:, at], slo.at[u % 2], w_l.at[3, u % 2]),
        ]

    def load_outlet():
        return pltpu.make_async_copy(outlet, obuf, loc.at[1])

    def load_intake(v):
        return pltpu.make_async_copy(intake.at[pl.ds(v * unit, unit)], wbuf.at[v % 4], w_l.at[4, v % 4])

    tdims = (((0,), (0,)), ((), ()))
    ndims = (((1,), (1,)), ((), ()))

    def mlp_one(u):
        k, half = u // 2, u % 2
        if u == 0:
            for copy in load(0):
                copy.start()
        if u + 1 < count_units:
            for copy in load(u + 1):
                copy.start()
        for copy in load(u):
            copy.wait()
        i = 2 * k

        def body(j, carry):
            cols = pl.ds(pl.multiple_of(j * 2 * top, 2 * top), 2 * top)
            g = lax.dot_general(act[u % 2, :, cols], cot[...], tdims, preferred_element_type=F32)
            made[i % slots, half, j] = g.astype(BF).reshape(2, top, width)
            return carry

        lax.fori_loop(0, unit // (2 * top), body, 0)

        def grad(j, carry):
            rows = pl.ds(pl.multiple_of(j * 256, 256), 256)
            to = pl.ds(pl.multiple_of(j * 256 + half * unit, 256), 256)
            g = lax.dot_general(cot[...], wbuf[u % 2, rows], ndims, preferred_element_type=F32)
            hg = (g * slo[u % 2, :, rows]).astype(BF)
            hgrad[:, to] = hg
            small[pl.ds(2 + k, 1), to] = jnp.sum(hg.astype(F32), axis=0, keepdims=True)
            return carry

        lax.fori_loop(0, unit // 256, grad, 0)

        def back(j, carry):
            cols = pl.ds(pl.multiple_of(j * 256, 256), 256)
            g = jnp.dot(hgrad[:, pl.ds(half * unit, unit)], wbuf[2 + u % 2, :, cols], preferred_element_type=F32)
            if u == 0:
                wide[:, cols] = g
            else:
                wide[:, cols] += g
            return carry

        lax.fori_loop(0, width // 256, back, 0)

    def mlp_two(k):
        i = 2 * k + 1

        def body(j, carry):
            cols = pl.ds(pl.multiple_of(j * 2 * top, 2 * top), 2 * top)
            g = lax.dot_general(hgrad[:, cols], second[...], tdims, preferred_element_type=F32)
            made[i % slots, j // 2, j % 2] = g.astype(BF).reshape(2, top, width)
            return carry

        lax.fori_loop(0, 4, body, 0)

    chunk = 64

    def norm_block(index, v_of, extra):
        gain = norm_gain[pl.ds(index, 1)]

        def body(i, carry):
            at = pl.ds(pl.multiple_of(i * chunk, chunk), chunk)
            v = v_of(at)
            center = v - jnp.mean(v, axis=-1, keepdims=True)
            r = lax.rsqrt(jnp.mean(center * center, axis=-1, keepdims=True) + norm_eps)
            nrm = center * r
            w = wide[at]
            u = w * gain
            down = r * (u - jnp.mean(u, axis=-1, keepdims=True) - nrm * jnp.mean(u * nrm, axis=-1, keepdims=True))
            sums = extra(at, down)
            new = [jnp.sum(w * nrm, axis=0, keepdims=True), jnp.sum(w, axis=0, keepdims=True)] + sums
            return tuple(a + b for a, b in zip(carry, new))

        zero = jnp.zeros((1, width), F32)
        out = lax.fori_loop(0, seq // chunk, body, (zero,) * (4 if index else 2))
        small[pl.ds(6 + index, 1)] = out[0]
        small[pl.ds(8 + index, 1)] = out[1]
        if index:
            small[pl.ds(10, 1)] = out[2]
            small[pl.ds(11, 1)] = out[3]

    def second_norm_back():
        load_outlet().start()
        for v in range(4):
            load_intake(v).start()

        def extra(at, down):
            g = cot[at].astype(F32)
            m = g + down
            mgrad[at] = m
            low = m.astype(BF)
            branch[at] = low
            return [jnp.sum(low.astype(F32), axis=0, keepdims=True), jnp.sum(g, axis=0, keepdims=True)]

        norm_block(1, lambda at: middle[at], extra)

    def outlet_piece(k):
        i = 8 + k
        cols = pl.ds(k * 8 * sizes[1], 8 * sizes[1])
        g = lax.dot_general(attended[:, cols], branch[...], tdims, preferred_element_type=F32)
        made[i % slots, :, :, :, pl.ds(0, sizes[1])] = g.astype(BF).reshape(2, 2, 2, sizes[1], width)

    def attended_back():
        load_outlet().wait()

        def body(j, carry):
            rows = pl.ds(pl.multiple_of(j * 256, 256), 256)
            g = lax.dot_general(branch[...], obuf[rows], ndims, preferred_element_type=F32)
            agrad[:, rows] = g.astype(BF)
            return carry

        lax.fori_loop(0, width // 256, body, 0)

    scale = HEAD_DIM ** (-0.5)

    def heads(first_pair, pairs):
        mask = live[...] > 0.0

        def body(p, carry):
            at = pl.ds(pl.multiple_of(p * 6 * HEAD_DIM, 6 * HEAD_DIM), 6 * HEAD_DIM)
            both = mixed[:, at]
            ag_both = agrad[:, pl.ds(pl.multiple_of(p * 2 * HEAD_DIM, 2 * HEAD_DIM), 2 * HEAD_DIM)]
            parts, sums = [], []
            for e in range(2):
                q, k, v = (both[:, (3 * e + b) * HEAD_DIM : (3 * e + b + 1) * HEAD_DIM] for b in range(3))
                ag = ag_both[:, e * HEAD_DIM : (e + 1) * HEAD_DIM]
                s = lax.dot_general(q, k, ndims, preferred_element_type=F32) * scale
                s = jnp.where(mask, s, masked_score)
                s = jnp.exp(s - jnp.max(s, axis=-1, keepdims=True))
                pr = s / jnp.sum(s, axis=-1, keepdims=True)
                vg = lax.dot_general(pr.astype(BF), ag, tdims, preferred_element_type=F32)
                dp = lax.dot_general(ag, v, ndims, preferred_element_type=F32)
                ds = (pr * (dp - jnp.sum(dp * pr, axis=-1, keepdims=True))).astype(BF)
                qg = jnp.dot(ds, k, preferred_element_type=F32) * scale
                kg = lax.dot_general(ds, q, tdims, preferred_element_type=F32) * scale
                parts += [qg.astype(BF), kg.astype(BF), vg.astype(BF)]
                sums.append((jnp.sum(parts[-3].astype(F32), 0, keepdims=True), jnp.sum(parts[-1].astype(F32), 0, keepdims=True)))
            mixed[:, at] = jnp.concatenate(parts, axis=1)
            to = pl.ds(pl.multiple_of(p * 2 * HEAD_DIM, 2 * HEAD_DIM), 2 * HEAD_DIM)
            small[pl.ds(0, 1), to] = jnp.concatenate([sums[0][0], sums[1][0]], axis=1)
            small[pl.ds(1, 1), to] = jnp.concatenate([sums[0][1], sums[1][1]], axis=1)
            return carry

        lax.fori_loop(first_pair, first_pair + pairs, body, 0)

    def intake_piece(k):
        i = 12 + k
        rows = 4 * sizes[0]

        def body(j, carry):
            cols = pl.ds(pl.multiple_of((2 * k + j) * rows, rows), rows)
            g = lax.dot_general(mixed[:, cols], first[...], tdims, preferred_element_type=F32)
            made[i % slots, j, :, :, pl.ds(0, sizes[0])] = g.astype(BF).reshape(2, 2, sizes[0], width)
            return carry

        lax.fori_loop(0, 2, body, 0)

    def first_back(v):
        load_intake(v).wait()

        def body(j, carry):
            cols = pl.ds(pl.multiple_of(j * 256, 256), 256)
            g = jnp.dot(mixed[:, pl.ds(v * unit, unit)], wbuf[v % 4, :, cols], preferred_element_type=F32)
            if v == 0:
                wide[:, cols] = g
            else:
                wide[:, cols] += g
            return carry

        lax.fori_loop(0, width // 256, body, 0)
        if v + 4 < intake.shape[0] // unit:
            load_intake(v + 4).start()

    def first_norm_back():
        def extra(at, down):
            token_grad[at] = (mgrad[at] + down).astype(BF)
            return []

        norm_block(0, lambda at: x_in[at].astype(F32), extra)

    work = {}
    blocks = []

    def block(name, us, piece, fn):
        work[name] = fn
        blocks.append((name, us, piece))

    for k in range(4):
        block(("m", 2 * k), 3.0, None, functools.partial(mlp_one, 2 * k))
        block(("m", 2 * k + 1), 3.0, 2 * k, functools.partial(mlp_one, 2 * k + 1))
        block(("e", k), 1.5, 2 * k + 1, functools.partial(mlp_two, k))
    block("n2", 3.0, None, second_norm_back)
    for k in range(4):
        block(("o", k), 0.5, 8 + k, functools.partial(outlet_piece, k))
    block("ab", 1.5, None, attended_back)
    for k in range(4):
        block(("h", k), 7.0, None, functools.partial(heads, 2 * k, 2))
        block(("i", k), 1.2, 12 + k, functools.partial(intake_piece, k))
    for v in range(intake.shape[0] // unit):
        block(("f", v), 0.8, None, functools.partial(first_back, v))
    block("n1", 3.0, None, first_norm_back)
    block("s0", 0.2, None, functools.partial(small_step, 0))

    small[pl.ds(12, 4)] = jnp.zeros((4, width), F32)
    moments(True)
    steps = plan(blocks, sizes, order, slots, width)
    pushed = {}
    stage = 1
    for step in steps:
        kind = step[0]
        if kind == "block":
            name = step[1]
            piece = {b[0]: b[2] for b in blocks}[name]
            first_piece = piece if piece is not None else (2 * (name[1] // 2) if name[0] == "m" else None)
            if first_piece is not None and first_piece - slots in pushed:
                pushed.pop(first_piece - slots).wait_send()
            work[name]()
        elif kind == "push":
            pushed[step[1]] = core_push(step[1])
            pushed[step[1]].start()
        elif kind == "one":
            one(step[1])
        elif kind == "two":
            two(step[1])
        elif kind == "three":
            three(step[1])
        elif kind == "four":
            four(step[1], 1)
        elif kind == "fourc":
            four(step[1], 2)
    for s in (1, 2, 3):
        small_step(s)
    for i in range(len(order)):
        five(i)
    for k in range(1, 4):
        slot = s_z.at[(z + 4 - k) % 4]
        push(slot, slot, (q_s.at[2 + k], q_r.at[2 + k]), zn[k - 1]).wait_recv()
    small_out[...] = s_z[0] + s_z[1] + s_z[2] + s_z[3]
    moments(False)
    for copy in pushed.values():
        copy.wait_send()
    for copy in held:
        copy.wait_send()
    for i in range(len(order)):
        for p in range(4):
            if p != PLANES[order[i][0]]:

                @pl.when(z == p)
                def _(i=i, p=p):
                    hop(i, p, lambda copy: copy.wait_send())


def backward_all(weights, saved, norm_gain, live, moms, sizes):
    intake, outlet, expand, shrink = weights
    active, slope, middle, mixed, attended, second, first, x, cot = saved
    seq, width = cot.shape
    top = max(sizes)
    order = []
    for k in range(4):
        order += [(3, k), (2, k)]
    order += [(1, k) for k in range(4)] + [(0, k) for k in range(4)]
    count = len(order)
    anyspace = pl.BlockSpec(memory_space=pl.ANY)
    vmem = pl.BlockSpec(memory_space=pltpu.VMEM)
    dma = pltpu.SemaphoreType.DMA
    unit = 512
    return pl.pallas_call(
        functools.partial(backward_kernel, sizes, order),
        out_shape=[
            jax.ShapeDtypeStruct((4, top, width), F32),
            jax.ShapeDtypeStruct((16, width), F32),
            jax.ShapeDtypeStruct((4, top, width), BF),
            jax.ShapeDtypeStruct((seq, width), BF),
        ],
        in_specs=[anyspace] * 6 + [vmem] * 9 + [anyspace] * 4,
        out_specs=[vmem, vmem, anyspace, vmem],
        scratch_shapes=[pltpu.VMEM((4, 2, 2, s, width), BF) for s in sizes]
        + [pltpu.VMEM((4, 2, 2, s // 2, width), BF) for s in sizes]
        + [pltpu.VMEM((4, s, width), BF) for s in sizes]
        + [pltpu.VMEM((2 if p in (1, 2) else 1, 4, s, width), BF) for s, p in zip(sizes, PLANES)]
        + [
            pltpu.VMEM((3, 2, 2, 2, top, width), BF),
            pltpu.VMEM((2, seq, unit), BF),
            pltpu.VMEM((2, seq, unit), F32),
            pltpu.VMEM((4, unit, width), BF),
            pltpu.VMEM((width, width), BF),
            pltpu.VMEM((seq, width), BF),
            pltpu.VMEM((seq, width), F32),
            pltpu.VMEM((seq, width), F32),
            pltpu.VMEM((seq, width), BF),
            pltpu.VMEM((seq, width), BF),
            pltpu.VMEM((16, width), F32),
            pltpu.VMEM((3, 16, width), F32),
            pltpu.VMEM((4, 16, width), F32),
            pltpu.VMEM((4, 16, width), F32),
            dma((2,)),
            dma((count,)),
            dma((count,)),
            dma((4, count)),
            dma((4, count)),
            dma((4, 4)),
            dma((4, 4, 2)),
            dma((6,)),
            dma((6,)),
            dma((4,)),
            dma((4,)),
            dma((5, 4)),
        ],
        compiler_params=pltpu.CompilerParams(collective_id=2, has_side_effects=True, vmem_limit_bytes=VMEM_LIMIT),
    )(shrink, expand, outlet, intake, active, slope, middle, mixed, attended, second, first, x, cot, norm_gain, live, *moms)


def gram_kernel(sizes, *refs):
    n = len(sizes)
    total, mom, outp, tokg = refs[:4]
    gram, upd, upl = refs[4:7]
    grads = refs[7 : 7 + n]
    outp_all, tokg_all = refs[7 + n : 9 + n]
    low_g, part, r_core, r_one, r_two, g_s, g_r, a_s, a_r, o_s, o_r, loc = refs[9 + n :]
    d, z, y, x, c = place()
    core, xn, yn, zn = partners(d, z, y, x, c)
    greet([core, xn, yn] + zn)
    held = []

    def start(copy):
        copy.start()
        held.append(copy)

    width = total.shape[2]
    top = total.shape[1]
    def cast(i, carry):
        at = pl.ds(pl.multiple_of((i % (top // 16)) * 16, 16), 16)
        low_g[i // (top // 16), at] = total[i // (top // 16), at].astype(BF)
        return carry

    lax.fori_loop(0, 4 * (top // 16), cast, 0)
    for t in range(n):
        p = PLANES[t]

        @pl.when(z == p)
        def _(t=t, p=p):
            s = sizes[t]
            for k in range(1, 4):
                v = (p + k) % 4
                push(low_g.at[v, pl.ds(0, s)], grads[t], (g_s.at[v], g_r.at[t]), (d, v)).start()
            pltpu.make_async_copy(low_g.at[p, pl.ds(0, s)], grads[t], loc.at[0]).start()

    height = 0
    for t in range(n):
        height = jnp.where(z == PLANES[t], sizes[t], height)

    def make(i, carry):
        k, r = i // (top // 16), (i % (top // 16)) * 16
        at = pl.ds(pl.multiple_of(r, 16), 16)
        g = total[k, at]
        u = g + muon_decay * (muon_decay * mom[k, at].astype(F32) + g)
        row = lax.broadcasted_iota(jnp.int32, u.shape, 0) + r
        u = jnp.where(row < height, u, 0.0)
        hi = u.astype(BF)
        to = pl.ds(pl.multiple_of(i * 16, 16), 16)
        upd[to] = hi
        upl[to] = (u - hi.astype(F32)).astype(BF)
        return carry

    lax.fori_loop(0, 4 * (top // 16), make, 0)
    tile = 256
    dims = (((0,), (0,)), ((), ()))

    def mul(i, carry):
        at = pl.ds(pl.multiple_of(i * tile, tile), tile)
        hi, lo = upd[:, at], upl[:, at]
        acc = lax.dot_general(upd[...], hi, dims, preferred_element_type=F32)
        acc = acc + lax.dot_general(upd[...], lo, dims, preferred_element_type=F32)
        part[:, at] = acc + lax.dot_general(upl[...], hi, dims, preferred_element_type=F32)
        return carry

    lax.fori_loop(0, width // tile, mul, 0)

    def add(dst, r0, src, rows, into=None, r1=None):
        def body(i, carry):
            at = pl.ds(pl.multiple_of(r0 + i * 8, 8), 8)
            v = dst[at] + src[pl.ds(pl.multiple_of(i * 8, 8), 8)]
            if into is None:
                dst[at] = v
            else:
                into[at] = v
            return carry

        lax.fori_loop(0, rows // 8, body, 0)

    half, quarter, eighth = width // 2, width // 8, width // 16

    def sem(i):
        return (a_s.at[i], a_r.at[i])

    def rows(ref, r, count):
        return ref.at[pl.ds(pl.multiple_of(r, 64), count)]

    start(push(rows(part, (1 - c) * half, half), r_core, sem(0), core))
    push(r_core, r_core, sem(0), core).wait_recv()
    base_a = c * half
    base_b = c * half + half // 2
    add(part, base_a, r_core, half)
    start(push(rows(part, base_a + (1 - y) * quarter, quarter), r_one.at[0], sem(1), yn))
    start(push(rows(part, base_b + (1 - x) * quarter, quarter), r_one.at[1], sem(2), xn))
    for i, (a, b) in enumerate(((outp, outp_all), (tokg, tokg_all))):
        pltpu.make_async_copy(a.at[z], b.at[z], loc.at[1 + i]).start()
        for k in range(1, 4):
            start(push(a.at[(z + k) % 4], b.at[z], (o_s.at[i, k - 1], o_r.at[i, k - 1]), zn[k - 1]))
    push(r_one.at[0], r_one.at[0], sem(1), yn).wait_recv()
    mine_a = base_a + y * quarter
    add(part, mine_a, r_one.at[0], quarter)
    start(push(rows(part, mine_a + (1 - x) * eighth, eighth), r_two.at[0], sem(3), xn))
    push(r_one.at[1], r_one.at[1], sem(2), xn).wait_recv()
    mine_b = base_b + x * quarter
    add(part, mine_b, r_one.at[1], quarter)
    start(push(rows(part, mine_b + (1 - y) * eighth, eighth), r_two.at[1], sem(4), yn))
    push(r_two.at[0], r_two.at[0], sem(3), xn).wait_recv()
    own_a = mine_a + x * eighth
    add(part, own_a, r_two.at[0], eighth, gram)
    start(push(rows(gram, own_a, eighth), rows(gram, own_a, eighth), sem(5), xn))
    push(r_two.at[1], r_two.at[1], sem(4), yn).wait_recv()
    own_b = mine_b + y * eighth
    add(part, own_b, r_two.at[1], eighth, gram)
    start(push(rows(gram, own_b, eighth), rows(gram, own_b, eighth), sem(6), yn))
    got_a = rows(gram, mine_a + (1 - x) * eighth, eighth)
    push(got_a, got_a, sem(5), xn).wait_recv()
    start(push(rows(gram, mine_a, quarter), rows(gram, mine_a, quarter), sem(7), yn))
    got_b = rows(gram, mine_b + (1 - y) * eighth, eighth)
    push(got_b, got_b, sem(6), yn).wait_recv()
    start(push(rows(gram, mine_b, quarter), rows(gram, mine_b, quarter), sem(8), xn))
    got_a = rows(gram, base_a + (1 - y) * quarter, quarter)
    push(got_a, got_a, sem(7), yn).wait_recv()
    start(push(rows(gram, base_a, half // 2), rows(gram, base_a, half // 2), sem(9), core))
    got_b = rows(gram, base_b + (1 - x) * quarter, quarter)
    push(got_b, got_b, sem(8), xn).wait_recv()
    start(push(rows(gram, base_b, half // 2), rows(gram, base_b, half // 2), sem(10), core))
    got_a = rows(gram, (1 - c) * half, half // 2)
    push(got_a, got_a, sem(9), core).wait_recv()
    got_b = rows(gram, (1 - c) * half + half // 2, half // 2)
    push(got_b, got_b, sem(10), core).wait_recv()

    for i, (a, b) in enumerate(((outp, outp_all), (tokg, tokg_all))):
        pltpu.make_async_copy(a.at[z], b.at[z], loc.at[1 + i]).wait()
        for k in range(1, 4):
            slot = b.at[(z + 4 - k) % 4]
            push(slot, slot, (o_s.at[i, k - 1], o_r.at[i, k - 1]), zn[k - 1]).wait_recv()
    for t in range(n):
        s, p = sizes[t], PLANES[t]

        @pl.when(z == p)
        def _(t=t, s=s, p=p):
            pltpu.make_async_copy(low_g.at[p, pl.ds(0, s)], grads[t], loc.at[0]).wait()
            for k in range(1, 4):
                v = (p + k) % 4
                push(low_g.at[v, pl.ds(0, s)], grads[t], (g_s.at[v], g_r.at[t]), (d, v)).wait_send()

        @pl.when(z != p)
        def _(t=t):
            push(grads[t], grads[t], (g_s.at[t], g_r.at[t]), (d, t)).wait_recv()
    for copy in held:
        copy.wait_send()


def gram_all(total, mom, outp, tokg, sizes):
    top, width = total.shape[1:]
    anyspace = pl.BlockSpec(memory_space=pl.ANY)
    vmem = pl.BlockSpec(memory_space=pltpu.VMEM)
    dma = pltpu.SemaphoreType.DMA
    return pl.pallas_call(
        functools.partial(gram_kernel, sizes),
        out_shape=[jax.ShapeDtypeStruct((width, width), F32)]
        + [jax.ShapeDtypeStruct((4 * top, width), BF)] * 2
        + [jax.ShapeDtypeStruct((s, width), BF) for s in sizes]
        + [jax.ShapeDtypeStruct(outp.shape, outp.dtype), jax.ShapeDtypeStruct(tokg.shape, tokg.dtype)],
        in_specs=[vmem, vmem, anyspace, anyspace],
        out_specs=[vmem] * 3 + [anyspace] * (len(sizes) + 2),
        scratch_shapes=[
            pltpu.VMEM((4, top, width), BF),
            pltpu.VMEM((width, width), F32),
            pltpu.VMEM((width // 2, width), F32),
            pltpu.VMEM((2, width // 8, width), F32),
            pltpu.VMEM((2, width // 16, width), F32),
            dma((4,)),
            dma((4,)),
            dma((11,)),
            dma((11,)),
            dma((2, 3)),
            dma((2, 3)),
            dma((3,)),
        ],
        compiler_params=pltpu.CompilerParams(collective_id=3, has_side_effects=True, vmem_limit_bytes=VMEM_LIMIT),
    )(total, mom, outp, tokg)


def split(v):
    hi = v.astype(BF)
    return hi, (v - hi.astype(F32)).astype(BF)


def dot(a, b):
    return jnp.dot(a, b, preferred_element_type=F32)


def polish_kernel(gram, hi, lo, out, gf, gh, gl, low, b, xf, xh, xl):
    width = gram.shape[0]
    rows = hi.shape[0]
    tile = 256
    step = 64
    eye = jnp.where(
        lax.broadcasted_iota(jnp.int32, (128, 128), 0) == lax.broadcasted_iota(jnp.int32, (128, 128), 1), 1.0, 0.0
    ).astype(F32)
    trace = jnp.zeros((1, 1), F32)
    for i in range(width // 128):
        block = gram[i * 128 : (i + 1) * 128, i * 128 : (i + 1) * 128] * eye
        trace = trace + jnp.sum(jnp.sum(block, axis=1, keepdims=True), axis=0, keepdims=True)
    inverse = 1.0 / (jnp.sqrt(trace) + frob_eps)
    squared = inverse * inverse

    def scale_gram(i, carry):
        at = pl.ds(pl.multiple_of(i * step, step), step)
        v = gram[at] * squared
        gf[at] = v
        gh[at], gl[at] = split(v)
        return carry

    lax.fori_loop(0, width // step, scale_gram, 0)

    def scale_x(i, carry):
        at = pl.ds(pl.multiple_of(i * step, step), step)
        v = (hi[at].astype(F32) + lo[at].astype(F32)) * inverse
        xf[at] = v
        xh[at], xl[at] = split(v)
        return carry

    lax.fori_loop(0, rows // step, scale_x, 0)

    def columns(i):
        return pl.ds(pl.multiple_of(i * tile, tile), tile)

    def iterate(shift, double, last):
        level = coef_a + coef_b * shift + coef_c * shift * shift
        slope = coef_b + 2.0 * coef_c * shift
        left = low if last else gh

        def poly(i, carry):
            at = columns(i)
            g = gf[:, at]
            if last:
                row = lax.broadcasted_iota(jnp.int32, g.shape, 0)
                col = lax.broadcasted_iota(jnp.int32, g.shape, 1) + i * tile
                g = g - jnp.where(row == col, shift, 0.0)
            b[:, at] = (slope * g + coef_c * dot(left[...], left[:, at])).astype(BF)
            return carry

        if last:

            def lower(i, carry):
                at = pl.ds(pl.multiple_of(i * step, step), step)
                g = gf[at]
                row = lax.broadcasted_iota(jnp.int32, g.shape, 0) + i * step
                col = lax.broadcasted_iota(jnp.int32, g.shape, 1)
                low[at] = (g - jnp.where(row == col, shift, 0.0)).astype(BF)
                return carry

            lax.fori_loop(0, width // step, lower, 0)
        lax.fori_loop(0, width // tile, poly, 0)

        def apply(i, carry):
            at = columns(i)
            right = b[:, at]
            v = level * xf[:, at] + dot(xh[...], right)
            if double:
                v = v + dot(xl[...], right)
            if last:
                out[:, at] = v.astype(BF)
                return carry
            xf[:, at] = v
            t = level * gf[:, at] + dot(gh[...], right)
            if double:
                t = t + dot(gl[...], right)
                th, tl = split(t)
                gf[:, at] = level * t + dot(b[...], th) + dot(b[...], tl)
            else:
                gf[:, at] = level * t + dot(b[...], t.astype(BF))
            return carry

        lax.fori_loop(0, width // tile, apply, 0)
        if not last:

            def lower_g(i, carry):
                at = pl.ds(pl.multiple_of(i * step, step), step)
                gh[at] = gf[at].astype(BF)
                return carry

            lax.fori_loop(0, width // step, lower_g, 0)

            def lower_x(i, carry):
                at = pl.ds(pl.multiple_of(i * step, step), step)
                xh[at] = xf[at].astype(BF)
                return carry

            lax.fori_loop(0, rows // step, lower_x, 0)

    iterate(0.0, True, False)

    def middle(i, carry):
        iterate(0.0, False, False)
        return carry

    lax.fori_loop(0, NS_STEPS - 2, middle, 0)
    iterate(0.8, False, True)


def polish(gram, hi, lo):
    rows, width = hi.shape
    vmem = pl.BlockSpec(memory_space=pltpu.VMEM)
    return pl.pallas_call(
        polish_kernel,
        out_shape=jax.ShapeDtypeStruct((rows, width), BF),
        in_specs=[vmem] * 3,
        out_specs=vmem,
        scratch_shapes=[pltpu.VMEM((width, width), F32)]
        + [pltpu.VMEM((width, width), BF)] * 4
        + [pltpu.VMEM((rows, width), F32)]
        + [pltpu.VMEM((rows, width), BF)] * 2,
        compiler_params=pltpu.CompilerParams(vmem_limit_bytes=VMEM_LIMIT),
        cost_estimate=pl.CostEstimate(flops=39 * 10**9, bytes_accessed=8 * 10**6, transcendentals=0),
    )(gram, hi, lo)


def return_kernel(sizes, *refs):
    n = len(sizes)
    done = refs[0]
    rows = refs[1 : 1 + n]
    s_s, s_r, loc = refs[1 + n :]
    d, z, y, x, c = place()
    core, xn, yn, zn = partners(d, z, y, x, c)
    greet(zn)
    for t in range(n):
        s, p = sizes[t], PLANES[t]

        @pl.when(z == p)
        def _(t=t, s=s, p=p):
            for k in range(1, 4):
                v = (p + k) % 4
                push(done.at[v, pl.ds(0, s)], rows[t], (s_s.at[v], s_r.at[t]), (d, v)).start()
            pltpu.make_async_copy(done.at[p, pl.ds(0, s)], rows[t], loc.at[0]).start()

    for t in range(n):
        s, p = sizes[t], PLANES[t]

        @pl.when(z == p)
        def _(t=t, s=s, p=p):
            pltpu.make_async_copy(done.at[p, pl.ds(0, s)], rows[t], loc.at[0]).wait()
            for k in range(1, 4):
                v = (p + k) % 4
                push(done.at[v, pl.ds(0, s)], rows[t], (s_s.at[v], s_r.at[t]), (d, v)).wait_send()

        @pl.when(z != p)
        def _(t=t):
            push(rows[t], rows[t], (s_s.at[t], s_r.at[t]), (d, t)).wait_recv()


def return_all(done, sizes):
    anyspace = pl.BlockSpec(memory_space=pl.ANY)
    dma = pltpu.SemaphoreType.DMA
    return pl.pallas_call(
        functools.partial(return_kernel, sizes),
        out_shape=[jax.ShapeDtypeStruct((s, done.shape[2]), BF) for s in sizes],
        in_specs=[anyspace],
        out_specs=[anyspace] * len(sizes),
        scratch_shapes=[dma((4,)), dma((4,)), dma((1,))],
        compiler_params=pltpu.CompilerParams(collective_id=4, has_side_effects=True, vmem_limit_bytes=8 << 20),
    )(done)


def whole_image(x, cot, live, weights, head_bias, expand_bias, norm_gain, model_bias):
    intake, outlet, expand, shrink = weights
    seq, width = x.shape
    heads = width // HEAD_DIM
    scale = HEAD_DIM ** (-0.5)
    query_bias = head_bias[0].reshape(heads, HEAD_DIM)
    value_bias = head_bias[1].reshape(heads, HEAD_DIM)
    mixed_bias = jnp.stack([query_bias, jnp.zeros_like(query_bias), value_bias], axis=1).reshape(3 * width)

    def ein(form, a, b):
        return jnp.einsum(form, a, b, preferred_element_type=F32)

    def norm(v, g, s):
        center = v - jnp.mean(v, axis=-1, keepdims=True)
        r = lax.rsqrt(jnp.mean(center * center, axis=-1, keepdims=True) + norm_eps)
        n = center * r
        return n * g + s, n, r

    rows = x.astype(F32)
    first, n1, r1 = norm(rows, norm_gain[0], model_bias[0])
    first = first.astype(BF)
    mixed = (ein("sd,rd->sr", first, intake) + mixed_bias).astype(BF).reshape(seq, heads, 3, HEAD_DIM)
    q, k, v = mixed[:, :, 0], mixed[:, :, 1], mixed[:, :, 2]
    scores = ein("qhe,khe->hqk", q, k) * scale
    scores = jnp.where(live[None, None, :], scores, masked_score)
    attention = softmax_rows(scores)
    attention16 = attention.astype(BF)
    attended = ein("hqk,khe->qhe", attention16, v).reshape(seq, width).astype(BF)
    middle = rows + ein("sc,cd->sd", attended, outlet) + model_bias[2]
    second, n2, r2 = norm(middle, norm_gain[1], model_bias[1])
    second = second.astype(BF)
    hidden = ein("sd,fd->sf", second, expand) + expand_bias
    bell = 0.5 * (1.0 + lax.erf(hidden * (0.5**0.5)))
    active = (hidden * bell).astype(BF)
    output = middle + ein("sf,fd->sd", active, shrink) + model_bias[3]
    slope = bell + hidden * jnp.exp(-0.5 * hidden * hidden) * (0.5 / jnp.pi) ** 0.5
    return output.astype(BF), (active, slope, middle, mixed.reshape(seq, 3 * width), attended, second, first, x, cot)


def per_device_fast(
    tokens,
    cotangent,
    keep_mask,
    intake,
    outlet,
    expand,
    shrink,
    intake_moment,
    outlet_moment,
    expand_moment,
    shrink_moment,
    head_bias,
    expand_bias,
    norm_gain,
    model_bias,
    head_first,
    head_second,
    expand_first,
    expand_second,
    gain_first,
    gain_second,
    bias_first,
    bias_second,
):
    shape = tokens.shape
    local, width = shape[2:]
    z = lax.axis_index("tensor")
    masters = (intake, outlet, expand, shrink)
    moments = (intake_moment, outlet_moment, expand_moment, shrink_moment)
    sizes = tuple(v.shape[0] for v in masters)
    gathered = gather_all(
        [v.astype(BF) for v in masters],
        tokens.reshape(-1, local, width),
        cotangent.reshape(-1, local, width),
    )
    whole = [v.reshape(-1, width) for v in gathered[:4]]
    x, cot = (v.reshape(-1, width) for v in gathered[4:6])
    seq = x.shape[0]
    keep = lax.dynamic_index_in_dim(keep_mask.reshape(-1, seq), z, 0, keepdims=False)
    live = jnp.logical_or(keep != 0, jnp.arange(seq) < BUF)
    out, saved = whole_image(x, cot, live, whole, head_bias, expand_bias, norm_gain, model_bias)
    moms = [v.astype(BF) for v in moments]
    total, small, mom, token_grad = backward_all(whole, saved, norm_gain, live.astype(F32)[None], moms, sizes)
    made = gram_all(total, mom, out.reshape(-1, local, width), token_grad.reshape(-1, local, width), sizes)
    gram, hi, lo = made[:3]
    shards = [g.astype(F32) for g in made[3:7]]
    output = made[7].reshape(shape).astype(F32)
    token_grad = made[8].reshape(shape).astype(F32)
    done = polish(gram, hi, lo).reshape(4, -1, width)
    returned = return_all(done, sizes)
    head_total = small[0:2]
    units = expand_bias.shape[0] // width
    hidden_total = small[2 : 2 + units].reshape(expand_bias.shape)
    gain_total = small[2 + units : 4 + units]
    bias_total = small[4 + units : 8 + units]
    moments_new = [muon_decay * moment + gradient for gradient, moment in zip(shards, moments)]
    rows_scale = lax.axis_size("dp") * lax.axis_size("tensor")
    masters_new = [
        weight - rate * (weight.shape[0] * rows_scale / width) ** 0.5 * rows.astype(F32)
        for weight, rate, rows in zip(masters, muon_rates, returned)
    ]
    head = adam_step(head_total, head_first, head_second)
    hidden = adam_step(hidden_total, expand_first, expand_second)
    gain = adam_step(gain_total, gain_first, gain_second)
    bias = adam_step(bias_total, bias_first, bias_second)
    return (
        (output, token_grad)
        + tuple(shards)
        + (head_total, hidden_total, gain_total, bias_total)
        + tuple(moments_new)
        + tuple(masters_new)
        + tuple(v.astype(BF) for v in masters_new)
        + (head[0], hidden[0], gain[0], bias[0])
        + head[1:]
        + hidden[1:]
        + gain[1:]
        + bias[1:]
    )


def solution(mesh):
    placed = (
        P(None, "dp", "tensor", None),
        P(None, "dp", "tensor", None),
        P(None, "dp", None),
        P(("tensor", "dp"), None),
        P(("tensor", "dp"), None),
        P(("tensor", "dp"), None),
        P(("tensor", "dp"), None),
        P(("tensor", "dp"), None),
        P(("tensor", "dp"), None),
        P(("tensor", "dp"), None),
        P(("tensor", "dp"), None),
        P(),
        P(),
        P(),
        P(),
        P(),
        P(),
        P(),
        P(),
        P(),
        P(),
        P(),
        P(),
    )
    fast = mesh.shape["dp"] == 8 and mesh.shape["tensor"] == 4
    return jax.shard_map(
        per_device_fast if fast else per_device,
        mesh=mesh,
        in_specs=placed,
        out_specs=(
            P(None, "dp", "tensor", None),
            P(None, "dp", "tensor", None),
            P(("tensor", "dp"), None),
            P(("tensor", "dp"), None),
            P(("tensor", "dp"), None),
            P(("tensor", "dp"), None),
            P(),
            P(),
            P(),
            P(),
            P(("tensor", "dp"), None),
            P(("tensor", "dp"), None),
            P(("tensor", "dp"), None),
            P(("tensor", "dp"), None),
            P(("tensor", "dp"), None),
            P(("tensor", "dp"), None),
            P(("tensor", "dp"), None),
            P(("tensor", "dp"), None),
            P(("tensor", "dp"), None),
            P(("tensor", "dp"), None),
            P(("tensor", "dp"), None),
            P(("tensor", "dp"), None),
            P(),
            P(),
            P(),
            P(),
            P(),
            P(),
            P(),
            P(),
            P(),
            P(),
            P(),
            P(),
        ),
        check_vma=False,
    )
```

```python
import functools

import jax
import jax.numpy as jnp
from jax import lax
from jax.experimental import pallas as pl
from jax.experimental.pallas import tpu as pltpu
from jax.sharding import PartitionSpec as P

HEAD_DIM = 64
BUF = 64
NS_STEPS = 5
ADAM_STEP = 10


norm_eps = 1e-06
first_decay = 0.9
second_decay = 0.95
adam_rate = 0.05
adam_eps = 1e-08
muon_decay = 0.5
muon_rates = (1.0, 4.0, 1.0, 1.0)
frob_eps = 1e-07
coef_a = 3.4445
coef_b = -4.775
coef_c = 2.0315
masked_score = -1000000000.0


def precise(form, left, right):
    return jnp.einsum(form, left, right, precision=lax.Precision.HIGHEST)


def layer_norm(inputs_row, gain_row, shift_row):
    center = inputs_row - jnp.mean(inputs_row, axis=-1, keepdims=True)
    spread = jnp.mean(center * center, axis=-1, keepdims=True)
    return center * lax.rsqrt(spread + norm_eps) * gain_row + shift_row


def softmax_rows(scores):
    largest = jnp.max(scores, axis=-1, keepdims=True)
    powers = jnp.exp(scores - largest)
    return powers / jnp.sum(powers, axis=-1, keepdims=True)


def exact_gelu(inputs_row):
    return jax.nn.gelu(inputs_row, approximate=False)


def attend_weights(queries, keys_all, live_keys):
    scores = jnp.einsum(
        "iqhe,ikhe->ihqk", queries, keys_all, preferred_element_type=jnp.float32
    ) * HEAD_DIM ** (-0.5)
    scores = jnp.where(live_keys[:, None, None, :], scores, masked_score)
    return softmax_rows(scores)


def reduce_blocks(blocks):
    return (
        lax.psum_scatter(blocks[0], "dp", scatter_dimension=0, tiled=True),
        lax.psum_scatter(blocks[1], "dp", scatter_dimension=0, tiled=True),
        lax.psum_scatter(blocks[2], "dp", scatter_dimension=0, tiled=True),
        lax.psum_scatter(blocks[3], "dp", scatter_dimension=0, tiled=True),
    )


def gram_whole(matrix):
    model_width = matrix.shape[1]
    own_rows = model_width // lax.axis_size("dp")
    shard_rows = lax.psum_scatter(
        precise(
            "rm,rn->mn", lax.slice_in_dim(matrix, 0, own_rows * lax.axis_size("dp"), axis=1), matrix
        ),
        "dp",
        scatter_dimension=0,
        tiled=True,
    )
    return lax.all_gather(shard_rows, "dp", axis=0, tiled=True)


def newton_step(scaled, gram):
    product = precise("rk,kn->rn", scaled, gram)
    return coef_a * scaled + coef_b * product + coef_c * precise("rk,kn->rn", product, gram)


def adam_step(gradient, first, second):
    first_new = first_decay * first + (1.0 - first_decay) * gradient
    second_new = second_decay * second + (1.0 - second_decay) * gradient * gradient
    first_hat = first_new / (1.0 - first_decay**ADAM_STEP)
    second_hat = second_new / (1.0 - second_decay**ADAM_STEP)
    change = -adam_rate * first_hat / (jnp.sqrt(second_hat) + adam_eps)
    return (change, first_new, second_new)


def per_device(
    tokens,
    cotangent,
    keep_mask,
    intake,
    outlet,
    expand,
    shrink,
    intake_moment,
    outlet_moment,
    expand_moment,
    shrink_moment,
    head_bias,
    expand_bias,
    norm_gain,
    model_bias,
    head_first,
    head_second,
    expand_first,
    expand_second,
    gain_first,
    gain_second,
    bias_first,
    bias_second,
):
    micro_count, images, local_seq, model_width = tokens.shape
    seq_len = keep_mask.shape[2]
    tensor_size = lax.axis_size("tensor")
    tensor_index = lax.axis_index("tensor")
    head_cols = model_width // tensor_size
    local_heads = head_cols // HEAD_DIM
    hidden_cols = expand_bias.shape[0] // tensor_size
    head_start = tensor_index * head_cols
    hidden_start = tensor_index * hidden_cols
    query_bias = lax.dynamic_slice_in_dim(head_bias[0], head_start, head_cols, 0).reshape(
        local_heads, HEAD_DIM
    )
    value_bias = lax.dynamic_slice_in_dim(head_bias[1], head_start, head_cols, 0).reshape(
        local_heads, HEAD_DIM
    )
    mixed_bias = jnp.stack([query_bias, jnp.zeros_like(query_bias), value_bias], axis=1).reshape(
        3 * head_cols
    )
    hidden_bias = lax.dynamic_slice_in_dim(expand_bias, hidden_start, hidden_cols, 0)
    position = jnp.arange(seq_len)
    masters = (intake, outlet, expand, shrink)
    block_shapes = (
        (3 * head_cols, model_width),
        (head_cols, model_width),
        (hidden_cols, model_width),
        (hidden_cols, model_width),
    )
    totals = tuple((jnp.zeros(shape_one, jnp.float32) for shape_one in block_shapes))
    gain_grad = jnp.zeros((2, model_width), jnp.float32)
    bias_grad = jnp.zeros((4, model_width), jnp.float32)
    mixed_bias_grad = jnp.zeros((2, head_cols), jnp.float32)
    hidden_bias_grad = jnp.zeros((hidden_cols,), jnp.float32)
    outputs = []
    token_grads = []
    for micro_index in range(micro_count):
        intake_block, outlet_block, expand_block, shrink_block = (
            lax.all_gather(intake.astype(jnp.bfloat16), "dp", axis=0, tiled=True),
            lax.all_gather(outlet.astype(jnp.bfloat16), "dp", axis=0, tiled=True),
            lax.all_gather(expand.astype(jnp.bfloat16), "dp", axis=0, tiled=True),
            lax.all_gather(shrink.astype(jnp.bfloat16), "dp", axis=0, tiled=True),
        )
        token_rows = tokens[micro_index].astype(jnp.float32)
        live_keys = jnp.logical_or(keep_mask[micro_index] > 0, position[None, :] < BUF)
        first_local = layer_norm(token_rows, norm_gain[0], model_bias[0]).astype(jnp.bfloat16)
        first_norm = lax.all_gather(first_local, "tensor", axis=1, tiled=True)
        mixed_rows = (
            jnp.einsum("isd,rd->isr", first_norm, intake_block, preferred_element_type=jnp.float32)
            + mixed_bias
        )
        mixed_rows = mixed_rows.astype(jnp.bfloat16).reshape(
            images, seq_len, local_heads, 3, HEAD_DIM
        )
        queries = mixed_rows[:, :, :, 0]
        keys_all = mixed_rows[:, :, :, 1]
        values = mixed_rows[:, :, :, 2]
        attention = attend_weights(queries, keys_all, live_keys)
        attention_low = attention.astype(jnp.bfloat16)
        attended = jnp.einsum(
            "ihqk,ikhe->iqhe", attention_low, values, preferred_element_type=jnp.float32
        )
        attended = attended.reshape(images, seq_len, head_cols).astype(jnp.bfloat16)
        part_sum = jnp.einsum(
            "isc,cd->isd", attended, outlet_block, preferred_element_type=jnp.float32
        )
        middle = (
            token_rows
            + lax.psum_scatter(part_sum, "tensor", scatter_dimension=1, tiled=True)
            + model_bias[2]
        )
        second_local = layer_norm(middle, norm_gain[1], model_bias[1]).astype(jnp.bfloat16)
        second_norm = lax.all_gather(second_local, "tensor", axis=1, tiled=True)
        hidden = (
            jnp.einsum("isd,fd->isf", second_norm, expand_block, preferred_element_type=jnp.float32)
            + hidden_bias
        )
        active = exact_gelu(hidden).astype(jnp.bfloat16)
        part_two = jnp.einsum(
            "isf,fd->isd", active, shrink_block, preferred_element_type=jnp.float32
        )
        outputs.append(
            middle
            + lax.psum_scatter(part_two, "tensor", scatter_dimension=1, tiled=True)
            + model_bias[3]
        )
        cot_local = cotangent[micro_index]
        cot_rows = lax.all_gather(cot_local, "tensor", axis=1, tiled=True)
        shrink_block_grad = jnp.einsum(
            "isf,isd->fd", active, cot_rows, preferred_element_type=jnp.float32
        )
        active_grad = jnp.einsum(
            "isd,fd->isf", cot_rows, shrink_block, preferred_element_type=jnp.float32
        )
        gelu_value, gelu_back = jax.vjp(exact_gelu, hidden)
        hidden_grad = gelu_back(active_grad)[0].astype(jnp.bfloat16)
        hidden_bias_grad = hidden_bias_grad + jnp.sum(hidden_grad.astype(jnp.float32), axis=(0, 1))
        expand_block_grad = jnp.einsum(
            "isf,isd->fd", hidden_grad, second_norm, preferred_element_type=jnp.float32
        )
        second_part = jnp.einsum(
            "isf,fd->isd", hidden_grad, expand_block, preferred_element_type=jnp.float32
        )
        second_grad = lax.psum_scatter(second_part, "tensor", scatter_dimension=1, tiled=True)
        norm_value, norm_back = jax.vjp(layer_norm, middle, norm_gain[1], model_bias[1])
        middle_from_norm, gain_two_grad, shift_two_grad = norm_back(second_grad)
        cot_float = cot_local.astype(jnp.float32)
        middle_grad = cot_float + middle_from_norm
        branch_grad = middle_grad.astype(jnp.bfloat16)
        branch_rows = lax.all_gather(branch_grad, "tensor", axis=1, tiled=True)
        outlet_block_grad = jnp.einsum(
            "isc,isd->cd", attended, branch_rows, preferred_element_type=jnp.float32
        )
        attended_grad = jnp.einsum(
            "isd,cd->isc", branch_rows, outlet_block, preferred_element_type=jnp.float32
        )
        attended_grad = attended_grad.astype(jnp.bfloat16).reshape(
            images, seq_len, local_heads, HEAD_DIM
        )
        attention = attend_weights(queries, keys_all, live_keys)
        attention_low = attention.astype(jnp.bfloat16)
        values_grad = jnp.einsum(
            "ihqk,iqhe->ikhe", attention_low, attended_grad, preferred_element_type=jnp.float32
        )
        attention_grad = jnp.einsum(
            "iqhe,ikhe->ihqk", attended_grad, values, preferred_element_type=jnp.float32
        )
        score_grad = attention * (
            attention_grad - jnp.sum(attention_grad * attention, axis=-1, keepdims=True)
        )
        score_grad = score_grad.astype(jnp.bfloat16)
        queries_grad = jnp.einsum(
            "ihqk,ikhe->iqhe", score_grad, keys_all, preferred_element_type=jnp.float32
        ) * HEAD_DIM ** (-0.5)
        keys_grad = jnp.einsum(
            "ihqk,iqhe->ikhe", score_grad, queries, preferred_element_type=jnp.float32
        ) * HEAD_DIM ** (-0.5)
        mixed_grad = jnp.stack([queries_grad, keys_grad, values_grad], axis=3).astype(jnp.bfloat16)
        mixed_sums = jnp.sum(mixed_grad.astype(jnp.float32), axis=(0, 1))
        mixed_bias_grad = mixed_bias_grad + jnp.stack(
            [mixed_sums[:, 0].reshape(head_cols), mixed_sums[:, 2].reshape(head_cols)]
        )
        mixed_grad = mixed_grad.reshape(images, seq_len, 3 * head_cols)
        intake_block_grad = jnp.einsum(
            "isr,isd->rd", mixed_grad, first_norm, preferred_element_type=jnp.float32
        )
        first_part = jnp.einsum(
            "isr,rd->isd", mixed_grad, intake_block, preferred_element_type=jnp.float32
        )
        first_grad = lax.psum_scatter(first_part, "tensor", scatter_dimension=1, tiled=True)
        first_value, first_back = jax.vjp(layer_norm, token_rows, norm_gain[0], model_bias[0])
        token_from_norm, gain_one_grad, shift_one_grad = first_back(first_grad)
        token_grads.append(middle_grad + token_from_norm)
        gain_grad = gain_grad + jnp.stack([gain_one_grad, gain_two_grad])
        bias_grad = bias_grad + jnp.stack(
            [
                shift_one_grad,
                shift_two_grad,
                jnp.sum(branch_grad.astype(jnp.float32), axis=(0, 1)),
                jnp.sum(cot_float, axis=(0, 1)),
            ]
        )
        block_grads = (intake_block_grad, outlet_block_grad, expand_block_grad, shrink_block_grad)
        totals = tuple((total + block_one for total, block_one in zip(totals, block_grads)))
    shards = reduce_blocks(totals)
    head_full = lax.dynamic_update_slice_in_dim(
        jnp.zeros((2, model_width), jnp.float32), mixed_bias_grad, head_start, 1
    )
    hidden_full = lax.dynamic_update_slice_in_dim(
        jnp.zeros(expand_bias.shape, jnp.float32), hidden_bias_grad, hidden_start, 0
    )
    gain_total, bias_total, head_total, hidden_total = lax.psum(
        (gain_grad, bias_grad, head_full, hidden_full), ("dp", "tensor")
    )
    moments = (intake_moment, outlet_moment, expand_moment, shrink_moment)
    moments_new = [muon_decay * moment + gradient for gradient, moment in zip(shards, moments)]
    updates = [gradient + muon_decay * moment for gradient, moment in zip(shards, moments_new)]
    rows_max = max((update.shape[0] for update in updates))
    padded = jnp.stack(
        [jnp.pad(update, ((0, rows_max - update.shape[0]), (0, 0))) for update in updates]
    )
    spread = lax.all_to_all(padded, "tensor", split_axis=0, concat_axis=0, tiled=True)
    own_matrix = spread.reshape(tensor_size * rows_max, model_width)
    raw_gram = gram_whole(own_matrix)
    measure = jnp.sqrt(jnp.trace(raw_gram)) + frob_eps
    scaled = own_matrix / measure
    gram = raw_gram / (measure * measure)
    for step in range(NS_STEPS):
        if step > 0:
            gram = gram_whole(scaled)
        scaled = newton_step(scaled, gram)
    returned = lax.all_to_all(
        scaled.reshape(tensor_size, rows_max, model_width),
        "tensor",
        split_axis=0,
        concat_axis=0,
        tiled=True,
    )
    rows_scale = lax.axis_size("dp") * tensor_size
    masters_new = [
        weight
        - muon_rates[position_one]
        * (weight.shape[0] * rows_scale / weight.shape[1]) ** 0.5
        * returned[position_one, : weight.shape[0]]
        for position_one, weight in enumerate(masters)
    ]
    head_bias_change, head_first_new, head_second_new = adam_step(
        head_total, head_first, head_second
    )
    expand_bias_change, expand_first_new, expand_second_new = adam_step(
        hidden_total, expand_first, expand_second
    )
    norm_gain_change, gain_first_new, gain_second_new = adam_step(
        gain_total, gain_first, gain_second
    )
    model_bias_change, bias_first_new, bias_second_new = adam_step(
        bias_total, bias_first, bias_second
    )
    output = jnp.stack(outputs)
    token_grad = jnp.stack(token_grads)
    return (
        output,
        token_grad,
        shards[0],
        shards[1],
        shards[2],
        shards[3],
        head_total,
        hidden_total,
        gain_total,
        bias_total,
        moments_new[0],
        moments_new[1],
        moments_new[2],
        moments_new[3],
        masters_new[0],
        masters_new[1],
        masters_new[2],
        masters_new[3],
        masters_new[0].astype(jnp.bfloat16),
        masters_new[1].astype(jnp.bfloat16),
        masters_new[2].astype(jnp.bfloat16),
        masters_new[3].astype(jnp.bfloat16),
        head_bias_change,
        expand_bias_change,
        norm_gain_change,
        model_bias_change,
        head_first_new,
        head_second_new,
        expand_first_new,
        expand_second_new,
        gain_first_new,
        gain_second_new,
        bias_first_new,
        bias_second_new,
    )


MESH = pl.DeviceIdType.MESH
BF = jnp.bfloat16
F32 = jnp.float32
VMEM_LIMIT = 60 * 1024 * 1024


def place():
    d = lax.axis_index("dp")
    z = lax.axis_index("tensor")
    y, x, c = d // 4, (d // 2) % 2, d % 2
    return d, z, y, x, c


def partners(d, z, y, x, c):
    core = (d + 1 - 2 * c, z)
    xn = (d + 2 - 4 * x, z)
    yn = (d + 4 - 8 * y, z)
    zn = [(d, (z + k) % 4) for k in range(1, 4)]
    return core, xn, yn, zn


def greet(others):
    barrier = pltpu.get_barrier_semaphore()
    for other in others:
        pl.semaphore_signal(barrier, inc=1, device_id=other, device_id_type=MESH)
    pl.semaphore_wait(barrier, len(others))


def push(src, dst, sems, to):
    return pltpu.make_async_remote_copy(
        src_ref=src, dst_ref=dst, send_sem=sems[0], recv_sem=sems[1], device_id=to, device_id_type=MESH
    )


LINK = 93.5e3


def plan_forward(blocks, order, sizes, width, slots):
    done, events = [], []
    link = {"x": 0.0, "y": 0.0, "z": 0.0}
    now, at_z = 0.0, 2.0

    def carry(lane, start, rows):
        link[lane] = max(start, link[lane]) + rows * width * 4 / LINK
        return link[lane] + 1.5

    for i, (m, k) in enumerate(order):
        if k == 0:
            events.append((0.1 * i, "one", i))
        else:
            at_z += sizes[m] * width * 4 / LINK
            events.append((at_z + 2.0 * k, "one", i))
    whole, loaded = {}, {}
    head = 0
    todo = list(range(len(blocks)))
    while events or todo:
        events.sort()
        if events and events[0][0] <= now:
            _, kind, i = events.pop(0)
            s = sizes[order[i][0]]
            if kind != "full":
                done.append((kind, i))
                now += 0.15
            if kind == "one":
                ready = max(carry("x", now, s / 2), carry("y", now, s / 2))
                events.append((ready, "two", i))
            elif kind == "two":
                ready = max(carry("x", now, s), carry("y", now, s))
                events.append((ready, "three", i))
            elif kind == "three":
                events.append((now + 3.0, "full", i))
            else:
                whole[i] = True
            continue
        busy = sum(1 for j in loaded if j in todo)
        while head < len(blocks) and (blocks[head][2] is None or (blocks[head][2] in whole and busy < slots)):
            if blocks[head][2] is not None:
                done.append(("load", head))
                loaded[head] = now + 2.0
                busy += 1
            head += 1
        wait = None
        if todo:
            j = todo[0]
            if blocks[j][2] is None or j in loaded:
                if blocks[j][2] is None or loaded[j] <= now:
                    todo.pop(0)
                    done.append(("block", j))
                    now += blocks[j][1]
                    continue
                wait = loaded[j]
        times = [v for v in (wait, events[0][0] if events else None) if v is not None]
        now = max(now, min(times))
    return done


def forward_kernel(sizes, order, *refs):
    n = 4
    w = refs[:n]
    tok, cot = refs[n : n + 2]
    norm_gain, model_bias, mixed_bias, expand_bias, live = refs[n + 2 : n + 7]
    refs = refs[n + 7 :]
    full = refs[:n]
    tok_all, cot_all, output, o_active, o_slope, o_middle, o_mixed, o_attended, o_second, o_first = refs[n : n + 10]
    refs = refs[n + 10 :]
    wbuf, xs, first, mixed, attended, acc, middle, second, active, slope = refs[:10]
    z_s, z_r, loc, t_s, t_r, p_s, p_r, w_l, out_l, s_l = refs[10:]
    d, z, y, x, c = place()
    core, xn, yn, zn = partners(d, z, y, x, c)
    greet([core, xn, yn] + zn)
    held = []
    written = []
    inner = z * (3 - z) > 0
    seq, width = first.shape

    def start(copy):
        copy.start()
        held.append(copy)
        return copy

    def source(j):
        return (z, z + 1 - 2 * (z % 2), 2 - z // 2, 3 - 3 * (z // 2))[j]

    def along(m, j, go):
        slot = full[m].at[source(j), y, x, c]
        if j == 0:

            @pl.when(z < 3)
            def _():
                go(push(w[m], slot, (z_s.at[m, 0], z_r.at[m, z]), (d, z + 1)))

            @pl.when(z > 0)
            def _():
                go(push(w[m], slot, (z_s.at[m, 1], z_r.at[m, z]), (d, z - 1)))

        else:
            beyond = 3 - z if j == 1 else 3 * (z - 1)

            @pl.when(inner)
            def _():
                go(push(slot, slot, (z_s.at[m, 1 + j], z_r.at[m, source(j)]), (d, beyond)))

    locals_ = []
    for m in range(n):
        copy = pltpu.make_async_copy(w[m], full[m].at[z, y, x, c], loc.at[m])
        copy.start()
        locals_.append(copy)
    for i, (a, b) in enumerate(((tok, tok_all), (cot, cot_all))):
        copy = pltpu.make_async_copy(a.at[z], b.at[z], loc.at[n + i])
        copy.start()
        locals_.append(copy)

    def rows_push(i, a, b):
        for k in range(1, 4):
            start(push(a.at[(z + k) % 4], b.at[z], (t_s.at[i, k - 1], t_r.at[i, k - 1]), zn[k - 1]))

    def rows_wait(i, b):
        locals_[n + i].wait()
        for k in range(1, 4):
            slot = b.at[(z + 4 - k) % 4]
            push(slot, slot, (t_s.at[i, k - 1], t_r.at[i, k - 1]), zn[k - 1]).wait_recv()

    def sem(i, stage):
        return (p_s.at[stage, i], p_r.at[stage, i])

    def one(i):
        m, k = order[i]
        h = sizes[m] // 2
        s = source(k)
        if k > 0:
            slot = full[m].at[s, y, x, c]
            push(slot, slot, (z_s.at[m, 1 + k], z_r.at[m, s]), core).wait_recv()
            along(m, k, lambda copy: copy.start())
        else:
            locals_[m].wait()
        a = full[m].at[s, y, x, c, pl.ds(0, h)]
        b = full[m].at[s, y, x, c, pl.ds(h, h)]
        start(push(a, a, sem(i, 0), xn))
        start(push(b, b, sem(i, 1), yn))

    def two(i):
        m, k = order[i]
        h = sizes[m] // 2
        s = source(k)
        a = full[m].at[s, y, 1 - x, c, pl.ds(0, h)]
        push(a, a, sem(i, 0), xn).wait_recv()
        a = full[m].at[s, y, :, c, pl.ds(0, h)]
        start(push(a, a, sem(i, 2), yn))
        b = full[m].at[s, 1 - y, x, c, pl.ds(h, h)]
        push(b, b, sem(i, 1), yn).wait_recv()
        b = full[m].at[s, :, x, c, pl.ds(h, h)]
        start(push(b, b, sem(i, 3), xn))

    def three(i):
        m, k = order[i]
        h = sizes[m] // 2
        s = source(k)
        a = full[m].at[s, 1 - y, :, c, pl.ds(0, h)]
        push(a, a, sem(i, 2), yn).wait_recv()
        b = full[m].at[s, :, 1 - x, c, pl.ds(h, h)]
        push(b, b, sem(i, 3), xn).wait_recv()
        e = full[m].at[s, :, :, c]
        start(push(e, e, sem(i, 4), core))

    slots = wbuf.shape[0]
    ndims = (((1,), (1,)), ((), ()))

    def fetch(m, k, slot):
        return pltpu.make_async_copy(full[m].at[source(k)], wbuf.at[slot, :, :, :, pl.ds(0, sizes[m])], w_l.at[slot])

    def load(m, k, slot):
        i = order.index((m, k))
        e = full[m].at[source(k), :, :, 1 - c]
        push(e, e, sem(i, 4), core).wait_recv()
        fetch(m, k, slot).start()

    def save(src, dst, i):
        copy = pltpu.make_async_copy(src, dst, out_l.at[i])
        copy.start()
        written.append(copy)

    chunk = 64

    def norm_rows(index, v_of, dst):
        gain, shift = norm_gain[pl.ds(index, 1)], model_bias[pl.ds(index, 1)]

        def body(i, carry):
            at = pl.ds(pl.multiple_of(i * chunk, chunk), chunk)
            v = v_of(at)
            center = v - jnp.mean(v, axis=-1, keepdims=True)
            r = lax.rsqrt(jnp.mean(center * center, axis=-1, keepdims=True) + norm_eps)
            dst[at] = (center * r * gain + shift).astype(BF)
            return carry

        lax.fori_loop(0, seq // chunk, body, 0)

    def first_norm():
        rows_wait(0, tok_all)
        copies = []
        for k in range(4):
            copy = pltpu.make_async_copy(
                tok_all.at[k], xs.at[pl.ds(k * (seq // 4), seq // 4)], out_l.at[k]
            )
            copy.start()
            copies.append(copy)
        for copy in copies:
            copy.wait()
        norm_rows(0, lambda at: xs[at].astype(F32), first)
        save(first, o_first, 0)

    def project(k, slot):
        s = source(k)
        fetch(0, k, slot).wait()
        rows = 4 * sizes[0]

        def body(j, carry):
            at = pl.ds(pl.multiple_of(s * 2 * rows + j * rows, rows), rows)
            right = wbuf[slot, j, :, :, pl.ds(0, sizes[0])].reshape(rows, width)
            g = lax.dot_general(first[...], right, ndims, preferred_element_type=F32)
            mixed[:, at] = (g + mixed_bias[:, at]).astype(BF)
            return carry

        lax.fori_loop(0, 2, body, 0)

    scale = HEAD_DIM ** (-0.5)

    def heads(k):
        s0 = source(k)
        mask = live[...] > 0.0

        def body(j, carry):
            p = s0 * 2 + j
            at = pl.ds(pl.multiple_of(p * 6 * HEAD_DIM, 6 * HEAD_DIM), 6 * HEAD_DIM)
            both = mixed[:, at]
            parts = []
            for e in range(2):
                q, kk, v = (both[:, (3 * e + b) * HEAD_DIM : (3 * e + b + 1) * HEAD_DIM] for b in range(3))
                s = lax.dot_general(q, kk, ndims, preferred_element_type=F32) * scale
                s = jnp.where(mask, s, masked_score)
                s = jnp.exp(s - jnp.max(s, axis=-1, keepdims=True))
                pr = (s / jnp.sum(s, axis=-1, keepdims=True)).astype(BF)
                parts.append(jnp.dot(pr, v, preferred_element_type=F32).astype(BF))
            to = pl.ds(pl.multiple_of(p * 2 * HEAD_DIM, 2 * HEAD_DIM), 2 * HEAD_DIM)
            attended[:, to] = jnp.concatenate(parts, axis=1)
            return carry

        lax.fori_loop(0, 2, body, 0)

    def outlet_part(k, slot):
        s = source(k)
        fetch(1, k, slot).wait()
        rows = 8 * sizes[1]
        at = pl.ds(pl.multiple_of(s * rows, rows), rows)
        right = wbuf[slot, :, :, :, pl.ds(0, sizes[1])].reshape(rows, width)
        g = jnp.dot(attended[:, at], right, preferred_element_type=F32)
        if k == 0:
            acc[...] = g
        else:
            acc[...] += g

    def second_norm():
        bias = model_bias[pl.ds(2, 1)]

        def body(i, carry):
            at = pl.ds(pl.multiple_of(i * chunk, chunk), chunk)
            middle[at] = xs[at].astype(F32) + acc[at] + bias
            return carry

        lax.fori_loop(0, seq // chunk, body, 0)
        norm_rows(1, lambda at: middle[at], second)
        save(mixed, o_mixed, 4)
        save(attended, o_attended, 5)
        save(middle, o_middle, 6)
        save(second, o_second, 7)

    def slope_copy(k):
        s = source(k)
        hidden = 8 * sizes[2]
        at = pl.ds(pl.multiple_of(s * hidden, hidden), hidden)
        return pltpu.make_async_copy(slope.at[k % 2], o_slope.at[:, at], s_l.at[k % 2])

    def expand_part(k, slot):
        s = source(k)
        fetch(2, k, slot).wait()
        if k >= 2:
            slope_copy(k - 2).wait()
        rows = 2 * sizes[2]

        def body(j, carry):
            at = pl.ds(pl.multiple_of(s * 4 * rows + j * rows, rows), rows)
            right = wbuf[slot, j // 2, j % 2].reshape(rows, width)
            hidden = lax.dot_general(second[...], right, ndims, preferred_element_type=F32)
            hidden = hidden + expand_bias[:, at]
            bell = 0.5 * (1.0 + lax.erf(hidden * (0.5**0.5)))
            active[:, at] = (hidden * bell).astype(BF)
            slope[k % 2, :, pl.ds(pl.multiple_of(j * rows, rows), rows)] = (
                bell + hidden * jnp.exp(-0.5 * hidden * hidden) * (0.5 / jnp.pi) ** 0.5
            )
            return carry

        lax.fori_loop(0, 4, body, 0)
        slope_copy(k).start()
        if k == 3:
            save(active, o_active, 8)

    def shrink_part(k, slot):
        s = source(k)
        fetch(3, k, slot).wait()
        hidden = 8 * sizes[3]

        def body(j, carry):
            cols = pl.ds(pl.multiple_of(j * 256, 256), 256)
            left = active[:, pl.ds(pl.multiple_of(s * hidden, hidden), hidden)]
            right = wbuf[slot, :, :, :, :, cols].reshape(hidden, 256)
            g = jnp.dot(left, right, preferred_element_type=F32)
            if k == 0:
                acc[:, cols] = g
            else:
                acc[:, cols] += g
            return carry

        lax.fori_loop(0, width // 256, body, 0)

    def last():
        bias = model_bias[pl.ds(3, 1)]

        def body(i, carry):
            at = pl.ds(pl.multiple_of(i * chunk, chunk), chunk)
            output[at] = (middle[at] + acc[at] + bias).astype(BF)
            return carry

        lax.fori_loop(0, seq // chunk, body, 0)

    blocks = [("n1", 4.0, None)]
    work = [first_norm]
    needs = [None]

    def block(us, piece, fn):
        blocks.append((len(blocks), us, order.index(piece) if piece else None))
        needs.append(piece)
        work.append(fn)

    for k in range(4):
        block(1.6, (0, k), functools.partial(project, k))
        block(5.0, None, functools.partial(heads, k))
    for k in range(4):
        block(0.8, (1, k), functools.partial(outlet_part, k))
    block(2.5, None, second_norm)
    for k in range(4):
        block(4.5, (2, k), functools.partial(expand_part, k))
    for k in range(4):
        block(1.5, (3, k), functools.partial(shrink_part, k))
    block(1.0, None, last)

    go = lambda copy: copy.start()
    along(0, 0, go)
    rows_push(0, tok, tok_all)
    along(1, 0, go)
    along(2, 0, go)
    ones = 0
    slot_of, used = {}, 0
    for kind, i in plan_forward(blocks, order, sizes, width, slots):
        if kind == "one":
            one(i)
            ones += 1
            if ones == 5:
                along(3, 0, go)
            if ones == 7:
                rows_push(1, cot, cot_all)
        elif kind == "two":
            two(i)
        elif kind == "three":
            three(i)
        elif kind == "load":
            slot_of[i] = used % slots
            used += 1
            load(*needs[i], slot_of[i])
        elif i in slot_of:
            work[i](slot_of[i])
        else:
            work[i]()
    rows_wait(1, cot_all)
    for k in (2, 3):
        slope_copy(k).wait()
    for copy in written:
        copy.wait()
    for copy in held:
        copy.wait_send()
    for m in range(n):
        for j in range(4):
            along(m, j, lambda copy: copy.wait_send())


def forward_all(weights, tok, cot, norm_gain, model_bias, mixed_bias, expand_bias, live):
    sizes = tuple(v.shape[0] for v in weights)
    width = weights[0].shape[1]
    seq = tok.shape[0] * tok.shape[1]
    hidden = expand_bias.shape[1]
    order = [(m, 0) for m in range(4)] + [(m, k) for m in range(4) for k in (1, 2, 3)]
    count = len(order)
    anyspace = pl.BlockSpec(memory_space=pl.ANY)
    vmem = pl.BlockSpec(memory_space=pltpu.VMEM)
    dma = pltpu.SemaphoreType.DMA
    shape = jax.ShapeDtypeStruct
    return pl.pallas_call(
        functools.partial(forward_kernel, sizes, order),
        out_shape=[shape((4, 2, 2, 2, s, width), BF) for s in sizes]
        + [
            shape(tok.shape, BF),
            shape(cot.shape, BF),
            shape((seq, width), BF),
            shape((seq, hidden), BF),
            shape((seq, hidden), F32),
            shape((seq, width), F32),
            shape((seq, 3 * width), BF),
            shape((seq, width), BF),
            shape((seq, width), BF),
            shape((seq, width), BF),
        ],
        in_specs=[anyspace] * (len(sizes) + 2) + [vmem] * 5,
        out_specs=[anyspace] * (len(sizes) + 2) + [vmem] + [anyspace] * 7,
        scratch_shapes=[
            pltpu.VMEM((4, 2, 2, 2, max(sizes), width), BF),
            pltpu.VMEM((seq, width), BF),
            pltpu.VMEM((seq, width), BF),
            pltpu.VMEM((seq, 3 * width), BF),
            pltpu.VMEM((seq, width), BF),
            pltpu.VMEM((seq, width), F32),
            pltpu.VMEM((seq, width), F32),
            pltpu.VMEM((seq, width), BF),
            pltpu.VMEM((seq, hidden), BF),
            pltpu.VMEM((2, seq, 8 * sizes[2]), F32),
            dma((4, 5)),
            dma((4, 4)),
            dma((6,)),
            dma((2, 3)),
            dma((2, 3)),
            dma((5, count)),
            dma((5, count)),
            dma((4,)),
            dma((9,)),
            dma((2,)),
        ],
        compiler_params=pltpu.CompilerParams(collective_id=1, has_side_effects=True, vmem_limit_bytes=VMEM_LIMIT),
    )(*weights, tok, cot, norm_gain, model_bias, mixed_bias, expand_bias, live)


def add_rows(dst, src, lead, rows):
    step = 16

    def body(i, carry):
        j, r = i // (rows // step), (i % (rows // step)) * step
        at = pl.ds(pl.multiple_of(r, step), step)
        dst[j, at] = dst[j, at] + src[j, at]
        return carry

    lax.fori_loop(0, lead * (rows // step), body, 0)


PLANES = (1, 0, 2, 3)


def plan(blocks, sizes, order, free_after, width):
    todo = list(blocks)
    done = []
    events = []
    link = {"x": 0.0, "y": 0.0, "z": 0.0}
    now = 0.0
    finished = set()

    def carry(lane, start, rows):
        begin = max(start, link[lane])
        link[lane] = begin + rows * width * 2 * 2 / LINK
        return link[lane] + 1.5

    def emit(step):
        nonlocal now
        kind, i = step[0], step[1]
        done.append(step)
        finished.add(step)
        s = sizes[order[i][0]]
        if kind == "one":
            now += s / 128 * 1.0
            ready = max(carry("y", now, s), carry("x", now, s))
            events.append((ready, ("two", i)))
        elif kind == "two":
            now += s / 128 * 0.6
            ready = max(carry("x", now, s / 2), carry("y", now, s / 2))
            events.append((ready, ("three", i)))
        elif kind == "three":
            now += s / 128 * 0.3
            ready = carry("z", now, s)
            events.append((ready, ("four", i)))
            events.append((ready + 0.001, ("fourb", i)))
        elif kind == "four":
            finished.discard(step)
            now += 0.2
        elif kind == "fourb":
            now += 0.2

    while todo or events:
        events.sort()
        if events and events[0][0] <= now:
            at, step = events.pop(0)
            if step[0] == "fourb":
                events.append((now + 3.0, ("fourc", step[1])))
                events.sort()
                continue
            emit(step)
            continue
        if todo:
            name, us, piece = todo[0]
            blocked = piece is not None and piece >= free_after and ("one", piece - free_after) not in finished
            if not blocked:
                todo.pop(0)
                done.append(("block", name))
                now += us
                if piece is not None:
                    done.append(("push", piece))
                    events.append((now + 3.0, ("one", piece)))
                continue
        now = max(now, events[0][0])
    return done


def backward_kernel(sizes, order, *refs):
    n = 4
    small_count = 16
    (shrink, expand, outlet, intake, active, slope, middle, mixed, attended, second, first, x_in, cot) = refs[:13]
    norm_gain, live = refs[13:15]
    mom = refs[15:19]
    total, small_out, mom_all, token_grad = refs[19:23]
    refs = refs[23:]
    own, mid, end, far = (refs[i * n : i * n + n] for i in range(4))
    refs = refs[4 * n :]
    (made, act, slo, wbuf, obuf, hgrad, wide, mgrad, branch, agrad) = refs[:10]
    small, s_got, s_acc, s_z = refs[10:14]
    loc, c_s, c_r, p_s, p_r, f_s, f_r, q_s, q_r, m_s, m_r, w_l = refs[14:]
    d, z, y, x, c = place()
    core, xn, yn, zn = partners(d, z, y, x, c)
    greet([core, xn, yn] + zn)
    seq, width = cot.shape
    held = []
    top = max(sizes)

    def start(copy):
        copy.start()
        held.append(copy)

    def sem(i, stage):
        return (p_s.at[stage, i], p_r.at[stage, i])

    slots = made.shape[0]

    def core_push(i):
        m, k = order[i]
        return push(
            made.at[i % slots, :, :, 1 - c, pl.ds(0, sizes[m])], own[m].at[k], (c_s.at[i], c_r.at[i]), core
        )

    def one(i):
        m, k = order[i]
        s, h = sizes[m], sizes[m] // 2
        core_push(i).wait_recv()
        for j in range(2):
            for l in range(2):
                add_rows(own[m].at[k, j, pl.ds(l, 1)], made.at[i % slots, j, l, pl.ds(c, 1)], 1, s)
        start(push(own[m].at[k, 1 - y, :, pl.ds(0, h)], mid[m].at[k, 0], sem(i, 0), yn))
        start(push(own[m].at[k, :, 1 - x, pl.ds(h, h)], mid[m].at[k, 1], sem(i, 1), xn))

    def two(i):
        m, k = order[i]
        h = sizes[m] // 2
        push(mid[m].at[k, 0], mid[m].at[k, 0], sem(i, 0), yn).wait_recv()
        add_rows(own[m].at[k, y, :, pl.ds(0, h)], mid[m].at[k, 0], 2, h)
        start(push(own[m].at[k, y, 1 - x, pl.ds(0, h)], end[m].at[k, pl.ds(0, h)], sem(i, 2), xn))
        push(mid[m].at[k, 1], mid[m].at[k, 1], sem(i, 1), xn).wait_recv()
        add_rows(own[m].at[k, :, x, pl.ds(h, h)], mid[m].at[k, 1], 2, h)
        start(push(own[m].at[k, 1 - y, x, pl.ds(h, h)], end[m].at[k, pl.ds(h, h)], sem(i, 3), yn))

    def hop(i, p, go):
        m, k = order[i]
        side, to = (0, p + 1) if p < PLANES[m] else (1, p - 1)
        at = side if PLANES[m] in (1, 2) else 0
        go(push(own[m].at[k, y, x], far[m].at[at, k], (f_s.at[m, k], f_r.at[m, k, side]), (d, to)))

    def came(m, k, side):
        slot = far[m].at[side if PLANES[m] in (1, 2) else 0, k]
        push(slot, slot, (f_s.at[m, k], f_r.at[m, k, side]), core).wait_recv()

    def three(i):
        m, k = order[i]
        s, h = sizes[m], sizes[m] // 2
        push(end[m].at[k, pl.ds(0, h)], end[m].at[k, pl.ds(0, h)], sem(i, 2), xn).wait_recv()
        push(end[m].at[k, pl.ds(h, h)], end[m].at[k, pl.ds(h, h)], sem(i, 3), yn).wait_recv()
        add_rows(own[m].at[k, pl.ds(y, 1), x], end[m].at[pl.ds(k, 1)], 1, s)
        for p in (0, 3):
            if p != PLANES[m]:

                @pl.when(z == p)
                def _(p=p):
                    hop(i, p, lambda copy: copy.start())

    def four(i, far_hop):
        m, k = order[i]
        for p in (1, 2):
            below = p < PLANES[m]
            if p == PLANES[m] or far_hop != (p if below else 3 - p):
                continue

            @pl.when(z == p)
            def _(p=p, below=below):
                side = 0 if below else 1
                came(m, k, side)
                at = side if PLANES[m] in (1, 2) else 0
                add_rows(own[m].at[k, pl.ds(y, 1), x], far[m].at[at, pl.ds(k, 1)], 1, sizes[m])
                hop(i, p, lambda copy: copy.start())

    def five(i):
        m, k = order[i]
        s, p = sizes[m], PLANES[m]
        sides = [v for v in (0, 1) if p != 3 * v]

        @pl.when(z == p)
        def _():
            for side in sides:
                came(m, k, side)

            def body(r, carry):
                at = pl.ds(pl.multiple_of(r * 16, 16), 16)
                acc = own[m][k, y, x, at].astype(F32)
                for side in range(len(sides)):
                    acc = acc + far[m][side, k, at].astype(F32)
                total[k, at] = acc
                return carry

            lax.fori_loop(0, s // 16, body, 0)
            if s < total.shape[1]:
                total[k, pl.ds(s, total.shape[1] - s)] = jnp.zeros((total.shape[1] - s, width), F32)

    def small_step(stage):
        to = (core, xn, yn)
        if stage > 0:
            here = s_got.at[stage - 1]
            push(here, here, (q_s.at[stage - 1], q_r.at[stage - 1]), to[stage - 1]).wait_recv()
            s_acc[stage] = s_acc[stage - 1] + s_got[stage - 1]
        else:
            s_acc[0] = small[...]
        if stage < 3:
            start(push(s_acc.at[stage], s_got.at[stage], (q_s.at[stage], q_r.at[stage]), to[stage]))
        else:
            s_z[z] = s_acc[3]
            for k in range(1, 4):
                start(push(s_acc.at[3], s_z.at[z], (q_s.at[2 + k], q_r.at[2 + k]), zn[k - 1]))

    def moments(first):
        for t in range(n):
            p = PLANES[t]
            here = mom_all.at[z, pl.ds(0, sizes[t])]

            @pl.when(z == p)
            def _(t=t, p=p, here=here):
                copy = pltpu.make_async_copy(mom[t], here, loc.at[0])
                if first:
                    copy.start()
                else:
                    copy.wait()
                    for k in range(1, 4):
                        s = (p + k) % 4
                        there = mom_all.at[s, pl.ds(0, sizes[t])]
                        push(mom[t], there, (m_s.at[t], m_r.at[s]), (d, s)).wait_recv()

            @pl.when(z != p)
            def _(t=t, p=p, here=here):
                copy = push(mom[t], here, (m_s.at[t], m_r.at[z]), (d, p))
                if first:
                    copy.start()
                else:
                    copy.wait_send()

    unit = wbuf.shape[1]
    count_units = shrink.shape[0] // unit

    def load(u):
        at = pl.ds(u * unit, unit)
        return [
            pltpu.make_async_copy(shrink.at[at], wbuf.at[u % 2], w_l.at[0, u % 2]),
            pltpu.make_async_copy(expand.at[at], wbuf.at[2 + u % 2], w_l.at[1, u % 2]),
            pltpu.make_async_copy(active.at[:, at], act.at[u % 2], w_l.at[2, u % 2]),
            pltpu.make_async_copy(slope.at[:, at], slo.at[u % 2], w_l.at[3, u % 2]),
        ]

    def load_outlet():
        return pltpu.make_async_copy(outlet, obuf, loc.at[1])

    def load_intake(v):
        return pltpu.make_async_copy(intake.at[pl.ds(v * unit, unit)], wbuf.at[v % 4], w_l.at[4, v % 4])

    tdims = (((0,), (0,)), ((), ()))
    ndims = (((1,), (1,)), ((), ()))

    def mlp_one(u):
        k, half = u // 2, u % 2
        if u == 0:
            for copy in load(0):
                copy.start()
        if u + 1 < count_units:
            for copy in load(u + 1):
                copy.start()
        for copy in load(u):
            copy.wait()
        i = 2 * k

        def body(j, carry):
            cols = pl.ds(pl.multiple_of(j * 2 * top, 2 * top), 2 * top)
            g = lax.dot_general(act[u % 2, :, cols], cot[...], tdims, preferred_element_type=F32)
            made[i % slots, half, j] = g.astype(BF).reshape(2, top, width)
            return carry

        lax.fori_loop(0, unit // (2 * top), body, 0)

        def grad(j, carry):
            rows = pl.ds(pl.multiple_of(j * 256, 256), 256)
            to = pl.ds(pl.multiple_of(j * 256 + half * unit, 256), 256)
            g = lax.dot_general(cot[...], wbuf[u % 2, rows], ndims, preferred_element_type=F32)
            hg = (g * slo[u % 2, :, rows]).astype(BF)
            hgrad[:, to] = hg
            small[pl.ds(2 + k, 1), to] = jnp.sum(hg.astype(F32), axis=0, keepdims=True)
            return carry

        lax.fori_loop(0, unit // 256, grad, 0)

        def back(j, carry):
            cols = pl.ds(pl.multiple_of(j * 256, 256), 256)
            g = jnp.dot(hgrad[:, pl.ds(half * unit, unit)], wbuf[2 + u % 2, :, cols], preferred_element_type=F32)
            if u == 0:
                wide[:, cols] = g
            else:
                wide[:, cols] += g
            return carry

        lax.fori_loop(0, width // 256, back, 0)

    def mlp_two(k):
        i = 2 * k + 1

        def body(j, carry):
            cols = pl.ds(pl.multiple_of(j * 2 * top, 2 * top), 2 * top)
            g = lax.dot_general(hgrad[:, cols], second[...], tdims, preferred_element_type=F32)
            made[i % slots, j // 2, j % 2] = g.astype(BF).reshape(2, top, width)
            return carry

        lax.fori_loop(0, 4, body, 0)

    chunk = 64

    def norm_block(index, v_of, extra):
        gain = norm_gain[pl.ds(index, 1)]

        def body(i, carry):
            at = pl.ds(pl.multiple_of(i * chunk, chunk), chunk)
            v = v_of(at)
            center = v - jnp.mean(v, axis=-1, keepdims=True)
            r = lax.rsqrt(jnp.mean(center * center, axis=-1, keepdims=True) + norm_eps)
            nrm = center * r
            w = wide[at]
            u = w * gain
            down = r * (u - jnp.mean(u, axis=-1, keepdims=True) - nrm * jnp.mean(u * nrm, axis=-1, keepdims=True))
            sums = extra(at, down)
            new = [jnp.sum(w * nrm, axis=0, keepdims=True), jnp.sum(w, axis=0, keepdims=True)] + sums
            return tuple(a + b for a, b in zip(carry, new))

        zero = jnp.zeros((1, width), F32)
        out = lax.fori_loop(0, seq // chunk, body, (zero,) * (4 if index else 2))
        small[pl.ds(6 + index, 1)] = out[0]
        small[pl.ds(8 + index, 1)] = out[1]
        if index:
            small[pl.ds(10, 1)] = out[2]
            small[pl.ds(11, 1)] = out[3]

    def second_norm_back():
        load_outlet().start()
        for v in range(4):
            load_intake(v).start()

        def extra(at, down):
            g = cot[at].astype(F32)
            m = g + down
            mgrad[at] = m
            low = m.astype(BF)
            branch[at] = low
            return [jnp.sum(low.astype(F32), axis=0, keepdims=True), jnp.sum(g, axis=0, keepdims=True)]

        norm_block(1, lambda at: middle[at], extra)

    def outlet_piece(k):
        i = 8 + k
        cols = pl.ds(k * 8 * sizes[1], 8 * sizes[1])
        g = lax.dot_general(attended[:, cols], branch[...], tdims, preferred_element_type=F32)
        made[i % slots, :, :, :, pl.ds(0, sizes[1])] = g.astype(BF).reshape(2, 2, 2, sizes[1], width)

    def attended_back():
        load_outlet().wait()

        def body(j, carry):
            rows = pl.ds(pl.multiple_of(j * 256, 256), 256)
            g = lax.dot_general(branch[...], obuf[rows], ndims, preferred_element_type=F32)
            agrad[:, rows] = g.astype(BF)
            return carry

        lax.fori_loop(0, width // 256, body, 0)

    scale = HEAD_DIM ** (-0.5)

    def heads(first_pair, pairs):
        mask = live[...] > 0.0

        def body(p, carry):
            at = pl.ds(pl.multiple_of(p * 6 * HEAD_DIM, 6 * HEAD_DIM), 6 * HEAD_DIM)
            both = mixed[:, at]
            ag_both = agrad[:, pl.ds(pl.multiple_of(p * 2 * HEAD_DIM, 2 * HEAD_DIM), 2 * HEAD_DIM)]
            parts, sums = [], []
            for e in range(2):
                q, k, v = (both[:, (3 * e + b) * HEAD_DIM : (3 * e + b + 1) * HEAD_DIM] for b in range(3))
                ag = ag_both[:, e * HEAD_DIM : (e + 1) * HEAD_DIM]
                s = lax.dot_general(q, k, ndims, preferred_element_type=F32) * scale
                s = jnp.where(mask, s, masked_score)
                s = jnp.exp(s - jnp.max(s, axis=-1, keepdims=True))
                pr = s / jnp.sum(s, axis=-1, keepdims=True)
                vg = lax.dot_general(pr.astype(BF), ag, tdims, preferred_element_type=F32)
                dp = lax.dot_general(ag, v, ndims, preferred_element_type=F32)
                ds = (pr * (dp - jnp.sum(dp * pr, axis=-1, keepdims=True))).astype(BF)
                qg = jnp.dot(ds, k, preferred_element_type=F32) * scale
                kg = lax.dot_general(ds, q, tdims, preferred_element_type=F32) * scale
                parts += [qg.astype(BF), kg.astype(BF), vg.astype(BF)]
                sums.append((jnp.sum(parts[-3].astype(F32), 0, keepdims=True), jnp.sum(parts[-1].astype(F32), 0, keepdims=True)))
            mixed[:, at] = jnp.concatenate(parts, axis=1)
            to = pl.ds(pl.multiple_of(p * 2 * HEAD_DIM, 2 * HEAD_DIM), 2 * HEAD_DIM)
            small[pl.ds(0, 1), to] = jnp.concatenate([sums[0][0], sums[1][0]], axis=1)
            small[pl.ds(1, 1), to] = jnp.concatenate([sums[0][1], sums[1][1]], axis=1)
            return carry

        lax.fori_loop(first_pair, first_pair + pairs, body, 0)

    def intake_piece(k):
        i = 12 + k
        rows = 4 * sizes[0]

        def body(j, carry):
            cols = pl.ds(pl.multiple_of((2 * k + j) * rows, rows), rows)
            g = lax.dot_general(mixed[:, cols], first[...], tdims, preferred_element_type=F32)
            made[i % slots, j, :, :, pl.ds(0, sizes[0])] = g.astype(BF).reshape(2, 2, sizes[0], width)
            return carry

        lax.fori_loop(0, 2, body, 0)

    def first_back(v):
        load_intake(v).wait()

        def body(j, carry):
            cols = pl.ds(pl.multiple_of(j * 256, 256), 256)
            g = jnp.dot(mixed[:, pl.ds(v * unit, unit)], wbuf[v % 4, :, cols], preferred_element_type=F32)
            if v == 0:
                wide[:, cols] = g
            else:
                wide[:, cols] += g
            return carry

        lax.fori_loop(0, width // 256, body, 0)
        if v + 4 < intake.shape[0] // unit:
            load_intake(v + 4).start()

    def first_norm_back():
        def extra(at, down):
            token_grad[at] = (mgrad[at] + down).astype(BF)
            return []

        norm_block(0, lambda at: x_in[at].astype(F32), extra)

    work = {}
    blocks = []

    def block(name, us, piece, fn):
        work[name] = fn
        blocks.append((name, us, piece))

    for k in range(4):
        block(("m", 2 * k), 3.0, None, functools.partial(mlp_one, 2 * k))
        block(("m", 2 * k + 1), 3.0, 2 * k, functools.partial(mlp_one, 2 * k + 1))
        block(("e", k), 1.5, 2 * k + 1, functools.partial(mlp_two, k))
    block("n2", 3.0, None, second_norm_back)
    for k in range(4):
        block(("o", k), 0.5, 8 + k, functools.partial(outlet_piece, k))
    block("ab", 1.5, None, attended_back)
    for k in range(4):
        block(("h", k), 7.0, None, functools.partial(heads, 2 * k, 2))
        block(("i", k), 1.2, 12 + k, functools.partial(intake_piece, k))
    for v in range(intake.shape[0] // unit):
        block(("f", v), 0.8, None, functools.partial(first_back, v))
    block("n1", 3.0, None, first_norm_back)
    block("s0", 0.2, None, functools.partial(small_step, 0))

    small[pl.ds(12, 4)] = jnp.zeros((4, width), F32)
    moments(True)
    steps = plan(blocks, sizes, order, slots, width)
    pushed = {}
    stage = 1
    for step in steps:
        kind = step[0]
        if kind == "block":
            name = step[1]
            piece = {b[0]: b[2] for b in blocks}[name]
            first_piece = piece if piece is not None else (2 * (name[1] // 2) if name[0] == "m" else None)
            if first_piece is not None and first_piece - slots in pushed:
                pushed.pop(first_piece - slots).wait_send()
            work[name]()
        elif kind == "push":
            pushed[step[1]] = core_push(step[1])
            pushed[step[1]].start()
        elif kind == "one":
            one(step[1])
        elif kind == "two":
            two(step[1])
        elif kind == "three":
            three(step[1])
        elif kind == "four":
            four(step[1], 1)
        elif kind == "fourc":
            four(step[1], 2)
    for s in (1, 2, 3):
        small_step(s)
    for i in range(len(order)):
        five(i)
    for k in range(1, 4):
        slot = s_z.at[(z + 4 - k) % 4]
        push(slot, slot, (q_s.at[2 + k], q_r.at[2 + k]), zn[k - 1]).wait_recv()
    small_out[...] = s_z[0] + s_z[1] + s_z[2] + s_z[3]
    moments(False)
    for copy in pushed.values():
        copy.wait_send()
    for copy in held:
        copy.wait_send()
    for i in range(len(order)):
        for p in range(4):
            if p != PLANES[order[i][0]]:

                @pl.when(z == p)
                def _(i=i, p=p):
                    hop(i, p, lambda copy: copy.wait_send())


def backward_all(weights, saved, norm_gain, live, moms, sizes):
    intake, outlet, expand, shrink = weights
    active, slope, middle, mixed, attended, second, first, x, cot = saved
    seq, width = cot.shape
    top = max(sizes)
    order = []
    for k in range(4):
        order += [(3, k), (2, k)]
    order += [(1, k) for k in range(4)] + [(0, k) for k in range(4)]
    count = len(order)
    anyspace = pl.BlockSpec(memory_space=pl.ANY)
    vmem = pl.BlockSpec(memory_space=pltpu.VMEM)
    dma = pltpu.SemaphoreType.DMA
    unit = 512
    return pl.pallas_call(
        functools.partial(backward_kernel, sizes, order),
        out_shape=[
            jax.ShapeDtypeStruct((4, top, width), F32),
            jax.ShapeDtypeStruct((16, width), F32),
            jax.ShapeDtypeStruct((4, top, width), BF),
            jax.ShapeDtypeStruct((seq, width), BF),
        ],
        in_specs=[anyspace] * 6 + [vmem] * 9 + [anyspace] * 4,
        out_specs=[vmem, vmem, anyspace, vmem],
        scratch_shapes=[pltpu.VMEM((4, 2, 2, s, width), BF) for s in sizes]
        + [pltpu.VMEM((4, 2, 2, s // 2, width), BF) for s in sizes]
        + [pltpu.VMEM((4, s, width), BF) for s in sizes]
        + [pltpu.VMEM((2 if p in (1, 2) else 1, 4, s, width), BF) for s, p in zip(sizes, PLANES)]
        + [
            pltpu.VMEM((3, 2, 2, 2, top, width), BF),
            pltpu.VMEM((2, seq, unit), BF),
            pltpu.VMEM((2, seq, unit), F32),
            pltpu.VMEM((4, unit, width), BF),
            pltpu.VMEM((width, width), BF),
            pltpu.VMEM((seq, width), BF),
            pltpu.VMEM((seq, width), F32),
            pltpu.VMEM((seq, width), F32),
            pltpu.VMEM((seq, width), BF),
            pltpu.VMEM((seq, width), BF),
            pltpu.VMEM((16, width), F32),
            pltpu.VMEM((3, 16, width), F32),
            pltpu.VMEM((4, 16, width), F32),
            pltpu.VMEM((4, 16, width), F32),
            dma((2,)),
            dma((count,)),
            dma((count,)),
            dma((4, count)),
            dma((4, count)),
            dma((4, 4)),
            dma((4, 4, 2)),
            dma((6,)),
            dma((6,)),
            dma((4,)),
            dma((4,)),
            dma((5, 4)),
        ],
        compiler_params=pltpu.CompilerParams(collective_id=2, has_side_effects=True, vmem_limit_bytes=VMEM_LIMIT),
    )(shrink, expand, outlet, intake, active, slope, middle, mixed, attended, second, first, x, cot, norm_gain, live, *moms)


def split(v):
    hi = v.astype(BF)
    return hi, (v - hi.astype(F32)).astype(BF)


def dot(a, b):
    return jnp.dot(a, b, preferred_element_type=F32)


def muon_kernel(sizes, *refs):
    n = len(sizes)
    total, mom, outp, tokg = refs[:4]
    rows_out = refs[4 : 4 + n]
    grads = refs[4 + n : 4 + 2 * n]
    outp_all, tokg_all = refs[4 + 2 * n : 6 + 2 * n]
    refs = refs[6 + 2 * n :]
    low_g, uh, ul, pack, r_core, r_one, r_two, gathered, gf, gh, gl, low, b, tf, xf, xh, xl = refs[:17]
    g_s, g_r, a_s, a_r, o_s, o_r, s_s, s_r, loc = refs[17:]
    d, z, y, x, c = place()
    core, xn, yn, zn = partners(d, z, y, x, c)
    greet([core, xn, yn] + zn)
    held = []

    def start(copy):
        copy.start()
        held.append(copy)

    top, width = total.shape[1:]
    count = 4 * top
    block = width // 4
    height = 0
    for t in range(n):
        height = jnp.where(z == PLANES[t], sizes[t], height)
    per = top // 16

    def make(i, carry):
        k, r = i // per, (i % per) * 16
        at = pl.ds(pl.multiple_of(r, 16), 16)
        g = total[k, at]
        low_g[k, at] = g.astype(BF)
        u = g + muon_decay * (muon_decay * mom[k, at].astype(F32) + g)
        row = lax.broadcasted_iota(jnp.int32, u.shape, 0) + r
        u = jnp.where(row < height, u, 0.0)
        to = pl.ds(pl.multiple_of(i * 16, 16), 16)
        uh[to], ul[to] = split(u)
        return carry

    lax.fori_loop(0, 4 * per, make, 0)

    def back_home(src, dst, sems, local, first):
        for t in range(n):
            s, p = sizes[t], PLANES[t]

            @pl.when(z == p)
            def _(t=t, s=s, p=p):
                own = pltpu.make_async_copy(src.at[p, pl.ds(0, s)], dst[t], loc.at[local])
                away = [
                    push(src.at[(p + k) % 4, pl.ds(0, s)], dst[t], (sems[0].at[k], sems[1].at[t]), (d, (p + k) % 4))
                    for k in range(1, 4)
                ]
                if first:
                    for copy in away:
                        copy.start()
                    own.start()
                else:
                    own.wait()
                    for copy in away:
                        copy.wait_send()

            if not first:

                @pl.when(z != p)
                def _(t=t, p=p):
                    push(dst[t], dst[t], (sems[0].at[0], sems[1].at[t]), (d, p)).wait_recv()

    back_home(low_g, grads, (g_s, g_r), 0, True)
    for i, (a, e) in enumerate(((outp, outp_all), (tokg, tokg_all))):
        pltpu.make_async_copy(a.at[z], e.at[z], loc.at[1 + i]).start()
        for k in range(1, 4):
            start(push(a.at[(z + k) % 4], e.at[z], (o_s.at[i, k - 1], o_r.at[i, k - 1]), zn[k - 1]))

    places = {0: (0, 0), 3: (0, 4 * block), 1: (1, 0), 2: (1, 3 * block)}
    tdims = (((0,), (0,)), ((), ()))

    def product(half):
        for r, (h, col) in places.items():
            if h != half:
                continue
            mine = slice(r * block, (r + 1) * block)
            rest = slice(r * block, width)
            acc = lax.dot_general(uh[:, mine], uh[:, rest], tdims, preferred_element_type=F32)
            acc = acc + lax.dot_general(uh[:, mine], ul[:, rest], tdims, preferred_element_type=F32)
            acc = acc + lax.dot_general(ul[:, mine], uh[:, rest], tdims, preferred_element_type=F32)
            pack[half, :, col : col + width - r * block] = acc

    def sem(i):
        return (a_s.at[i], a_r.at[i])

    for v in (0, 1):

        @pl.when(c == v)
        def _(v=v):
            product(1 - v)
            push(pack.at[1 - v], r_core, sem(0), core).start()
            product(v)

    def add(dst, r0, src, rows, into=None):
        def body(i, carry):
            at = pl.ds(pl.multiple_of(r0 + i * 8, 8), 8)
            v = dst[at] + src[pl.ds(pl.multiple_of(i * 8, 8), 8)]
            (dst if into is None else into)[at] = v
            return carry

        lax.fori_loop(0, rows // 8, body, 0)

    def rows(ref, r, size):
        return ref.at[pl.ds(pl.multiple_of(r, 32), size)]

    half, quarter, eighth = block // 2, block // 4, block // 8
    push(r_core, r_core, sem(0), core).wait_recv()
    mine, whole = pack.at[c], gathered.at[c]
    add(mine, 0, r_core, block)
    base_a, base_b = 0, half
    start(push(rows(mine, base_a + (1 - y) * quarter, quarter), r_one.at[0], sem(1), yn))
    start(push(rows(mine, base_b + (1 - x) * quarter, quarter), r_one.at[1], sem(2), xn))
    push(r_one.at[0], r_one.at[0], sem(1), yn).wait_recv()
    mine_a = base_a + y * quarter
    add(mine, mine_a, r_one.at[0], quarter)
    start(push(rows(mine, mine_a + (1 - x) * eighth, eighth), r_two.at[0], sem(3), xn))
    push(r_one.at[1], r_one.at[1], sem(2), xn).wait_recv()
    mine_b = base_b + x * quarter
    add(mine, mine_b, r_one.at[1], quarter)
    start(push(rows(mine, mine_b + (1 - y) * eighth, eighth), r_two.at[1], sem(4), yn))
    push(r_two.at[0], r_two.at[0], sem(3), xn).wait_recv()
    own_a = mine_a + x * eighth
    add(mine, own_a, r_two.at[0], eighth, whole)
    start(push(rows(whole, own_a, eighth), rows(whole, own_a, eighth), sem(5), xn))
    push(r_two.at[1], r_two.at[1], sem(4), yn).wait_recv()
    own_b = mine_b + y * eighth
    add(mine, own_b, r_two.at[1], eighth, whole)
    start(push(rows(whole, own_b, eighth), rows(whole, own_b, eighth), sem(6), yn))
    got = rows(whole, mine_a + (1 - x) * eighth, eighth)
    push(got, got, sem(5), xn).wait_recv()
    start(push(rows(whole, mine_a, quarter), rows(whole, mine_a, quarter), sem(7), yn))
    got = rows(whole, mine_b + (1 - y) * eighth, eighth)
    push(got, got, sem(6), yn).wait_recv()
    start(push(rows(whole, mine_b, quarter), rows(whole, mine_b, quarter), sem(8), xn))
    start(push(rows(whole, mine_a, quarter), rows(whole, mine_a, quarter), sem(9), core))
    start(push(rows(whole, mine_b, quarter), rows(whole, mine_b, quarter), sem(10), core))
    other_a = base_a + (1 - y) * quarter
    got = rows(whole, other_a, quarter)
    push(got, got, sem(7), yn).wait_recv()
    start(push(got, got, sem(11), core))
    other_b = base_b + (1 - x) * quarter
    got = rows(whole, other_b, quarter)
    push(got, got, sem(8), xn).wait_recv()
    start(push(got, got, sem(12), core))
    beside = gathered.at[1 - c]
    for r, i in ((mine_a, 9), (mine_b, 10), (other_a, 11), (other_b, 12)):
        got = rows(beside, r, quarter)
        push(got, got, sem(i), core).wait_recv()

    eye = lax.broadcasted_iota(jnp.int32, (block, block), 0) == lax.broadcasted_iota(jnp.int32, (block, block), 1)
    trace = jnp.zeros((1, 1), F32)
    for r, (h, col) in places.items():
        v = jnp.where(eye, gathered[h, :, col : col + block], 0.0)
        trace = trace + jnp.sum(jnp.sum(v, axis=1, keepdims=True), axis=0, keepdims=True)
    inverse = 1.0 / (jnp.sqrt(trace) + frob_eps)
    squared = inverse * inverse
    for r, (h, col) in places.items():
        for k in range(r, 4):
            v = gathered[h, :, col + (k - r) * block : col + (k - r + 1) * block] * squared
            a, e = slice(r * block, (r + 1) * block), slice(k * block, (k + 1) * block)
            gf[a, e] = v
            gh[a, e], gl[a, e] = split(v)
            if k > r:
                v = v.T
                gf[e, a] = v
                gh[e, a], gl[e, a] = split(v)

    step = 64

    def scale_x(i, carry):
        at = pl.ds(pl.multiple_of(i * step, step), step)
        v = (uh[at].astype(F32) + ul[at].astype(F32)) * inverse
        xf[at] = v
        xh[at], xl[at] = split(v)
        return carry

    lax.fori_loop(0, count // step, scale_x, 0)

    def iterate(shift, double, last):
        level = coef_a + coef_b * shift + coef_c * shift * shift
        slope = coef_b + 2.0 * coef_c * shift
        if last:

            def lower(i, carry):
                at = pl.ds(pl.multiple_of(i * step, step), step)
                g = gf[at]
                row = lax.broadcasted_iota(jnp.int32, g.shape, 0) + i * step
                col = lax.broadcasted_iota(jnp.int32, g.shape, 1)
                g = g - jnp.where(row == col, shift, 0.0)
                gf[at] = g
                low[at] = g.astype(BF)
                return carry

            lax.fori_loop(0, width // step, lower, 0)
            b[...] = (slope * gf[...] + coef_c * dot(low[...], low[...])).astype(BF)
            xh[...] = (level * xf[...] + dot(xh[...], b[...])).astype(BF)
            return
        b[...] = (slope * gf[...] + coef_c * dot(gh[...], gh[...])).astype(BF)
        v = level * xf[...] + dot(xh[...], b[...])
        t = level * gf[...] + dot(gh[...], b[...])
        if double:
            v = v + dot(xl[...], b[...])
            t = t + dot(gl[...], b[...])
        xf[...] = v
        xh[...] = v.astype(BF)
        tf[...] = t
        low[...] = t.astype(BF)
        g = level * tf[...] + dot(b[...], low[...])
        if double:
            gl[...] = (tf[...] - low[...].astype(F32)).astype(BF)
            g = g + dot(b[...], gl[...])
        gf[...] = g
        gh[...] = g.astype(BF)

    iterate(0.0, True, False)

    def middle(i, carry):
        iterate(0.0, False, False)
        return carry

    lax.fori_loop(0, NS_STEPS - 2, middle, 0)
    iterate(0.8, False, True)

    back_home(xh.reshape(4, top, width), rows_out, (s_s, s_r), 3, True)

    for v in (0, 1):

        @pl.when(c == v)
        def _(v=v):
            push(pack.at[1 - v], r_core, sem(0), core).wait_send()

    for i, (a, e) in enumerate(((outp, outp_all), (tokg, tokg_all))):
        pltpu.make_async_copy(a.at[z], e.at[z], loc.at[1 + i]).wait()
        for k in range(1, 4):
            slot = e.at[(z + 4 - k) % 4]
            push(slot, slot, (o_s.at[i, k - 1], o_r.at[i, k - 1]), zn[k - 1]).wait_recv()
    back_home(low_g, grads, (g_s, g_r), 0, False)
    for copy in held:
        copy.wait_send()
    back_home(xh.reshape(4, top, width), rows_out, (s_s, s_r), 3, False)


def muon_all(total, mom, outp, tokg, sizes):
    top, width = total.shape[1:]
    count, block = 4 * top, width // 4
    anyspace = pl.BlockSpec(memory_space=pl.ANY)
    vmem = pl.BlockSpec(memory_space=pltpu.VMEM)
    dma = pltpu.SemaphoreType.DMA
    wide = block * 5
    return pl.pallas_call(
        functools.partial(muon_kernel, sizes),
        out_shape=[jax.ShapeDtypeStruct((s, width), BF) for s in sizes] * 2
        + [jax.ShapeDtypeStruct(outp.shape, outp.dtype), jax.ShapeDtypeStruct(tokg.shape, tokg.dtype)],
        in_specs=[vmem, vmem, anyspace, anyspace],
        out_specs=[anyspace] * (2 * len(sizes) + 2),
        scratch_shapes=[
            pltpu.VMEM((4, top, width), BF),
            pltpu.VMEM((count, width), BF),
            pltpu.VMEM((count, width), BF),
            pltpu.VMEM((2, block, wide), F32),
            pltpu.VMEM((block, wide), F32),
            pltpu.VMEM((2, block // 4, wide), F32),
            pltpu.VMEM((2, block // 8, wide), F32),
            pltpu.VMEM((2, block, wide), F32),
            pltpu.VMEM((width, width), F32),
            pltpu.VMEM((width, width), BF),
            pltpu.VMEM((width, width), BF),
            pltpu.VMEM((width, width), BF),
            pltpu.VMEM((width, width), BF),
            pltpu.VMEM((width, width), F32),
            pltpu.VMEM((count, width), F32),
            pltpu.VMEM((count, width), BF),
            pltpu.VMEM((count, width), BF),
            dma((4,)),
            dma((4,)),
            dma((13,)),
            dma((13,)),
            dma((2, 3)),
            dma((2, 3)),
            dma((4,)),
            dma((4,)),
            dma((4,)),
        ],
        compiler_params=pltpu.CompilerParams(collective_id=3, has_side_effects=True, vmem_limit_bytes=VMEM_LIMIT),
    )(total, mom, outp, tokg)


def finish_kernel(factors, *refs):
    n = len(factors)
    grads, rows, masters, moments = (refs[i * n : i * n + n] for i in range(4))
    outp, tokg, small = refs[4 * n : 4 * n + 3]
    state = refs[4 * n + 3 : 4 * n + 9]
    refs = refs[4 * n + 9 :]
    output, token_grad = refs[:2]
    shards, moments_new, masters_new, copies = (refs[2 + i * n : 2 + i * n + n] for i in range(4))
    vectors = refs[2 + 4 * n :]
    step = 16

    def over(rows, body):
        def one(i, carry):
            body(pl.ds(pl.multiple_of(i * step, step), step))
            return carry

        lax.fori_loop(0, rows // step, one, 0)

    for src, dst in ((outp, output), (tokg, token_grad)):
        for k in range(src.shape[0]):

            def body(at, src=src, dst=dst, k=k):
                dst[k, at] = src[k, at].astype(F32)

            over(src.shape[1], body)
    for m in range(n):

        def body(at, m=m):
            g = grads[m][at].astype(F32)
            shards[m][at] = g
            moments_new[m][at] = muon_decay * moments[m][at] + g
            new = masters[m][at] - factors[m] * rows[m][at].astype(F32)
            masters_new[m][at] = new
            copies[m][at] = new.astype(BF)

        over(grads[m].shape[0], body)
    width = small.shape[1]
    at = 0
    for i, (lo, hi) in enumerate(((0, 2), (6, 8), (8, 12))):
        g = small[lo:hi]
        change, first, second = adam_step(g, state[2 * i][...], state[2 * i + 1][...])
        for value in (g, change, first, second):
            vectors[at][...] = value
            at += 1


def finish(grads, rows, masters, moments, outp, tokg, small, state, factors):
    vmem = pl.BlockSpec(memory_space=pltpu.VMEM)
    args = [*grads, *rows, *masters, *moments, outp, tokg, small, *state]
    sized = [jax.ShapeDtypeStruct(v.shape, F32) for v in masters]
    shapes = [jax.ShapeDtypeStruct(v.shape, F32) for v in (outp, tokg)] + sized * 3
    shapes += [jax.ShapeDtypeStruct(v.shape, BF) for v in masters]
    for v in state[::2]:
        shapes += [jax.ShapeDtypeStruct(v.shape, F32)] * 4
    return pl.pallas_call(
        functools.partial(finish_kernel, factors),
        out_shape=shapes,
        in_specs=[vmem] * len(args),
        out_specs=[vmem] * len(shapes),
        compiler_params=pltpu.CompilerParams(vmem_limit_bytes=VMEM_LIMIT),
        cost_estimate=pl.CostEstimate(flops=10**7, bytes_accessed=15 * 10**6, transcendentals=0),
    )(*args)


def per_device_fast(
    tokens,
    cotangent,
    keep_mask,
    intake,
    outlet,
    expand,
    shrink,
    intake_moment,
    outlet_moment,
    expand_moment,
    shrink_moment,
    head_bias,
    expand_bias,
    norm_gain,
    model_bias,
    head_first,
    head_second,
    expand_first,
    expand_second,
    gain_first,
    gain_second,
    bias_first,
    bias_second,
):
    shape = tokens.shape
    local, width = shape[2:]
    z = lax.axis_index("tensor")
    masters = (intake, outlet, expand, shrink)
    moments = (intake_moment, outlet_moment, expand_moment, shrink_moment)
    sizes = tuple(v.shape[0] for v in masters)
    seq = keep_mask.shape[2]
    keep = lax.dynamic_index_in_dim(keep_mask.reshape(-1, seq), z, 0, keepdims=True)
    live = jnp.logical_or(keep != 0, jnp.arange(seq)[None] < BUF).astype(F32)
    parts = head_bias.reshape(2, -1, HEAD_DIM)
    mixed_bias = jnp.stack([parts[0], jnp.zeros_like(parts[0]), parts[1]], axis=1).reshape(1, -1)
    made = forward_all(
        [v.astype(BF) for v in masters],
        tokens.reshape(-1, local, width),
        cotangent.reshape(-1, local, width),
        norm_gain,
        model_bias,
        mixed_bias,
        expand_bias[None],
        live,
    )
    whole = [v.reshape(-1, width) for v in made[:4]]
    x, cot = (v.reshape(-1, width) for v in made[4:6])
    out, saved = made[6], tuple(made[7:]) + (x, cot)
    moms = [v.astype(BF) for v in moments]
    total, small, mom, token_grad = backward_all(whole, saved, norm_gain, live, moms, sizes)
    made = muon_all(total, mom, out.reshape(-1, local, width), token_grad.reshape(-1, local, width), sizes)
    rows_scale = lax.axis_size("dp") * lax.axis_size("tensor")
    factors = [rate * (s * rows_scale / width) ** 0.5 for s, rate in zip(sizes, muon_rates)]
    state = (head_first, head_second, gain_first, gain_second, bias_first, bias_second)
    done = finish(made[4:8], made[:4], masters, moments, made[8], made[9], small, state, factors)
    output, token_grad = (v.reshape(shape) for v in done[:2])
    shards, moments_new, masters_new, copies = (tuple(done[2 + 4 * i : 6 + 4 * i]) for i in range(4))
    head, gain, bias = (done[18 + 4 * i : 22 + 4 * i] for i in range(3))
    hidden_total = small[2:6].reshape(expand_bias.shape)
    hidden = adam_step(hidden_total, expand_first, expand_second)
    return (
        (output, token_grad)
        + shards
        + (head[0], hidden_total, gain[0], bias[0])
        + moments_new
        + masters_new
        + copies
        + (head[1], hidden[0], gain[1], bias[1])
        + tuple(head[2:])
        + tuple(hidden[1:])
        + tuple(gain[2:])
        + tuple(bias[2:])
    )


def solution(mesh):
    placed = (
        P(None, "dp", "tensor", None),
        P(None, "dp", "tensor", None),
        P(None, "dp", None),
        P(("tensor", "dp"), None),
        P(("tensor", "dp"), None),
        P(("tensor", "dp"), None),
        P(("tensor", "dp"), None),
        P(("tensor", "dp"), None),
        P(("tensor", "dp"), None),
        P(("tensor", "dp"), None),
        P(("tensor", "dp"), None),
        P(),
        P(),
        P(),
        P(),
        P(),
        P(),
        P(),
        P(),
        P(),
        P(),
        P(),
        P(),
    )
    fast = mesh.shape["dp"] == 8 and mesh.shape["tensor"] == 4
    return jax.shard_map(
        per_device_fast if fast else per_device,
        mesh=mesh,
        in_specs=placed,
        out_specs=(
            P(None, "dp", "tensor", None),
            P(None, "dp", "tensor", None),
            P(("tensor", "dp"), None),
            P(("tensor", "dp"), None),
            P(("tensor", "dp"), None),
            P(("tensor", "dp"), None),
            P(),
            P(),
            P(),
            P(),
            P(("tensor", "dp"), None),
            P(("tensor", "dp"), None),
            P(("tensor", "dp"), None),
            P(("tensor", "dp"), None),
            P(("tensor", "dp"), None),
            P(("tensor", "dp"), None),
            P(("tensor", "dp"), None),
            P(("tensor", "dp"), None),
            P(("tensor", "dp"), None),
            P(("tensor", "dp"), None),
            P(("tensor", "dp"), None),
            P(("tensor", "dp"), None),
            P(),
            P(),
            P(),
            P(),
            P(),
            P(),
            P(),
            P(),
            P(),
            P(),
            P(),
            P(),
        ),
        check_vma=False,
    )
```

```python
import functools

import jax
import jax.numpy as jnp
from jax import lax
from jax.experimental import pallas as pl
from jax.experimental.pallas import tpu as pltpu
from jax.sharding import PartitionSpec as P

HEAD_DIM = 64
BUF = 64
NS_STEPS = 5
ADAM_STEP = 10


norm_eps = 1e-06
first_decay = 0.9
second_decay = 0.95
adam_rate = 0.05
adam_eps = 1e-08
muon_decay = 0.5
muon_rates = (1.0, 4.0, 1.0, 1.0)
frob_eps = 1e-07
coef_a = 3.4445
coef_b = -4.775
coef_c = 2.0315
masked_score = -1000000000.0


def precise(form, left, right):
    return jnp.einsum(form, left, right, precision=lax.Precision.HIGHEST)


def layer_norm(inputs_row, gain_row, shift_row):
    center = inputs_row - jnp.mean(inputs_row, axis=-1, keepdims=True)
    spread = jnp.mean(center * center, axis=-1, keepdims=True)
    return center * lax.rsqrt(spread + norm_eps) * gain_row + shift_row


def softmax_rows(scores):
    largest = jnp.max(scores, axis=-1, keepdims=True)
    powers = jnp.exp(scores - largest)
    return powers / jnp.sum(powers, axis=-1, keepdims=True)


def exact_gelu(inputs_row):
    return jax.nn.gelu(inputs_row, approximate=False)


def attend_weights(queries, keys_all, live_keys):
    scores = jnp.einsum(
        "iqhe,ikhe->ihqk", queries, keys_all, preferred_element_type=jnp.float32
    ) * HEAD_DIM ** (-0.5)
    scores = jnp.where(live_keys[:, None, None, :], scores, masked_score)
    return softmax_rows(scores)


def reduce_blocks(blocks):
    return (
        lax.psum_scatter(blocks[0], "dp", scatter_dimension=0, tiled=True),
        lax.psum_scatter(blocks[1], "dp", scatter_dimension=0, tiled=True),
        lax.psum_scatter(blocks[2], "dp", scatter_dimension=0, tiled=True),
        lax.psum_scatter(blocks[3], "dp", scatter_dimension=0, tiled=True),
    )


def gram_whole(matrix):
    model_width = matrix.shape[1]
    own_rows = model_width // lax.axis_size("dp")
    shard_rows = lax.psum_scatter(
        precise(
            "rm,rn->mn", lax.slice_in_dim(matrix, 0, own_rows * lax.axis_size("dp"), axis=1), matrix
        ),
        "dp",
        scatter_dimension=0,
        tiled=True,
    )
    return lax.all_gather(shard_rows, "dp", axis=0, tiled=True)


def newton_step(scaled, gram):
    product = precise("rk,kn->rn", scaled, gram)
    return coef_a * scaled + coef_b * product + coef_c * precise("rk,kn->rn", product, gram)


def adam_step(gradient, first, second):
    first_new = first_decay * first + (1.0 - first_decay) * gradient
    second_new = second_decay * second + (1.0 - second_decay) * gradient * gradient
    first_hat = first_new / (1.0 - first_decay**ADAM_STEP)
    second_hat = second_new / (1.0 - second_decay**ADAM_STEP)
    change = -adam_rate * first_hat / (jnp.sqrt(second_hat) + adam_eps)
    return (change, first_new, second_new)


def per_device(
    tokens,
    cotangent,
    keep_mask,
    intake,
    outlet,
    expand,
    shrink,
    intake_moment,
    outlet_moment,
    expand_moment,
    shrink_moment,
    head_bias,
    expand_bias,
    norm_gain,
    model_bias,
    head_first,
    head_second,
    expand_first,
    expand_second,
    gain_first,
    gain_second,
    bias_first,
    bias_second,
):
    micro_count, images, local_seq, model_width = tokens.shape
    seq_len = keep_mask.shape[2]
    tensor_size = lax.axis_size("tensor")
    tensor_index = lax.axis_index("tensor")
    head_cols = model_width // tensor_size
    local_heads = head_cols // HEAD_DIM
    hidden_cols = expand_bias.shape[0] // tensor_size
    head_start = tensor_index * head_cols
    hidden_start = tensor_index * hidden_cols
    query_bias = lax.dynamic_slice_in_dim(head_bias[0], head_start, head_cols, 0).reshape(
        local_heads, HEAD_DIM
    )
    value_bias = lax.dynamic_slice_in_dim(head_bias[1], head_start, head_cols, 0).reshape(
        local_heads, HEAD_DIM
    )
    mixed_bias = jnp.stack([query_bias, jnp.zeros_like(query_bias), value_bias], axis=1).reshape(
        3 * head_cols
    )
    hidden_bias = lax.dynamic_slice_in_dim(expand_bias, hidden_start, hidden_cols, 0)
    position = jnp.arange(seq_len)
    masters = (intake, outlet, expand, shrink)
    block_shapes = (
        (3 * head_cols, model_width),
        (head_cols, model_width),
        (hidden_cols, model_width),
        (hidden_cols, model_width),
    )
    totals = tuple((jnp.zeros(shape_one, jnp.float32) for shape_one in block_shapes))
    gain_grad = jnp.zeros((2, model_width), jnp.float32)
    bias_grad = jnp.zeros((4, model_width), jnp.float32)
    mixed_bias_grad = jnp.zeros((2, head_cols), jnp.float32)
    hidden_bias_grad = jnp.zeros((hidden_cols,), jnp.float32)
    outputs = []
    token_grads = []
    for micro_index in range(micro_count):
        intake_block, outlet_block, expand_block, shrink_block = (
            lax.all_gather(intake.astype(jnp.bfloat16), "dp", axis=0, tiled=True),
            lax.all_gather(outlet.astype(jnp.bfloat16), "dp", axis=0, tiled=True),
            lax.all_gather(expand.astype(jnp.bfloat16), "dp", axis=0, tiled=True),
            lax.all_gather(shrink.astype(jnp.bfloat16), "dp", axis=0, tiled=True),
        )
        token_rows = tokens[micro_index].astype(jnp.float32)
        live_keys = jnp.logical_or(keep_mask[micro_index] > 0, position[None, :] < BUF)
        first_local = layer_norm(token_rows, norm_gain[0], model_bias[0]).astype(jnp.bfloat16)
        first_norm = lax.all_gather(first_local, "tensor", axis=1, tiled=True)
        mixed_rows = (
            jnp.einsum("isd,rd->isr", first_norm, intake_block, preferred_element_type=jnp.float32)
            + mixed_bias
        )
        mixed_rows = mixed_rows.astype(jnp.bfloat16).reshape(
            images, seq_len, local_heads, 3, HEAD_DIM
        )
        queries = mixed_rows[:, :, :, 0]
        keys_all = mixed_rows[:, :, :, 1]
        values = mixed_rows[:, :, :, 2]
        attention = attend_weights(queries, keys_all, live_keys)
        attention_low = attention.astype(jnp.bfloat16)
        attended = jnp.einsum(
            "ihqk,ikhe->iqhe", attention_low, values, preferred_element_type=jnp.float32
        )
        attended = attended.reshape(images, seq_len, head_cols).astype(jnp.bfloat16)
        part_sum = jnp.einsum(
            "isc,cd->isd", attended, outlet_block, preferred_element_type=jnp.float32
        )
        middle = (
            token_rows
            + lax.psum_scatter(part_sum, "tensor", scatter_dimension=1, tiled=True)
            + model_bias[2]
        )
        second_local = layer_norm(middle, norm_gain[1], model_bias[1]).astype(jnp.bfloat16)
        second_norm = lax.all_gather(second_local, "tensor", axis=1, tiled=True)
        hidden = (
            jnp.einsum("isd,fd->isf", second_norm, expand_block, preferred_element_type=jnp.float32)
            + hidden_bias
        )
        active = exact_gelu(hidden).astype(jnp.bfloat16)
        part_two = jnp.einsum(
            "isf,fd->isd", active, shrink_block, preferred_element_type=jnp.float32
        )
        outputs.append(
            middle
            + lax.psum_scatter(part_two, "tensor", scatter_dimension=1, tiled=True)
            + model_bias[3]
        )
        cot_local = cotangent[micro_index]
        cot_rows = lax.all_gather(cot_local, "tensor", axis=1, tiled=True)
        shrink_block_grad = jnp.einsum(
            "isf,isd->fd", active, cot_rows, preferred_element_type=jnp.float32
        )
        active_grad = jnp.einsum(
            "isd,fd->isf", cot_rows, shrink_block, preferred_element_type=jnp.float32
        )
        gelu_value, gelu_back = jax.vjp(exact_gelu, hidden)
        hidden_grad = gelu_back(active_grad)[0].astype(jnp.bfloat16)
        hidden_bias_grad = hidden_bias_grad + jnp.sum(hidden_grad.astype(jnp.float32), axis=(0, 1))
        expand_block_grad = jnp.einsum(
            "isf,isd->fd", hidden_grad, second_norm, preferred_element_type=jnp.float32
        )
        second_part = jnp.einsum(
            "isf,fd->isd", hidden_grad, expand_block, preferred_element_type=jnp.float32
        )
        second_grad = lax.psum_scatter(second_part, "tensor", scatter_dimension=1, tiled=True)
        norm_value, norm_back = jax.vjp(layer_norm, middle, norm_gain[1], model_bias[1])
        middle_from_norm, gain_two_grad, shift_two_grad = norm_back(second_grad)
        cot_float = cot_local.astype(jnp.float32)
        middle_grad = cot_float + middle_from_norm
        branch_grad = middle_grad.astype(jnp.bfloat16)
        branch_rows = lax.all_gather(branch_grad, "tensor", axis=1, tiled=True)
        outlet_block_grad = jnp.einsum(
            "isc,isd->cd", attended, branch_rows, preferred_element_type=jnp.float32
        )
        attended_grad = jnp.einsum(
            "isd,cd->isc", branch_rows, outlet_block, preferred_element_type=jnp.float32
        )
        attended_grad = attended_grad.astype(jnp.bfloat16).reshape(
            images, seq_len, local_heads, HEAD_DIM
        )
        attention = attend_weights(queries, keys_all, live_keys)
        attention_low = attention.astype(jnp.bfloat16)
        values_grad = jnp.einsum(
            "ihqk,iqhe->ikhe", attention_low, attended_grad, preferred_element_type=jnp.float32
        )
        attention_grad = jnp.einsum(
            "iqhe,ikhe->ihqk", attended_grad, values, preferred_element_type=jnp.float32
        )
        score_grad = attention * (
            attention_grad - jnp.sum(attention_grad * attention, axis=-1, keepdims=True)
        )
        score_grad = score_grad.astype(jnp.bfloat16)
        queries_grad = jnp.einsum(
            "ihqk,ikhe->iqhe", score_grad, keys_all, preferred_element_type=jnp.float32
        ) * HEAD_DIM ** (-0.5)
        keys_grad = jnp.einsum(
            "ihqk,iqhe->ikhe", score_grad, queries, preferred_element_type=jnp.float32
        ) * HEAD_DIM ** (-0.5)
        mixed_grad = jnp.stack([queries_grad, keys_grad, values_grad], axis=3).astype(jnp.bfloat16)
        mixed_sums = jnp.sum(mixed_grad.astype(jnp.float32), axis=(0, 1))
        mixed_bias_grad = mixed_bias_grad + jnp.stack(
            [mixed_sums[:, 0].reshape(head_cols), mixed_sums[:, 2].reshape(head_cols)]
        )
        mixed_grad = mixed_grad.reshape(images, seq_len, 3 * head_cols)
        intake_block_grad = jnp.einsum(
            "isr,isd->rd", mixed_grad, first_norm, preferred_element_type=jnp.float32
        )
        first_part = jnp.einsum(
            "isr,rd->isd", mixed_grad, intake_block, preferred_element_type=jnp.float32
        )
        first_grad = lax.psum_scatter(first_part, "tensor", scatter_dimension=1, tiled=True)
        first_value, first_back = jax.vjp(layer_norm, token_rows, norm_gain[0], model_bias[0])
        token_from_norm, gain_one_grad, shift_one_grad = first_back(first_grad)
        token_grads.append(middle_grad + token_from_norm)
        gain_grad = gain_grad + jnp.stack([gain_one_grad, gain_two_grad])
        bias_grad = bias_grad + jnp.stack(
            [
                shift_one_grad,
                shift_two_grad,
                jnp.sum(branch_grad.astype(jnp.float32), axis=(0, 1)),
                jnp.sum(cot_float, axis=(0, 1)),
            ]
        )
        block_grads = (intake_block_grad, outlet_block_grad, expand_block_grad, shrink_block_grad)
        totals = tuple((total + block_one for total, block_one in zip(totals, block_grads)))
    shards = reduce_blocks(totals)
    head_full = lax.dynamic_update_slice_in_dim(
        jnp.zeros((2, model_width), jnp.float32), mixed_bias_grad, head_start, 1
    )
    hidden_full = lax.dynamic_update_slice_in_dim(
        jnp.zeros(expand_bias.shape, jnp.float32), hidden_bias_grad, hidden_start, 0
    )
    gain_total, bias_total, head_total, hidden_total = lax.psum(
        (gain_grad, bias_grad, head_full, hidden_full), ("dp", "tensor")
    )
    moments = (intake_moment, outlet_moment, expand_moment, shrink_moment)
    moments_new = [muon_decay * moment + gradient for gradient, moment in zip(shards, moments)]
    updates = [gradient + muon_decay * moment for gradient, moment in zip(shards, moments_new)]
    rows_max = max((update.shape[0] for update in updates))
    padded = jnp.stack(
        [jnp.pad(update, ((0, rows_max - update.shape[0]), (0, 0))) for update in updates]
    )
    spread = lax.all_to_all(padded, "tensor", split_axis=0, concat_axis=0, tiled=True)
    own_matrix = spread.reshape(tensor_size * rows_max, model_width)
    raw_gram = gram_whole(own_matrix)
    measure = jnp.sqrt(jnp.trace(raw_gram)) + frob_eps
    scaled = own_matrix / measure
    gram = raw_gram / (measure * measure)
    for step in range(NS_STEPS):
        if step > 0:
            gram = gram_whole(scaled)
        scaled = newton_step(scaled, gram)
    returned = lax.all_to_all(
        scaled.reshape(tensor_size, rows_max, model_width),
        "tensor",
        split_axis=0,
        concat_axis=0,
        tiled=True,
    )
    rows_scale = lax.axis_size("dp") * tensor_size
    masters_new = [
        weight
        - muon_rates[position_one]
        * (weight.shape[0] * rows_scale / weight.shape[1]) ** 0.5
        * returned[position_one, : weight.shape[0]]
        for position_one, weight in enumerate(masters)
    ]
    head_bias_change, head_first_new, head_second_new = adam_step(
        head_total, head_first, head_second
    )
    expand_bias_change, expand_first_new, expand_second_new = adam_step(
        hidden_total, expand_first, expand_second
    )
    norm_gain_change, gain_first_new, gain_second_new = adam_step(
        gain_total, gain_first, gain_second
    )
    model_bias_change, bias_first_new, bias_second_new = adam_step(
        bias_total, bias_first, bias_second
    )
    output = jnp.stack(outputs)
    token_grad = jnp.stack(token_grads)
    return (
        output,
        token_grad,
        shards[0],
        shards[1],
        shards[2],
        shards[3],
        head_total,
        hidden_total,
        gain_total,
        bias_total,
        moments_new[0],
        moments_new[1],
        moments_new[2],
        moments_new[3],
        masters_new[0],
        masters_new[1],
        masters_new[2],
        masters_new[3],
        masters_new[0].astype(jnp.bfloat16),
        masters_new[1].astype(jnp.bfloat16),
        masters_new[2].astype(jnp.bfloat16),
        masters_new[3].astype(jnp.bfloat16),
        head_bias_change,
        expand_bias_change,
        norm_gain_change,
        model_bias_change,
        head_first_new,
        head_second_new,
        expand_first_new,
        expand_second_new,
        gain_first_new,
        gain_second_new,
        bias_first_new,
        bias_second_new,
    )


MESH = pl.DeviceIdType.MESH
BF = jnp.bfloat16
F32 = jnp.float32
VMEM_LIMIT = 60 * 1024 * 1024


def place():
    d = lax.axis_index("dp")
    z = lax.axis_index("tensor")
    y, x, c = d // 4, (d // 2) % 2, d % 2
    return d, z, y, x, c


def partners(d, z, y, x, c):
    core = (d + 1 - 2 * c, z)
    xn = (d + 2 - 4 * x, z)
    yn = (d + 4 - 8 * y, z)
    zn = [(d, (z + k) % 4) for k in range(1, 4)]
    return core, xn, yn, zn


def greet(others):
    barrier = pltpu.get_barrier_semaphore()
    for other in others:
        pl.semaphore_signal(barrier, inc=1, device_id=other, device_id_type=MESH)
    pl.semaphore_wait(barrier, len(others))


def push(src, dst, sems, to):
    return pltpu.make_async_remote_copy(
        src_ref=src, dst_ref=dst, send_sem=sems[0], recv_sem=sems[1], device_id=to, device_id_type=MESH
    )


LINK = 93.5e3


OPT = dict(a2=0, a3=5, order=0, static=0, lagz=2.0, rate=93.5e3, lat=1.5, full=3.0, work=1.0, brate=93.5e3, blat=1.5, bone=3.0, bwork=1.3, bhop=3.0, bwin=3, bz=0.0)


def live_keys(keep, z):
    count = keep.shape[1]
    row = keep[z // count, pl.ds(z % count, 1)]
    position = lax.broadcasted_iota(jnp.int32, row.shape, 1)
    return jnp.logical_or(row != 0, position < BUF)


def plan_forward(blocks, order, sizes, width, slots):
    done, events = [], []
    link = {"x": 0.0, "y": 0.0, "z": 0.0}
    now, at_z = 0.0, 2.0

    def carry(lane, start, rows):
        link[lane] = max(start, link[lane]) + rows * width * 4 / OPT["rate"]
        return link[lane] + OPT["lat"]

    for i, (m, k) in enumerate(order):
        if k == 0:
            events.append((0.1 * i, "one", i))
        else:
            at_z += sizes[m] * width * 4 / OPT["rate"]
            events.append((at_z + OPT["lagz"] * k, "one", i))
    whole, loaded = {}, {}
    head = 0
    todo = list(range(len(blocks)))
    if OPT["static"]:
        count = len(order)
        pieces = {}
        def ready(j):
            return blocks[j][2] is None or blocks[j][2] in pieces
        at = 0
        for i in range(count + 2 + OPT["static"]):
            if i < count:
                done.append(("one", i))
            if 1 <= i <= count:
                done.append(("two", i - 1))
            if 2 <= i <= count + 1:
                done.append(("three", i - 2))
            if i >= 2 + OPT["static"]:
                pieces[i - 2 - OPT["static"]] = True
            budget = OPT["budget"]
            while todo and ready(todo[0]) and budget > 0:
                j = todo.pop(0)
                while head < len(blocks) and head <= j + 2 and ready(head):
                    if blocks[head][2] is not None:
                        done.append(("load", head))
                    head += 1
                done.append(("block", j))
                budget -= blocks[j][1]
        while todo:
            j = todo.pop(0)
            while head < len(blocks) and head <= j + 2:
                if blocks[head][2] is not None:
                    done.append(("load", head))
                head += 1
            done.append(("block", j))
        return done
    while events or todo:
        events.sort()
        if events and events[0][0] <= now:
            _, kind, i = events.pop(0)
            s = sizes[order[i][0]]
            if kind != "full":
                done.append((kind, i))
                now += 0.15
            if kind == "one":
                ready = max(carry("x", now, s / 2), carry("y", now, s / 2))
                events.append((ready, "two", i))
            elif kind == "two":
                ready = max(carry("x", now, s), carry("y", now, s))
                events.append((ready, "three", i))
            elif kind == "three":
                events.append((now + OPT["full"], "full", i))
            else:
                whole[i] = True
            continue
        busy = sum(1 for j in loaded if j in todo)
        while head < len(blocks) and (blocks[head][2] is None or (blocks[head][2] in whole and busy < slots)):
            if blocks[head][2] is not None:
                done.append(("load", head))
                loaded[head] = now + 2.0
                busy += 1
            head += 1
        wait = None
        if todo:
            j = todo[0]
            if blocks[j][2] is None or j in loaded:
                if blocks[j][2] is None or loaded[j] <= now:
                    todo.pop(0)
                    done.append(("block", j))
                    now += blocks[j][1] * OPT["work"]
                    continue
                wait = loaded[j]
        times = [v for v in (wait, events[0][0] if events else None) if v is not None]
        now = max(now, min(times))
    return done


def forward_kernel(sizes, order, *refs):
    n = 4
    w = refs[:n]
    tok, cot = refs[n : n + 2]
    norm_gain, model_bias, head_bias, expand_bias, keep = refs[n + 2 : n + 7]
    refs = refs[n + 7 :]
    o_full = refs[:n]
    o_x, cot_all, output, o_active, o_slope, o_middle, o_mixed, o_attended, o_second, o_first = refs[n : n + 10]
    refs = refs[n + 10 :]
    full = refs[:n]
    xs, first, mixed, attended, acc, middle, second, active, slope, mixed_bias = refs[n : n + 10]
    z_s, z_r, loc, t_s, t_r, p_s, p_r, w_l, out_l, s_l = refs[n + 10 :]
    d, z, y, x, c = place()
    core, xn, yn, zn = partners(d, z, y, x, c)
    for m in range(n):
        full[m][z, y, x, c] = w[m][...].astype(BF)
    greet([core, xn, yn] + zn)
    held = []
    written = []
    inner = z * (3 - z) > 0
    seq, width = first.shape

    def start(copy):
        copy.start()
        held.append(copy)
        return copy

    def source(j):
        return (z, z + 1 - 2 * (z % 2), 2 - z // 2, 3 - 3 * (z // 2))[j]

    def along(m, j, go):
        slot = full[m].at[source(j), y, x, c]
        if j == 0:

            @pl.when(z < 3)
            def _():
                go(push(slot, slot, (z_s.at[m, 0], z_r.at[m, z]), (d, z + 1)))

            @pl.when(z > 0)
            def _():
                go(push(slot, slot, (z_s.at[m, 1], z_r.at[m, z]), (d, z - 1)))

        else:
            beyond = 3 - z if j == 1 else 3 * (z - 1)

            @pl.when(inner)
            def _():
                go(push(slot, slot, (z_s.at[m, 1 + j], z_r.at[m, source(j)]), (d, beyond)))

    locals_ = []
    for i, (a, b) in enumerate(((tok, xs), (cot, cot_all))):
        copy = pltpu.make_async_copy(a.at[z], b.at[z], loc.at[i])
        copy.start()
        locals_.append(copy)

    def rows_push(i, a, b):
        for k in range(1, 4):
            start(push(a.at[(z + k) % 4], b.at[z], (t_s.at[i, k - 1], t_r.at[i, k - 1]), zn[k - 1]))

    def rows_wait(i, b):
        locals_[i].wait()
        for k in range(1, 4):
            slot = b.at[(z + 4 - k) % 4]
            push(slot, slot, (t_s.at[i, k - 1], t_r.at[i, k - 1]), zn[k - 1]).wait_recv()

    def sem(i, stage):
        return (p_s.at[stage, i], p_r.at[stage, i])

    def one(i):
        m, k = order[i]
        h = sizes[m] // 2
        s = source(k)
        if k > 0:
            slot = full[m].at[s, y, x, c]
            push(slot, slot, (z_s.at[m, 1 + k], z_r.at[m, s]), core).wait_recv()
            along(m, k, lambda copy: copy.start())
        a = full[m].at[s, y, x, c, pl.ds(0, h)]
        b = full[m].at[s, y, x, c, pl.ds(h, h)]
        start(push(a, a, sem(i, 0), xn))
        start(push(b, b, sem(i, 1), yn))

    def two(i):
        m, k = order[i]
        h = sizes[m] // 2
        s = source(k)
        a = full[m].at[s, y, 1 - x, c, pl.ds(0, h)]
        push(a, a, sem(i, 0), xn).wait_recv()
        a = full[m].at[s, y, :, c, pl.ds(0, h)]
        start(push(a, a, sem(i, 2), yn))
        b = full[m].at[s, 1 - y, x, c, pl.ds(h, h)]
        push(b, b, sem(i, 1), yn).wait_recv()
        b = full[m].at[s, :, x, c, pl.ds(h, h)]
        start(push(b, b, sem(i, 3), xn))

    def three(i):
        m, k = order[i]
        h = sizes[m] // 2
        s = source(k)
        a = full[m].at[s, 1 - y, :, c, pl.ds(0, h)]
        push(a, a, sem(i, 2), yn).wait_recv()
        b = full[m].at[s, :, 1 - x, c, pl.ds(h, h)]
        push(b, b, sem(i, 3), xn).wait_recv()
        e = full[m].at[s, :, :, c]
        start(push(e, e, sem(i, 4), core))

    ndims = (((1,), (1,)), ((), ()))
    kept = []

    def load(m, k):
        i = order.index((m, k))
        e = full[m].at[source(k), :, :, 1 - c]
        push(e, e, sem(i, 4), core).wait_recv()
        copy = pltpu.make_async_copy(full[m].at[source(k)], o_full[m].at[source(k)], w_l.at[i])
        copy.start()
        kept.append(copy)

    def save(src, dst, i):
        copy = pltpu.make_async_copy(src, dst, out_l.at[i])
        copy.start()
        written.append(copy)

    chunk = seq // 4

    def norm_rows(index, v_of, dst):
        gain, shift = norm_gain[pl.ds(index, 1)], model_bias[pl.ds(index, 1)]

        def body(i, carry):
            at = pl.ds(pl.multiple_of(i * chunk, chunk), chunk)
            v = v_of(at, i)
            center = v - jnp.mean(v, axis=-1, keepdims=True)
            r = lax.rsqrt(jnp.mean(center * center, axis=-1, keepdims=True) + norm_eps)
            dst[at] = (center * r * gain + shift).astype(BF)
            return carry

        lax.fori_loop(0, seq // chunk, body, 0)

    def first_norm():
        rows_wait(0, xs)
        for h in range(width // HEAD_DIM):
            at, to = h * HEAD_DIM, 3 * h * HEAD_DIM
            mixed_bias[:, to : to + HEAD_DIM] = head_bias[0:1, at : at + HEAD_DIM]
            mixed_bias[:, to + HEAD_DIM : to + 2 * HEAD_DIM] = jnp.zeros((1, HEAD_DIM), F32)
            mixed_bias[:, to + 2 * HEAD_DIM : to + 3 * HEAD_DIM] = head_bias[1:2, at : at + HEAD_DIM]
        norm_rows(0, lambda at, i: xs[i].astype(F32), first)
        save(xs, o_x, 1)
        save(first, o_first, 0)

    def project(k):
        s = source(k)
        rows = 4 * sizes[0]

        def body(j, carry):
            at = pl.ds(pl.multiple_of(s * 2 * rows + j * rows, rows), rows)
            right = full[0][s, j].reshape(rows, width)
            g = lax.dot_general(first[...], right, ndims, preferred_element_type=F32)
            mixed[:, at] = (g + mixed_bias[:, at]).astype(BF)
            return carry

        lax.fori_loop(0, 2, body, 0)

    scale = HEAD_DIM ** (-0.5)

    def heads(k):
        s0 = source(k)
        mask = live_keys(keep, z)

        def body(j, carry):
            p = s0 * 2 + j
            at = pl.ds(pl.multiple_of(p * 6 * HEAD_DIM, 6 * HEAD_DIM), 6 * HEAD_DIM)
            both = mixed[:, at]
            parts = []
            for e in range(2):
                q, kk, v = (both[:, (3 * e + b) * HEAD_DIM : (3 * e + b + 1) * HEAD_DIM] for b in range(3))
                s = lax.dot_general(q, kk, ndims, preferred_element_type=F32) * scale
                s = jnp.where(mask, s, masked_score)
                s = jnp.exp(s - jnp.max(s, axis=-1, keepdims=True))
                pr = (s / jnp.sum(s, axis=-1, keepdims=True)).astype(BF)
                parts.append(jnp.dot(pr, v, preferred_element_type=F32).astype(BF))
            to = pl.ds(pl.multiple_of(p * 2 * HEAD_DIM, 2 * HEAD_DIM), 2 * HEAD_DIM)
            attended[:, to] = jnp.concatenate(parts, axis=1)
            return carry

        lax.fori_loop(0, 2, body, 0)

    def outlet_part(k):
        s = source(k)
        rows = 8 * sizes[1]
        at = pl.ds(pl.multiple_of(s * rows, rows), rows)
        right = full[1][s].reshape(rows, width)
        g = jnp.dot(attended[:, at], right, preferred_element_type=F32)
        if k == 0:
            acc[...] = g
        else:
            acc[...] += g

    def second_norm():
        bias = model_bias[pl.ds(2, 1)]

        def body(i, carry):
            at = pl.ds(pl.multiple_of(i * chunk, chunk), chunk)
            middle[at] = xs[i].astype(F32) + acc[at] + bias
            return carry

        lax.fori_loop(0, seq // chunk, body, 0)
        norm_rows(1, lambda at, i: middle[at], second)
        save(mixed, o_mixed, 4)
        save(attended, o_attended, 5)
        save(middle, o_middle, 6)
        save(second, o_second, 7)

    def slope_copy(k):
        s = source(k)
        hidden = 8 * sizes[2]
        at = pl.ds(pl.multiple_of(s * hidden, hidden), hidden)
        return pltpu.make_async_copy(slope.at[k % 2], o_slope.at[:, at], s_l.at[k % 2])

    def expand_part(k):
        s = source(k)
        if k >= 2:
            slope_copy(k - 2).wait()
        rows = 2 * sizes[2]

        def body(j, carry):
            at = pl.ds(pl.multiple_of(s * 4 * rows + j * rows, rows), rows)
            right = full[2][s, j // 2, j % 2].reshape(rows, width)
            hidden = lax.dot_general(second[...], right, ndims, preferred_element_type=F32)
            hidden = hidden + expand_bias[:, at]
            bell = 0.5 * (1.0 + lax.erf(hidden * (0.5**0.5)))
            active[:, at] = (hidden * bell).astype(BF)
            slope[k % 2, :, pl.ds(pl.multiple_of(j * rows, rows), rows)] = (
                bell + hidden * jnp.exp(-0.5 * hidden * hidden) * (0.5 / jnp.pi) ** 0.5
            )
            return carry

        lax.fori_loop(0, 4, body, 0)
        slope_copy(k).start()
        if k == 3:
            save(active, o_active, 8)

    def shrink_part(k):
        s = source(k)
        hidden = 8 * sizes[3]

        def body(j, carry):
            cols = pl.ds(pl.multiple_of(j * 256, 256), 256)
            left = active[:, pl.ds(pl.multiple_of(s * hidden, hidden), hidden)]
            right = full[3][s, :, :, :, :, cols].reshape(hidden, 256)
            g = jnp.dot(left, right, preferred_element_type=F32)
            if k == 0:
                acc[:, cols] = g
            else:
                acc[:, cols] += g
            return carry

        lax.fori_loop(0, width // 256, body, 0)

    def last():
        bias = model_bias[pl.ds(3, 1)]

        def body(i, carry):
            at = pl.ds(pl.multiple_of(i * chunk, chunk), chunk)
            output[at] = (middle[at] + acc[at] + bias).astype(BF)
            return carry

        lax.fori_loop(0, seq // chunk, body, 0)

    blocks = [("n1", 4.0, None)]
    work = [first_norm]
    needs = [None]

    def block(us, piece, fn):
        blocks.append((len(blocks), us, order.index(piece) if piece else None))
        needs.append(piece)
        work.append(fn)

    for k in range(4):
        block(1.6, (0, k), functools.partial(project, k))
        block(5.0, None, functools.partial(heads, k))
    for k in range(4):
        block(0.8, (1, k), functools.partial(outlet_part, k))
    block(2.5, None, second_norm)
    for k in range(4):
        block(4.5, (2, k), functools.partial(expand_part, k))
    for k in range(4):
        block(1.5, (3, k), functools.partial(shrink_part, k))
    block(1.0, None, last)

    go = lambda copy: copy.start()
    along(0, 0, go)
    rows_push(0, tok, xs)
    along(1, 0, go)
    ones = 0
    if OPT["a2"] == 0:
        along(2, 0, go)
    if OPT["a3"] == 0:
        along(3, 0, go)
    for kind, i in plan_forward(blocks, order, sizes, width, len(order)):
        if kind == "one":
            one(i)
            ones += 1
            if ones == OPT["a2"]:
                along(2, 0, go)
            if ones == OPT["a3"]:
                along(3, 0, go)
            if ones == 16:
                rows_push(1, cot, cot_all)
        elif kind == "two":
            two(i)
        elif kind == "three":
            three(i)
        elif kind == "load":
            load(*needs[i])
        else:
            work[i]()
    rows_wait(1, cot_all)
    for k in (2, 3):
        slope_copy(k).wait()
    for copy in written + kept:
        copy.wait()
    for copy in held:
        copy.wait_send()
    for m in range(n):
        for j in range(4):
            along(m, j, lambda copy: copy.wait_send())


def forward_all(weights, tok, cot, norm_gain, model_bias, head_bias, expand_bias, keep):
    sizes = tuple(v.shape[0] for v in weights)
    width = weights[0].shape[1]
    seq = tok.shape[0] * tok.shape[1]
    hidden = expand_bias.shape[1]
    order = [(m, 0) for m in range(4)] + [(m, k) for m in range(4) for k in (1, 2, 3)]
    if OPT["order"] == 1:
        order = [(0, 0), (1, 0), (0, 1), (2, 0), (0, 2), (0, 3), (1, 1), (1, 2), (1, 3), (2, 1), (2, 2), (2, 3)] + [(3, k) for k in range(4)]
    if OPT["order"] == 2:
        order = [(0, 0), (1, 0), (2, 0)] + [(m, k) for m in range(3) for k in (1, 2, 3)] + [(3, k) for k in range(4)]
    count = len(order)
    anyspace = pl.BlockSpec(memory_space=pl.ANY)
    vmem = pl.BlockSpec(memory_space=pltpu.VMEM)
    dma = pltpu.SemaphoreType.DMA
    shape = jax.ShapeDtypeStruct
    return pl.pallas_call(
        functools.partial(forward_kernel, sizes, order),
        out_shape=[shape((4, 2, 2, 2, s, width), BF) for s in sizes]
        + [
            shape(tok.shape, BF),
            shape(cot.shape, BF),
            shape((seq, width), BF),
            shape((seq, hidden), BF),
            shape((seq, hidden), F32),
            shape((seq, width), F32),
            shape((seq, 3 * width), BF),
            shape((seq, width), BF),
            shape((seq, width), BF),
            shape((seq, width), BF),
        ],
        in_specs=[vmem] * len(sizes) + [anyspace] * 2 + [vmem] * 5,
        out_specs=[anyspace] * (len(sizes) + 2) + [vmem] + [anyspace] * 7,
        scratch_shapes=[pltpu.VMEM((4, 2, 2, 2, s, width), BF) for s in sizes]
        + [
            pltpu.VMEM(tok.shape, BF),
            pltpu.VMEM((seq, width), BF),
            pltpu.VMEM((seq, 3 * width), BF),
            pltpu.VMEM((seq, width), BF),
            pltpu.VMEM((seq, width), F32),
            pltpu.VMEM((seq, width), F32),
            pltpu.VMEM((seq, width), BF),
            pltpu.VMEM((seq, hidden), BF),
            pltpu.VMEM((2, seq, 8 * sizes[2]), F32),
            pltpu.VMEM((1, 3 * width), F32),
            dma((4, 5)),
            dma((4, 4)),
            dma((2,)),
            dma((2, 3)),
            dma((2, 3)),
            dma((5, count)),
            dma((5, count)),
            dma((count,)),
            dma((9,)),
            dma((2,)),
        ],
        compiler_params=pltpu.CompilerParams(collective_id=1, has_side_effects=True, vmem_limit_bytes=VMEM_LIMIT),
    )(*weights, tok, cot, norm_gain, model_bias, head_bias, expand_bias, keep)


def add_rows(dst, src, lead, rows):
    step = 16

    def body(i, carry):
        j, r = i // (rows // step), (i % (rows // step)) * step
        at = pl.ds(pl.multiple_of(r, step), step)
        dst[j, at] = dst[j, at] + src[j, at]
        return carry

    lax.fori_loop(0, lead * (rows // step), body, 0)


PLANES = (1, 2, 0, 3)


def plan(blocks, sizes, order, free_after, width):
    todo = list(blocks)
    done = []
    events = []
    link = {"x": 0.0, "y": 0.0, "z": 0.0}
    now = 0.0
    finished = set()

    def carry(lane, start, rows):
        begin = max(start, link[lane])
        link[lane] = begin + rows * width * 2 * 2 / OPT["brate"]
        return link[lane] + OPT["blat"]

    def emit(step):
        nonlocal now
        kind, i = step[0], step[1]
        done.append(step)
        finished.add(step)
        s = sizes[order[i][0]]
        if kind == "one":
            now += s / 128 * 1.0
            ready = max(carry("y", now, s), carry("x", now, s))
            events.append((ready, ("two", i)))
        elif kind == "two":
            now += s / 128 * 0.6
            ready = max(carry("x", now, s / 2), carry("y", now, s / 2))
            events.append((ready, ("three", i)))
        elif kind == "three":
            now += s / 128 * 0.3
            ready = carry("z", now, s)
            events.append((ready + OPT["bz"], ("four", i)))
            events.append((ready + OPT["bz"] + 0.001, ("fourb", i)))
        elif kind == "four":
            finished.discard(step)
            now += 0.2
        elif kind == "fourb":
            now += 0.2

    def open_now():
        ones = sum(1 for v in finished if v[0] == "one")
        twos = sum(1 for v in finished if v[0] == "two")
        for v in events:
            if v[1][0] != "one" or ones - twos < OPT["bwin"]:
                return v
        return events[0]

    while todo or events:
        events.sort()
        if events and open_now()[0] <= now:
            event = open_now()
            events.remove(event)
            step = event[1]
            if step[0] == "fourb":
                events.append((now + OPT["bhop"], ("fourc", step[1])))
                continue
            emit(step)
            continue
        if todo:
            name, us, piece = todo[0]
            blocked = piece is not None and piece >= free_after and ("one", piece - free_after) not in finished
            if not blocked:
                todo.pop(0)
                done.append(("block", name))
                now += us * OPT["bwork"]
                if piece is not None:
                    done.append(("push", piece))
                    events.append((now + OPT["bone"], ("one", piece)))
                continue
        now = max(now, open_now()[0])
    return done


def backward_kernel(sizes, order, *refs):
    n = 4
    small_count = 16
    shrink, expand, outlet, intake, active, slope = refs[:6]
    inputs = refs[6:13]
    norm_gain, keep = refs[13:15]
    mom_f = refs[15:19]
    total, small_out, mom_all, token_grad = refs[19:23]
    refs = refs[23:]
    own, mid, end, far = (refs[i * n : i * n + n] for i in range(4))
    refs = refs[4 * n :]
    (made, act, slo, wbuf, obuf, hgrad, wide, mgrad, branch, agrad) = refs[:10]
    small, s_got, s_acc, s_z = refs[10:14]
    loc, c_s, c_r, p_s, p_r, f_s, f_r, q_s, q_r, m_s, m_r, w_l = refs[14:26]
    mom = refs[26:30]
    middle, mixed, attended, second, first, x_in, cot, in_l = refs[30:]
    held_in = (middle, mixed, attended, second, first, x_in, cot)
    d, z, y, x, c = place()
    unit = wbuf.shape[1]
    count_units = shrink.shape[0] // unit

    def load(u):
        at = pl.ds(u * unit, unit)
        return [
            pltpu.make_async_copy(shrink.at[at], wbuf.at[u % 2], w_l.at[0, u % 2]),
            pltpu.make_async_copy(expand.at[at], wbuf.at[2 + u % 2], w_l.at[1, u % 2]),
            pltpu.make_async_copy(active.at[:, at], act.at[u % 2], w_l.at[2, u % 2]),
            pltpu.make_async_copy(slope.at[:, at], slo.at[u % 2], w_l.at[3, u % 2]),
        ]

    fetches = [
        pltpu.make_async_copy(src, dst, in_l.at[i]) for i, (src, dst) in enumerate(zip(inputs, held_in))
    ]
    fetches[6].start()
    for copy in load(0):
        copy.start()
    for i in (3, 0, 2, 1, 4, 5):
        fetches[i].start()
    for m in range(n):
        mom[m][...] = mom_f[m][...].astype(BF)
    core, xn, yn, zn = partners(d, z, y, x, c)
    greet([core, xn, yn] + zn)
    seq, width = cot.shape
    held = []
    top = max(sizes)

    def start(copy):
        copy.start()
        held.append(copy)

    def sem(i, stage):
        return (p_s.at[stage, i], p_r.at[stage, i])

    slots = made.shape[0]

    def core_push(i):
        m, k = order[i]
        return push(
            made.at[i % slots, :, :, 1 - c, pl.ds(0, sizes[m])], own[m].at[k], (c_s.at[i], c_r.at[i]), core
        )

    def one(i):
        m, k = order[i]
        s, h = sizes[m], sizes[m] // 2
        core_push(i).wait_recv()
        for j in range(2):
            for l in range(2):
                add_rows(own[m].at[k, j, pl.ds(l, 1)], made.at[i % slots, j, l, pl.ds(c, 1)], 1, s)
        start(push(own[m].at[k, 1 - y, :, pl.ds(0, h)], mid[m].at[k, 0], sem(i, 0), yn))
        start(push(own[m].at[k, :, 1 - x, pl.ds(h, h)], mid[m].at[k, 1], sem(i, 1), xn))

    def two(i):
        m, k = order[i]
        h = sizes[m] // 2
        push(mid[m].at[k, 0], mid[m].at[k, 0], sem(i, 0), yn).wait_recv()
        add_rows(own[m].at[k, y, :, pl.ds(0, h)], mid[m].at[k, 0], 2, h)
        start(push(own[m].at[k, y, 1 - x, pl.ds(0, h)], end[m].at[k, pl.ds(0, h)], sem(i, 2), xn))
        push(mid[m].at[k, 1], mid[m].at[k, 1], sem(i, 1), xn).wait_recv()
        add_rows(own[m].at[k, :, x, pl.ds(h, h)], mid[m].at[k, 1], 2, h)
        start(push(own[m].at[k, 1 - y, x, pl.ds(h, h)], end[m].at[k, pl.ds(h, h)], sem(i, 3), yn))

    def hop(i, p, go):
        m, k = order[i]
        side, to = (0, p + 1) if p < PLANES[m] else (1, p - 1)
        at = side if PLANES[m] in (1, 2) else 0
        go(push(own[m].at[k, y, x], far[m].at[at, k], (f_s.at[m, k], f_r.at[m, k, side]), (d, to)))

    def came(m, k, side):
        slot = far[m].at[side if PLANES[m] in (1, 2) else 0, k]
        push(slot, slot, (f_s.at[m, k], f_r.at[m, k, side]), core).wait_recv()

    def three(i):
        m, k = order[i]
        s, h = sizes[m], sizes[m] // 2
        push(end[m].at[k, pl.ds(0, h)], end[m].at[k, pl.ds(0, h)], sem(i, 2), xn).wait_recv()
        push(end[m].at[k, pl.ds(h, h)], end[m].at[k, pl.ds(h, h)], sem(i, 3), yn).wait_recv()
        add_rows(own[m].at[k, pl.ds(y, 1), x], end[m].at[pl.ds(k, 1)], 1, s)
        for p in (0, 3):
            if p != PLANES[m]:

                @pl.when(z == p)
                def _(p=p):
                    hop(i, p, lambda copy: copy.start())

    def four(i, far_hop):
        m, k = order[i]
        for p in (1, 2):
            below = p < PLANES[m]
            if p == PLANES[m] or far_hop != (p if below else 3 - p):
                continue

            @pl.when(z == p)
            def _(p=p, below=below):
                side = 0 if below else 1
                came(m, k, side)
                at = side if PLANES[m] in (1, 2) else 0
                add_rows(own[m].at[k, pl.ds(y, 1), x], far[m].at[at, pl.ds(k, 1)], 1, sizes[m])
                hop(i, p, lambda copy: copy.start())

    def five(i):
        m, k = order[i]
        s, p = sizes[m], PLANES[m]
        sides = [v for v in (0, 1) if p != 3 * v]

        @pl.when(z == p)
        def _():
            for side in sides:
                came(m, k, side)

            def body(r, carry):
                at = pl.ds(pl.multiple_of(r * 16, 16), 16)
                acc = own[m][k, y, x, at].astype(F32)
                for side in range(len(sides)):
                    acc = acc + far[m][side, k, at].astype(F32)
                total[k, at] = acc
                return carry

            lax.fori_loop(0, s // 16, body, 0)
            if s < total.shape[1]:
                total[k, pl.ds(s, total.shape[1] - s)] = jnp.zeros((total.shape[1] - s, width), F32)

    def small_step(stage):
        to = (core, xn, yn)
        if stage > 0:
            here = s_got.at[stage - 1]
            push(here, here, (q_s.at[stage - 1], q_r.at[stage - 1]), to[stage - 1]).wait_recv()
            s_acc[stage] = s_acc[stage - 1] + s_got[stage - 1]
        else:
            s_acc[0] = small[...]
        if stage < 3:
            start(push(s_acc.at[stage], s_got.at[stage], (q_s.at[stage], q_r.at[stage]), to[stage]))
        else:
            s_z[z] = s_acc[3]
            for k in range(1, 4):
                start(push(s_acc.at[3], s_z.at[z], (q_s.at[2 + k], q_r.at[2 + k]), zn[k - 1]))

    def moments(first):
        for t in range(n):
            p = PLANES[t]
            here = mom_all.at[z, pl.ds(0, sizes[t])]

            @pl.when(z == p)
            def _(t=t, p=p, here=here):
                copy = pltpu.make_async_copy(mom[t], here, loc.at[0])
                if first:
                    copy.start()
                else:
                    copy.wait()
                    for k in range(1, 4):
                        s = (p + k) % 4
                        there = mom_all.at[s, pl.ds(0, sizes[t])]
                        push(mom[t], there, (m_s.at[t], m_r.at[s]), (d, s)).wait_recv()

            @pl.when(z != p)
            def _(t=t, p=p, here=here):
                copy = push(mom[t], here, (m_s.at[t], m_r.at[z]), (d, p))
                if first:
                    copy.start()
                else:
                    copy.wait_send()

    def load_outlet():
        return pltpu.make_async_copy(outlet, obuf, loc.at[1])

    def load_intake(v):
        return pltpu.make_async_copy(intake.at[pl.ds(v * unit, unit)], wbuf.at[v % 4], w_l.at[4, v % 4])

    tdims = (((0,), (0,)), ((), ()))
    ndims = (((1,), (1,)), ((), ()))

    def mlp_one(u):
        k, half = u // 2, u % 2
        if u == 0:
            fetches[6].wait()
        if u + 1 < count_units:
            for copy in load(u + 1):
                copy.start()
        for copy in load(u):
            copy.wait()
        i = 2 * k

        def body(j, carry):
            cols = pl.ds(pl.multiple_of(j * 2 * top, 2 * top), 2 * top)
            g = lax.dot_general(act[u % 2, :, cols], cot[...], tdims, preferred_element_type=F32)
            made[i % slots, half, j] = g.astype(BF).reshape(2, top, width)
            return carry

        lax.fori_loop(0, unit // (2 * top), body, 0)

        def grad(j, carry):
            rows = pl.ds(pl.multiple_of(j * 256, 256), 256)
            to = pl.ds(pl.multiple_of(j * 256 + half * unit, 256), 256)
            g = lax.dot_general(cot[...], wbuf[u % 2, rows], ndims, preferred_element_type=F32)
            hg = (g * slo[u % 2, :, rows]).astype(BF)
            hgrad[:, to] = hg
            small[pl.ds(2 + k, 1), to] = jnp.sum(hg.astype(F32), axis=0, keepdims=True)
            return carry

        lax.fori_loop(0, unit // 256, grad, 0)

        def back(j, carry):
            cols = pl.ds(pl.multiple_of(j * 256, 256), 256)
            g = jnp.dot(hgrad[:, pl.ds(half * unit, unit)], wbuf[2 + u % 2, :, cols], preferred_element_type=F32)
            if u == 0:
                wide[:, cols] = g
            else:
                wide[:, cols] += g
            return carry

        lax.fori_loop(0, width // 256, back, 0)

    def mlp_two(k):
        i = 2 * k + 1
        if k == 0:
            fetches[3].wait()

        def body(j, carry):
            cols = pl.ds(pl.multiple_of(j * 2 * top, 2 * top), 2 * top)
            g = lax.dot_general(hgrad[:, cols], second[...], tdims, preferred_element_type=F32)
            made[i % slots, j // 2, j % 2] = g.astype(BF).reshape(2, top, width)
            return carry

        lax.fori_loop(0, 4, body, 0)

    chunk = 64

    def norm_block(index, v_of, extra):
        gain = norm_gain[pl.ds(index, 1)]

        def body(i, carry):
            at = pl.ds(pl.multiple_of(i * chunk, chunk), chunk)
            v = v_of(at)
            center = v - jnp.mean(v, axis=-1, keepdims=True)
            r = lax.rsqrt(jnp.mean(center * center, axis=-1, keepdims=True) + norm_eps)
            nrm = center * r
            w = wide[at]
            u = w * gain
            down = r * (u - jnp.mean(u, axis=-1, keepdims=True) - nrm * jnp.mean(u * nrm, axis=-1, keepdims=True))
            sums = extra(at, down)
            new = [jnp.sum(w * nrm, axis=0, keepdims=True), jnp.sum(w, axis=0, keepdims=True)] + sums
            return tuple(a + b for a, b in zip(carry, new))

        zero = jnp.zeros((1, width), F32)
        out = lax.fori_loop(0, seq // chunk, body, (zero,) * (4 if index else 2))
        small[pl.ds(6 + index, 1)] = out[0]
        small[pl.ds(8 + index, 1)] = out[1]
        if index:
            small[pl.ds(10, 1)] = out[2]
            small[pl.ds(11, 1)] = out[3]

    def second_norm_back():
        fetches[0].wait()
        load_outlet().start()
        for v in range(4):
            load_intake(v).start()

        def extra(at, down):
            g = cot[at].astype(F32)
            m = g + down
            mgrad[at] = m
            low = m.astype(BF)
            branch[at] = low
            return [jnp.sum(low.astype(F32), axis=0, keepdims=True), jnp.sum(g, axis=0, keepdims=True)]

        norm_block(1, lambda at: middle[at], extra)

    def outlet_piece(k):
        i = 12 + k
        if k == 0:
            fetches[2].wait()
        cols = pl.ds(k * 8 * sizes[1], 8 * sizes[1])
        g = lax.dot_general(attended[:, cols], branch[...], tdims, preferred_element_type=F32)
        made[i % slots, :, :, :, pl.ds(0, sizes[1])] = g.astype(BF).reshape(2, 2, 2, sizes[1], width)

    def attended_back():
        load_outlet().wait()

        def body(j, carry):
            rows = pl.ds(pl.multiple_of(j * 256, 256), 256)
            g = lax.dot_general(branch[...], obuf[rows], ndims, preferred_element_type=F32)
            agrad[:, rows] = g.astype(BF)
            return carry

        lax.fori_loop(0, width // 256, body, 0)

    scale = HEAD_DIM ** (-0.5)

    def heads(first_pair, pairs):
        if first_pair == 0:
            fetches[1].wait()
        mask = live_keys(keep, z)

        def body(p, carry):
            at = pl.ds(pl.multiple_of(p * 6 * HEAD_DIM, 6 * HEAD_DIM), 6 * HEAD_DIM)
            both = mixed[:, at]
            ag_both = agrad[:, pl.ds(pl.multiple_of(p * 2 * HEAD_DIM, 2 * HEAD_DIM), 2 * HEAD_DIM)]
            parts, sums = [], []
            for e in range(2):
                q, k, v = (both[:, (3 * e + b) * HEAD_DIM : (3 * e + b + 1) * HEAD_DIM] for b in range(3))
                ag = ag_both[:, e * HEAD_DIM : (e + 1) * HEAD_DIM]
                s = lax.dot_general(q, k, ndims, preferred_element_type=F32) * scale
                s = jnp.where(mask, s, masked_score)
                s = jnp.exp(s - jnp.max(s, axis=-1, keepdims=True))
                pr = s / jnp.sum(s, axis=-1, keepdims=True)
                vg = lax.dot_general(pr.astype(BF), ag, tdims, preferred_element_type=F32)
                dp = lax.dot_general(ag, v, ndims, preferred_element_type=F32)
                ds = (pr * (dp - jnp.sum(dp * pr, axis=-1, keepdims=True))).astype(BF)
                qg = jnp.dot(ds, k, preferred_element_type=F32) * scale
                kg = lax.dot_general(ds, q, tdims, preferred_element_type=F32) * scale
                parts += [qg.astype(BF), kg.astype(BF), vg.astype(BF)]
                sums.append((jnp.sum(parts[-3].astype(F32), 0, keepdims=True), jnp.sum(parts[-1].astype(F32), 0, keepdims=True)))
            mixed[:, at] = jnp.concatenate(parts, axis=1)
            to = pl.ds(pl.multiple_of(p * 2 * HEAD_DIM, 2 * HEAD_DIM), 2 * HEAD_DIM)
            small[pl.ds(0, 1), to] = jnp.concatenate([sums[0][0], sums[1][0]], axis=1)
            small[pl.ds(1, 1), to] = jnp.concatenate([sums[0][1], sums[1][1]], axis=1)
            return carry

        lax.fori_loop(first_pair, first_pair + pairs, body, 0)

    def intake_piece(k):
        i = 8 + k
        if k == 0:
            fetches[4].wait()
        rows = 4 * sizes[0]

        def body(j, carry):
            cols = pl.ds(pl.multiple_of((2 * k + j) * rows, rows), rows)
            g = lax.dot_general(mixed[:, cols], first[...], tdims, preferred_element_type=F32)
            made[i % slots, j, :, :, pl.ds(0, sizes[0])] = g.astype(BF).reshape(2, 2, sizes[0], width)
            return carry

        lax.fori_loop(0, 2, body, 0)

    def first_back(v):
        load_intake(v).wait()

        def body(j, carry):
            cols = pl.ds(pl.multiple_of(j * 256, 256), 256)
            g = jnp.dot(mixed[:, pl.ds(v * unit, unit)], wbuf[v % 4, :, cols], preferred_element_type=F32)
            if v == 0:
                wide[:, cols] = g
            else:
                wide[:, cols] += g
            return carry

        lax.fori_loop(0, width // 256, body, 0)
        if v + 4 < intake.shape[0] // unit:
            load_intake(v + 4).start()

    def first_norm_back():
        fetches[5].wait()

        def extra(at, down):
            token_grad[at] = (mgrad[at] + down).astype(BF)
            return []

        norm_block(0, lambda at: x_in[at].astype(F32), extra)

    work = {}
    blocks = []

    def block(name, us, piece, fn):
        work[name] = fn
        blocks.append((name, us, piece))

    for k in range(4):
        block(("m", 2 * k), 3.0, None, functools.partial(mlp_one, 2 * k))
        block(("m", 2 * k + 1), 3.0, 2 * k, functools.partial(mlp_one, 2 * k + 1))
        block(("e", k), 1.5, 2 * k + 1, functools.partial(mlp_two, k))
    block("n2", 3.0, None, second_norm_back)
    block("ab", 1.5, None, attended_back)
    for k in range(4):
        block(("h", k), 7.0, None, functools.partial(heads, 2 * k, 2))
        block(("i", k), 1.2, 8 + k, functools.partial(intake_piece, k))
    for k in range(4):
        block(("o", k), 0.5, 12 + k, functools.partial(outlet_piece, k))
    for v in range(intake.shape[0] // unit):
        block(("f", v), 0.8, None, functools.partial(first_back, v))
    block("n1", 3.0, None, first_norm_back)
    for stage in range(4):
        block(("s", stage), 2.0, None, functools.partial(small_step, stage))

    small[pl.ds(12, 4)] = jnp.zeros((4, width), F32)
    steps = plan(blocks, sizes, order, slots, width)
    pushed = {}
    stage = 1
    for step in steps:
        kind = step[0]
        if kind == "block":
            name = step[1]
            piece = {b[0]: b[2] for b in blocks}[name]
            first_piece = piece if piece is not None else (2 * (name[1] // 2) if name[0] == "m" else None)
            if first_piece is not None and first_piece - slots in pushed:
                pushed.pop(first_piece - slots).wait_send()
            work[name]()
            if name == ("m", 1):
                moments(True)
        elif kind == "push":
            pushed[step[1]] = core_push(step[1])
            pushed[step[1]].start()
        elif kind == "one":
            one(step[1])
        elif kind == "two":
            two(step[1])
        elif kind == "three":
            three(step[1])
        elif kind == "four":
            four(step[1], 1)
        elif kind == "fourc":
            four(step[1], 2)
    for i in range(len(order)):
        five(i)
    for k in range(1, 4):
        slot = s_z.at[(z + 4 - k) % 4]
        push(slot, slot, (q_s.at[2 + k], q_r.at[2 + k]), zn[k - 1]).wait_recv()
    small_out[...] = s_z[0] + s_z[1] + s_z[2] + s_z[3]
    moments(False)
    for copy in pushed.values():
        copy.wait_send()
    for copy in held:
        copy.wait_send()
    for i in range(len(order)):
        for p in range(4):
            if p != PLANES[order[i][0]]:

                @pl.when(z == p)
                def _(i=i, p=p):
                    hop(i, p, lambda copy: copy.wait_send())


def backward_all(weights, saved, norm_gain, keep, moms, sizes):
    intake, outlet, expand, shrink = weights
    active, slope, middle, mixed, attended, second, first, x, cot = saved
    seq, width = cot.shape
    top = max(sizes)
    order = []
    for k in range(4):
        order += [(3, k), (2, k)]
    order += [(0, k) for k in range(4)] + [(1, k) for k in range(4)]
    count = len(order)
    anyspace = pl.BlockSpec(memory_space=pl.ANY)
    vmem = pl.BlockSpec(memory_space=pltpu.VMEM)
    dma = pltpu.SemaphoreType.DMA
    unit = 512
    return pl.pallas_call(
        functools.partial(backward_kernel, sizes, order),
        out_shape=[
            jax.ShapeDtypeStruct((4, top, width), F32),
            jax.ShapeDtypeStruct((16, width), F32),
            jax.ShapeDtypeStruct((4, top, width), BF),
            jax.ShapeDtypeStruct((seq, width), BF),
        ],
        in_specs=[anyspace] * 13 + [vmem] * 6,
        out_specs=[vmem, vmem, anyspace, vmem],
        scratch_shapes=[pltpu.VMEM((4, 2, 2, s, width), BF) for s in sizes]
        + [pltpu.VMEM((4, 2, 2, s // 2, width), BF) for s in sizes]
        + [pltpu.VMEM((4, s, width), BF) for s in sizes]
        + [pltpu.VMEM((2 if p in (1, 2) else 1, 4, s, width), BF) for s, p in zip(sizes, PLANES)]
        + [
            pltpu.VMEM((3, 2, 2, 2, top, width), BF),
            pltpu.VMEM((2, seq, unit), BF),
            pltpu.VMEM((2, seq, unit), F32),
            pltpu.VMEM((4, unit, width), BF),
            pltpu.VMEM((width, width), BF),
            pltpu.VMEM((seq, width), BF),
            pltpu.VMEM((seq, width), F32),
            pltpu.VMEM((seq, width), F32),
            pltpu.VMEM((seq, width), BF),
            pltpu.VMEM((seq, width), BF),
            pltpu.VMEM((16, width), F32),
            pltpu.VMEM((3, 16, width), F32),
            pltpu.VMEM((4, 16, width), F32),
            pltpu.VMEM((4, 16, width), F32),
            dma((2,)),
            dma((count,)),
            dma((count,)),
            dma((4, count)),
            dma((4, count)),
            dma((4, 4)),
            dma((4, 4, 2)),
            dma((6,)),
            dma((6,)),
            dma((4,)),
            dma((4,)),
            dma((5, 4)),
        ]
        + [pltpu.VMEM((s, width), BF) for s in sizes]
        + [pltpu.VMEM(v.shape, v.dtype) for v in saved[2:]]
        + [dma((7,))],
        compiler_params=pltpu.CompilerParams(collective_id=2, has_side_effects=True, vmem_limit_bytes=VMEM_LIMIT),
    )(shrink, expand, outlet, intake, active, slope, middle, mixed, attended, second, first, x, cot, norm_gain, keep, *moms)


def split(v):
    hi = v.astype(BF)
    return hi, (v - hi.astype(F32)).astype(BF)


def dot(a, b):
    return jnp.dot(a, b, preferred_element_type=F32)


def muon_kernel(sizes, *refs):
    n = len(sizes)
    total, mom, outp, tokg = refs[:4]
    rows_out = refs[4 : 4 + n]
    grads = refs[4 + n : 4 + 2 * n]
    outp_all, tokg_all = refs[4 + 2 * n : 6 + 2 * n]
    refs = refs[6 + 2 * n :]
    low_g, uh, ul, pack, r_core, r_one, r_two, gathered, gf, gh, gl, low, b, tf, xf, xh, xl = refs[:17]
    g_s, g_r, a_s, a_r, o_s, o_r, s_s, s_r, loc = refs[17:]
    d, z, y, x, c = place()
    core, xn, yn, zn = partners(d, z, y, x, c)
    greet([core, xn, yn] + zn)
    held = []

    def start(copy):
        copy.start()
        held.append(copy)

    top, width = total.shape[1:]
    count = 4 * top
    block = width // 4
    height = 0
    for t in range(n):
        height = jnp.where(z == PLANES[t], sizes[t], height)
    per = top // 16

    def make(i, carry):
        k, r = i // per, (i % per) * 16
        at = pl.ds(pl.multiple_of(r, 16), 16)
        g = total[k, at]
        low_g[k, at] = g.astype(BF)
        u = g + muon_decay * (muon_decay * mom[k, at].astype(F32) + g)
        row = lax.broadcasted_iota(jnp.int32, u.shape, 0) + r
        u = jnp.where(row < height, u, 0.0)
        to = pl.ds(pl.multiple_of(i * 16, 16), 16)
        uh[to], ul[to] = split(u)
        return carry

    lax.fori_loop(0, 4 * per, make, 0)

    def back_home(src, dst, sems, local, first):
        for t in range(n):
            s, p = sizes[t], PLANES[t]

            @pl.when(z == p)
            def _(t=t, s=s, p=p):
                own = pltpu.make_async_copy(src.at[p, pl.ds(0, s)], dst[t], loc.at[local])
                away = [
                    push(src.at[(p + k) % 4, pl.ds(0, s)], dst[t], (sems[0].at[k], sems[1].at[t]), (d, (p + k) % 4))
                    for k in range(1, 4)
                ]
                if first:
                    for copy in away:
                        copy.start()
                    own.start()
                else:
                    own.wait()
                    for copy in away:
                        copy.wait_send()

            if not first:

                @pl.when(z != p)
                def _(t=t, p=p):
                    push(dst[t], dst[t], (sems[0].at[0], sems[1].at[t]), (d, p)).wait_recv()

    back_home(low_g, grads, (g_s, g_r), 0, True)
    for i, (a, e) in enumerate(((outp, outp_all), (tokg, tokg_all))):
        pltpu.make_async_copy(a.at[z], e.at[z], loc.at[1 + i]).start()
        for k in range(1, 4):
            start(push(a.at[(z + k) % 4], e.at[z], (o_s.at[i, k - 1], o_r.at[i, k - 1]), zn[k - 1]))

    places = {0: (0, 0), 3: (0, 4 * block), 1: (1, 0), 2: (1, 3 * block)}
    tdims = (((0,), (0,)), ((), ()))

    def product(half):
        for r, (h, col) in places.items():
            if h != half:
                continue
            mine = slice(r * block, (r + 1) * block)
            rest = slice(r * block, width)
            acc = lax.dot_general(uh[:, mine], uh[:, rest], tdims, preferred_element_type=F32)
            acc = acc + lax.dot_general(uh[:, mine], ul[:, rest], tdims, preferred_element_type=F32)
            acc = acc + lax.dot_general(ul[:, mine], uh[:, rest], tdims, preferred_element_type=F32)
            pack[half, :, col : col + width - r * block] = acc

    def sem(i):
        return (a_s.at[i], a_r.at[i])

    for v in (0, 1):

        @pl.when(c == v)
        def _(v=v):
            product(1 - v)
            push(pack.at[1 - v], r_core, sem(0), core).start()
            product(v)

    def add(dst, r0, src, rows, into=None):
        def body(i, carry):
            at = pl.ds(pl.multiple_of(r0 + i * 8, 8), 8)
            v = dst[at] + src[pl.ds(pl.multiple_of(i * 8, 8), 8)]
            (dst if into is None else into)[at] = v
            return carry

        lax.fori_loop(0, rows // 8, body, 0)

    def rows(ref, r, size):
        return ref.at[pl.ds(pl.multiple_of(r, 32), size)]

    half, quarter, eighth = block // 2, block // 4, block // 8
    push(r_core, r_core, sem(0), core).wait_recv()
    mine, whole = pack.at[c], gathered.at[c]
    add(mine, 0, r_core, block)
    base_a, base_b = 0, half
    start(push(rows(mine, base_a + (1 - y) * quarter, quarter), r_one.at[0], sem(1), yn))
    start(push(rows(mine, base_b + (1 - x) * quarter, quarter), r_one.at[1], sem(2), xn))
    push(r_one.at[0], r_one.at[0], sem(1), yn).wait_recv()
    mine_a = base_a + y * quarter
    add(mine, mine_a, r_one.at[0], quarter)
    start(push(rows(mine, mine_a + (1 - x) * eighth, eighth), r_two.at[0], sem(3), xn))
    push(r_one.at[1], r_one.at[1], sem(2), xn).wait_recv()
    mine_b = base_b + x * quarter
    add(mine, mine_b, r_one.at[1], quarter)
    start(push(rows(mine, mine_b + (1 - y) * eighth, eighth), r_two.at[1], sem(4), yn))
    push(r_two.at[0], r_two.at[0], sem(3), xn).wait_recv()
    own_a = mine_a + x * eighth
    add(mine, own_a, r_two.at[0], eighth, whole)
    start(push(rows(whole, own_a, eighth), rows(whole, own_a, eighth), sem(5), xn))
    push(r_two.at[1], r_two.at[1], sem(4), yn).wait_recv()
    own_b = mine_b + y * eighth
    add(mine, own_b, r_two.at[1], eighth, whole)
    start(push(rows(whole, own_b, eighth), rows(whole, own_b, eighth), sem(6), yn))
    got = rows(whole, mine_a + (1 - x) * eighth, eighth)
    push(got, got, sem(5), xn).wait_recv()
    start(push(rows(whole, mine_a, quarter), rows(whole, mine_a, quarter), sem(7), yn))
    got = rows(whole, mine_b + (1 - y) * eighth, eighth)
    push(got, got, sem(6), yn).wait_recv()
    start(push(rows(whole, mine_b, quarter), rows(whole, mine_b, quarter), sem(8), xn))
    start(push(rows(whole, mine_a, quarter), rows(whole, mine_a, quarter), sem(9), core))
    start(push(rows(whole, mine_b, quarter), rows(whole, mine_b, quarter), sem(10), core))
    other_a = base_a + (1 - y) * quarter
    got = rows(whole, other_a, quarter)
    push(got, got, sem(7), yn).wait_recv()
    start(push(got, got, sem(11), core))
    other_b = base_b + (1 - x) * quarter
    got = rows(whole, other_b, quarter)
    push(got, got, sem(8), xn).wait_recv()
    start(push(got, got, sem(12), core))
    beside = gathered.at[1 - c]
    for r, i in ((mine_a, 9), (mine_b, 10), (other_a, 11), (other_b, 12)):
        got = rows(beside, r, quarter)
        push(got, got, sem(i), core).wait_recv()

    eye = lax.broadcasted_iota(jnp.int32, (block, block), 0) == lax.broadcasted_iota(jnp.int32, (block, block), 1)
    trace = jnp.zeros((1, 1), F32)
    for r, (h, col) in places.items():
        v = jnp.where(eye, gathered[h, :, col : col + block], 0.0)
        trace = trace + jnp.sum(jnp.sum(v, axis=1, keepdims=True), axis=0, keepdims=True)
    inverse = 1.0 / (jnp.sqrt(trace) + frob_eps)
    squared = inverse * inverse
    for r, (h, col) in places.items():
        for k in range(r, 4):
            v = gathered[h, :, col + (k - r) * block : col + (k - r + 1) * block] * squared
            a, e = slice(r * block, (r + 1) * block), slice(k * block, (k + 1) * block)
            gf[a, e] = v
            gh[a, e], gl[a, e] = split(v)
            if k > r:
                v = v.T
                gf[e, a] = v
                gh[e, a], gl[e, a] = split(v)

    step = 64

    def scale_x(i, carry):
        at = pl.ds(pl.multiple_of(i * step, step), step)
        v = (uh[at].astype(F32) + ul[at].astype(F32)) * inverse
        xf[at] = v
        xh[at], xl[at] = split(v)
        return carry

    lax.fori_loop(0, count // step, scale_x, 0)

    def iterate(shift, double, last):
        level = coef_a + coef_b * shift + coef_c * shift * shift
        slope = coef_b + 2.0 * coef_c * shift
        if last:

            def lower(i, carry):
                at = pl.ds(pl.multiple_of(i * step, step), step)
                g = gf[at]
                row = lax.broadcasted_iota(jnp.int32, g.shape, 0) + i * step
                col = lax.broadcasted_iota(jnp.int32, g.shape, 1)
                g = g - jnp.where(row == col, shift, 0.0)
                gf[at] = g
                low[at] = g.astype(BF)
                return carry

            lax.fori_loop(0, width // step, lower, 0)
            b[...] = (slope * gf[...] + coef_c * dot(low[...], low[...])).astype(BF)
            xh[...] = (level * xf[...] + dot(xh[...], b[...])).astype(BF)
            return
        b[...] = (slope * gf[...] + coef_c * dot(gh[...], gh[...])).astype(BF)
        v = level * xf[...] + dot(xh[...], b[...])
        t = level * gf[...] + dot(gh[...], b[...])
        if double:
            v = v + dot(xl[...], b[...])
            t = t + dot(gl[...], b[...])
        xf[...] = v
        xh[...] = v.astype(BF)
        tf[...] = t
        low[...] = t.astype(BF)
        g = level * tf[...] + dot(b[...], low[...])
        if double:
            gl[...] = (tf[...] - low[...].astype(F32)).astype(BF)
            g = g + dot(b[...], gl[...])
        gf[...] = g
        gh[...] = g.astype(BF)

    iterate(0.0, True, False)

    def middle(i, carry):
        iterate(0.0, False, False)
        return carry

    lax.fori_loop(0, NS_STEPS - 2, middle, 0)
    iterate(0.8, False, True)

    back_home(xh.reshape(4, top, width), rows_out, (s_s, s_r), 3, True)

    for v in (0, 1):

        @pl.when(c == v)
        def _(v=v):
            push(pack.at[1 - v], r_core, sem(0), core).wait_send()

    for i, (a, e) in enumerate(((outp, outp_all), (tokg, tokg_all))):
        pltpu.make_async_copy(a.at[z], e.at[z], loc.at[1 + i]).wait()
        for k in range(1, 4):
            slot = e.at[(z + 4 - k) % 4]
            push(slot, slot, (o_s.at[i, k - 1], o_r.at[i, k - 1]), zn[k - 1]).wait_recv()
    back_home(low_g, grads, (g_s, g_r), 0, False)
    for copy in held:
        copy.wait_send()
    back_home(xh.reshape(4, top, width), rows_out, (s_s, s_r), 3, False)


def muon_all(total, mom, outp, tokg, sizes):
    top, width = total.shape[1:]
    count, block = 4 * top, width // 4
    anyspace = pl.BlockSpec(memory_space=pl.ANY)
    vmem = pl.BlockSpec(memory_space=pltpu.VMEM)
    dma = pltpu.SemaphoreType.DMA
    wide = block * 5
    return pl.pallas_call(
        functools.partial(muon_kernel, sizes),
        out_shape=[jax.ShapeDtypeStruct((s, width), BF) for s in sizes] * 2
        + [jax.ShapeDtypeStruct(outp.shape, outp.dtype), jax.ShapeDtypeStruct(tokg.shape, tokg.dtype)],
        in_specs=[vmem, vmem, anyspace, anyspace],
        out_specs=[anyspace] * (2 * len(sizes) + 2),
        scratch_shapes=[
            pltpu.VMEM((4, top, width), BF),
            pltpu.VMEM((count, width), BF),
            pltpu.VMEM((count, width), BF),
            pltpu.VMEM((2, block, wide), F32),
            pltpu.VMEM((block, wide), F32),
            pltpu.VMEM((2, block // 4, wide), F32),
            pltpu.VMEM((2, block // 8, wide), F32),
            pltpu.VMEM((2, block, wide), F32),
            pltpu.VMEM((width, width), F32),
            pltpu.VMEM((width, width), BF),
            pltpu.VMEM((width, width), BF),
            pltpu.VMEM((width, width), BF),
            pltpu.VMEM((width, width), BF),
            pltpu.VMEM((width, width), F32),
            pltpu.VMEM((count, width), F32),
            pltpu.VMEM((count, width), BF),
            pltpu.VMEM((count, width), BF),
            dma((4,)),
            dma((4,)),
            dma((13,)),
            dma((13,)),
            dma((2, 3)),
            dma((2, 3)),
            dma((4,)),
            dma((4,)),
            dma((4,)),
        ],
        compiler_params=pltpu.CompilerParams(collective_id=3, has_side_effects=True, vmem_limit_bytes=VMEM_LIMIT),
    )(total, mom, outp, tokg)


def finish_kernel(factors, *refs):
    n = len(factors)
    grads, rows, masters, moments = (refs[i * n : i * n + n] for i in range(4))
    outp, tokg, small = refs[4 * n : 4 * n + 3]
    state = refs[4 * n + 3 : 4 * n + 9]
    refs = refs[4 * n + 9 :]
    output, token_grad = refs[:2]
    shards, moments_new, masters_new, copies = (refs[2 + i * n : 2 + i * n + n] for i in range(4))
    vectors = refs[2 + 4 * n :]
    step = 16

    def over(rows, body):
        def one(i, carry):
            body(pl.ds(pl.multiple_of(i * step, step), step))
            return carry

        lax.fori_loop(0, rows // step, one, 0)

    for src, dst in ((outp, output), (tokg, token_grad)):
        for k in range(src.shape[0]):

            def body(at, src=src, dst=dst, k=k):
                dst[k, at] = src[k, at].astype(F32)

            over(src.shape[1], body)
    for m in range(n):

        def body(at, m=m):
            g = grads[m][at].astype(F32)
            shards[m][at] = g
            moments_new[m][at] = muon_decay * moments[m][at] + g
            new = masters[m][at] - factors[m] * rows[m][at].astype(F32)
            masters_new[m][at] = new
            copies[m][at] = new.astype(BF)

        over(grads[m].shape[0], body)
    width = small.shape[1]
    at = 0
    for i, (lo, hi) in enumerate(((0, 2), (6, 8), (8, 12))):
        g = small[lo:hi]
        change, first, second = adam_step(g, state[2 * i][...], state[2 * i + 1][...])
        for value in (g, change, first, second):
            vectors[at][...] = value
            at += 1


def finish(grads, rows, masters, moments, outp, tokg, small, state, factors):
    vmem = pl.BlockSpec(memory_space=pltpu.VMEM)
    args = [*grads, *rows, *masters, *moments, outp, tokg, small, *state]
    sized = [jax.ShapeDtypeStruct(v.shape, F32) for v in masters]
    shapes = [jax.ShapeDtypeStruct(v.shape, F32) for v in (outp, tokg)] + sized * 3
    shapes += [jax.ShapeDtypeStruct(v.shape, BF) for v in masters]
    for v in state[::2]:
        shapes += [jax.ShapeDtypeStruct(v.shape, F32)] * 4
    return pl.pallas_call(
        functools.partial(finish_kernel, factors),
        out_shape=shapes,
        in_specs=[vmem] * len(args),
        out_specs=[vmem] * len(shapes),
        compiler_params=pltpu.CompilerParams(vmem_limit_bytes=VMEM_LIMIT),
        cost_estimate=pl.CostEstimate(flops=10**7, bytes_accessed=15 * 10**6, transcendentals=0),
    )(*args)


def per_device_fast(
    tokens,
    cotangent,
    keep_mask,
    intake,
    outlet,
    expand,
    shrink,
    intake_moment,
    outlet_moment,
    expand_moment,
    shrink_moment,
    head_bias,
    expand_bias,
    norm_gain,
    model_bias,
    head_first,
    head_second,
    expand_first,
    expand_second,
    gain_first,
    gain_second,
    bias_first,
    bias_second,
):
    shape = tokens.shape
    local, width = shape[2:]
    z = lax.axis_index("tensor")
    masters = (intake, outlet, expand, shrink)
    moments = (intake_moment, outlet_moment, expand_moment, shrink_moment)
    sizes = tuple(v.shape[0] for v in masters)
    made = forward_all(
        masters,
        tokens.reshape(-1, local, width),
        cotangent.reshape(-1, local, width),
        norm_gain,
        model_bias,
        head_bias,
        expand_bias[None],
        keep_mask,
    )
    whole = [v.reshape(-1, width) for v in made[:4]]
    x, cot = (v.reshape(-1, width) for v in made[4:6])
    out, saved = made[6], tuple(made[7:]) + (x, cot)
    total, small, mom, token_grad = backward_all(whole, saved, norm_gain, keep_mask, moments, sizes)
    made = muon_all(total, mom, out.reshape(-1, local, width), token_grad.reshape(-1, local, width), sizes)
    rows_scale = lax.axis_size("dp") * lax.axis_size("tensor")
    factors = [rate * (s * rows_scale / width) ** 0.5 for s, rate in zip(sizes, muon_rates)]
    state = (head_first, head_second, gain_first, gain_second, bias_first, bias_second)
    done = finish(made[4:8], made[:4], masters, moments, made[8], made[9], small, state, factors)
    output, token_grad = (v.reshape(shape) for v in done[:2])
    shards, moments_new, masters_new, copies = (tuple(done[2 + 4 * i : 6 + 4 * i]) for i in range(4))
    head, gain, bias = (done[18 + 4 * i : 22 + 4 * i] for i in range(3))
    hidden_total = small[2:6].reshape(expand_bias.shape)
    hidden = adam_step(hidden_total, expand_first, expand_second)
    return (
        (output, token_grad)
        + shards
        + (head[0], hidden_total, gain[0], bias[0])
        + moments_new
        + masters_new
        + copies
        + (head[1], hidden[0], gain[1], bias[1])
        + tuple(head[2:])
        + tuple(hidden[1:])
        + tuple(gain[2:])
        + tuple(bias[2:])
    )


def solution(mesh):
    placed = (
        P(None, "dp", "tensor", None),
        P(None, "dp", "tensor", None),
        P(None, "dp", None),
        P(("tensor", "dp"), None),
        P(("tensor", "dp"), None),
        P(("tensor", "dp"), None),
        P(("tensor", "dp"), None),
        P(("tensor", "dp"), None),
        P(("tensor", "dp"), None),
        P(("tensor", "dp"), None),
        P(("tensor", "dp"), None),
        P(),
        P(),
        P(),
        P(),
        P(),
        P(),
        P(),
        P(),
        P(),
        P(),
        P(),
        P(),
    )
    fast = mesh.shape["dp"] == 8 and mesh.shape["tensor"] == 4
    return jax.shard_map(
        per_device_fast if fast else per_device,
        mesh=mesh,
        in_specs=placed,
        out_specs=(
            P(None, "dp", "tensor", None),
            P(None, "dp", "tensor", None),
            P(("tensor", "dp"), None),
            P(("tensor", "dp"), None),
            P(("tensor", "dp"), None),
            P(("tensor", "dp"), None),
            P(),
            P(),
            P(),
            P(),
            P(("tensor", "dp"), None),
            P(("tensor", "dp"), None),
            P(("tensor", "dp"), None),
            P(("tensor", "dp"), None),
            P(("tensor", "dp"), None),
            P(("tensor", "dp"), None),
            P(("tensor", "dp"), None),
            P(("tensor", "dp"), None),
            P(("tensor", "dp"), None),
            P(("tensor", "dp"), None),
            P(("tensor", "dp"), None),
            P(("tensor", "dp"), None),
            P(),
            P(),
            P(),
            P(),
            P(),
            P(),
            P(),
            P(),
            P(),
            P(),
            P(),
            P(),
        ),
        check_vma=False,
    )
```

```python
import functools

import jax
import jax.numpy as jnp
from jax import lax
from jax.experimental import pallas as pl
from jax.experimental.pallas import tpu as pltpu
from jax.sharding import PartitionSpec as P

HEAD_DIM = 64
BUF = 64
NS_STEPS = 5
ADAM_STEP = 10


norm_eps = 1e-06
first_decay = 0.9
second_decay = 0.95
adam_rate = 0.05
adam_eps = 1e-08
muon_decay = 0.5
muon_rates = (1.0, 4.0, 1.0, 1.0)
frob_eps = 1e-07
coef_a = 3.4445
coef_b = -4.775
coef_c = 2.0315
masked_score = -1000000000.0


def precise(form, left, right):
    return jnp.einsum(form, left, right, precision=lax.Precision.HIGHEST)


def layer_norm(inputs_row, gain_row, shift_row):
    center = inputs_row - jnp.mean(inputs_row, axis=-1, keepdims=True)
    spread = jnp.mean(center * center, axis=-1, keepdims=True)
    return center * lax.rsqrt(spread + norm_eps) * gain_row + shift_row


def softmax_rows(scores):
    largest = jnp.max(scores, axis=-1, keepdims=True)
    powers = jnp.exp(scores - largest)
    return powers / jnp.sum(powers, axis=-1, keepdims=True)


def exact_gelu(inputs_row):
    return jax.nn.gelu(inputs_row, approximate=False)


def attend_weights(queries, keys_all, live_keys):
    scores = jnp.einsum(
        "iqhe,ikhe->ihqk", queries, keys_all, preferred_element_type=jnp.float32
    ) * HEAD_DIM ** (-0.5)
    scores = jnp.where(live_keys[:, None, None, :], scores, masked_score)
    return softmax_rows(scores)


def reduce_blocks(blocks):
    return (
        lax.psum_scatter(blocks[0], "dp", scatter_dimension=0, tiled=True),
        lax.psum_scatter(blocks[1], "dp", scatter_dimension=0, tiled=True),
        lax.psum_scatter(blocks[2], "dp", scatter_dimension=0, tiled=True),
        lax.psum_scatter(blocks[3], "dp", scatter_dimension=0, tiled=True),
    )


def gram_whole(matrix):
    model_width = matrix.shape[1]
    own_rows = model_width // lax.axis_size("dp")
    shard_rows = lax.psum_scatter(
        precise(
            "rm,rn->mn", lax.slice_in_dim(matrix, 0, own_rows * lax.axis_size("dp"), axis=1), matrix
        ),
        "dp",
        scatter_dimension=0,
        tiled=True,
    )
    return lax.all_gather(shard_rows, "dp", axis=0, tiled=True)


def newton_step(scaled, gram):
    product = precise("rk,kn->rn", scaled, gram)
    return coef_a * scaled + coef_b * product + coef_c * precise("rk,kn->rn", product, gram)


def adam_step(gradient, first, second):
    first_new = first_decay * first + (1.0 - first_decay) * gradient
    second_new = second_decay * second + (1.0 - second_decay) * gradient * gradient
    first_hat = first_new / (1.0 - first_decay**ADAM_STEP)
    second_hat = second_new / (1.0 - second_decay**ADAM_STEP)
    change = -adam_rate * first_hat / (jnp.sqrt(second_hat) + adam_eps)
    return (change, first_new, second_new)


def per_device(
    tokens,
    cotangent,
    keep_mask,
    intake,
    outlet,
    expand,
    shrink,
    intake_moment,
    outlet_moment,
    expand_moment,
    shrink_moment,
    head_bias,
    expand_bias,
    norm_gain,
    model_bias,
    head_first,
    head_second,
    expand_first,
    expand_second,
    gain_first,
    gain_second,
    bias_first,
    bias_second,
):
    micro_count, images, local_seq, model_width = tokens.shape
    seq_len = keep_mask.shape[2]
    tensor_size = lax.axis_size("tensor")
    tensor_index = lax.axis_index("tensor")
    head_cols = model_width // tensor_size
    local_heads = head_cols // HEAD_DIM
    hidden_cols = expand_bias.shape[0] // tensor_size
    head_start = tensor_index * head_cols
    hidden_start = tensor_index * hidden_cols
    query_bias = lax.dynamic_slice_in_dim(head_bias[0], head_start, head_cols, 0).reshape(
        local_heads, HEAD_DIM
    )
    value_bias = lax.dynamic_slice_in_dim(head_bias[1], head_start, head_cols, 0).reshape(
        local_heads, HEAD_DIM
    )
    mixed_bias = jnp.stack([query_bias, jnp.zeros_like(query_bias), value_bias], axis=1).reshape(
        3 * head_cols
    )
    hidden_bias = lax.dynamic_slice_in_dim(expand_bias, hidden_start, hidden_cols, 0)
    position = jnp.arange(seq_len)
    masters = (intake, outlet, expand, shrink)
    block_shapes = (
        (3 * head_cols, model_width),
        (head_cols, model_width),
        (hidden_cols, model_width),
        (hidden_cols, model_width),
    )
    totals = tuple((jnp.zeros(shape_one, jnp.float32) for shape_one in block_shapes))
    gain_grad = jnp.zeros((2, model_width), jnp.float32)
    bias_grad = jnp.zeros((4, model_width), jnp.float32)
    mixed_bias_grad = jnp.zeros((2, head_cols), jnp.float32)
    hidden_bias_grad = jnp.zeros((hidden_cols,), jnp.float32)
    outputs = []
    token_grads = []
    for micro_index in range(micro_count):
        intake_block, outlet_block, expand_block, shrink_block = (
            lax.all_gather(intake.astype(jnp.bfloat16), "dp", axis=0, tiled=True),
            lax.all_gather(outlet.astype(jnp.bfloat16), "dp", axis=0, tiled=True),
            lax.all_gather(expand.astype(jnp.bfloat16), "dp", axis=0, tiled=True),
            lax.all_gather(shrink.astype(jnp.bfloat16), "dp", axis=0, tiled=True),
        )
        token_rows = tokens[micro_index].astype(jnp.float32)
        live_keys = jnp.logical_or(keep_mask[micro_index] > 0, position[None, :] < BUF)
        first_local = layer_norm(token_rows, norm_gain[0], model_bias[0]).astype(jnp.bfloat16)
        first_norm = lax.all_gather(first_local, "tensor", axis=1, tiled=True)
        mixed_rows = (
            jnp.einsum("isd,rd->isr", first_norm, intake_block, preferred_element_type=jnp.float32)
            + mixed_bias
        )
        mixed_rows = mixed_rows.astype(jnp.bfloat16).reshape(
            images, seq_len, local_heads, 3, HEAD_DIM
        )
        queries = mixed_rows[:, :, :, 0]
        keys_all = mixed_rows[:, :, :, 1]
        values = mixed_rows[:, :, :, 2]
        attention = attend_weights(queries, keys_all, live_keys)
        attention_low = attention.astype(jnp.bfloat16)
        attended = jnp.einsum(
            "ihqk,ikhe->iqhe", attention_low, values, preferred_element_type=jnp.float32
        )
        attended = attended.reshape(images, seq_len, head_cols).astype(jnp.bfloat16)
        part_sum = jnp.einsum(
            "isc,cd->isd", attended, outlet_block, preferred_element_type=jnp.float32
        )
        middle = (
            token_rows
            + lax.psum_scatter(part_sum, "tensor", scatter_dimension=1, tiled=True)
            + model_bias[2]
        )
        second_local = layer_norm(middle, norm_gain[1], model_bias[1]).astype(jnp.bfloat16)
        second_norm = lax.all_gather(second_local, "tensor", axis=1, tiled=True)
        hidden = (
            jnp.einsum("isd,fd->isf", second_norm, expand_block, preferred_element_type=jnp.float32)
            + hidden_bias
        )
        active = exact_gelu(hidden).astype(jnp.bfloat16)
        part_two = jnp.einsum(
            "isf,fd->isd", active, shrink_block, preferred_element_type=jnp.float32
        )
        outputs.append(
            middle
            + lax.psum_scatter(part_two, "tensor", scatter_dimension=1, tiled=True)
            + model_bias[3]
        )
        cot_local = cotangent[micro_index]
        cot_rows = lax.all_gather(cot_local, "tensor", axis=1, tiled=True)
        shrink_block_grad = jnp.einsum(
            "isf,isd->fd", active, cot_rows, preferred_element_type=jnp.float32
        )
        active_grad = jnp.einsum(
            "isd,fd->isf", cot_rows, shrink_block, preferred_element_type=jnp.float32
        )
        gelu_value, gelu_back = jax.vjp(exact_gelu, hidden)
        hidden_grad = gelu_back(active_grad)[0].astype(jnp.bfloat16)
        hidden_bias_grad = hidden_bias_grad + jnp.sum(hidden_grad.astype(jnp.float32), axis=(0, 1))
        expand_block_grad = jnp.einsum(
            "isf,isd->fd", hidden_grad, second_norm, preferred_element_type=jnp.float32
        )
        second_part = jnp.einsum(
            "isf,fd->isd", hidden_grad, expand_block, preferred_element_type=jnp.float32
        )
        second_grad = lax.psum_scatter(second_part, "tensor", scatter_dimension=1, tiled=True)
        norm_value, norm_back = jax.vjp(layer_norm, middle, norm_gain[1], model_bias[1])
        middle_from_norm, gain_two_grad, shift_two_grad = norm_back(second_grad)
        cot_float = cot_local.astype(jnp.float32)
        middle_grad = cot_float + middle_from_norm
        branch_grad = middle_grad.astype(jnp.bfloat16)
        branch_rows = lax.all_gather(branch_grad, "tensor", axis=1, tiled=True)
        outlet_block_grad = jnp.einsum(
            "isc,isd->cd", attended, branch_rows, preferred_element_type=jnp.float32
        )
        attended_grad = jnp.einsum(
            "isd,cd->isc", branch_rows, outlet_block, preferred_element_type=jnp.float32
        )
        attended_grad = attended_grad.astype(jnp.bfloat16).reshape(
            images, seq_len, local_heads, HEAD_DIM
        )
        attention = attend_weights(queries, keys_all, live_keys)
        attention_low = attention.astype(jnp.bfloat16)
        values_grad = jnp.einsum(
            "ihqk,iqhe->ikhe", attention_low, attended_grad, preferred_element_type=jnp.float32
        )
        attention_grad = jnp.einsum(
            "iqhe,ikhe->ihqk", attended_grad, values, preferred_element_type=jnp.float32
        )
        score_grad = attention * (
            attention_grad - jnp.sum(attention_grad * attention, axis=-1, keepdims=True)
        )
        score_grad = score_grad.astype(jnp.bfloat16)
        queries_grad = jnp.einsum(
            "ihqk,ikhe->iqhe", score_grad, keys_all, preferred_element_type=jnp.float32
        ) * HEAD_DIM ** (-0.5)
        keys_grad = jnp.einsum(
            "ihqk,iqhe->ikhe", score_grad, queries, preferred_element_type=jnp.float32
        ) * HEAD_DIM ** (-0.5)
        mixed_grad = jnp.stack([queries_grad, keys_grad, values_grad], axis=3).astype(jnp.bfloat16)
        mixed_sums = jnp.sum(mixed_grad.astype(jnp.float32), axis=(0, 1))
        mixed_bias_grad = mixed_bias_grad + jnp.stack(
            [mixed_sums[:, 0].reshape(head_cols), mixed_sums[:, 2].reshape(head_cols)]
        )
        mixed_grad = mixed_grad.reshape(images, seq_len, 3 * head_cols)
        intake_block_grad = jnp.einsum(
            "isr,isd->rd", mixed_grad, first_norm, preferred_element_type=jnp.float32
        )
        first_part = jnp.einsum(
            "isr,rd->isd", mixed_grad, intake_block, preferred_element_type=jnp.float32
        )
        first_grad = lax.psum_scatter(first_part, "tensor", scatter_dimension=1, tiled=True)
        first_value, first_back = jax.vjp(layer_norm, token_rows, norm_gain[0], model_bias[0])
        token_from_norm, gain_one_grad, shift_one_grad = first_back(first_grad)
        token_grads.append(middle_grad + token_from_norm)
        gain_grad = gain_grad + jnp.stack([gain_one_grad, gain_two_grad])
        bias_grad = bias_grad + jnp.stack(
            [
                shift_one_grad,
                shift_two_grad,
                jnp.sum(branch_grad.astype(jnp.float32), axis=(0, 1)),
                jnp.sum(cot_float, axis=(0, 1)),
            ]
        )
        block_grads = (intake_block_grad, outlet_block_grad, expand_block_grad, shrink_block_grad)
        totals = tuple((total + block_one for total, block_one in zip(totals, block_grads)))
    shards = reduce_blocks(totals)
    head_full = lax.dynamic_update_slice_in_dim(
        jnp.zeros((2, model_width), jnp.float32), mixed_bias_grad, head_start, 1
    )
    hidden_full = lax.dynamic_update_slice_in_dim(
        jnp.zeros(expand_bias.shape, jnp.float32), hidden_bias_grad, hidden_start, 0
    )
    gain_total, bias_total, head_total, hidden_total = lax.psum(
        (gain_grad, bias_grad, head_full, hidden_full), ("dp", "tensor")
    )
    moments = (intake_moment, outlet_moment, expand_moment, shrink_moment)
    moments_new = [muon_decay * moment + gradient for gradient, moment in zip(shards, moments)]
    updates = [gradient + muon_decay * moment for gradient, moment in zip(shards, moments_new)]
    rows_max = max((update.shape[0] for update in updates))
    padded = jnp.stack(
        [jnp.pad(update, ((0, rows_max - update.shape[0]), (0, 0))) for update in updates]
    )
    spread = lax.all_to_all(padded, "tensor", split_axis=0, concat_axis=0, tiled=True)
    own_matrix = spread.reshape(tensor_size * rows_max, model_width)
    raw_gram = gram_whole(own_matrix)
    measure = jnp.sqrt(jnp.trace(raw_gram)) + frob_eps
    scaled = own_matrix / measure
    gram = raw_gram / (measure * measure)
    for step in range(NS_STEPS):
        if step > 0:
            gram = gram_whole(scaled)
        scaled = newton_step(scaled, gram)
    returned = lax.all_to_all(
        scaled.reshape(tensor_size, rows_max, model_width),
        "tensor",
        split_axis=0,
        concat_axis=0,
        tiled=True,
    )
    rows_scale = lax.axis_size("dp") * tensor_size
    masters_new = [
        weight
        - muon_rates[position_one]
        * (weight.shape[0] * rows_scale / weight.shape[1]) ** 0.5
        * returned[position_one, : weight.shape[0]]
        for position_one, weight in enumerate(masters)
    ]
    head_bias_change, head_first_new, head_second_new = adam_step(
        head_total, head_first, head_second
    )
    expand_bias_change, expand_first_new, expand_second_new = adam_step(
        hidden_total, expand_first, expand_second
    )
    norm_gain_change, gain_first_new, gain_second_new = adam_step(
        gain_total, gain_first, gain_second
    )
    model_bias_change, bias_first_new, bias_second_new = adam_step(
        bias_total, bias_first, bias_second
    )
    output = jnp.stack(outputs)
    token_grad = jnp.stack(token_grads)
    return (
        output,
        token_grad,
        shards[0],
        shards[1],
        shards[2],
        shards[3],
        head_total,
        hidden_total,
        gain_total,
        bias_total,
        moments_new[0],
        moments_new[1],
        moments_new[2],
        moments_new[3],
        masters_new[0],
        masters_new[1],
        masters_new[2],
        masters_new[3],
        masters_new[0].astype(jnp.bfloat16),
        masters_new[1].astype(jnp.bfloat16),
        masters_new[2].astype(jnp.bfloat16),
        masters_new[3].astype(jnp.bfloat16),
        head_bias_change,
        expand_bias_change,
        norm_gain_change,
        model_bias_change,
        head_first_new,
        head_second_new,
        expand_first_new,
        expand_second_new,
        gain_first_new,
        gain_second_new,
        bias_first_new,
        bias_second_new,
    )


MESH = pl.DeviceIdType.MESH
BF = jnp.bfloat16
F32 = jnp.float32
VMEM_LIMIT = 60 * 1024 * 1024


def place():
    d = lax.axis_index("dp")
    z = lax.axis_index("tensor")
    y, x, c = d // 4, (d // 2) % 2, d % 2
    return d, z, y, x, c


def partners(d, z, y, x, c):
    core = (d + 1 - 2 * c, z)
    xn = (d + 2 - 4 * x, z)
    yn = (d + 4 - 8 * y, z)
    zn = [(d, (z + k) % 4) for k in range(1, 4)]
    return core, xn, yn, zn


def greet(others):
    barrier = pltpu.get_barrier_semaphore()
    for other in others:
        pl.semaphore_signal(barrier, inc=1, device_id=other, device_id_type=MESH)
    pl.semaphore_wait(barrier, len(others))


def push(src, dst, sems, to):
    return pltpu.make_async_remote_copy(
        src_ref=src, dst_ref=dst, send_sem=sems[0], recv_sem=sems[1], device_id=to, device_id_type=MESH
    )


LINK = 93.5e3


OPT = dict(a2=0, a3=5, order=0, static=0, lagz=2.0, rate=86e3, lat=1.5, full=3.0, work=1.0, brate=93.5e3, blat=1.5, bone=3.0, bwork=1.3, bhop=3.0, bwin=3, bz=0.0, wait=10.0)


def live_keys(keep, z):
    count = keep.shape[1]
    row = keep[z // count, pl.ds(z % count, 1)]
    position = lax.broadcasted_iota(jnp.int32, row.shape, 1)
    return jnp.logical_or(row != 0, position < BUF)


def plan_forward(blocks, order, sizes, width, slots):
    done, events = [], []
    link = {"x": 0.0, "y": 0.0, "z": 0.0}
    now, at_z = 0.0, 2.0

    def carry(lane, start, rows):
        link[lane] = max(start, link[lane]) + rows * width * 4 / OPT["rate"]
        return link[lane] + OPT["lat"]

    for i, (m, k) in enumerate(order):
        if k == 0:
            events.append((0.1 * i, "one", i))
        elif m != 1:
            at_z += sizes[m] * width * 4 / OPT["rate"]
            events.append((at_z + OPT["lagz"] * k, "one", i))
    whole, loaded = {}, {}
    head = 0
    todo = list(range(len(blocks)))
    if OPT["static"]:
        count = len(order)
        pieces = {}
        def ready(j):
            return blocks[j][2] is None or blocks[j][2] in pieces
        at = 0
        for i in range(count + 2 + OPT["static"]):
            if i < count:
                done.append(("one", i))
            if 1 <= i <= count:
                done.append(("two", i - 1))
            if 2 <= i <= count + 1:
                done.append(("three", i - 2))
            if i >= 2 + OPT["static"]:
                pieces[i - 2 - OPT["static"]] = True
            budget = OPT["budget"]
            while todo and ready(todo[0]) and budget > 0:
                j = todo.pop(0)
                while head < len(blocks) and head <= j + 2 and ready(head):
                    if blocks[head][2] is not None:
                        done.append(("load", head))
                    head += 1
                done.append(("block", j))
                budget -= blocks[j][1]
        while todo:
            j = todo.pop(0)
            while head < len(blocks) and head <= j + 2:
                if blocks[head][2] is not None:
                    done.append(("load", head))
                head += 1
            done.append(("block", j))
        return done
    while events or todo:
        events.sort()
        if events and events[0][0] <= now:
            _, kind, i = events.pop(0)
            s = sizes[order[i][0]]
            if kind != "full":
                done.append((kind, i))
                now += 0.15
            if kind == "one" and order[i][0] == 1 and order[i][1] > 0:
                events.append((now + OPT["full"], "full", i))
            elif kind == "one":
                ready = max(carry("x", now, s / 2), carry("y", now, s / 2))
                events.append((ready, "two", i))
            elif kind == "two":
                ready = max(carry("x", now, s), carry("y", now, s))
                events.append((ready, "three", i))
            elif kind == "three":
                events.append((now + OPT["full"], "full", i))
                if order[i] == (1, 0):
                    for k in (1, 2, 3):
                        events.append((now + k * (16 * s * width / OPT["rate"] + 2.0) + OPT["wait"], "one", order.index((1, k))))
            else:
                whole[i] = True
            continue
        busy = sum(1 for j in loaded if j in todo)
        while head < len(blocks) and (blocks[head][2] is None or (blocks[head][2] in whole and busy < slots)):
            if blocks[head][2] is not None:
                done.append(("load", head))
                loaded[head] = now + 2.0
                busy += 1
            head += 1
        wait = None
        if todo:
            j = todo[0]
            if blocks[j][2] is None or j in loaded:
                if blocks[j][2] is None or loaded[j] <= now:
                    todo.pop(0)
                    done.append(("block", j))
                    now += blocks[j][1] * OPT["work"]
                    continue
                wait = loaded[j]
        times = [v for v in (wait, events[0][0] if events else None) if v is not None]
        now = max(now, min(times))
    return done


def forward_kernel(sizes, order, *refs):
    n = 4
    w = refs[:n]
    tok, cot = refs[n : n + 2]
    norm_gain, model_bias, head_bias, expand_bias, keep = refs[n + 2 : n + 7]
    refs = refs[n + 7 :]
    o_full = refs[:n]
    o_x, cot_all, output, o_active, o_slope, o_middle, o_mixed, o_attended, o_second, o_first = refs[n : n + 10]
    refs = refs[n + 10 :]
    full = refs[:n]
    xs, first, mixed, attended, acc, middle, second, active, slope, mixed_bias = refs[n : n + 10]
    z_s, z_r, loc, t_s, t_r, p_s, p_r, w_l, out_l, s_l = refs[n + 10 :]
    d, z, y, x, c = place()
    core, xn, yn, zn = partners(d, z, y, x, c)
    for m in range(n):
        full[m][z, y, x, c] = w[m][...].astype(BF)
    greet([core, xn, yn] + zn)
    held = []
    written = []
    inner = z * (3 - z) > 0
    seq, width = first.shape

    def start(copy):
        copy.start()
        held.append(copy)
        return copy

    def source(j):
        return (z, z + 1 - 2 * (z % 2), 2 - z // 2, 3 - 3 * (z // 2))[j]

    def along(m, j, go):
        slot = full[m].at[source(j), :, :, c] if m == 1 else full[m].at[source(j), y, x, c]
        if j == 0:

            @pl.when(z < 3)
            def _():
                go(push(slot, slot, (z_s.at[m, 0], z_r.at[m, z]), (d, z + 1)))

            @pl.when(z > 0)
            def _():
                go(push(slot, slot, (z_s.at[m, 1], z_r.at[m, z]), (d, z - 1)))

        else:
            beyond = 3 - z if j == 1 else 3 * (z - 1)

            @pl.when(inner)
            def _():
                go(push(slot, slot, (z_s.at[m, 1 + j], z_r.at[m, source(j)]), (d, beyond)))

    locals_ = []
    for i, (a, b) in enumerate(((tok, xs), (cot, cot_all))):
        copy = pltpu.make_async_copy(a.at[z], b.at[z], loc.at[i])
        copy.start()
        locals_.append(copy)

    def rows_push(i, a, b):
        for k in range(1, 4):
            start(push(a.at[(z + k) % 4], b.at[z], (t_s.at[i, k - 1], t_r.at[i, k - 1]), zn[k - 1]))

    def rows_wait(i, b):
        locals_[i].wait()
        for k in range(1, 4):
            slot = b.at[(z + 4 - k) % 4]
            push(slot, slot, (t_s.at[i, k - 1], t_r.at[i, k - 1]), zn[k - 1]).wait_recv()

    def sem(i, stage):
        return (p_s.at[stage, i], p_r.at[stage, i])

    def one(i):
        m, k = order[i]
        h = sizes[m] // 2
        s = source(k)
        if k > 0:
            slot = full[m].at[s, :, :, c] if m == 1 else full[m].at[s, y, x, c]
            push(slot, slot, (z_s.at[m, 1 + k], z_r.at[m, s]), core).wait_recv()
            along(m, k, lambda copy: copy.start())
            if m == 1:
                start(push(slot, slot, sem(i, 4), core))
                return
        a = full[m].at[s, y, x, c, pl.ds(0, h)]
        b = full[m].at[s, y, x, c, pl.ds(h, h)]
        start(push(a, a, sem(i, 0), xn))
        start(push(b, b, sem(i, 1), yn))

    def two(i):
        m, k = order[i]
        h = sizes[m] // 2
        s = source(k)
        a = full[m].at[s, y, 1 - x, c, pl.ds(0, h)]
        push(a, a, sem(i, 0), xn).wait_recv()
        a = full[m].at[s, y, :, c, pl.ds(0, h)]
        start(push(a, a, sem(i, 2), yn))
        b = full[m].at[s, 1 - y, x, c, pl.ds(h, h)]
        push(b, b, sem(i, 1), yn).wait_recv()
        b = full[m].at[s, :, x, c, pl.ds(h, h)]
        start(push(b, b, sem(i, 3), xn))

    def three(i):
        m, k = order[i]
        h = sizes[m] // 2
        s = source(k)
        a = full[m].at[s, 1 - y, :, c, pl.ds(0, h)]
        push(a, a, sem(i, 2), yn).wait_recv()
        b = full[m].at[s, :, 1 - x, c, pl.ds(h, h)]
        push(b, b, sem(i, 3), xn).wait_recv()
        e = full[m].at[s, :, :, c]
        start(push(e, e, sem(i, 4), core))
        if m == 1:
            along(1, 0, lambda copy: copy.start())

    ndims = (((1,), (1,)), ((), ()))
    kept = []

    def load(m, k):
        i = order.index((m, k))
        e = full[m].at[source(k), :, :, 1 - c]
        push(e, e, sem(i, 4), core).wait_recv()
        copy = pltpu.make_async_copy(full[m].at[source(k)], o_full[m].at[source(k)], w_l.at[i])
        copy.start()
        kept.append(copy)

    def save(src, dst, i):
        copy = pltpu.make_async_copy(src, dst, out_l.at[i])
        copy.start()
        written.append(copy)

    chunk = seq // 4

    def norm_rows(index, v_of, dst):
        gain, shift = norm_gain[pl.ds(index, 1)], model_bias[pl.ds(index, 1)]

        def body(i, carry):
            at = pl.ds(pl.multiple_of(i * chunk, chunk), chunk)
            v = v_of(at, i)
            center = v - jnp.mean(v, axis=-1, keepdims=True)
            r = lax.rsqrt(jnp.mean(center * center, axis=-1, keepdims=True) + norm_eps)
            dst[at] = (center * r * gain + shift).astype(BF)
            return carry

        lax.fori_loop(0, seq // chunk, body, 0)

    def first_norm():
        rows_wait(0, xs)
        for h in range(width // HEAD_DIM):
            at, to = h * HEAD_DIM, 3 * h * HEAD_DIM
            mixed_bias[:, to : to + HEAD_DIM] = head_bias[0:1, at : at + HEAD_DIM]
            mixed_bias[:, to + HEAD_DIM : to + 2 * HEAD_DIM] = jnp.zeros((1, HEAD_DIM), F32)
            mixed_bias[:, to + 2 * HEAD_DIM : to + 3 * HEAD_DIM] = head_bias[1:2, at : at + HEAD_DIM]
        norm_rows(0, lambda at, i: xs[i].astype(F32), first)
        save(xs, o_x, 1)
        save(first, o_first, 0)

    def project(k):
        s = source(k)
        rows = 4 * sizes[0]

        def body(j, carry):
            at = pl.ds(pl.multiple_of(s * 2 * rows + j * rows, rows), rows)
            right = full[0][s, j].reshape(rows, width)
            g = lax.dot_general(first[...], right, ndims, preferred_element_type=F32)
            mixed[:, at] = (g + mixed_bias[:, at]).astype(BF)
            return carry

        lax.fori_loop(0, 2, body, 0)

    scale = HEAD_DIM ** (-0.5)

    def heads(k):
        s0 = source(k)
        mask = live_keys(keep, z)

        def body(j, carry):
            p = s0 * 2 + j
            at = pl.ds(pl.multiple_of(p * 6 * HEAD_DIM, 6 * HEAD_DIM), 6 * HEAD_DIM)
            both = mixed[:, at]
            parts = []
            for e in range(2):
                q, kk, v = (both[:, (3 * e + b) * HEAD_DIM : (3 * e + b + 1) * HEAD_DIM] for b in range(3))
                s = lax.dot_general(q, kk, ndims, preferred_element_type=F32) * scale
                s = jnp.where(mask, s, masked_score)
                s = jnp.exp(s - jnp.max(s, axis=-1, keepdims=True))
                pr = (s / jnp.sum(s, axis=-1, keepdims=True)).astype(BF)
                parts.append(jnp.dot(pr, v, preferred_element_type=F32).astype(BF))
            to = pl.ds(pl.multiple_of(p * 2 * HEAD_DIM, 2 * HEAD_DIM), 2 * HEAD_DIM)
            attended[:, to] = jnp.concatenate(parts, axis=1)
            return carry

        lax.fori_loop(0, 2, body, 0)

    def outlet_part(k):
        s = source(k)
        rows = 8 * sizes[1]
        at = pl.ds(pl.multiple_of(s * rows, rows), rows)
        right = full[1][s].reshape(rows, width)
        g = jnp.dot(attended[:, at], right, preferred_element_type=F32)
        if k == 0:
            acc[...] = g
        else:
            acc[...] += g

    def second_norm():
        bias = model_bias[pl.ds(2, 1)]

        def body(i, carry):
            at = pl.ds(pl.multiple_of(i * chunk, chunk), chunk)
            middle[at] = xs[i].astype(F32) + acc[at] + bias
            return carry

        lax.fori_loop(0, seq // chunk, body, 0)
        norm_rows(1, lambda at, i: middle[at], second)
        save(mixed, o_mixed, 4)
        save(attended, o_attended, 5)
        save(middle, o_middle, 6)
        save(second, o_second, 7)

    def slope_copy(k):
        s = source(k)
        hidden = 8 * sizes[2]
        at = pl.ds(pl.multiple_of(s * hidden, hidden), hidden)
        return pltpu.make_async_copy(slope.at[k % 2], o_slope.at[:, at], s_l.at[k % 2])

    def expand_part(k):
        s = source(k)
        if k >= 2:
            slope_copy(k - 2).wait()
        rows = 2 * sizes[2]

        def body(j, carry):
            at = pl.ds(pl.multiple_of(s * 4 * rows + j * rows, rows), rows)
            right = full[2][s, j // 2, j % 2].reshape(rows, width)
            hidden = lax.dot_general(second[...], right, ndims, preferred_element_type=F32)
            hidden = hidden + expand_bias[:, at]
            bell = 0.5 * (1.0 + lax.erf(hidden * (0.5**0.5)))
            active[:, at] = (hidden * bell).astype(BF)
            slope[k % 2, :, pl.ds(pl.multiple_of(j * rows, rows), rows)] = (
                bell + hidden * jnp.exp(-0.5 * hidden * hidden) * (0.5 / jnp.pi) ** 0.5
            )
            return carry

        lax.fori_loop(0, 4, body, 0)
        slope_copy(k).start()
        if k == 3:
            save(active, o_active, 8)

    def shrink_part(k):
        s = source(k)
        hidden = 8 * sizes[3]

        def body(j, carry):
            cols = pl.ds(pl.multiple_of(j * 256, 256), 256)
            left = active[:, pl.ds(pl.multiple_of(s * hidden, hidden), hidden)]
            right = full[3][s, :, :, :, :, cols].reshape(hidden, 256)
            g = jnp.dot(left, right, preferred_element_type=F32)
            if k == 0:
                acc[:, cols] = g
            else:
                acc[:, cols] += g
            return carry

        lax.fori_loop(0, width // 256, body, 0)

    def last():
        bias = model_bias[pl.ds(3, 1)]

        def body(i, carry):
            at = pl.ds(pl.multiple_of(i * chunk, chunk), chunk)
            output[at] = (middle[at] + acc[at] + bias).astype(BF)
            return carry

        lax.fori_loop(0, seq // chunk, body, 0)

    blocks = [("n1", 4.0, None)]
    work = [first_norm]
    needs = [None]

    def block(us, piece, fn):
        blocks.append((len(blocks), us, order.index(piece) if piece else None))
        needs.append(piece)
        work.append(fn)

    for k in range(4):
        block(1.6, (0, k), functools.partial(project, k))
        block(5.0, None, functools.partial(heads, k))
    for k in range(4):
        block(0.8, (1, k), functools.partial(outlet_part, k))
    block(2.5, None, second_norm)
    for k in range(4):
        block(4.5, (2, k), functools.partial(expand_part, k))
    for k in range(4):
        block(1.5, (3, k), functools.partial(shrink_part, k))
    block(1.0, None, last)

    go = lambda copy: copy.start()
    along(0, 0, go)
    rows_push(0, tok, xs)
    ones = 0
    if OPT["a2"] == 0:
        along(2, 0, go)
    if OPT["a3"] == 0:
        along(3, 0, go)
    for kind, i in plan_forward(blocks, order, sizes, width, len(order)):
        if kind == "one":
            one(i)
            ones += 1
            if ones == OPT["a2"]:
                along(2, 0, go)
            if ones == OPT["a3"]:
                along(3, 0, go)
            if ones == 16:
                rows_push(1, cot, cot_all)
        elif kind == "two":
            two(i)
        elif kind == "three":
            three(i)
        elif kind == "load":
            load(*needs[i])
        else:
            work[i]()
    rows_wait(1, cot_all)
    for k in (2, 3):
        slope_copy(k).wait()
    for copy in written + kept:
        copy.wait()
    for copy in held:
        copy.wait_send()
    for m in range(n):
        for j in range(4):
            along(m, j, lambda copy: copy.wait_send())


def forward_all(weights, tok, cot, norm_gain, model_bias, head_bias, expand_bias, keep):
    sizes = tuple(v.shape[0] for v in weights)
    width = weights[0].shape[1]
    seq = tok.shape[0] * tok.shape[1]
    hidden = expand_bias.shape[1]
    order = [(m, 0) for m in range(4)] + [(m, k) for m in range(4) for k in (1, 2, 3)]
    if OPT["order"] == 1:
        order = [(0, 0), (1, 0), (0, 1), (2, 0), (0, 2), (0, 3), (1, 1), (1, 2), (1, 3), (2, 1), (2, 2), (2, 3)] + [(3, k) for k in range(4)]
    if OPT["order"] == 2:
        order = [(0, 0), (1, 0), (2, 0)] + [(m, k) for m in range(3) for k in (1, 2, 3)] + [(3, k) for k in range(4)]
    count = len(order)
    anyspace = pl.BlockSpec(memory_space=pl.ANY)
    vmem = pl.BlockSpec(memory_space=pltpu.VMEM)
    dma = pltpu.SemaphoreType.DMA
    shape = jax.ShapeDtypeStruct
    return pl.pallas_call(
        functools.partial(forward_kernel, sizes, order),
        out_shape=[shape((4, 2, 2, 2, s, width), BF) for s in sizes]
        + [
            shape(tok.shape, BF),
            shape(cot.shape, BF),
            shape((seq, width), BF),
            shape((seq, hidden), BF),
            shape((seq, hidden), F32),
            shape((seq, width), F32),
            shape((seq, 3 * width), BF),
            shape((seq, width), BF),
            shape((seq, width), BF),
            shape((seq, width), BF),
        ],
        in_specs=[vmem] * len(sizes) + [anyspace] * 2 + [vmem] * 5,
        out_specs=[anyspace] * (len(sizes) + 2) + [vmem] + [anyspace] * 7,
        scratch_shapes=[pltpu.VMEM((4, 2, 2, 2, s, width), BF) for s in sizes]
        + [
            pltpu.VMEM(tok.shape, BF),
            pltpu.VMEM((seq, width), BF),
            pltpu.VMEM((seq, 3 * width), BF),
            pltpu.VMEM((seq, width), BF),
            pltpu.VMEM((seq, width), F32),
            pltpu.VMEM((seq, width), F32),
            pltpu.VMEM((seq, width), BF),
            pltpu.VMEM((seq, hidden), BF),
            pltpu.VMEM((2, seq, 8 * sizes[2]), F32),
            pltpu.VMEM((1, 3 * width), F32),
            dma((4, 5)),
            dma((4, 4)),
            dma((2,)),
            dma((2, 3)),
            dma((2, 3)),
            dma((5, count)),
            dma((5, count)),
            dma((count,)),
            dma((9,)),
            dma((2,)),
        ],
        compiler_params=pltpu.CompilerParams(collective_id=1, has_side_effects=True, vmem_limit_bytes=VMEM_LIMIT),
    )(*weights, tok, cot, norm_gain, model_bias, head_bias, expand_bias, keep)


def add_rows(dst, src, lead, rows):
    step = 16

    def body(i, carry):
        j, r = i // (rows // step), (i % (rows // step)) * step
        at = pl.ds(pl.multiple_of(r, step), step)
        dst[j, at] = dst[j, at] + src[j, at]
        return carry

    lax.fori_loop(0, lead * (rows // step), body, 0)


PLANES = (1, 2, 0, 3)


def plan(blocks, sizes, order, free_after, width):
    todo = list(blocks)
    done = []
    events = []
    link = {"x": 0.0, "y": 0.0, "z": 0.0}
    now = 0.0
    finished = set()

    def carry(lane, start, rows):
        begin = max(start, link[lane])
        link[lane] = begin + rows * width * 2 * 2 / OPT["brate"]
        return link[lane] + OPT["blat"]

    def emit(step):
        nonlocal now
        kind, i = step[0], step[1]
        done.append(step)
        finished.add(step)
        s = sizes[order[i][0]]
        if kind == "one":
            now += s / 128 * 1.0
            ready = max(carry("y", now, s), carry("x", now, s))
            events.append((ready, ("two", i)))
        elif kind == "two":
            now += s / 128 * 0.6
            ready = max(carry("x", now, s / 2), carry("y", now, s / 2))
            events.append((ready, ("three", i)))
        elif kind == "three":
            now += s / 128 * 0.3
            ready = carry("z", now, s)
            events.append((ready + OPT["bz"], ("four", i)))
            events.append((ready + OPT["bz"] + 0.001, ("fourb", i)))
        elif kind == "four":
            finished.discard(step)
            now += 0.2
        elif kind == "fourb":
            now += 0.2

    def open_now():
        ones = sum(1 for v in finished if v[0] == "one")
        twos = sum(1 for v in finished if v[0] == "two")
        for v in events:
            if v[1][0] != "one" or ones - twos < OPT["bwin"]:
                return v
        return events[0]

    while todo or events:
        events.sort()
        if events and open_now()[0] <= now:
            event = open_now()
            events.remove(event)
            step = event[1]
            if step[0] == "fourb":
                events.append((now + OPT["bhop"], ("fourc", step[1])))
                continue
            emit(step)
            continue
        if todo:
            name, us, piece = todo[0]
            blocked = piece is not None and piece >= free_after and ("one", piece - free_after) not in finished
            if not blocked:
                todo.pop(0)
                done.append(("block", name))
                now += us * OPT["bwork"]
                if piece is not None:
                    done.append(("push", piece))
                    events.append((now + OPT["bone"], ("one", piece)))
                continue
        now = max(now, open_now()[0])
    return done


def backward_kernel(sizes, order, *refs):
    n = 4
    small_count = 16
    shrink, expand, outlet, intake, active, slope = refs[:6]
    inputs = refs[6:13]
    norm_gain, keep = refs[13:15]
    mom_f = refs[15:19]
    total, small_out, mom_all, token_grad = refs[19:23]
    refs = refs[23:]
    own, mid, end, far = (refs[i * n : i * n + n] for i in range(4))
    refs = refs[4 * n :]
    (made, act, slo, wbuf, obuf, hgrad, wide, mgrad, branch, agrad) = refs[:10]
    small, s_got, s_acc, s_z = refs[10:14]
    loc, c_s, c_r, p_s, p_r, f_s, f_r, q_s, q_r, m_s, m_r, w_l = refs[14:26]
    mom = refs[26:30]
    middle, mixed, attended, second, first, x_in, cot, in_l = refs[30:]
    held_in = (middle, mixed, attended, second, first, x_in, cot)
    d, z, y, x, c = place()
    unit = wbuf.shape[1]
    count_units = shrink.shape[0] // unit

    def load(u):
        at = pl.ds(u * unit, unit)
        return [
            pltpu.make_async_copy(shrink.at[at], wbuf.at[u % 2], w_l.at[0, u % 2]),
            pltpu.make_async_copy(expand.at[at], wbuf.at[2 + u % 2], w_l.at[1, u % 2]),
            pltpu.make_async_copy(slope.at[:, at], slo.at[u % 2], w_l.at[3, u % 2]),
        ]

    def load_active(u):
        return pltpu.make_async_copy(active.at[:, pl.ds(u * unit, unit)], act.at[u % 2], w_l.at[2, u % 2])


    fetches = [
        pltpu.make_async_copy(src, dst, in_l.at[i]) for i, (src, dst) in enumerate(zip(inputs, held_in))
    ]
    fetches[6].start()
    for u in (0, 1):
        load_active(u).start()
    for copy in load(0) + load(1):
        copy.start()
    for i in (3, 0, 2, 1, 4, 5):
        fetches[i].start()
    for m in range(n):
        mom[m][...] = mom_f[m][...].astype(BF)
    core, xn, yn, zn = partners(d, z, y, x, c)
    greet([core, xn, yn] + zn)
    seq, width = cot.shape
    held = []
    top = max(sizes)

    def start(copy):
        copy.start()
        held.append(copy)

    def sem(i, stage):
        return (p_s.at[stage, i], p_r.at[stage, i])

    slots = made.shape[0]

    def core_push(i):
        m, k = order[i]
        return push(
            made.at[i % slots, :, :, 1 - c, pl.ds(0, sizes[m])], own[m].at[k], (c_s.at[i], c_r.at[i]), core
        )

    def one(i):
        m, k = order[i]
        s, h = sizes[m], sizes[m] // 2
        core_push(i).wait_recv()
        for j in range(2):
            for l in range(2):
                add_rows(own[m].at[k, j, pl.ds(l, 1)], made.at[i % slots, j, l, pl.ds(c, 1)], 1, s)
        start(push(own[m].at[k, 1 - y, :, pl.ds(0, h)], mid[m].at[k, 0], sem(i, 0), yn))
        start(push(own[m].at[k, :, 1 - x, pl.ds(h, h)], mid[m].at[k, 1], sem(i, 1), xn))

    def two(i):
        m, k = order[i]
        h = sizes[m] // 2
        push(mid[m].at[k, 0], mid[m].at[k, 0], sem(i, 0), yn).wait_recv()
        add_rows(own[m].at[k, y, :, pl.ds(0, h)], mid[m].at[k, 0], 2, h)
        start(push(own[m].at[k, y, 1 - x, pl.ds(0, h)], end[m].at[k, pl.ds(0, h)], sem(i, 2), xn))
        push(mid[m].at[k, 1], mid[m].at[k, 1], sem(i, 1), xn).wait_recv()
        add_rows(own[m].at[k, :, x, pl.ds(h, h)], mid[m].at[k, 1], 2, h)
        start(push(own[m].at[k, 1 - y, x, pl.ds(h, h)], end[m].at[k, pl.ds(h, h)], sem(i, 3), yn))

    def hop(i, p, go):
        m, k = order[i]
        side, to = (0, p + 1) if p < PLANES[m] else (1, p - 1)
        at = side if PLANES[m] in (1, 2) else 0
        go(push(own[m].at[k, y, x], far[m].at[at, k], (f_s.at[m, k], f_r.at[m, k, side]), (d, to)))

    def came(m, k, side):
        slot = far[m].at[side if PLANES[m] in (1, 2) else 0, k]
        push(slot, slot, (f_s.at[m, k], f_r.at[m, k, side]), core).wait_recv()

    def three(i):
        m, k = order[i]
        s, h = sizes[m], sizes[m] // 2
        push(end[m].at[k, pl.ds(0, h)], end[m].at[k, pl.ds(0, h)], sem(i, 2), xn).wait_recv()
        push(end[m].at[k, pl.ds(h, h)], end[m].at[k, pl.ds(h, h)], sem(i, 3), yn).wait_recv()
        add_rows(own[m].at[k, pl.ds(y, 1), x], end[m].at[pl.ds(k, 1)], 1, s)
        for p in (0, 3):
            if p != PLANES[m]:

                @pl.when(z == p)
                def _(p=p):
                    hop(i, p, lambda copy: copy.start())

    def four(i, far_hop):
        m, k = order[i]
        for p in (1, 2):
            below = p < PLANES[m]
            if p == PLANES[m] or far_hop != (p if below else 3 - p):
                continue

            @pl.when(z == p)
            def _(p=p, below=below):
                side = 0 if below else 1
                came(m, k, side)
                at = side if PLANES[m] in (1, 2) else 0
                add_rows(own[m].at[k, pl.ds(y, 1), x], far[m].at[at, pl.ds(k, 1)], 1, sizes[m])
                hop(i, p, lambda copy: copy.start())

    def five(i):
        m, k = order[i]
        s, p = sizes[m], PLANES[m]
        sides = [v for v in (0, 1) if p != 3 * v]

        @pl.when(z == p)
        def _():
            for side in sides:
                came(m, k, side)

            def body(r, carry):
                at = pl.ds(pl.multiple_of(r * 16, 16), 16)
                acc = own[m][k, y, x, at].astype(F32)
                for side in range(len(sides)):
                    acc = acc + far[m][side, k, at].astype(F32)
                total[k, at] = acc
                return carry

            lax.fori_loop(0, s // 16, body, 0)
            if s < total.shape[1]:
                total[k, pl.ds(s, total.shape[1] - s)] = jnp.zeros((total.shape[1] - s, width), F32)

    def small_step(stage):
        to = (core, xn, yn)
        if stage > 0:
            here = s_got.at[stage - 1]
            push(here, here, (q_s.at[stage - 1], q_r.at[stage - 1]), to[stage - 1]).wait_recv()
            s_acc[stage] = s_acc[stage - 1] + s_got[stage - 1]
        else:
            s_acc[0] = small[...]
        if stage < 3:
            start(push(s_acc.at[stage], s_got.at[stage], (q_s.at[stage], q_r.at[stage]), to[stage]))
        else:
            s_z[z] = s_acc[3]
            for k in range(1, 4):
                start(push(s_acc.at[3], s_z.at[z], (q_s.at[2 + k], q_r.at[2 + k]), zn[k - 1]))

    def moments(first):
        for t in range(n):
            p = PLANES[t]
            here = mom_all.at[z, pl.ds(0, sizes[t])]

            @pl.when(z == p)
            def _(t=t, p=p, here=here):
                copy = pltpu.make_async_copy(mom[t], here, loc.at[0])
                if first:
                    copy.start()
                else:
                    copy.wait()
                    for k in range(1, 4):
                        s = (p + k) % 4
                        there = mom_all.at[s, pl.ds(0, sizes[t])]
                        push(mom[t], there, (m_s.at[t], m_r.at[s]), (d, s)).wait_recv()

            @pl.when(z != p)
            def _(t=t, p=p, here=here):
                copy = push(mom[t], here, (m_s.at[t], m_r.at[z]), (d, p))
                if first:
                    copy.start()
                else:
                    copy.wait_send()

    def load_outlet():
        return pltpu.make_async_copy(outlet, obuf, loc.at[1])

    def load_intake(v):
        return pltpu.make_async_copy(intake.at[pl.ds(v * unit, unit)], wbuf.at[v % 4], w_l.at[4, v % 4])

    tdims = (((0,), (0,)), ((), ()))
    ndims = (((1,), (1,)), ((), ()))

    def shrink_rows(k):
        if k == 0:
            fetches[6].wait()
        i = 2 * k
        for half in (0, 1):
            u = 2 * k + half
            load_active(u).wait()

            def body(j, carry, half=half, u=u):
                cols = pl.ds(pl.multiple_of(j * 2 * top, 2 * top), 2 * top)
                g = lax.dot_general(act[u % 2, :, cols], cot[...], tdims, preferred_element_type=F32)
                made[i % slots, half, j] = g.astype(BF).reshape(2, top, width)
                return carry

            lax.fori_loop(0, unit // (2 * top), body, 0)
            if u + 2 < count_units:
                load_active(u + 2).start()

    def mlp_back(u):
        k, half = u // 2, u % 2
        for copy in load(u):
            copy.wait()

        def grad(j, carry):
            rows = pl.ds(pl.multiple_of(j * 256, 256), 256)
            to = pl.ds(pl.multiple_of(j * 256 + half * unit, 256), 256)
            g = lax.dot_general(cot[...], wbuf[u % 2, rows], ndims, preferred_element_type=F32)
            hg = (g * slo[u % 2, :, rows]).astype(BF)
            hgrad[:, to] = hg
            small[pl.ds(2 + k, 1), to] = jnp.sum(hg.astype(F32), axis=0, keepdims=True)
            return carry

        lax.fori_loop(0, unit // 256, grad, 0)

        def back(j, carry):
            cols = pl.ds(pl.multiple_of(j * 256, 256), 256)
            g = jnp.dot(hgrad[:, pl.ds(half * unit, unit)], wbuf[2 + u % 2, :, cols], preferred_element_type=F32)
            if u == 0:
                wide[:, cols] = g
            else:
                wide[:, cols] += g
            return carry

        lax.fori_loop(0, width // 256, back, 0)
        if u + 2 < count_units:
            for copy in load(u + 2):
                copy.start()

    def mlp_two(k):
        i = 2 * k + 1
        if k == 0:
            fetches[3].wait()

        def body(j, carry):
            cols = pl.ds(pl.multiple_of(j * 2 * top, 2 * top), 2 * top)
            g = lax.dot_general(hgrad[:, cols], second[...], tdims, preferred_element_type=F32)
            made[i % slots, j // 2, j % 2] = g.astype(BF).reshape(2, top, width)
            return carry

        lax.fori_loop(0, 4, body, 0)

    chunk = 64

    def norm_block(index, v_of, extra):
        gain = norm_gain[pl.ds(index, 1)]

        def body(i, carry):
            at = pl.ds(pl.multiple_of(i * chunk, chunk), chunk)
            v = v_of(at)
            center = v - jnp.mean(v, axis=-1, keepdims=True)
            r = lax.rsqrt(jnp.mean(center * center, axis=-1, keepdims=True) + norm_eps)
            nrm = center * r
            w = wide[at]
            u = w * gain
            down = r * (u - jnp.mean(u, axis=-1, keepdims=True) - nrm * jnp.mean(u * nrm, axis=-1, keepdims=True))
            sums = extra(at, down)
            new = [jnp.sum(w * nrm, axis=0, keepdims=True), jnp.sum(w, axis=0, keepdims=True)] + sums
            return tuple(a + b for a, b in zip(carry, new))

        zero = jnp.zeros((1, width), F32)
        out = lax.fori_loop(0, seq // chunk, body, (zero,) * (4 if index else 2))
        small[pl.ds(6 + index, 1)] = out[0]
        small[pl.ds(8 + index, 1)] = out[1]
        if index:
            small[pl.ds(10, 1)] = out[2]
            small[pl.ds(11, 1)] = out[3]

    def second_norm_back():
        fetches[0].wait()
        load_outlet().start()
        for v in range(4):
            load_intake(v).start()

        def extra(at, down):
            g = cot[at].astype(F32)
            m = g + down
            mgrad[at] = m
            low = m.astype(BF)
            branch[at] = low
            return [jnp.sum(low.astype(F32), axis=0, keepdims=True), jnp.sum(g, axis=0, keepdims=True)]

        norm_block(1, lambda at: middle[at], extra)

    def outlet_piece(k):
        i = 12 + k
        if k == 0:
            fetches[2].wait()
        cols = pl.ds(k * 8 * sizes[1], 8 * sizes[1])
        g = lax.dot_general(attended[:, cols], branch[...], tdims, preferred_element_type=F32)
        made[i % slots, :, :, :, pl.ds(0, sizes[1])] = g.astype(BF).reshape(2, 2, 2, sizes[1], width)

    def attended_back():
        load_outlet().wait()

        def body(j, carry):
            rows = pl.ds(pl.multiple_of(j * 256, 256), 256)
            g = lax.dot_general(branch[...], obuf[rows], ndims, preferred_element_type=F32)
            agrad[:, rows] = g.astype(BF)
            return carry

        lax.fori_loop(0, width // 256, body, 0)

    scale = HEAD_DIM ** (-0.5)

    def heads(first_pair, pairs):
        if first_pair == 0:
            fetches[1].wait()
        mask = live_keys(keep, z)

        def body(p, carry):
            at = pl.ds(pl.multiple_of(p * 6 * HEAD_DIM, 6 * HEAD_DIM), 6 * HEAD_DIM)
            both = mixed[:, at]
            ag_both = agrad[:, pl.ds(pl.multiple_of(p * 2 * HEAD_DIM, 2 * HEAD_DIM), 2 * HEAD_DIM)]
            parts, sums = [], []
            for e in range(2):
                q, k, v = (both[:, (3 * e + b) * HEAD_DIM : (3 * e + b + 1) * HEAD_DIM] for b in range(3))
                ag = ag_both[:, e * HEAD_DIM : (e + 1) * HEAD_DIM]
                s = lax.dot_general(q, k, ndims, preferred_element_type=F32) * scale
                s = jnp.where(mask, s, masked_score)
                s = jnp.exp(s - jnp.max(s, axis=-1, keepdims=True))
                pr = s / jnp.sum(s, axis=-1, keepdims=True)
                vg = lax.dot_general(pr.astype(BF), ag, tdims, preferred_element_type=F32)
                dp = lax.dot_general(ag, v, ndims, preferred_element_type=F32)
                ds = (pr * (dp - jnp.sum(dp * pr, axis=-1, keepdims=True))).astype(BF)
                qg = jnp.dot(ds, k, preferred_element_type=F32) * scale
                kg = lax.dot_general(ds, q, tdims, preferred_element_type=F32) * scale
                parts += [qg.astype(BF), kg.astype(BF), vg.astype(BF)]
                sums.append((jnp.sum(parts[-3].astype(F32), 0, keepdims=True), jnp.sum(parts[-1].astype(F32), 0, keepdims=True)))
            mixed[:, at] = jnp.concatenate(parts, axis=1)
            to = pl.ds(pl.multiple_of(p * 2 * HEAD_DIM, 2 * HEAD_DIM), 2 * HEAD_DIM)
            small[pl.ds(0, 1), to] = jnp.concatenate([sums[0][0], sums[1][0]], axis=1)
            small[pl.ds(1, 1), to] = jnp.concatenate([sums[0][1], sums[1][1]], axis=1)
            return carry

        lax.fori_loop(first_pair, first_pair + pairs, body, 0)

    def intake_piece(k):
        i = 8 + k
        if k == 0:
            fetches[4].wait()
        rows = 4 * sizes[0]

        def body(j, carry):
            cols = pl.ds(pl.multiple_of((2 * k + j) * rows, rows), rows)
            g = lax.dot_general(mixed[:, cols], first[...], tdims, preferred_element_type=F32)
            made[i % slots, j, :, :, pl.ds(0, sizes[0])] = g.astype(BF).reshape(2, 2, sizes[0], width)
            return carry

        lax.fori_loop(0, 2, body, 0)

    def first_back(v):
        load_intake(v).wait()

        def body(j, carry):
            cols = pl.ds(pl.multiple_of(j * 256, 256), 256)
            g = jnp.dot(mixed[:, pl.ds(v * unit, unit)], wbuf[v % 4, :, cols], preferred_element_type=F32)
            if v == 0:
                wide[:, cols] = g
            else:
                wide[:, cols] += g
            return carry

        lax.fori_loop(0, width // 256, body, 0)
        if v + 4 < intake.shape[0] // unit:
            load_intake(v + 4).start()

    def first_norm_back():
        fetches[5].wait()

        def extra(at, down):
            token_grad[at] = (mgrad[at] + down).astype(BF)
            return []

        norm_block(0, lambda at: x_in[at].astype(F32), extra)

    work = {}
    blocks = []

    def block(name, us, piece, fn):
        work[name] = fn
        blocks.append((name, us, piece))

    for k in range(4):
        block(("a", k), 2.0, 2 * k, functools.partial(shrink_rows, k))
        block(("m", 2 * k), 2.0, None, functools.partial(mlp_back, 2 * k))
        block(("m", 2 * k + 1), 2.0, None, functools.partial(mlp_back, 2 * k + 1))
        block(("e", k), 1.5, 2 * k + 1, functools.partial(mlp_two, k))
    block("n2", 3.0, None, second_norm_back)
    block("ab", 1.5, None, attended_back)
    for k in range(4):
        block(("h", k), 7.0, None, functools.partial(heads, 2 * k, 2))
        block(("i", k), 1.2, 8 + k, functools.partial(intake_piece, k))
    for k in range(4):
        block(("o", k), 0.5, 12 + k, functools.partial(outlet_piece, k))
    for v in range(intake.shape[0] // unit):
        block(("f", v), 0.8, None, functools.partial(first_back, v))
    block("n1", 3.0, None, first_norm_back)
    for stage in range(4):
        block(("s", stage), 2.0, None, functools.partial(small_step, stage))

    small[pl.ds(12, 4)] = jnp.zeros((4, width), F32)
    steps = plan(blocks, sizes, order, slots, width)
    pushed = {}
    stage = 1
    for step in steps:
        kind = step[0]
        if kind == "block":
            name = step[1]
            piece = {b[0]: b[2] for b in blocks}[name]
            if piece is not None and piece - slots in pushed:
                pushed.pop(piece - slots).wait_send()
            work[name]()
            if name == ("m", 1):
                moments(True)
        elif kind == "push":
            pushed[step[1]] = core_push(step[1])
            pushed[step[1]].start()
        elif kind == "one":
            one(step[1])
        elif kind == "two":
            two(step[1])
        elif kind == "three":
            three(step[1])
        elif kind == "four":
            four(step[1], 1)
        elif kind == "fourc":
            four(step[1], 2)
    for i in range(len(order)):
        five(i)
    for k in range(1, 4):
        slot = s_z.at[(z + 4 - k) % 4]
        push(slot, slot, (q_s.at[2 + k], q_r.at[2 + k]), zn[k - 1]).wait_recv()
    small_out[...] = s_z[0] + s_z[1] + s_z[2] + s_z[3]
    moments(False)
    for copy in pushed.values():
        copy.wait_send()
    for copy in held:
        copy.wait_send()
    for i in range(len(order)):
        for p in range(4):
            if p != PLANES[order[i][0]]:

                @pl.when(z == p)
                def _(i=i, p=p):
                    hop(i, p, lambda copy: copy.wait_send())


def backward_all(weights, saved, norm_gain, keep, moms, sizes):
    intake, outlet, expand, shrink = weights
    active, slope, middle, mixed, attended, second, first, x, cot = saved
    seq, width = cot.shape
    top = max(sizes)
    order = []
    for k in range(4):
        order += [(3, k), (2, k)]
    order += [(0, k) for k in range(4)] + [(1, k) for k in range(4)]
    count = len(order)
    anyspace = pl.BlockSpec(memory_space=pl.ANY)
    vmem = pl.BlockSpec(memory_space=pltpu.VMEM)
    dma = pltpu.SemaphoreType.DMA
    unit = 512
    return pl.pallas_call(
        functools.partial(backward_kernel, sizes, order),
        out_shape=[
            jax.ShapeDtypeStruct((4, top, width), F32),
            jax.ShapeDtypeStruct((16, width), F32),
            jax.ShapeDtypeStruct((4, top, width), BF),
            jax.ShapeDtypeStruct((seq, width), BF),
        ],
        in_specs=[anyspace] * 13 + [vmem] * 6,
        out_specs=[vmem, vmem, anyspace, vmem],
        scratch_shapes=[pltpu.VMEM((4, 2, 2, s, width), BF) for s in sizes]
        + [pltpu.VMEM((4, 2, 2, s // 2, width), BF) for s in sizes]
        + [pltpu.VMEM((4, s, width), BF) for s in sizes]
        + [pltpu.VMEM((2 if p in (1, 2) else 1, 4, s, width), BF) for s, p in zip(sizes, PLANES)]
        + [
            pltpu.VMEM((3, 2, 2, 2, top, width), BF),
            pltpu.VMEM((2, seq, unit), BF),
            pltpu.VMEM((2, seq, unit), F32),
            pltpu.VMEM((4, unit, width), BF),
            pltpu.VMEM((width, width), BF),
            pltpu.VMEM((seq, width), BF),
            pltpu.VMEM((seq, width), F32),
            pltpu.VMEM((seq, width), F32),
            pltpu.VMEM((seq, width), BF),
            pltpu.VMEM((seq, width), BF),
            pltpu.VMEM((16, width), F32),
            pltpu.VMEM((3, 16, width), F32),
            pltpu.VMEM((4, 16, width), F32),
            pltpu.VMEM((4, 16, width), F32),
            dma((2,)),
            dma((count,)),
            dma((count,)),
            dma((4, count)),
            dma((4, count)),
            dma((4, 4)),
            dma((4, 4, 2)),
            dma((6,)),
            dma((6,)),
            dma((4,)),
            dma((4,)),
            dma((5, 4)),
        ]
        + [pltpu.VMEM((s, width), BF) for s in sizes]
        + [pltpu.VMEM(v.shape, v.dtype) for v in saved[2:]]
        + [dma((7,))],
        compiler_params=pltpu.CompilerParams(collective_id=2, has_side_effects=True, vmem_limit_bytes=VMEM_LIMIT),
    )(shrink, expand, outlet, intake, active, slope, middle, mixed, attended, second, first, x, cot, norm_gain, keep, *moms)


def split(v):
    hi = v.astype(BF)
    return hi, (v - hi.astype(F32)).astype(BF)


def dot(a, b):
    return jnp.dot(a, b, preferred_element_type=F32)


def muon_kernel(sizes, *refs):
    n = len(sizes)
    total, mom, outp, tokg = refs[:4]
    rows_out = refs[4 : 4 + n]
    grads = refs[4 + n : 4 + 2 * n]
    outp_all, tokg_all = refs[4 + 2 * n : 6 + 2 * n]
    refs = refs[6 + 2 * n :]
    low_g, uh, ul, pack, r_core, r_one, r_two, gathered, gf, gh, low, b, tf, xf, xh = refs[:15]
    g_s, g_r, a_s, a_r, o_s, o_r, s_s, s_r, loc = refs[15:]
    d, z, y, x, c = place()
    core, xn, yn, zn = partners(d, z, y, x, c)
    greet([core, xn, yn] + zn)
    held = []

    def start(copy):
        copy.start()
        held.append(copy)

    top, width = total.shape[1:]
    count = 4 * top
    block = width // 4
    height = 0
    for t in range(n):
        height = jnp.where(z == PLANES[t], sizes[t], height)
    per = top // 16

    def make(i, carry):
        k, r = i // per, (i % per) * 16
        at = pl.ds(pl.multiple_of(r, 16), 16)
        g = total[k, at]
        low_g[k, at] = g.astype(BF)
        u = g + muon_decay * (muon_decay * mom[k, at].astype(F32) + g)
        row = lax.broadcasted_iota(jnp.int32, u.shape, 0) + r
        u = jnp.where(row < height, u, 0.0)
        to = pl.ds(pl.multiple_of(i * 16, 16), 16)
        uh[to], ul[to] = split(u)
        return carry

    lax.fori_loop(0, 4 * per, make, 0)

    def back_home(src, dst, sems, local, first):
        for t in range(n):
            s, p = sizes[t], PLANES[t]

            @pl.when(z == p)
            def _(t=t, s=s, p=p):
                own = pltpu.make_async_copy(src.at[p, pl.ds(0, s)], dst[t], loc.at[local])
                away = [
                    push(src.at[(p + k) % 4, pl.ds(0, s)], dst[t], (sems[0].at[k], sems[1].at[t]), (d, (p + k) % 4))
                    for k in range(1, 4)
                ]
                if first:
                    for copy in away:
                        copy.start()
                    own.start()
                else:
                    own.wait()
                    for copy in away:
                        copy.wait_send()

            if not first:

                @pl.when(z != p)
                def _(t=t, p=p):
                    push(dst[t], dst[t], (sems[0].at[0], sems[1].at[t]), (d, p)).wait_recv()

    back_home(low_g, grads, (g_s, g_r), 0, True)
    for i, (a, e) in enumerate(((outp, outp_all), (tokg, tokg_all))):
        pltpu.make_async_copy(a.at[z], e.at[z], loc.at[1 + i]).start()
        for k in range(1, 4):
            start(push(a.at[(z + k) % 4], e.at[z], (o_s.at[i, k - 1], o_r.at[i, k - 1]), zn[k - 1]))

    places = {0: (0, 0), 3: (0, 4 * block), 1: (1, 0), 2: (1, 3 * block)}
    tdims = (((0,), (0,)), ((), ()))

    def product(half):
        for r, (h, col) in places.items():
            if h != half:
                continue
            mine = slice(r * block, (r + 1) * block)
            rest = slice(r * block, width)
            acc = lax.dot_general(uh[:, mine], uh[:, rest], tdims, preferred_element_type=F32)
            acc = acc + lax.dot_general(uh[:, mine], ul[:, rest], tdims, preferred_element_type=F32)
            acc = acc + lax.dot_general(ul[:, mine], uh[:, rest], tdims, preferred_element_type=F32)
            pack[half, :, col : col + width - r * block] = acc

    def sem(i):
        return (a_s.at[i], a_r.at[i])

    for v in (0, 1):

        @pl.when(c == v)
        def _(v=v):
            product(1 - v)
            push(pack.at[1 - v], r_core, sem(0), core).start()
            product(v)

    def add(dst, r0, src, rows, into=None):
        def body(i, carry):
            at = pl.ds(pl.multiple_of(r0 + i * 8, 8), 8)
            v = dst[at] + src[pl.ds(pl.multiple_of(i * 8, 8), 8)]
            (dst if into is None else into)[at] = v
            return carry

        lax.fori_loop(0, rows // 8, body, 0)

    def rows(ref, r, size):
        return ref.at[pl.ds(pl.multiple_of(r, 32), size)]

    half, quarter, eighth = block // 2, block // 4, block // 8
    push(r_core, r_core, sem(0), core).wait_recv()
    mine, whole = pack.at[c], gathered.at[c]
    add(mine, 0, r_core, block)
    base_a, base_b = 0, half
    start(push(rows(mine, base_a + (1 - y) * quarter, quarter), r_one.at[0], sem(1), yn))
    start(push(rows(mine, base_b + (1 - x) * quarter, quarter), r_one.at[1], sem(2), xn))
    push(r_one.at[0], r_one.at[0], sem(1), yn).wait_recv()
    mine_a = base_a + y * quarter
    add(mine, mine_a, r_one.at[0], quarter)
    start(push(rows(mine, mine_a + (1 - x) * eighth, eighth), r_two.at[0], sem(3), xn))
    push(r_one.at[1], r_one.at[1], sem(2), xn).wait_recv()
    mine_b = base_b + x * quarter
    add(mine, mine_b, r_one.at[1], quarter)
    start(push(rows(mine, mine_b + (1 - y) * eighth, eighth), r_two.at[1], sem(4), yn))
    push(r_two.at[0], r_two.at[0], sem(3), xn).wait_recv()
    own_a = mine_a + x * eighth
    add(mine, own_a, r_two.at[0], eighth, whole)
    start(push(rows(whole, own_a, eighth), rows(whole, own_a, eighth), sem(5), xn))
    push(r_two.at[1], r_two.at[1], sem(4), yn).wait_recv()
    own_b = mine_b + y * eighth
    add(mine, own_b, r_two.at[1], eighth, whole)
    start(push(rows(whole, own_b, eighth), rows(whole, own_b, eighth), sem(6), yn))
    got = rows(whole, mine_a + (1 - x) * eighth, eighth)
    push(got, got, sem(5), xn).wait_recv()
    start(push(rows(whole, mine_a, quarter), rows(whole, mine_a, quarter), sem(7), yn))
    got = rows(whole, mine_b + (1 - y) * eighth, eighth)
    push(got, got, sem(6), yn).wait_recv()
    start(push(rows(whole, mine_b, quarter), rows(whole, mine_b, quarter), sem(8), xn))
    start(push(rows(whole, mine_a, quarter), rows(whole, mine_a, quarter), sem(9), core))
    start(push(rows(whole, mine_b, quarter), rows(whole, mine_b, quarter), sem(10), core))
    other_a = base_a + (1 - y) * quarter
    got = rows(whole, other_a, quarter)
    push(got, got, sem(7), yn).wait_recv()
    start(push(got, got, sem(11), core))
    other_b = base_b + (1 - x) * quarter
    got = rows(whole, other_b, quarter)
    push(got, got, sem(8), xn).wait_recv()
    start(push(got, got, sem(12), core))
    beside = gathered.at[1 - c]
    for r, i in ((mine_a, 9), (mine_b, 10), (other_a, 11), (other_b, 12)):
        got = rows(beside, r, quarter)
        push(got, got, sem(i), core).wait_recv()

    eye = lax.broadcasted_iota(jnp.int32, (block, block), 0) == lax.broadcasted_iota(jnp.int32, (block, block), 1)
    trace = jnp.zeros((1, 1), F32)
    for r, (h, col) in places.items():
        v = jnp.where(eye, gathered[h, :, col : col + block], 0.0)
        trace = trace + jnp.sum(jnp.sum(v, axis=1, keepdims=True), axis=0, keepdims=True)
    inverse = 1.0 / (jnp.sqrt(trace) + frob_eps)
    squared = inverse * inverse
    for r, (h, col) in places.items():
        for k in range(r, 4):
            v = gathered[h, :, col + (k - r) * block : col + (k - r + 1) * block] * squared
            a, e = slice(r * block, (r + 1) * block), slice(k * block, (k + 1) * block)
            gf[a, e] = v
            gh[a, e] = v.astype(BF)
            if k > r:
                v = v.T
                gf[e, a] = v
                gh[e, a] = v.astype(BF)

    step = 64

    def scale_x(i, carry):
        at = pl.ds(pl.multiple_of(i * step, step), step)
        v = (uh[at].astype(F32) + ul[at].astype(F32)) * inverse
        xf[at] = v
        xh[at] = v.astype(BF)
        return carry

    lax.fori_loop(0, count // step, scale_x, 0)

    def iterate(shift, last):
        level = coef_a + coef_b * shift + coef_c * shift * shift
        slope = coef_b + 2.0 * coef_c * shift
        if last:

            def lower(i, carry):
                at = pl.ds(pl.multiple_of(i * step, step), step)
                g = gf[at]
                row = lax.broadcasted_iota(jnp.int32, g.shape, 0) + i * step
                col = lax.broadcasted_iota(jnp.int32, g.shape, 1)
                g = g - jnp.where(row == col, shift, 0.0)
                gf[at] = g
                low[at] = g.astype(BF)
                return carry

            lax.fori_loop(0, width // step, lower, 0)
            b[...] = (slope * gf[...] + coef_c * dot(low[...], low[...])).astype(BF)
            xh[...] = (level * xf[...] + dot(xh[...], b[...])).astype(BF)
            return
        b[...] = (slope * gf[...] + coef_c * dot(gh[...], gh[...])).astype(BF)
        v = level * xf[...] + dot(xh[...], b[...])
        t = level * gf[...] + dot(gh[...], b[...])
        xf[...] = v
        xh[...] = v.astype(BF)
        tf[...] = t
        low[...] = t.astype(BF)
        g = level * tf[...] + dot(b[...], low[...])
        gf[...] = g
        gh[...] = g.astype(BF)

    def middle(i, carry):
        iterate(0.0, False)
        return carry

    lax.fori_loop(0, NS_STEPS - 1, middle, 0)
    iterate(0.8, True)

    back_home(xh.reshape(4, top, width), rows_out, (s_s, s_r), 3, True)

    for v in (0, 1):

        @pl.when(c == v)
        def _(v=v):
            push(pack.at[1 - v], r_core, sem(0), core).wait_send()

    for i, (a, e) in enumerate(((outp, outp_all), (tokg, tokg_all))):
        pltpu.make_async_copy(a.at[z], e.at[z], loc.at[1 + i]).wait()
        for k in range(1, 4):
            slot = e.at[(z + 4 - k) % 4]
            push(slot, slot, (o_s.at[i, k - 1], o_r.at[i, k - 1]), zn[k - 1]).wait_recv()
    back_home(low_g, grads, (g_s, g_r), 0, False)
    for copy in held:
        copy.wait_send()
    back_home(xh.reshape(4, top, width), rows_out, (s_s, s_r), 3, False)


def muon_all(total, mom, outp, tokg, sizes):
    top, width = total.shape[1:]
    count, block = 4 * top, width // 4
    anyspace = pl.BlockSpec(memory_space=pl.ANY)
    vmem = pl.BlockSpec(memory_space=pltpu.VMEM)
    dma = pltpu.SemaphoreType.DMA
    wide = block * 5
    return pl.pallas_call(
        functools.partial(muon_kernel, sizes),
        out_shape=[jax.ShapeDtypeStruct((s, width), BF) for s in sizes] * 2
        + [jax.ShapeDtypeStruct(outp.shape, outp.dtype), jax.ShapeDtypeStruct(tokg.shape, tokg.dtype)],
        in_specs=[vmem, vmem, anyspace, anyspace],
        out_specs=[anyspace] * (2 * len(sizes) + 2),
        scratch_shapes=[
            pltpu.VMEM((4, top, width), BF),
            pltpu.VMEM((count, width), BF),
            pltpu.VMEM((count, width), BF),
            pltpu.VMEM((2, block, wide), F32),
            pltpu.VMEM((block, wide), F32),
            pltpu.VMEM((2, block // 4, wide), F32),
            pltpu.VMEM((2, block // 8, wide), F32),
            pltpu.VMEM((2, block, wide), F32),
            pltpu.VMEM((width, width), F32),
            pltpu.VMEM((width, width), BF),
            pltpu.VMEM((width, width), BF),
            pltpu.VMEM((width, width), BF),
            pltpu.VMEM((width, width), F32),
            pltpu.VMEM((count, width), F32),
            pltpu.VMEM((count, width), BF),
            dma((4,)),
            dma((4,)),
            dma((13,)),
            dma((13,)),
            dma((2, 3)),
            dma((2, 3)),
            dma((4,)),
            dma((4,)),
            dma((4,)),
        ],
        compiler_params=pltpu.CompilerParams(collective_id=3, has_side_effects=True, vmem_limit_bytes=VMEM_LIMIT),
    )(total, mom, outp, tokg)


def finish_kernel(factors, *refs):
    n = len(factors)
    grads, rows, masters, moments = (refs[i * n : i * n + n] for i in range(4))
    outp, tokg, small = refs[4 * n : 4 * n + 3]
    state = refs[4 * n + 3 : 4 * n + 9]
    refs = refs[4 * n + 9 :]
    output, token_grad = refs[:2]
    shards, moments_new, masters_new, copies = (refs[2 + i * n : 2 + i * n + n] for i in range(4))
    vectors = refs[2 + 4 * n :]
    step = 16

    def over(rows, body):
        def one(i, carry):
            body(pl.ds(pl.multiple_of(i * step, step), step))
            return carry

        lax.fori_loop(0, rows // step, one, 0)

    for src, dst in ((outp, output), (tokg, token_grad)):
        for k in range(src.shape[0]):

            def body(at, src=src, dst=dst, k=k):
                dst[k, at] = src[k, at].astype(F32)

            over(src.shape[1], body)
    for m in range(n):

        def body(at, m=m):
            g = grads[m][at].astype(F32)
            shards[m][at] = g
            moments_new[m][at] = muon_decay * moments[m][at] + g
            new = masters[m][at] - factors[m] * rows[m][at].astype(F32)
            masters_new[m][at] = new
            copies[m][at] = new.astype(BF)

        over(grads[m].shape[0], body)
    width = small.shape[1]
    at = 0
    for i, (lo, hi) in enumerate(((0, 2), (6, 8), (8, 12))):
        g = small[lo:hi]
        change, first, second = adam_step(g, state[2 * i][...], state[2 * i + 1][...])
        for value in (g, change, first, second):
            vectors[at][...] = value
            at += 1


def finish(grads, rows, masters, moments, outp, tokg, small, state, factors):
    vmem = pl.BlockSpec(memory_space=pltpu.VMEM)
    args = [*grads, *rows, *masters, *moments, outp, tokg, small, *state]
    sized = [jax.ShapeDtypeStruct(v.shape, F32) for v in masters]
    shapes = [jax.ShapeDtypeStruct(v.shape, F32) for v in (outp, tokg)] + sized * 3
    shapes += [jax.ShapeDtypeStruct(v.shape, BF) for v in masters]
    for v in state[::2]:
        shapes += [jax.ShapeDtypeStruct(v.shape, F32)] * 4
    return pl.pallas_call(
        functools.partial(finish_kernel, factors),
        out_shape=shapes,
        in_specs=[vmem] * len(args),
        out_specs=[vmem] * len(shapes),
        compiler_params=pltpu.CompilerParams(vmem_limit_bytes=VMEM_LIMIT),
        cost_estimate=pl.CostEstimate(flops=10**7, bytes_accessed=15 * 10**6, transcendentals=0),
    )(*args)


def per_device_fast(
    tokens,
    cotangent,
    keep_mask,
    intake,
    outlet,
    expand,
    shrink,
    intake_moment,
    outlet_moment,
    expand_moment,
    shrink_moment,
    head_bias,
    expand_bias,
    norm_gain,
    model_bias,
    head_first,
    head_second,
    expand_first,
    expand_second,
    gain_first,
    gain_second,
    bias_first,
    bias_second,
):
    shape = tokens.shape
    local, width = shape[2:]
    z = lax.axis_index("tensor")
    masters = (intake, outlet, expand, shrink)
    moments = (intake_moment, outlet_moment, expand_moment, shrink_moment)
    sizes = tuple(v.shape[0] for v in masters)
    made = forward_all(
        masters,
        tokens.reshape(-1, local, width),
        cotangent.reshape(-1, local, width),
        norm_gain,
        model_bias,
        head_bias,
        expand_bias[None],
        keep_mask,
    )
    whole = [v.reshape(-1, width) for v in made[:4]]
    x, cot = (v.reshape(-1, width) for v in made[4:6])
    out, saved = made[6], tuple(made[7:]) + (x, cot)
    total, small, mom, token_grad = backward_all(whole, saved, norm_gain, keep_mask, moments, sizes)
    made = muon_all(total, mom, out.reshape(-1, local, width), token_grad.reshape(-1, local, width), sizes)
    rows_scale = lax.axis_size("dp") * lax.axis_size("tensor")
    factors = [rate * (s * rows_scale / width) ** 0.5 for s, rate in zip(sizes, muon_rates)]
    state = (head_first, head_second, gain_first, gain_second, bias_first, bias_second)
    done = finish(made[4:8], made[:4], masters, moments, made[8], made[9], small, state, factors)
    output, token_grad = (v.reshape(shape) for v in done[:2])
    shards, moments_new, masters_new, copies = (tuple(done[2 + 4 * i : 6 + 4 * i]) for i in range(4))
    head, gain, bias = (done[18 + 4 * i : 22 + 4 * i] for i in range(3))
    hidden_total = small[2:6].reshape(expand_bias.shape)
    hidden = adam_step(hidden_total, expand_first, expand_second)
    return (
        (output, token_grad)
        + shards
        + (head[0], hidden_total, gain[0], bias[0])
        + moments_new
        + masters_new
        + copies
        + (head[1], hidden[0], gain[1], bias[1])
        + tuple(head[2:])
        + tuple(hidden[1:])
        + tuple(gain[2:])
        + tuple(bias[2:])
    )


def solution(mesh):
    placed = (
        P(None, "dp", "tensor", None),
        P(None, "dp", "tensor", None),
        P(None, "dp", None),
        P(("tensor", "dp"), None),
        P(("tensor", "dp"), None),
        P(("tensor", "dp"), None),
        P(("tensor", "dp"), None),
        P(("tensor", "dp"), None),
        P(("tensor", "dp"), None),
        P(("tensor", "dp"), None),
        P(("tensor", "dp"), None),
        P(),
        P(),
        P(),
        P(),
        P(),
        P(),
        P(),
        P(),
        P(),
        P(),
        P(),
        P(),
    )
    fast = mesh.shape["dp"] == 8 and mesh.shape["tensor"] == 4
    return jax.shard_map(
        per_device_fast if fast else per_device,
        mesh=mesh,
        in_specs=placed,
        out_specs=(
            P(None, "dp", "tensor", None),
            P(None, "dp", "tensor", None),
            P(("tensor", "dp"), None),
            P(("tensor", "dp"), None),
            P(("tensor", "dp"), None),
            P(("tensor", "dp"), None),
            P(),
            P(),
            P(),
            P(),
            P(("tensor", "dp"), None),
            P(("tensor", "dp"), None),
            P(("tensor", "dp"), None),
            P(("tensor", "dp"), None),
            P(("tensor", "dp"), None),
            P(("tensor", "dp"), None),
            P(("tensor", "dp"), None),
            P(("tensor", "dp"), None),
            P(("tensor", "dp"), None),
            P(("tensor", "dp"), None),
            P(("tensor", "dp"), None),
            P(("tensor", "dp"), None),
            P(),
            P(),
            P(),
            P(),
            P(),
            P(),
            P(),
            P(),
            P(),
            P(),
            P(),
            P(),
        ),
        check_vma=False,
    )
```

```python
import functools

import jax
import jax.numpy as jnp
from jax import lax
from jax.experimental import pallas as pl
from jax.experimental.pallas import tpu as pltpu
from jax.sharding import PartitionSpec as P

HEAD_DIM = 64
BUF = 64
NS_STEPS = 5
ADAM_STEP = 10


norm_eps = 1e-06
first_decay = 0.9
second_decay = 0.95
adam_rate = 0.05
adam_eps = 1e-08
muon_decay = 0.5
muon_rates = (1.0, 4.0, 1.0, 1.0)
frob_eps = 1e-07
coef_a = 3.4445
coef_b = -4.775
coef_c = 2.0315
masked_score = -1000000000.0


def precise(form, left, right):
    return jnp.einsum(form, left, right, precision=lax.Precision.HIGHEST)


def layer_norm(inputs_row, gain_row, shift_row):
    center = inputs_row - jnp.mean(inputs_row, axis=-1, keepdims=True)
    spread = jnp.mean(center * center, axis=-1, keepdims=True)
    return center * lax.rsqrt(spread + norm_eps) * gain_row + shift_row


def softmax_rows(scores):
    largest = jnp.max(scores, axis=-1, keepdims=True)
    powers = jnp.exp(scores - largest)
    return powers / jnp.sum(powers, axis=-1, keepdims=True)


def exact_gelu(inputs_row):
    return jax.nn.gelu(inputs_row, approximate=False)


def attend_weights(queries, keys_all, live_keys):
    scores = jnp.einsum(
        "iqhe,ikhe->ihqk", queries, keys_all, preferred_element_type=jnp.float32
    ) * HEAD_DIM ** (-0.5)
    scores = jnp.where(live_keys[:, None, None, :], scores, masked_score)
    return softmax_rows(scores)


def reduce_blocks(blocks):
    return (
        lax.psum_scatter(blocks[0], "dp", scatter_dimension=0, tiled=True),
        lax.psum_scatter(blocks[1], "dp", scatter_dimension=0, tiled=True),
        lax.psum_scatter(blocks[2], "dp", scatter_dimension=0, tiled=True),
        lax.psum_scatter(blocks[3], "dp", scatter_dimension=0, tiled=True),
    )


def gram_whole(matrix):
    model_width = matrix.shape[1]
    own_rows = model_width // lax.axis_size("dp")
    shard_rows = lax.psum_scatter(
        precise(
            "rm,rn->mn", lax.slice_in_dim(matrix, 0, own_rows * lax.axis_size("dp"), axis=1), matrix
        ),
        "dp",
        scatter_dimension=0,
        tiled=True,
    )
    return lax.all_gather(shard_rows, "dp", axis=0, tiled=True)


def newton_step(scaled, gram):
    product = precise("rk,kn->rn", scaled, gram)
    return coef_a * scaled + coef_b * product + coef_c * precise("rk,kn->rn", product, gram)


def adam_step(gradient, first, second):
    first_new = first_decay * first + (1.0 - first_decay) * gradient
    second_new = second_decay * second + (1.0 - second_decay) * gradient * gradient
    first_hat = first_new / (1.0 - first_decay**ADAM_STEP)
    second_hat = second_new / (1.0 - second_decay**ADAM_STEP)
    change = -adam_rate * first_hat / (jnp.sqrt(second_hat) + adam_eps)
    return (change, first_new, second_new)


def per_device(
    tokens,
    cotangent,
    keep_mask,
    intake,
    outlet,
    expand,
    shrink,
    intake_moment,
    outlet_moment,
    expand_moment,
    shrink_moment,
    head_bias,
    expand_bias,
    norm_gain,
    model_bias,
    head_first,
    head_second,
    expand_first,
    expand_second,
    gain_first,
    gain_second,
    bias_first,
    bias_second,
):
    micro_count, images, local_seq, model_width = tokens.shape
    seq_len = keep_mask.shape[2]
    tensor_size = lax.axis_size("tensor")
    tensor_index = lax.axis_index("tensor")
    head_cols = model_width // tensor_size
    local_heads = head_cols // HEAD_DIM
    hidden_cols = expand_bias.shape[0] // tensor_size
    head_start = tensor_index * head_cols
    hidden_start = tensor_index * hidden_cols
    query_bias = lax.dynamic_slice_in_dim(head_bias[0], head_start, head_cols, 0).reshape(
        local_heads, HEAD_DIM
    )
    value_bias = lax.dynamic_slice_in_dim(head_bias[1], head_start, head_cols, 0).reshape(
        local_heads, HEAD_DIM
    )
    mixed_bias = jnp.stack([query_bias, jnp.zeros_like(query_bias), value_bias], axis=1).reshape(
        3 * head_cols
    )
    hidden_bias = lax.dynamic_slice_in_dim(expand_bias, hidden_start, hidden_cols, 0)
    position = jnp.arange(seq_len)
    masters = (intake, outlet, expand, shrink)
    block_shapes = (
        (3 * head_cols, model_width),
        (head_cols, model_width),
        (hidden_cols, model_width),
        (hidden_cols, model_width),
    )
    totals = tuple((jnp.zeros(shape_one, jnp.float32) for shape_one in block_shapes))
    gain_grad = jnp.zeros((2, model_width), jnp.float32)
    bias_grad = jnp.zeros((4, model_width), jnp.float32)
    mixed_bias_grad = jnp.zeros((2, head_cols), jnp.float32)
    hidden_bias_grad = jnp.zeros((hidden_cols,), jnp.float32)
    outputs = []
    token_grads = []
    for micro_index in range(micro_count):
        intake_block, outlet_block, expand_block, shrink_block = (
            lax.all_gather(intake.astype(jnp.bfloat16), "dp", axis=0, tiled=True),
            lax.all_gather(outlet.astype(jnp.bfloat16), "dp", axis=0, tiled=True),
            lax.all_gather(expand.astype(jnp.bfloat16), "dp", axis=0, tiled=True),
            lax.all_gather(shrink.astype(jnp.bfloat16), "dp", axis=0, tiled=True),
        )
        token_rows = tokens[micro_index].astype(jnp.float32)
        live_keys = jnp.logical_or(keep_mask[micro_index] > 0, position[None, :] < BUF)
        first_local = layer_norm(token_rows, norm_gain[0], model_bias[0]).astype(jnp.bfloat16)
        first_norm = lax.all_gather(first_local, "tensor", axis=1, tiled=True)
        mixed_rows = (
            jnp.einsum("isd,rd->isr", first_norm, intake_block, preferred_element_type=jnp.float32)
            + mixed_bias
        )
        mixed_rows = mixed_rows.astype(jnp.bfloat16).reshape(
            images, seq_len, local_heads, 3, HEAD_DIM
        )
        queries = mixed_rows[:, :, :, 0]
        keys_all = mixed_rows[:, :, :, 1]
        values = mixed_rows[:, :, :, 2]
        attention = attend_weights(queries, keys_all, live_keys)
        attention_low = attention.astype(jnp.bfloat16)
        attended = jnp.einsum(
            "ihqk,ikhe->iqhe", attention_low, values, preferred_element_type=jnp.float32
        )
        attended = attended.reshape(images, seq_len, head_cols).astype(jnp.bfloat16)
        part_sum = jnp.einsum(
            "isc,cd->isd", attended, outlet_block, preferred_element_type=jnp.float32
        )
        middle = (
            token_rows
            + lax.psum_scatter(part_sum, "tensor", scatter_dimension=1, tiled=True)
            + model_bias[2]
        )
        second_local = layer_norm(middle, norm_gain[1], model_bias[1]).astype(jnp.bfloat16)
        second_norm = lax.all_gather(second_local, "tensor", axis=1, tiled=True)
        hidden = (
            jnp.einsum("isd,fd->isf", second_norm, expand_block, preferred_element_type=jnp.float32)
            + hidden_bias
        )
        active = exact_gelu(hidden).astype(jnp.bfloat16)
        part_two = jnp.einsum(
            "isf,fd->isd", active, shrink_block, preferred_element_type=jnp.float32
        )
        outputs.append(
            middle
            + lax.psum_scatter(part_two, "tensor", scatter_dimension=1, tiled=True)
            + model_bias[3]
        )
        cot_local = cotangent[micro_index]
        cot_rows = lax.all_gather(cot_local, "tensor", axis=1, tiled=True)
        shrink_block_grad = jnp.einsum(
            "isf,isd->fd", active, cot_rows, preferred_element_type=jnp.float32
        )
        active_grad = jnp.einsum(
            "isd,fd->isf", cot_rows, shrink_block, preferred_element_type=jnp.float32
        )
        gelu_value, gelu_back = jax.vjp(exact_gelu, hidden)
        hidden_grad = gelu_back(active_grad)[0].astype(jnp.bfloat16)
        hidden_bias_grad = hidden_bias_grad + jnp.sum(hidden_grad.astype(jnp.float32), axis=(0, 1))
        expand_block_grad = jnp.einsum(
            "isf,isd->fd", hidden_grad, second_norm, preferred_element_type=jnp.float32
        )
        second_part = jnp.einsum(
            "isf,fd->isd", hidden_grad, expand_block, preferred_element_type=jnp.float32
        )
        second_grad = lax.psum_scatter(second_part, "tensor", scatter_dimension=1, tiled=True)
        norm_value, norm_back = jax.vjp(layer_norm, middle, norm_gain[1], model_bias[1])
        middle_from_norm, gain_two_grad, shift_two_grad = norm_back(second_grad)
        cot_float = cot_local.astype(jnp.float32)
        middle_grad = cot_float + middle_from_norm
        branch_grad = middle_grad.astype(jnp.bfloat16)
        branch_rows = lax.all_gather(branch_grad, "tensor", axis=1, tiled=True)
        outlet_block_grad = jnp.einsum(
            "isc,isd->cd", attended, branch_rows, preferred_element_type=jnp.float32
        )
        attended_grad = jnp.einsum(
            "isd,cd->isc", branch_rows, outlet_block, preferred_element_type=jnp.float32
        )
        attended_grad = attended_grad.astype(jnp.bfloat16).reshape(
            images, seq_len, local_heads, HEAD_DIM
        )
        attention = attend_weights(queries, keys_all, live_keys)
        attention_low = attention.astype(jnp.bfloat16)
        values_grad = jnp.einsum(
            "ihqk,iqhe->ikhe", attention_low, attended_grad, preferred_element_type=jnp.float32
        )
        attention_grad = jnp.einsum(
            "iqhe,ikhe->ihqk", attended_grad, values, preferred_element_type=jnp.float32
        )
        score_grad = attention * (
            attention_grad - jnp.sum(attention_grad * attention, axis=-1, keepdims=True)
        )
        score_grad = score_grad.astype(jnp.bfloat16)
        queries_grad = jnp.einsum(
            "ihqk,ikhe->iqhe", score_grad, keys_all, preferred_element_type=jnp.float32
        ) * HEAD_DIM ** (-0.5)
        keys_grad = jnp.einsum(
            "ihqk,iqhe->ikhe", score_grad, queries, preferred_element_type=jnp.float32
        ) * HEAD_DIM ** (-0.5)
        mixed_grad = jnp.stack([queries_grad, keys_grad, values_grad], axis=3).astype(jnp.bfloat16)
        mixed_sums = jnp.sum(mixed_grad.astype(jnp.float32), axis=(0, 1))
        mixed_bias_grad = mixed_bias_grad + jnp.stack(
            [mixed_sums[:, 0].reshape(head_cols), mixed_sums[:, 2].reshape(head_cols)]
        )
        mixed_grad = mixed_grad.reshape(images, seq_len, 3 * head_cols)
        intake_block_grad = jnp.einsum(
            "isr,isd->rd", mixed_grad, first_norm, preferred_element_type=jnp.float32
        )
        first_part = jnp.einsum(
            "isr,rd->isd", mixed_grad, intake_block, preferred_element_type=jnp.float32
        )
        first_grad = lax.psum_scatter(first_part, "tensor", scatter_dimension=1, tiled=True)
        first_value, first_back = jax.vjp(layer_norm, token_rows, norm_gain[0], model_bias[0])
        token_from_norm, gain_one_grad, shift_one_grad = first_back(first_grad)
        token_grads.append(middle_grad + token_from_norm)
        gain_grad = gain_grad + jnp.stack([gain_one_grad, gain_two_grad])
        bias_grad = bias_grad + jnp.stack(
            [
                shift_one_grad,
                shift_two_grad,
                jnp.sum(branch_grad.astype(jnp.float32), axis=(0, 1)),
                jnp.sum(cot_float, axis=(0, 1)),
            ]
        )
        block_grads = (intake_block_grad, outlet_block_grad, expand_block_grad, shrink_block_grad)
        totals = tuple((total + block_one for total, block_one in zip(totals, block_grads)))
    shards = reduce_blocks(totals)
    head_full = lax.dynamic_update_slice_in_dim(
        jnp.zeros((2, model_width), jnp.float32), mixed_bias_grad, head_start, 1
    )
    hidden_full = lax.dynamic_update_slice_in_dim(
        jnp.zeros(expand_bias.shape, jnp.float32), hidden_bias_grad, hidden_start, 0
    )
    gain_total, bias_total, head_total, hidden_total = lax.psum(
        (gain_grad, bias_grad, head_full, hidden_full), ("dp", "tensor")
    )
    moments = (intake_moment, outlet_moment, expand_moment, shrink_moment)
    moments_new = [muon_decay * moment + gradient for gradient, moment in zip(shards, moments)]
    updates = [gradient + muon_decay * moment for gradient, moment in zip(shards, moments_new)]
    rows_max = max((update.shape[0] for update in updates))
    padded = jnp.stack(
        [jnp.pad(update, ((0, rows_max - update.shape[0]), (0, 0))) for update in updates]
    )
    spread = lax.all_to_all(padded, "tensor", split_axis=0, concat_axis=0, tiled=True)
    own_matrix = spread.reshape(tensor_size * rows_max, model_width)
    raw_gram = gram_whole(own_matrix)
    measure = jnp.sqrt(jnp.trace(raw_gram)) + frob_eps
    scaled = own_matrix / measure
    gram = raw_gram / (measure * measure)
    for step in range(NS_STEPS):
        if step > 0:
            gram = gram_whole(scaled)
        scaled = newton_step(scaled, gram)
    returned = lax.all_to_all(
        scaled.reshape(tensor_size, rows_max, model_width),
        "tensor",
        split_axis=0,
        concat_axis=0,
        tiled=True,
    )
    rows_scale = lax.axis_size("dp") * tensor_size
    masters_new = [
        weight
        - muon_rates[position_one]
        * (weight.shape[0] * rows_scale / weight.shape[1]) ** 0.5
        * returned[position_one, : weight.shape[0]]
        for position_one, weight in enumerate(masters)
    ]
    head_bias_change, head_first_new, head_second_new = adam_step(
        head_total, head_first, head_second
    )
    expand_bias_change, expand_first_new, expand_second_new = adam_step(
        hidden_total, expand_first, expand_second
    )
    norm_gain_change, gain_first_new, gain_second_new = adam_step(
        gain_total, gain_first, gain_second
    )
    model_bias_change, bias_first_new, bias_second_new = adam_step(
        bias_total, bias_first, bias_second
    )
    output = jnp.stack(outputs)
    token_grad = jnp.stack(token_grads)
    return (
        output,
        token_grad,
        shards[0],
        shards[1],
        shards[2],
        shards[3],
        head_total,
        hidden_total,
        gain_total,
        bias_total,
        moments_new[0],
        moments_new[1],
        moments_new[2],
        moments_new[3],
        masters_new[0],
        masters_new[1],
        masters_new[2],
        masters_new[3],
        masters_new[0].astype(jnp.bfloat16),
        masters_new[1].astype(jnp.bfloat16),
        masters_new[2].astype(jnp.bfloat16),
        masters_new[3].astype(jnp.bfloat16),
        head_bias_change,
        expand_bias_change,
        norm_gain_change,
        model_bias_change,
        head_first_new,
        head_second_new,
        expand_first_new,
        expand_second_new,
        gain_first_new,
        gain_second_new,
        bias_first_new,
        bias_second_new,
    )


MESH = pl.DeviceIdType.MESH
BF = jnp.bfloat16
F32 = jnp.float32
VMEM_LIMIT = 60 * 1024 * 1024


def place():
    d = lax.axis_index("dp")
    z = lax.axis_index("tensor")
    y, x, c = d // 4, (d // 2) % 2, d % 2
    return d, z, y, x, c


def partners(d, z, y, x, c):
    core = (d + 1 - 2 * c, z)
    xn = (d + 2 - 4 * x, z)
    yn = (d + 4 - 8 * y, z)
    zn = [(d, (z + k) % 4) for k in range(1, 4)]
    return core, xn, yn, zn


def greet(others):
    barrier = pltpu.get_barrier_semaphore()
    for other in others:
        pl.semaphore_signal(barrier, inc=1, device_id=other, device_id_type=MESH)
    pl.semaphore_wait(barrier, len(others))


def push(src, dst, sems, to):
    return pltpu.make_async_remote_copy(
        src_ref=src, dst_ref=dst, send_sem=sems[0], recv_sem=sems[1], device_id=to, device_id_type=MESH
    )


LINK = 93.5e3


OPT = dict(lagz=2.0, rate=86e3, lat=1.5, full=3.0, work=1.0, brate=93.5e3, blat=1.5, bone=3.0, bwork=1.3, bhop=3.0, bwin=3, bz=0.0, wait=10.0)


def live_keys(keep, z):
    count = keep.shape[1]
    row = keep[z // count, pl.ds(z % count, 1)]
    position = lax.broadcasted_iota(jnp.int32, row.shape, 1)
    return jnp.logical_or(row != 0, position < BUF)


def plan_forward(blocks, order, sizes, width, slots):
    done, events = [], []
    link = {"x": 0.0, "y": 0.0, "z": 0.0}
    now, at_z = 0.0, 2.0

    def carry(lane, start, rows):
        link[lane] = max(start, link[lane]) + rows * width * 4 / OPT["rate"]
        return link[lane] + OPT["lat"]

    for i, (m, k) in enumerate(order):
        if k == 0:
            events.append((0.1 * i, "one", i))
        elif m != 1:
            at_z += sizes[m] * width * 4 / OPT["rate"]
            events.append((at_z + OPT["lagz"] * k, "one", i))
    whole, loaded = {}, {}
    head = 0
    todo = list(range(len(blocks)))
    while events or todo:
        events.sort()
        if events and events[0][0] <= now:
            _, kind, i = events.pop(0)
            s = sizes[order[i][0]]
            if kind != "full":
                done.append((kind, i))
                now += 0.15
            if kind == "one" and order[i][0] == 1 and order[i][1] > 0:
                events.append((now + OPT["full"], "full", i))
            elif kind == "one":
                ready = max(carry("x", now, s / 2), carry("y", now, s / 2))
                events.append((ready, "two", i))
            elif kind == "two":
                ready = max(carry("x", now, s), carry("y", now, s))
                events.append((ready, "three", i))
            elif kind == "three":
                events.append((now + OPT["full"], "full", i))
                if order[i] == (1, 0):
                    for k in (1, 2, 3):
                        events.append((now + k * (16 * s * width / OPT["rate"] + 2.0) + OPT["wait"], "one", order.index((1, k))))
            else:
                whole[i] = True
            continue
        busy = sum(1 for j in loaded if j in todo)
        while head < len(blocks) and (blocks[head][2] is None or (blocks[head][2] in whole and busy < slots)):
            if blocks[head][2] is not None:
                done.append(("load", head))
                loaded[head] = now + 2.0
                busy += 1
            head += 1
        wait = None
        if todo:
            j = todo[0]
            if blocks[j][2] is None or j in loaded:
                if blocks[j][2] is None or loaded[j] <= now:
                    todo.pop(0)
                    done.append(("block", j))
                    now += blocks[j][1] * OPT["work"]
                    continue
                wait = loaded[j]
        times = [v for v in (wait, events[0][0] if events else None) if v is not None]
        now = max(now, min(times))
    return done


def forward_kernel(sizes, order, *refs):
    n = 4
    w = refs[:n]
    tok, cot = refs[n : n + 2]
    norm_gain, model_bias, head_bias, expand_bias, keep = refs[n + 2 : n + 7]
    refs = refs[n + 7 :]
    o_full = refs[:n]
    o_x, cot_all, output, o_active, o_slope, o_middle, o_mixed, o_attended, o_second, o_first = refs[n : n + 10]
    refs = refs[n + 10 :]
    full = refs[:n]
    xs, first, mixed, attended, acc, middle, second, active, slope, mixed_bias = refs[n : n + 10]
    z_s, z_r, loc, t_s, t_r, p_s, p_r, w_l, out_l, s_l = refs[n + 10 :]
    d, z, y, x, c = place()
    core, xn, yn, zn = partners(d, z, y, x, c)
    for m in range(n):
        full[m][z, y, x, c] = w[m][...].astype(BF)
    greet([core, xn, yn] + zn)
    held = []
    written = []
    inner = z * (3 - z) > 0
    seq, width = first.shape

    def start(copy):
        copy.start()
        held.append(copy)
        return copy

    def source(j):
        return (z, z + 1 - 2 * (z % 2), 2 - z // 2, 3 - 3 * (z // 2))[j]

    def along(m, j, go):
        slot = full[m].at[source(j), :, :, c] if m == 1 else full[m].at[source(j), y, x, c]
        if j == 0:

            @pl.when(z < 3)
            def _():
                go(push(slot, slot, (z_s.at[m, 0], z_r.at[m, z]), (d, z + 1)))

            @pl.when(z > 0)
            def _():
                go(push(slot, slot, (z_s.at[m, 1], z_r.at[m, z]), (d, z - 1)))

        else:
            beyond = 3 - z if j == 1 else 3 * (z - 1)

            @pl.when(inner)
            def _():
                go(push(slot, slot, (z_s.at[m, 1 + j], z_r.at[m, source(j)]), (d, beyond)))

    locals_ = []
    for i, (a, b) in enumerate(((tok, xs), (cot, cot_all))):
        copy = pltpu.make_async_copy(a.at[z], b.at[z], loc.at[i])
        copy.start()
        locals_.append(copy)

    def rows_push(i, a, b):
        for k in range(1, 4):
            to = source(k)
            start(push(a.at[to], b.at[z], (t_s.at[i, k - 1], t_r.at[i, z]), (d, to)))

    def rows_wait(i, b):
        locals_[i].wait()
        for k in range(1, 4):
            s = source(k)
            push(b.at[s], b.at[s], (t_s.at[i, k - 1], t_r.at[i, s]), core).wait_recv()

    def sem(i, stage):
        return (p_s.at[stage, i], p_r.at[stage, i])

    def one(i):
        m, k = order[i]
        h = sizes[m] // 2
        s = source(k)
        if k > 0:
            slot = full[m].at[s, :, :, c] if m == 1 else full[m].at[s, y, x, c]
            push(slot, slot, (z_s.at[m, 1 + k], z_r.at[m, s]), core).wait_recv()
            along(m, k, lambda copy: copy.start())
            if m == 1:
                start(push(slot, slot, sem(i, 4), core))
                return
        a = full[m].at[s, y, x, c, pl.ds(0, h)]
        b = full[m].at[s, y, x, c, pl.ds(h, h)]
        start(push(a, a, sem(i, 0), xn))
        start(push(b, b, sem(i, 1), yn))

    def two(i):
        m, k = order[i]
        h = sizes[m] // 2
        s = source(k)
        a = full[m].at[s, y, 1 - x, c, pl.ds(0, h)]
        push(a, a, sem(i, 0), xn).wait_recv()
        a = full[m].at[s, y, :, c, pl.ds(0, h)]
        start(push(a, a, sem(i, 2), yn))
        b = full[m].at[s, 1 - y, x, c, pl.ds(h, h)]
        push(b, b, sem(i, 1), yn).wait_recv()
        b = full[m].at[s, :, x, c, pl.ds(h, h)]
        start(push(b, b, sem(i, 3), xn))

    def three(i):
        m, k = order[i]
        h = sizes[m] // 2
        s = source(k)
        a = full[m].at[s, 1 - y, :, c, pl.ds(0, h)]
        push(a, a, sem(i, 2), yn).wait_recv()
        b = full[m].at[s, :, 1 - x, c, pl.ds(h, h)]
        push(b, b, sem(i, 3), xn).wait_recv()
        e = full[m].at[s, :, :, c]
        start(push(e, e, sem(i, 4), core))
        if m == 1:
            along(1, 0, lambda copy: copy.start())

    ndims = (((1,), (1,)), ((), ()))
    kept = []

    def load(m, k):
        i = order.index((m, k))
        e = full[m].at[source(k), :, :, 1 - c]
        push(e, e, sem(i, 4), core).wait_recv()
        copy = pltpu.make_async_copy(full[m].at[source(k)], o_full[m].at[source(k)], w_l.at[i])
        copy.start()
        kept.append(copy)

    def save(src, dst, i):
        copy = pltpu.make_async_copy(src, dst, out_l.at[i])
        copy.start()
        written.append(copy)

    chunk = seq // 4

    def norm_rows(index, v_of, dst):
        gain, shift = norm_gain[pl.ds(index, 1)], model_bias[pl.ds(index, 1)]

        def body(i, carry):
            at = pl.ds(pl.multiple_of(i * chunk, chunk), chunk)
            v = v_of(at, i)
            center = v - jnp.mean(v, axis=-1, keepdims=True)
            r = lax.rsqrt(jnp.mean(center * center, axis=-1, keepdims=True) + norm_eps)
            dst[at] = (center * r * gain + shift).astype(BF)
            return carry

        lax.fori_loop(0, seq // chunk, body, 0)

    def first_norm():
        rows_wait(0, xs)
        for h in range(width // HEAD_DIM):
            at, to = h * HEAD_DIM, 3 * h * HEAD_DIM
            mixed_bias[:, to : to + HEAD_DIM] = head_bias[0:1, at : at + HEAD_DIM]
            mixed_bias[:, to + HEAD_DIM : to + 2 * HEAD_DIM] = jnp.zeros((1, HEAD_DIM), F32)
            mixed_bias[:, to + 2 * HEAD_DIM : to + 3 * HEAD_DIM] = head_bias[1:2, at : at + HEAD_DIM]
        norm_rows(0, lambda at, i: xs[i].astype(F32), first)
        save(xs, o_x, 1)
        save(first, o_first, 0)

    def project(k):
        s = source(k)
        rows = 4 * sizes[0]

        def body(j, carry):
            at = pl.ds(pl.multiple_of(s * 2 * rows + j * rows, rows), rows)
            right = full[0][s, j].reshape(rows, width)
            g = lax.dot_general(first[...], right, ndims, preferred_element_type=F32)
            mixed[:, at] = (g + mixed_bias[:, at]).astype(BF)
            return carry

        lax.fori_loop(0, 2, body, 0)

    scale = HEAD_DIM ** (-0.5)

    def heads(k):
        s0 = source(k)
        mask = live_keys(keep, z)

        def body(j, carry):
            p = s0 * 2 + j
            at = pl.ds(pl.multiple_of(p * 6 * HEAD_DIM, 6 * HEAD_DIM), 6 * HEAD_DIM)
            both = mixed[:, at]
            parts = []
            for e in range(2):
                q, kk, v = (both[:, (3 * e + b) * HEAD_DIM : (3 * e + b + 1) * HEAD_DIM] for b in range(3))
                s = lax.dot_general(q, kk, ndims, preferred_element_type=F32) * scale
                s = jnp.where(mask, s, masked_score)
                s = jnp.exp(s - jnp.max(s, axis=-1, keepdims=True))
                pr = (s / jnp.sum(s, axis=-1, keepdims=True)).astype(BF)
                parts.append(jnp.dot(pr, v, preferred_element_type=F32).astype(BF))
            to = pl.ds(pl.multiple_of(p * 2 * HEAD_DIM, 2 * HEAD_DIM), 2 * HEAD_DIM)
            attended[:, to] = jnp.concatenate(parts, axis=1)
            return carry

        lax.fori_loop(0, 2, body, 0)

    def outlet_part(k):
        s = source(k)
        rows = 8 * sizes[1]
        at = pl.ds(pl.multiple_of(s * rows, rows), rows)
        right = full[1][s].reshape(rows, width)
        g = jnp.dot(attended[:, at], right, preferred_element_type=F32)
        if k == 0:
            acc[...] = g
        else:
            acc[...] += g

    def second_norm():
        bias = model_bias[pl.ds(2, 1)]

        def body(i, carry):
            at = pl.ds(pl.multiple_of(i * chunk, chunk), chunk)
            middle[at] = xs[i].astype(F32) + acc[at] + bias
            return carry

        lax.fori_loop(0, seq // chunk, body, 0)
        norm_rows(1, lambda at, i: middle[at], second)
        save(mixed, o_mixed, 4)
        save(attended, o_attended, 5)
        save(middle, o_middle, 6)
        save(second, o_second, 7)

    def slope_copy(k):
        s = source(k)
        hidden = 8 * sizes[2]
        at = pl.ds(pl.multiple_of(s * hidden, hidden), hidden)
        return pltpu.make_async_copy(slope.at[k % 2], o_slope.at[:, at], s_l.at[k % 2])

    def expand_part(k):
        s = source(k)
        if k >= 2:
            slope_copy(k - 2).wait()
        rows = 2 * sizes[2]

        def body(j, carry):
            at = pl.ds(pl.multiple_of(s * 4 * rows + j * rows, rows), rows)
            right = full[2][s, j // 2, j % 2].reshape(rows, width)
            hidden = lax.dot_general(second[...], right, ndims, preferred_element_type=F32)
            hidden = hidden + expand_bias[:, at]
            bell = 0.5 * (1.0 + lax.erf(hidden * (0.5**0.5)))
            active[:, at] = (hidden * bell).astype(BF)
            slope[k % 2, :, pl.ds(pl.multiple_of(j * rows, rows), rows)] = (
                bell + hidden * jnp.exp(-0.5 * hidden * hidden) * (0.5 / jnp.pi) ** 0.5
            )
            return carry

        lax.fori_loop(0, 4, body, 0)
        slope_copy(k).start()
        if k == 3:
            save(active, o_active, 8)

    def shrink_part(k):
        s = source(k)
        hidden = 8 * sizes[3]

        def body(j, carry):
            cols = pl.ds(pl.multiple_of(j * 256, 256), 256)
            left = active[:, pl.ds(pl.multiple_of(s * hidden, hidden), hidden)]
            right = full[3][s, :, :, :, :, cols].reshape(hidden, 256)
            g = jnp.dot(left, right, preferred_element_type=F32)
            if k == 0:
                acc[:, cols] = g
            else:
                acc[:, cols] += g
            return carry

        lax.fori_loop(0, width // 256, body, 0)

    def last():
        bias = model_bias[pl.ds(3, 1)]

        def body(i, carry):
            at = pl.ds(pl.multiple_of(i * chunk, chunk), chunk)
            output[at] = (middle[at] + acc[at] + bias).astype(BF)
            return carry

        lax.fori_loop(0, seq // chunk, body, 0)

    blocks = [("n1", 4.0, None)]
    work = [first_norm]
    needs = [None]

    def block(us, piece, fn):
        blocks.append((len(blocks), us, order.index(piece) if piece else None))
        needs.append(piece)
        work.append(fn)

    for k in range(4):
        block(1.6, (0, k), functools.partial(project, k))
        block(5.0, None, functools.partial(heads, k))
    for k in range(4):
        block(0.8, (1, k), functools.partial(outlet_part, k))
    block(2.5, None, second_norm)
    for k in range(4):
        block(4.5, (2, k), functools.partial(expand_part, k))
    for k in range(4):
        block(1.5, (3, k), functools.partial(shrink_part, k))
    block(1.0, None, last)

    go = lambda copy: copy.start()
    along(0, 0, go)
    rows_push(0, tok, xs)
    ones = 0
    along(2, 0, go)
    for kind, i in plan_forward(blocks, order, sizes, width, len(order)):
        if kind == "one":
            one(i)
            ones += 1
            if ones == 5:
                along(3, 0, go)
            if ones == len(order):
                rows_push(1, cot, cot_all)
        elif kind == "two":
            two(i)
        elif kind == "three":
            three(i)
        elif kind == "load":
            load(*needs[i])
        else:
            work[i]()
    rows_wait(1, cot_all)
    for k in (2, 3):
        slope_copy(k).wait()
    for copy in written + kept:
        copy.wait()
    for copy in held:
        copy.wait_send()
    for m in range(n):
        for j in range(4):
            along(m, j, lambda copy: copy.wait_send())


def forward_all(weights, tok, cot, norm_gain, model_bias, head_bias, expand_bias, keep):
    sizes = tuple(v.shape[0] for v in weights)
    width = weights[0].shape[1]
    seq = tok.shape[0] * tok.shape[1]
    hidden = expand_bias.shape[1]
    order = [(m, 0) for m in range(4)] + [(m, k) for m in range(4) for k in (1, 2, 3)]
    count = len(order)
    anyspace = pl.BlockSpec(memory_space=pl.ANY)
    vmem = pl.BlockSpec(memory_space=pltpu.VMEM)
    dma = pltpu.SemaphoreType.DMA
    shape = jax.ShapeDtypeStruct
    return pl.pallas_call(
        functools.partial(forward_kernel, sizes, order),
        out_shape=[shape((4, 2, 2, 2, s, width), BF) for s in sizes]
        + [
            shape(tok.shape, BF),
            shape(cot.shape, BF),
            shape((seq, width), BF),
            shape((seq, hidden), BF),
            shape((seq, hidden), F32),
            shape((seq, width), F32),
            shape((seq, 3 * width), BF),
            shape((seq, width), BF),
            shape((seq, width), BF),
            shape((seq, width), BF),
        ],
        in_specs=[vmem] * len(sizes) + [anyspace] * 2 + [vmem] * 5,
        out_specs=[anyspace] * (len(sizes) + 2) + [vmem] + [anyspace] * 7,
        scratch_shapes=[pltpu.VMEM((4, 2, 2, 2, s, width), BF) for s in sizes]
        + [
            pltpu.VMEM(tok.shape, BF),
            pltpu.VMEM((seq, width), BF),
            pltpu.VMEM((seq, 3 * width), BF),
            pltpu.VMEM((seq, width), BF),
            pltpu.VMEM((seq, width), F32),
            pltpu.VMEM((seq, width), F32),
            pltpu.VMEM((seq, width), BF),
            pltpu.VMEM((seq, hidden), BF),
            pltpu.VMEM((2, seq, 8 * sizes[2]), F32),
            pltpu.VMEM((1, 3 * width), F32),
            dma((4, 5)),
            dma((4, 4)),
            dma((2,)),
            dma((2, 3)),
            dma((2, 4)),
            dma((5, count)),
            dma((5, count)),
            dma((count,)),
            dma((9,)),
            dma((2,)),
        ],
        compiler_params=pltpu.CompilerParams(collective_id=1, has_side_effects=True, vmem_limit_bytes=VMEM_LIMIT),
    )(*weights, tok, cot, norm_gain, model_bias, head_bias, expand_bias, keep)


def add_rows(dst, src, lead, rows):
    step = 16

    def body(i, carry):
        j, r = i // (rows // step), (i % (rows // step)) * step
        at = pl.ds(pl.multiple_of(r, step), step)
        dst[j, at] = dst[j, at] + src[j, at]
        return carry

    lax.fori_loop(0, lead * (rows // step), body, 0)


PLANES = (1, 2, 0, 3)


def plan(blocks, sizes, order, free_after, width):
    todo = list(blocks)
    done = []
    events = []
    link = {"x": 0.0, "y": 0.0, "z": 0.0}
    now = 0.0
    finished = set()

    def carry(lane, start, rows):
        begin = max(start, link[lane])
        link[lane] = begin + rows * width * 2 * 2 / OPT["brate"]
        return link[lane] + OPT["blat"]

    def emit(step):
        nonlocal now
        kind, i = step[0], step[1]
        done.append(step)
        finished.add(step)
        s = sizes[order[i][0]]
        if kind == "one":
            now += s / 128 * 1.0
            ready = max(carry("y", now, s), carry("x", now, s))
            events.append((ready, ("two", i)))
        elif kind == "two":
            now += s / 128 * 0.6
            ready = max(carry("x", now, s / 2), carry("y", now, s / 2))
            events.append((ready, ("three", i)))
        elif kind == "three":
            now += s / 128 * 0.3
            ready = carry("z", now, s)
            events.append((ready + OPT["bz"], ("four", i)))
            events.append((ready + OPT["bz"] + 0.001, ("fourb", i)))
        elif kind == "four":
            finished.discard(step)
            now += 0.2
        elif kind == "fourb":
            now += 0.2

    def open_now():
        ones = sum(1 for v in finished if v[0] == "one")
        twos = sum(1 for v in finished if v[0] == "two")
        for v in events:
            if v[1][0] != "one" or ones - twos < OPT["bwin"]:
                return v
        return events[0]

    while todo or events:
        events.sort()
        if events and open_now()[0] <= now:
            event = open_now()
            events.remove(event)
            step = event[1]
            if step[0] == "fourb":
                events.append((now + OPT["bhop"], ("fourc", step[1])))
                continue
            emit(step)
            continue
        if todo:
            name, us, piece = todo[0]
            blocked = piece is not None and piece >= free_after and ("one", piece - free_after) not in finished
            if not blocked:
                todo.pop(0)
                done.append(("block", name))
                now += us * OPT["bwork"]
                if piece is not None:
                    done.append(("push", piece))
                    events.append((now + OPT["bone"], ("one", piece)))
                continue
        now = max(now, open_now()[0])
    return done


def backward_kernel(sizes, order, *refs):
    n = 4
    small_count = 16
    shrink, expand, outlet, intake, active, slope = refs[:6]
    inputs = refs[6:13]
    norm_gain, keep = refs[13:15]
    mom_f = refs[15:19]
    total, small_out, mom_all, token_grad = refs[19:23]
    refs = refs[23:]
    own, mid, end, far = (refs[i * n : i * n + n] for i in range(4))
    refs = refs[4 * n :]
    (made, act, slo, wbuf, obuf, hgrad, wide, mgrad, branch, agrad) = refs[:10]
    small, s_got, s_acc, s_z = refs[10:14]
    loc, c_s, c_r, p_s, p_r, f_s, f_r, q_s, q_r, m_s, m_r, w_l = refs[14:26]
    mom = refs[26:30]
    middle, mixed, attended, second, first, x_in, cot, in_l = refs[30:]
    held_in = (middle, mixed, attended, second, first, x_in, cot)
    d, z, y, x, c = place()
    unit = wbuf.shape[1]
    count_units = shrink.shape[0] // unit

    def load(u):
        at = pl.ds(u * unit, unit)
        return [
            pltpu.make_async_copy(shrink.at[at], wbuf.at[u % 2], w_l.at[0, u % 2]),
            pltpu.make_async_copy(expand.at[at], wbuf.at[2 + u % 2], w_l.at[1, u % 2]),
            pltpu.make_async_copy(slope.at[:, at], slo.at[u % 2], w_l.at[3, u % 2]),
        ]

    def load_active(u):
        return pltpu.make_async_copy(active.at[:, pl.ds(u * unit, unit)], act.at[u % 2], w_l.at[2, u % 2])


    fetches = [
        pltpu.make_async_copy(src, dst, in_l.at[i]) for i, (src, dst) in enumerate(zip(inputs, held_in))
    ]
    fetches[6].start()
    for u in (0, 1):
        load_active(u).start()
    for copy in load(0) + load(1):
        copy.start()
    for i in (3, 0, 2, 1, 4, 5):
        fetches[i].start()
    for m in range(n):
        mom[m][...] = mom_f[m][...].astype(BF)
    core, xn, yn, zn = partners(d, z, y, x, c)
    greet([core, xn, yn] + zn)
    seq, width = cot.shape
    held = []
    top = max(sizes)

    def start(copy):
        copy.start()
        held.append(copy)

    def sem(i, stage):
        return (p_s.at[stage, i], p_r.at[stage, i])

    slots = made.shape[0]

    def core_push(i):
        m, k = order[i]
        return push(
            made.at[i % slots, :, :, 1 - c, pl.ds(0, sizes[m])], own[m].at[k], (c_s.at[i], c_r.at[i]), core
        )

    def one(i):
        m, k = order[i]
        s, h = sizes[m], sizes[m] // 2
        core_push(i).wait_recv()
        for j in range(2):
            for l in range(2):
                add_rows(own[m].at[k, j, pl.ds(l, 1)], made.at[i % slots, j, l, pl.ds(c, 1)], 1, s)
        start(push(own[m].at[k, 1 - y, :, pl.ds(0, h)], mid[m].at[k, 0], sem(i, 0), yn))
        start(push(own[m].at[k, :, 1 - x, pl.ds(h, h)], mid[m].at[k, 1], sem(i, 1), xn))

    def two(i):
        m, k = order[i]
        h = sizes[m] // 2
        push(mid[m].at[k, 0], mid[m].at[k, 0], sem(i, 0), yn).wait_recv()
        add_rows(own[m].at[k, y, :, pl.ds(0, h)], mid[m].at[k, 0], 2, h)
        start(push(own[m].at[k, y, 1 - x, pl.ds(0, h)], end[m].at[k, pl.ds(0, h)], sem(i, 2), xn))
        push(mid[m].at[k, 1], mid[m].at[k, 1], sem(i, 1), xn).wait_recv()
        add_rows(own[m].at[k, :, x, pl.ds(h, h)], mid[m].at[k, 1], 2, h)
        start(push(own[m].at[k, 1 - y, x, pl.ds(h, h)], end[m].at[k, pl.ds(h, h)], sem(i, 3), yn))

    def hop(i, p, go):
        m, k = order[i]
        side, to = (0, p + 1) if p < PLANES[m] else (1, p - 1)
        at = side if PLANES[m] in (1, 2) else 0
        go(push(own[m].at[k, y, x], far[m].at[at, k], (f_s.at[m, k], f_r.at[m, k, side]), (d, to)))

    def came(m, k, side):
        slot = far[m].at[side if PLANES[m] in (1, 2) else 0, k]
        push(slot, slot, (f_s.at[m, k], f_r.at[m, k, side]), core).wait_recv()

    def three(i):
        m, k = order[i]
        s, h = sizes[m], sizes[m] // 2
        push(end[m].at[k, pl.ds(0, h)], end[m].at[k, pl.ds(0, h)], sem(i, 2), xn).wait_recv()
        push(end[m].at[k, pl.ds(h, h)], end[m].at[k, pl.ds(h, h)], sem(i, 3), yn).wait_recv()
        add_rows(own[m].at[k, pl.ds(y, 1), x], end[m].at[pl.ds(k, 1)], 1, s)
        for p in (0, 3):
            if p != PLANES[m]:

                @pl.when(z == p)
                def _(p=p):
                    hop(i, p, lambda copy: copy.start())

    def four(i, far_hop):
        m, k = order[i]
        for p in (1, 2):
            below = p < PLANES[m]
            if p == PLANES[m] or far_hop != (p if below else 3 - p):
                continue

            @pl.when(z == p)
            def _(p=p, below=below):
                side = 0 if below else 1
                came(m, k, side)
                at = side if PLANES[m] in (1, 2) else 0
                add_rows(own[m].at[k, pl.ds(y, 1), x], far[m].at[at, pl.ds(k, 1)], 1, sizes[m])
                hop(i, p, lambda copy: copy.start())

    def five(i):
        m, k = order[i]
        s, p = sizes[m], PLANES[m]
        sides = [v for v in (0, 1) if p != 3 * v]

        @pl.when(z == p)
        def _():
            for side in sides:
                came(m, k, side)

            def body(r, carry):
                at = pl.ds(pl.multiple_of(r * 16, 16), 16)
                acc = own[m][k, y, x, at].astype(F32)
                for side in range(len(sides)):
                    acc = acc + far[m][side, k, at].astype(F32)
                total[k, at] = acc
                return carry

            lax.fori_loop(0, s // 16, body, 0)
            if s < total.shape[1]:
                total[k, pl.ds(s, total.shape[1] - s)] = jnp.zeros((total.shape[1] - s, width), F32)

    def small_step(stage):
        to = (core, xn, yn)
        if stage > 0:
            here = s_got.at[stage - 1]
            push(here, here, (q_s.at[stage - 1], q_r.at[stage - 1]), to[stage - 1]).wait_recv()
            s_acc[stage] = s_acc[stage - 1] + s_got[stage - 1]
        else:
            s_acc[0] = small[...]
        if stage < 3:
            start(push(s_acc.at[stage], s_got.at[stage], (q_s.at[stage], q_r.at[stage]), to[stage]))
        else:
            s_z[z] = s_acc[3]
            for k in range(1, 4):
                start(push(s_acc.at[3], s_z.at[z], (q_s.at[2 + k], q_r.at[2 + k]), zn[k - 1]))

    def moments(first):
        for t in range(n):
            p = PLANES[t]
            here = mom_all.at[z, pl.ds(0, sizes[t])]

            @pl.when(z == p)
            def _(t=t, p=p, here=here):
                copy = pltpu.make_async_copy(mom[t], here, loc.at[0])
                if first:
                    copy.start()
                else:
                    copy.wait()
                    for k in range(1, 4):
                        s = (p + k) % 4
                        there = mom_all.at[s, pl.ds(0, sizes[t])]
                        push(mom[t], there, (m_s.at[t], m_r.at[s]), (d, s)).wait_recv()

            @pl.when(z != p)
            def _(t=t, p=p, here=here):
                copy = push(mom[t], here, (m_s.at[t], m_r.at[z]), (d, p))
                if first:
                    copy.start()
                else:
                    copy.wait_send()

    def load_outlet():
        return pltpu.make_async_copy(outlet, obuf, loc.at[1])

    def load_intake(v):
        return pltpu.make_async_copy(intake.at[pl.ds(v * unit, unit)], wbuf.at[v % 4], w_l.at[4, v % 4])

    tdims = (((0,), (0,)), ((), ()))
    ndims = (((1,), (1,)), ((), ()))

    def shrink_rows(k):
        if k == 0:
            fetches[6].wait()
        i = 2 * k
        for half in (0, 1):
            u = 2 * k + half
            load_active(u).wait()

            def body(j, carry, half=half, u=u):
                cols = pl.ds(pl.multiple_of(j * 2 * top, 2 * top), 2 * top)
                g = lax.dot_general(act[u % 2, :, cols], cot[...], tdims, preferred_element_type=F32)
                made[i % slots, half, j] = g.astype(BF).reshape(2, top, width)
                return carry

            lax.fori_loop(0, unit // (2 * top), body, 0)
            if u + 2 < count_units:
                load_active(u + 2).start()

    def mlp_back(u):
        k, half = u // 2, u % 2
        for copy in load(u):
            copy.wait()

        def grad(j, carry):
            rows = pl.ds(pl.multiple_of(j * 256, 256), 256)
            to = pl.ds(pl.multiple_of(j * 256 + half * unit, 256), 256)
            g = lax.dot_general(cot[...], wbuf[u % 2, rows], ndims, preferred_element_type=F32)
            hg = (g * slo[u % 2, :, rows]).astype(BF)
            hgrad[:, to] = hg
            small[pl.ds(2 + k, 1), to] = jnp.sum(hg.astype(F32), axis=0, keepdims=True)
            return carry

        lax.fori_loop(0, unit // 256, grad, 0)

        def back(j, carry):
            cols = pl.ds(pl.multiple_of(j * 256, 256), 256)
            g = jnp.dot(hgrad[:, pl.ds(half * unit, unit)], wbuf[2 + u % 2, :, cols], preferred_element_type=F32)
            if u == 0:
                wide[:, cols] = g
            else:
                wide[:, cols] += g
            return carry

        lax.fori_loop(0, width // 256, back, 0)
        if u + 2 < count_units:
            for copy in load(u + 2):
                copy.start()

    def mlp_two(k):
        i = 2 * k + 1
        if k == 0:
            fetches[3].wait()

        def body(j, carry):
            cols = pl.ds(pl.multiple_of(j * 2 * top, 2 * top), 2 * top)
            g = lax.dot_general(hgrad[:, cols], second[...], tdims, preferred_element_type=F32)
            made[i % slots, j // 2, j % 2] = g.astype(BF).reshape(2, top, width)
            return carry

        lax.fori_loop(0, 4, body, 0)

    chunk = 64

    def norm_block(index, v_of, extra):
        gain = norm_gain[pl.ds(index, 1)]

        def body(i, carry):
            at = pl.ds(pl.multiple_of(i * chunk, chunk), chunk)
            v = v_of(at)
            center = v - jnp.mean(v, axis=-1, keepdims=True)
            r = lax.rsqrt(jnp.mean(center * center, axis=-1, keepdims=True) + norm_eps)
            nrm = center * r
            w = wide[at]
            u = w * gain
            down = r * (u - jnp.mean(u, axis=-1, keepdims=True) - nrm * jnp.mean(u * nrm, axis=-1, keepdims=True))
            sums = extra(at, down)
            new = [jnp.sum(w * nrm, axis=0, keepdims=True), jnp.sum(w, axis=0, keepdims=True)] + sums
            return tuple(a + b for a, b in zip(carry, new))

        zero = jnp.zeros((1, width), F32)
        out = lax.fori_loop(0, seq // chunk, body, (zero,) * (4 if index else 2))
        small[pl.ds(6 + index, 1)] = out[0]
        small[pl.ds(8 + index, 1)] = out[1]
        if index:
            small[pl.ds(10, 1)] = out[2]
            small[pl.ds(11, 1)] = out[3]

    def second_norm_back():
        fetches[0].wait()
        load_outlet().start()
        for v in range(4):
            load_intake(v).start()

        def extra(at, down):
            g = cot[at].astype(F32)
            m = g + down
            mgrad[at] = m
            low = m.astype(BF)
            branch[at] = low
            return [jnp.sum(low.astype(F32), axis=0, keepdims=True), jnp.sum(g, axis=0, keepdims=True)]

        norm_block(1, lambda at: middle[at], extra)

    def outlet_piece(k):
        i = 12 + k
        if k == 0:
            fetches[2].wait()
        cols = pl.ds(k * 8 * sizes[1], 8 * sizes[1])
        g = lax.dot_general(attended[:, cols], branch[...], tdims, preferred_element_type=F32)
        made[i % slots, :, :, :, pl.ds(0, sizes[1])] = g.astype(BF).reshape(2, 2, 2, sizes[1], width)

    def attended_back():
        load_outlet().wait()

        def body(j, carry):
            rows = pl.ds(pl.multiple_of(j * 256, 256), 256)
            g = lax.dot_general(branch[...], obuf[rows], ndims, preferred_element_type=F32)
            agrad[:, rows] = g.astype(BF)
            return carry

        lax.fori_loop(0, width // 256, body, 0)

    scale = HEAD_DIM ** (-0.5)

    def heads(first_pair, pairs):
        if first_pair == 0:
            fetches[1].wait()
        mask = live_keys(keep, z)

        def body(p, carry):
            at = pl.ds(pl.multiple_of(p * 6 * HEAD_DIM, 6 * HEAD_DIM), 6 * HEAD_DIM)
            both = mixed[:, at]
            ag_both = agrad[:, pl.ds(pl.multiple_of(p * 2 * HEAD_DIM, 2 * HEAD_DIM), 2 * HEAD_DIM)]
            parts, sums = [], []
            for e in range(2):
                q, k, v = (both[:, (3 * e + b) * HEAD_DIM : (3 * e + b + 1) * HEAD_DIM] for b in range(3))
                ag = ag_both[:, e * HEAD_DIM : (e + 1) * HEAD_DIM]
                s = lax.dot_general(q, k, ndims, preferred_element_type=F32) * scale
                s = jnp.where(mask, s, masked_score)
                s = jnp.exp(s - jnp.max(s, axis=-1, keepdims=True))
                pr = s / jnp.sum(s, axis=-1, keepdims=True)
                vg = lax.dot_general(pr.astype(BF), ag, tdims, preferred_element_type=F32)
                dp = lax.dot_general(ag, v, ndims, preferred_element_type=F32)
                ds = (pr * (dp - jnp.sum(dp * pr, axis=-1, keepdims=True))).astype(BF)
                qg = jnp.dot(ds, k, preferred_element_type=F32) * scale
                kg = lax.dot_general(ds, q, tdims, preferred_element_type=F32) * scale
                parts += [qg.astype(BF), kg.astype(BF), vg.astype(BF)]
                sums.append((jnp.sum(parts[-3].astype(F32), 0, keepdims=True), jnp.sum(parts[-1].astype(F32), 0, keepdims=True)))
            mixed[:, at] = jnp.concatenate(parts, axis=1)
            to = pl.ds(pl.multiple_of(p * 2 * HEAD_DIM, 2 * HEAD_DIM), 2 * HEAD_DIM)
            small[pl.ds(0, 1), to] = jnp.concatenate([sums[0][0], sums[1][0]], axis=1)
            small[pl.ds(1, 1), to] = jnp.concatenate([sums[0][1], sums[1][1]], axis=1)
            return carry

        lax.fori_loop(first_pair, first_pair + pairs, body, 0)

    def intake_piece(k):
        i = 8 + k
        if k == 0:
            fetches[4].wait()
        rows = 4 * sizes[0]

        def body(j, carry):
            cols = pl.ds(pl.multiple_of((2 * k + j) * rows, rows), rows)
            g = lax.dot_general(mixed[:, cols], first[...], tdims, preferred_element_type=F32)
            made[i % slots, j, :, :, pl.ds(0, sizes[0])] = g.astype(BF).reshape(2, 2, sizes[0], width)
            return carry

        lax.fori_loop(0, 2, body, 0)

    def first_back(v):
        load_intake(v).wait()

        def body(j, carry):
            cols = pl.ds(pl.multiple_of(j * 256, 256), 256)
            g = jnp.dot(mixed[:, pl.ds(v * unit, unit)], wbuf[v % 4, :, cols], preferred_element_type=F32)
            if v == 0:
                wide[:, cols] = g
            else:
                wide[:, cols] += g
            return carry

        lax.fori_loop(0, width // 256, body, 0)
        if v + 4 < intake.shape[0] // unit:
            load_intake(v + 4).start()

    def first_norm_back():
        fetches[5].wait()

        def extra(at, down):
            token_grad[at] = (mgrad[at] + down).astype(BF)
            return []

        norm_block(0, lambda at: x_in[at].astype(F32), extra)

    work = {}
    blocks = []

    def block(name, us, piece, fn):
        work[name] = fn
        blocks.append((name, us, piece))

    for k in range(4):
        block(("a", k), 2.0, 2 * k, functools.partial(shrink_rows, k))
        block(("m", 2 * k), 2.0, None, functools.partial(mlp_back, 2 * k))
        block(("m", 2 * k + 1), 2.0, None, functools.partial(mlp_back, 2 * k + 1))
        block(("e", k), 1.5, 2 * k + 1, functools.partial(mlp_two, k))
    block("n2", 3.0, None, second_norm_back)
    block("ab", 1.5, None, attended_back)
    for k in range(4):
        block(("h", k), 7.0, None, functools.partial(heads, 2 * k, 2))
        block(("i", k), 1.2, 8 + k, functools.partial(intake_piece, k))
    for k in range(4):
        block(("o", k), 0.5, 12 + k, functools.partial(outlet_piece, k))
    for v in range(intake.shape[0] // unit):
        block(("f", v), 0.8, None, functools.partial(first_back, v))
    block("n1", 3.0, None, first_norm_back)
    for stage in range(4):
        block(("s", stage), 2.0, None, functools.partial(small_step, stage))

    small[pl.ds(12, 4)] = jnp.zeros((4, width), F32)
    steps = plan(blocks, sizes, order, slots, width)
    pushed = {}
    stage = 1
    for step in steps:
        kind = step[0]
        if kind == "block":
            name = step[1]
            piece = {b[0]: b[2] for b in blocks}[name]
            if piece is not None and piece - slots in pushed:
                pushed.pop(piece - slots).wait_send()
            work[name]()
            if name == ("m", 1):
                moments(True)
        elif kind == "push":
            pushed[step[1]] = core_push(step[1])
            pushed[step[1]].start()
        elif kind == "one":
            one(step[1])
        elif kind == "two":
            two(step[1])
        elif kind == "three":
            three(step[1])
        elif kind == "four":
            four(step[1], 1)
        elif kind == "fourc":
            four(step[1], 2)
    for i in range(len(order)):
        five(i)
    for k in range(1, 4):
        slot = s_z.at[(z + 4 - k) % 4]
        push(slot, slot, (q_s.at[2 + k], q_r.at[2 + k]), zn[k - 1]).wait_recv()
    small_out[...] = s_z[0] + s_z[1] + s_z[2] + s_z[3]
    moments(False)
    for copy in pushed.values():
        copy.wait_send()
    for copy in held:
        copy.wait_send()
    for i in range(len(order)):
        for p in range(4):
            if p != PLANES[order[i][0]]:

                @pl.when(z == p)
                def _(i=i, p=p):
                    hop(i, p, lambda copy: copy.wait_send())


def backward_all(weights, saved, norm_gain, keep, moms, sizes):
    intake, outlet, expand, shrink = weights
    active, slope, middle, mixed, attended, second, first, x, cot = saved
    seq, width = cot.shape
    top = max(sizes)
    order = []
    for k in range(4):
        order += [(3, k), (2, k)]
    order += [(0, k) for k in range(4)] + [(1, k) for k in range(4)]
    count = len(order)
    anyspace = pl.BlockSpec(memory_space=pl.ANY)
    vmem = pl.BlockSpec(memory_space=pltpu.VMEM)
    dma = pltpu.SemaphoreType.DMA
    unit = 512
    return pl.pallas_call(
        functools.partial(backward_kernel, sizes, order),
        out_shape=[
            jax.ShapeDtypeStruct((4, top, width), F32),
            jax.ShapeDtypeStruct((16, width), F32),
            jax.ShapeDtypeStruct((4, top, width), BF),
            jax.ShapeDtypeStruct((seq, width), BF),
        ],
        in_specs=[anyspace] * 13 + [vmem] * 6,
        out_specs=[vmem, vmem, anyspace, vmem],
        scratch_shapes=[pltpu.VMEM((4, 2, 2, s, width), BF) for s in sizes]
        + [pltpu.VMEM((4, 2, 2, s // 2, width), BF) for s in sizes]
        + [pltpu.VMEM((4, s, width), BF) for s in sizes]
        + [pltpu.VMEM((2 if p in (1, 2) else 1, 4, s, width), BF) for s, p in zip(sizes, PLANES)]
        + [
            pltpu.VMEM((3, 2, 2, 2, top, width), BF),
            pltpu.VMEM((2, seq, unit), BF),
            pltpu.VMEM((2, seq, unit), F32),
            pltpu.VMEM((4, unit, width), BF),
            pltpu.VMEM((width, width), BF),
            pltpu.VMEM((seq, width), BF),
            pltpu.VMEM((seq, width), F32),
            pltpu.VMEM((seq, width), F32),
            pltpu.VMEM((seq, width), BF),
            pltpu.VMEM((seq, width), BF),
            pltpu.VMEM((16, width), F32),
            pltpu.VMEM((3, 16, width), F32),
            pltpu.VMEM((4, 16, width), F32),
            pltpu.VMEM((4, 16, width), F32),
            dma((2,)),
            dma((count,)),
            dma((count,)),
            dma((4, count)),
            dma((4, count)),
            dma((4, 4)),
            dma((4, 4, 2)),
            dma((6,)),
            dma((6,)),
            dma((4,)),
            dma((4,)),
            dma((5, 4)),
        ]
        + [pltpu.VMEM((s, width), BF) for s in sizes]
        + [pltpu.VMEM(v.shape, v.dtype) for v in saved[2:]]
        + [dma((7,))],
        compiler_params=pltpu.CompilerParams(collective_id=2, has_side_effects=True, vmem_limit_bytes=VMEM_LIMIT),
    )(shrink, expand, outlet, intake, active, slope, middle, mixed, attended, second, first, x, cot, norm_gain, keep, *moms)


def split(v):
    hi = v.astype(BF)
    return hi, (v - hi.astype(F32)).astype(BF)


def dot(a, b):
    return jnp.dot(a, b, preferred_element_type=F32)


def muon_kernel(sizes, *refs):
    n = len(sizes)
    total, mom, outp, tokg = refs[:4]
    rows_out = refs[4 : 4 + n]
    grads = refs[4 + n : 4 + 2 * n]
    outp_all, tokg_all = refs[4 + 2 * n : 6 + 2 * n]
    refs = refs[6 + 2 * n :]
    low_g, uh, ul, pack, r_core, r_one, r_two, gathered, gf, gh, low, b, tf, xf, xh = refs[:15]
    g_s, g_r, a_s, a_r, o_s, o_r, s_s, s_r, loc = refs[15:]
    d, z, y, x, c = place()
    core, xn, yn, zn = partners(d, z, y, x, c)
    greet([core, xn, yn] + zn)
    held = []

    def start(copy):
        copy.start()
        held.append(copy)

    top, width = total.shape[1:]
    count = 4 * top
    block = width // 4
    height = 0
    for t in range(n):
        height = jnp.where(z == PLANES[t], sizes[t], height)
    per = top // 16

    def make(i, carry):
        k, r = i // per, (i % per) * 16
        at = pl.ds(pl.multiple_of(r, 16), 16)
        g = total[k, at]
        low_g[k, at] = g.astype(BF)
        u = g + muon_decay * (muon_decay * mom[k, at].astype(F32) + g)
        row = lax.broadcasted_iota(jnp.int32, u.shape, 0) + r
        u = jnp.where(row < height, u, 0.0)
        to = pl.ds(pl.multiple_of(i * 16, 16), 16)
        uh[to], ul[to] = split(u)
        return carry

    lax.fori_loop(0, 4 * per, make, 0)

    def back_home(src, dst, sems, local, first):
        for t in range(n):
            s, p = sizes[t], PLANES[t]

            @pl.when(z == p)
            def _(t=t, s=s, p=p):
                own = pltpu.make_async_copy(src.at[p, pl.ds(0, s)], dst[t], loc.at[local])
                away = [
                    push(src.at[(p + k) % 4, pl.ds(0, s)], dst[t], (sems[0].at[k], sems[1].at[t]), (d, (p + k) % 4))
                    for k in range(1, 4)
                ]
                if first:
                    for copy in away:
                        copy.start()
                    own.start()
                else:
                    own.wait()
                    for copy in away:
                        copy.wait_send()

            if not first:

                @pl.when(z != p)
                def _(t=t, p=p):
                    push(dst[t], dst[t], (sems[0].at[0], sems[1].at[t]), (d, p)).wait_recv()

    back_home(low_g, grads, (g_s, g_r), 0, True)
    for i, (a, e) in enumerate(((outp, outp_all), (tokg, tokg_all))):
        pltpu.make_async_copy(a.at[z], e.at[z], loc.at[1 + i]).start()
        for k in range(1, 4):
            start(push(a.at[(z + k) % 4], e.at[z], (o_s.at[i, k - 1], o_r.at[i, k - 1]), zn[k - 1]))

    places = {0: (0, 0), 3: (0, 4 * block), 1: (1, 0), 2: (1, 3 * block)}
    tdims = (((0,), (0,)), ((), ()))

    def product(half):
        for r, (h, col) in places.items():
            if h != half:
                continue
            mine = slice(r * block, (r + 1) * block)
            rest = slice(r * block, width)
            acc = lax.dot_general(uh[:, mine], uh[:, rest], tdims, preferred_element_type=F32)
            acc = acc + lax.dot_general(uh[:, mine], ul[:, rest], tdims, preferred_element_type=F32)
            acc = acc + lax.dot_general(ul[:, mine], uh[:, rest], tdims, preferred_element_type=F32)
            pack[half, :, col : col + width - r * block] = acc

    def sem(i):
        return (a_s.at[i], a_r.at[i])

    for v in (0, 1):

        @pl.when(c == v)
        def _(v=v):
            product(1 - v)
            push(pack.at[1 - v], r_core, sem(0), core).start()
            product(v)

    def add(dst, r0, src, rows, into=None):
        def body(i, carry):
            at = pl.ds(pl.multiple_of(r0 + i * 8, 8), 8)
            v = dst[at] + src[pl.ds(pl.multiple_of(i * 8, 8), 8)]
            (dst if into is None else into)[at] = v
            return carry

        lax.fori_loop(0, rows // 8, body, 0)

    def rows(ref, r, size):
        return ref.at[pl.ds(pl.multiple_of(r, 32), size)]

    half, quarter, eighth = block // 2, block // 4, block // 8
    push(r_core, r_core, sem(0), core).wait_recv()
    mine, whole = pack.at[c], gathered.at[c]
    add(mine, 0, r_core, block)
    base_a, base_b = 0, half
    start(push(rows(mine, base_a + (1 - y) * quarter, quarter), r_one.at[0], sem(1), yn))
    start(push(rows(mine, base_b + (1 - x) * quarter, quarter), r_one.at[1], sem(2), xn))
    push(r_one.at[0], r_one.at[0], sem(1), yn).wait_recv()
    mine_a = base_a + y * quarter
    add(mine, mine_a, r_one.at[0], quarter)
    start(push(rows(mine, mine_a + (1 - x) * eighth, eighth), r_two.at[0], sem(3), xn))
    push(r_one.at[1], r_one.at[1], sem(2), xn).wait_recv()
    mine_b = base_b + x * quarter
    add(mine, mine_b, r_one.at[1], quarter)
    start(push(rows(mine, mine_b + (1 - y) * eighth, eighth), r_two.at[1], sem(4), yn))
    push(r_two.at[0], r_two.at[0], sem(3), xn).wait_recv()
    own_a = mine_a + x * eighth
    add(mine, own_a, r_two.at[0], eighth, whole)
    start(push(rows(whole, own_a, eighth), rows(whole, own_a, eighth), sem(5), xn))
    push(r_two.at[1], r_two.at[1], sem(4), yn).wait_recv()
    own_b = mine_b + y * eighth
    add(mine, own_b, r_two.at[1], eighth, whole)
    start(push(rows(whole, own_b, eighth), rows(whole, own_b, eighth), sem(6), yn))
    got = rows(whole, mine_a + (1 - x) * eighth, eighth)
    push(got, got, sem(5), xn).wait_recv()
    start(push(rows(whole, mine_a, quarter), rows(whole, mine_a, quarter), sem(7), yn))
    got = rows(whole, mine_b + (1 - y) * eighth, eighth)
    push(got, got, sem(6), yn).wait_recv()
    start(push(rows(whole, mine_b, quarter), rows(whole, mine_b, quarter), sem(8), xn))
    start(push(rows(whole, mine_a, quarter), rows(whole, mine_a, quarter), sem(9), core))
    start(push(rows(whole, mine_b, quarter), rows(whole, mine_b, quarter), sem(10), core))
    other_a = base_a + (1 - y) * quarter
    got = rows(whole, other_a, quarter)
    push(got, got, sem(7), yn).wait_recv()
    start(push(got, got, sem(11), core))
    other_b = base_b + (1 - x) * quarter
    got = rows(whole, other_b, quarter)
    push(got, got, sem(8), xn).wait_recv()
    start(push(got, got, sem(12), core))
    beside = gathered.at[1 - c]
    for r, i in ((mine_a, 9), (mine_b, 10), (other_a, 11), (other_b, 12)):
        got = rows(beside, r, quarter)
        push(got, got, sem(i), core).wait_recv()

    eye = lax.broadcasted_iota(jnp.int32, (block, block), 0) == lax.broadcasted_iota(jnp.int32, (block, block), 1)
    trace = jnp.zeros((1, 1), F32)
    for r, (h, col) in places.items():
        v = jnp.where(eye, gathered[h, :, col : col + block], 0.0)
        trace = trace + jnp.sum(jnp.sum(v, axis=1, keepdims=True), axis=0, keepdims=True)
    inverse = 1.0 / (jnp.sqrt(trace) + frob_eps)
    squared = inverse * inverse
    for r, (h, col) in places.items():
        for k in range(r, 4):
            v = gathered[h, :, col + (k - r) * block : col + (k - r + 1) * block] * squared
            a, e = slice(r * block, (r + 1) * block), slice(k * block, (k + 1) * block)
            gf[a, e] = v
            gh[a, e] = v.astype(BF)
            if k > r:
                v = v.T
                gf[e, a] = v
                gh[e, a] = v.astype(BF)

    step = 64

    def scale_x(i, carry):
        at = pl.ds(pl.multiple_of(i * step, step), step)
        v = (uh[at].astype(F32) + ul[at].astype(F32)) * inverse
        xf[at] = v
        xh[at] = v.astype(BF)
        return carry

    lax.fori_loop(0, count // step, scale_x, 0)

    def iterate(shift, last):
        level = coef_a + coef_b * shift + coef_c * shift * shift
        slope = coef_b + 2.0 * coef_c * shift
        if last:

            def lower(i, carry):
                at = pl.ds(pl.multiple_of(i * step, step), step)
                g = gf[at]
                row = lax.broadcasted_iota(jnp.int32, g.shape, 0) + i * step
                col = lax.broadcasted_iota(jnp.int32, g.shape, 1)
                g = g - jnp.where(row == col, shift, 0.0)
                gf[at] = g
                low[at] = g.astype(BF)
                return carry

            lax.fori_loop(0, width // step, lower, 0)
            b[...] = (slope * gf[...] + coef_c * dot(low[...], low[...])).astype(BF)
            xh[...] = (level * xf[...] + dot(xh[...], b[...])).astype(BF)
            return
        b[...] = (slope * gf[...] + coef_c * dot(gh[...], gh[...])).astype(BF)
        v = level * xf[...] + dot(xh[...], b[...])
        t = level * gf[...] + dot(gh[...], b[...])
        xf[...] = v
        xh[...] = v.astype(BF)
        tf[...] = t
        low[...] = t.astype(BF)
        g = level * tf[...] + dot(b[...], low[...])
        gf[...] = g
        gh[...] = g.astype(BF)

    def middle(i, carry):
        iterate(0.0, False)
        return carry

    lax.fori_loop(0, NS_STEPS - 1, middle, 0)
    iterate(0.8, True)

    back_home(xh.reshape(4, top, width), rows_out, (s_s, s_r), 3, True)

    for v in (0, 1):

        @pl.when(c == v)
        def _(v=v):
            push(pack.at[1 - v], r_core, sem(0), core).wait_send()

    for i, (a, e) in enumerate(((outp, outp_all), (tokg, tokg_all))):
        pltpu.make_async_copy(a.at[z], e.at[z], loc.at[1 + i]).wait()
        for k in range(1, 4):
            slot = e.at[(z + 4 - k) % 4]
            push(slot, slot, (o_s.at[i, k - 1], o_r.at[i, k - 1]), zn[k - 1]).wait_recv()
    back_home(low_g, grads, (g_s, g_r), 0, False)
    for copy in held:
        copy.wait_send()
    back_home(xh.reshape(4, top, width), rows_out, (s_s, s_r), 3, False)


def muon_all(total, mom, outp, tokg, sizes):
    top, width = total.shape[1:]
    count, block = 4 * top, width // 4
    anyspace = pl.BlockSpec(memory_space=pl.ANY)
    vmem = pl.BlockSpec(memory_space=pltpu.VMEM)
    dma = pltpu.SemaphoreType.DMA
    wide = block * 5
    return pl.pallas_call(
        functools.partial(muon_kernel, sizes),
        out_shape=[jax.ShapeDtypeStruct((s, width), BF) for s in sizes] * 2
        + [jax.ShapeDtypeStruct(outp.shape, outp.dtype), jax.ShapeDtypeStruct(tokg.shape, tokg.dtype)],
        in_specs=[vmem, vmem, anyspace, anyspace],
        out_specs=[anyspace] * (2 * len(sizes) + 2),
        scratch_shapes=[
            pltpu.VMEM((4, top, width), BF),
            pltpu.VMEM((count, width), BF),
            pltpu.VMEM((count, width), BF),
            pltpu.VMEM((2, block, wide), F32),
            pltpu.VMEM((block, wide), F32),
            pltpu.VMEM((2, block // 4, wide), F32),
            pltpu.VMEM((2, block // 8, wide), F32),
            pltpu.VMEM((2, block, wide), F32),
            pltpu.VMEM((width, width), F32),
            pltpu.VMEM((width, width), BF),
            pltpu.VMEM((width, width), BF),
            pltpu.VMEM((width, width), BF),
            pltpu.VMEM((width, width), F32),
            pltpu.VMEM((count, width), F32),
            pltpu.VMEM((count, width), BF),
            dma((4,)),
            dma((4,)),
            dma((13,)),
            dma((13,)),
            dma((2, 3)),
            dma((2, 3)),
            dma((4,)),
            dma((4,)),
            dma((4,)),
        ],
        compiler_params=pltpu.CompilerParams(collective_id=3, has_side_effects=True, vmem_limit_bytes=VMEM_LIMIT),
    )(total, mom, outp, tokg)


def finish_kernel(factors, *refs):
    n = len(factors)
    grads, rows, masters, moments = (refs[i * n : i * n + n] for i in range(4))
    outp, tokg, small = refs[4 * n : 4 * n + 3]
    state = refs[4 * n + 3 : 4 * n + 9]
    refs = refs[4 * n + 9 :]
    output, token_grad = refs[:2]
    shards, moments_new, masters_new, copies = (refs[2 + i * n : 2 + i * n + n] for i in range(4))
    vectors = refs[2 + 4 * n :]
    step = 16

    def over(rows, body):
        def one(i, carry):
            body(pl.ds(pl.multiple_of(i * step, step), step))
            return carry

        lax.fori_loop(0, rows // step, one, 0)

    for src, dst in ((outp, output), (tokg, token_grad)):
        for k in range(src.shape[0]):

            def body(at, src=src, dst=dst, k=k):
                dst[k, at] = src[k, at].astype(F32)

            over(src.shape[1], body)
    for m in range(n):

        def body(at, m=m):
            g = grads[m][at].astype(F32)
            shards[m][at] = g
            moments_new[m][at] = muon_decay * moments[m][at] + g
            new = masters[m][at] - factors[m] * rows[m][at].astype(F32)
            masters_new[m][at] = new
            copies[m][at] = new.astype(BF)

        over(grads[m].shape[0], body)
    width = small.shape[1]
    at = 0
    for i, (lo, hi) in enumerate(((0, 2), (6, 8), (8, 12))):
        g = small[lo:hi]
        change, first, second = adam_step(g, state[2 * i][...], state[2 * i + 1][...])
        for value in (g, change, first, second):
            vectors[at][...] = value
            at += 1


def finish(grads, rows, masters, moments, outp, tokg, small, state, factors):
    vmem = pl.BlockSpec(memory_space=pltpu.VMEM)
    args = [*grads, *rows, *masters, *moments, outp, tokg, small, *state]
    sized = [jax.ShapeDtypeStruct(v.shape, F32) for v in masters]
    shapes = [jax.ShapeDtypeStruct(v.shape, F32) for v in (outp, tokg)] + sized * 3
    shapes += [jax.ShapeDtypeStruct(v.shape, BF) for v in masters]
    for v in state[::2]:
        shapes += [jax.ShapeDtypeStruct(v.shape, F32)] * 4
    return pl.pallas_call(
        functools.partial(finish_kernel, factors),
        out_shape=shapes,
        in_specs=[vmem] * len(args),
        out_specs=[vmem] * len(shapes),
        compiler_params=pltpu.CompilerParams(vmem_limit_bytes=VMEM_LIMIT),
        cost_estimate=pl.CostEstimate(flops=10**7, bytes_accessed=15 * 10**6, transcendentals=0),
    )(*args)


def per_device_fast(
    tokens,
    cotangent,
    keep_mask,
    intake,
    outlet,
    expand,
    shrink,
    intake_moment,
    outlet_moment,
    expand_moment,
    shrink_moment,
    head_bias,
    expand_bias,
    norm_gain,
    model_bias,
    head_first,
    head_second,
    expand_first,
    expand_second,
    gain_first,
    gain_second,
    bias_first,
    bias_second,
):
    shape = tokens.shape
    local, width = shape[2:]
    z = lax.axis_index("tensor")
    masters = (intake, outlet, expand, shrink)
    moments = (intake_moment, outlet_moment, expand_moment, shrink_moment)
    sizes = tuple(v.shape[0] for v in masters)
    made = forward_all(
        masters,
        tokens.reshape(-1, local, width),
        cotangent.reshape(-1, local, width),
        norm_gain,
        model_bias,
        head_bias,
        expand_bias[None],
        keep_mask,
    )
    whole = [v.reshape(-1, width) for v in made[:4]]
    x, cot = (v.reshape(-1, width) for v in made[4:6])
    out, saved = made[6], tuple(made[7:]) + (x, cot)
    total, small, mom, token_grad = backward_all(whole, saved, norm_gain, keep_mask, moments, sizes)
    made = muon_all(total, mom, out.reshape(-1, local, width), token_grad.reshape(-1, local, width), sizes)
    rows_scale = lax.axis_size("dp") * lax.axis_size("tensor")
    factors = [rate * (s * rows_scale / width) ** 0.5 for s, rate in zip(sizes, muon_rates)]
    state = (head_first, head_second, gain_first, gain_second, bias_first, bias_second)
    done = finish(made[4:8], made[:4], masters, moments, made[8], made[9], small, state, factors)
    output, token_grad = (v.reshape(shape) for v in done[:2])
    shards, moments_new, masters_new, copies = (tuple(done[2 + 4 * i : 6 + 4 * i]) for i in range(4))
    head, gain, bias = (done[18 + 4 * i : 22 + 4 * i] for i in range(3))
    hidden_total = small[2:6].reshape(expand_bias.shape)
    hidden = adam_step(hidden_total, expand_first, expand_second)
    return (
        (output, token_grad)
        + shards
        + (head[0], hidden_total, gain[0], bias[0])
        + moments_new
        + masters_new
        + copies
        + (head[1], hidden[0], gain[1], bias[1])
        + tuple(head[2:])
        + tuple(hidden[1:])
        + tuple(gain[2:])
        + tuple(bias[2:])
    )


def solution(mesh):
    placed = (
        P(None, "dp", "tensor", None),
        P(None, "dp", "tensor", None),
        P(None, "dp", None),
        P(("tensor", "dp"), None),
        P(("tensor", "dp"), None),
        P(("tensor", "dp"), None),
        P(("tensor", "dp"), None),
        P(("tensor", "dp"), None),
        P(("tensor", "dp"), None),
        P(("tensor", "dp"), None),
        P(("tensor", "dp"), None),
        P(),
        P(),
        P(),
        P(),
        P(),
        P(),
        P(),
        P(),
        P(),
        P(),
        P(),
        P(),
    )
    fast = mesh.shape["dp"] == 8 and mesh.shape["tensor"] == 4
    return jax.shard_map(
        per_device_fast if fast else per_device,
        mesh=mesh,
        in_specs=placed,
        out_specs=(
            P(None, "dp", "tensor", None),
            P(None, "dp", "tensor", None),
            P(("tensor", "dp"), None),
            P(("tensor", "dp"), None),
            P(("tensor", "dp"), None),
            P(("tensor", "dp"), None),
            P(),
            P(),
            P(),
            P(),
            P(("tensor", "dp"), None),
            P(("tensor", "dp"), None),
            P(("tensor", "dp"), None),
            P(("tensor", "dp"), None),
            P(("tensor", "dp"), None),
            P(("tensor", "dp"), None),
            P(("tensor", "dp"), None),
            P(("tensor", "dp"), None),
            P(("tensor", "dp"), None),
            P(("tensor", "dp"), None),
            P(("tensor", "dp"), None),
            P(("tensor", "dp"), None),
            P(),
            P(),
            P(),
            P(),
            P(),
            P(),
            P(),
            P(),
            P(),
            P(),
            P(),
            P(),
        ),
        check_vma=False,
    )
```

```python
import functools

import jax
import jax.numpy as jnp
from jax import lax
from jax.experimental import pallas as pl
from jax.experimental.pallas import tpu as pltpu
from jax.sharding import PartitionSpec as P

HEAD_DIM = 64
BUF = 64
NS_STEPS = 5
ADAM_STEP = 10


norm_eps = 1e-06
first_decay = 0.9
second_decay = 0.95
adam_rate = 0.05
adam_eps = 1e-08
muon_decay = 0.5
muon_rates = (1.0, 4.0, 1.0, 1.0)
frob_eps = 1e-07
coef_a = 3.4445
coef_b = -4.775
coef_c = 2.0315
masked_score = -1000000000.0


def precise(form, left, right):
    return jnp.einsum(form, left, right, precision=lax.Precision.HIGHEST)


def layer_norm(inputs_row, gain_row, shift_row):
    center = inputs_row - jnp.mean(inputs_row, axis=-1, keepdims=True)
    spread = jnp.mean(center * center, axis=-1, keepdims=True)
    return center * lax.rsqrt(spread + norm_eps) * gain_row + shift_row


def softmax_rows(scores):
    largest = jnp.max(scores, axis=-1, keepdims=True)
    powers = jnp.exp(scores - largest)
    return powers / jnp.sum(powers, axis=-1, keepdims=True)


def exact_gelu(inputs_row):
    return jax.nn.gelu(inputs_row, approximate=False)


def attend_weights(queries, keys_all, live_keys):
    scores = jnp.einsum(
        "iqhe,ikhe->ihqk", queries, keys_all, preferred_element_type=jnp.float32
    ) * HEAD_DIM ** (-0.5)
    scores = jnp.where(live_keys[:, None, None, :], scores, masked_score)
    return softmax_rows(scores)


def reduce_blocks(blocks):
    return (
        lax.psum_scatter(blocks[0], "dp", scatter_dimension=0, tiled=True),
        lax.psum_scatter(blocks[1], "dp", scatter_dimension=0, tiled=True),
        lax.psum_scatter(blocks[2], "dp", scatter_dimension=0, tiled=True),
        lax.psum_scatter(blocks[3], "dp", scatter_dimension=0, tiled=True),
    )


def gram_whole(matrix):
    model_width = matrix.shape[1]
    own_rows = model_width // lax.axis_size("dp")
    shard_rows = lax.psum_scatter(
        precise(
            "rm,rn->mn", lax.slice_in_dim(matrix, 0, own_rows * lax.axis_size("dp"), axis=1), matrix
        ),
        "dp",
        scatter_dimension=0,
        tiled=True,
    )
    return lax.all_gather(shard_rows, "dp", axis=0, tiled=True)


def newton_step(scaled, gram):
    product = precise("rk,kn->rn", scaled, gram)
    return coef_a * scaled + coef_b * product + coef_c * precise("rk,kn->rn", product, gram)


def adam_step(gradient, first, second):
    first_new = first_decay * first + (1.0 - first_decay) * gradient
    second_new = second_decay * second + (1.0 - second_decay) * gradient * gradient
    first_hat = first_new / (1.0 - first_decay**ADAM_STEP)
    second_hat = second_new / (1.0 - second_decay**ADAM_STEP)
    change = -adam_rate * first_hat / (jnp.sqrt(second_hat) + adam_eps)
    return (change, first_new, second_new)


def per_device(
    tokens,
    cotangent,
    keep_mask,
    intake,
    outlet,
    expand,
    shrink,
    intake_moment,
    outlet_moment,
    expand_moment,
    shrink_moment,
    head_bias,
    expand_bias,
    norm_gain,
    model_bias,
    head_first,
    head_second,
    expand_first,
    expand_second,
    gain_first,
    gain_second,
    bias_first,
    bias_second,
):
    micro_count, images, local_seq, model_width = tokens.shape
    seq_len = keep_mask.shape[2]
    tensor_size = lax.axis_size("tensor")
    tensor_index = lax.axis_index("tensor")
    head_cols = model_width // tensor_size
    local_heads = head_cols // HEAD_DIM
    hidden_cols = expand_bias.shape[0] // tensor_size
    head_start = tensor_index * head_cols
    hidden_start = tensor_index * hidden_cols
    query_bias = lax.dynamic_slice_in_dim(head_bias[0], head_start, head_cols, 0).reshape(
        local_heads, HEAD_DIM
    )
    value_bias = lax.dynamic_slice_in_dim(head_bias[1], head_start, head_cols, 0).reshape(
        local_heads, HEAD_DIM
    )
    mixed_bias = jnp.stack([query_bias, jnp.zeros_like(query_bias), value_bias], axis=1).reshape(
        3 * head_cols
    )
    hidden_bias = lax.dynamic_slice_in_dim(expand_bias, hidden_start, hidden_cols, 0)
    position = jnp.arange(seq_len)
    masters = (intake, outlet, expand, shrink)
    block_shapes = (
        (3 * head_cols, model_width),
        (head_cols, model_width),
        (hidden_cols, model_width),
        (hidden_cols, model_width),
    )
    totals = tuple((jnp.zeros(shape_one, jnp.float32) for shape_one in block_shapes))
    gain_grad = jnp.zeros((2, model_width), jnp.float32)
    bias_grad = jnp.zeros((4, model_width), jnp.float32)
    mixed_bias_grad = jnp.zeros((2, head_cols), jnp.float32)
    hidden_bias_grad = jnp.zeros((hidden_cols,), jnp.float32)
    outputs = []
    token_grads = []
    for micro_index in range(micro_count):
        intake_block, outlet_block, expand_block, shrink_block = (
            lax.all_gather(intake.astype(jnp.bfloat16), "dp", axis=0, tiled=True),
            lax.all_gather(outlet.astype(jnp.bfloat16), "dp", axis=0, tiled=True),
            lax.all_gather(expand.astype(jnp.bfloat16), "dp", axis=0, tiled=True),
            lax.all_gather(shrink.astype(jnp.bfloat16), "dp", axis=0, tiled=True),
        )
        token_rows = tokens[micro_index].astype(jnp.float32)
        live_keys = jnp.logical_or(keep_mask[micro_index] > 0, position[None, :] < BUF)
        first_local = layer_norm(token_rows, norm_gain[0], model_bias[0]).astype(jnp.bfloat16)
        first_norm = lax.all_gather(first_local, "tensor", axis=1, tiled=True)
        mixed_rows = (
            jnp.einsum("isd,rd->isr", first_norm, intake_block, preferred_element_type=jnp.float32)
            + mixed_bias
        )
        mixed_rows = mixed_rows.astype(jnp.bfloat16).reshape(
            images, seq_len, local_heads, 3, HEAD_DIM
        )
        queries = mixed_rows[:, :, :, 0]
        keys_all = mixed_rows[:, :, :, 1]
        values = mixed_rows[:, :, :, 2]
        attention = attend_weights(queries, keys_all, live_keys)
        attention_low = attention.astype(jnp.bfloat16)
        attended = jnp.einsum(
            "ihqk,ikhe->iqhe", attention_low, values, preferred_element_type=jnp.float32
        )
        attended = attended.reshape(images, seq_len, head_cols).astype(jnp.bfloat16)
        part_sum = jnp.einsum(
            "isc,cd->isd", attended, outlet_block, preferred_element_type=jnp.float32
        )
        middle = (
            token_rows
            + lax.psum_scatter(part_sum, "tensor", scatter_dimension=1, tiled=True)
            + model_bias[2]
        )
        second_local = layer_norm(middle, norm_gain[1], model_bias[1]).astype(jnp.bfloat16)
        second_norm = lax.all_gather(second_local, "tensor", axis=1, tiled=True)
        hidden = (
            jnp.einsum("isd,fd->isf", second_norm, expand_block, preferred_element_type=jnp.float32)
            + hidden_bias
        )
        active = exact_gelu(hidden).astype(jnp.bfloat16)
        part_two = jnp.einsum(
            "isf,fd->isd", active, shrink_block, preferred_element_type=jnp.float32
        )
        outputs.append(
            middle
            + lax.psum_scatter(part_two, "tensor", scatter_dimension=1, tiled=True)
            + model_bias[3]
        )
        cot_local = cotangent[micro_index]
        cot_rows = lax.all_gather(cot_local, "tensor", axis=1, tiled=True)
        shrink_block_grad = jnp.einsum(
            "isf,isd->fd", active, cot_rows, preferred_element_type=jnp.float32
        )
        active_grad = jnp.einsum(
            "isd,fd->isf", cot_rows, shrink_block, preferred_element_type=jnp.float32
        )
        gelu_value, gelu_back = jax.vjp(exact_gelu, hidden)
        hidden_grad = gelu_back(active_grad)[0].astype(jnp.bfloat16)
        hidden_bias_grad = hidden_bias_grad + jnp.sum(hidden_grad.astype(jnp.float32), axis=(0, 1))
        expand_block_grad = jnp.einsum(
            "isf,isd->fd", hidden_grad, second_norm, preferred_element_type=jnp.float32
        )
        second_part = jnp.einsum(
            "isf,fd->isd", hidden_grad, expand_block, preferred_element_type=jnp.float32
        )
        second_grad = lax.psum_scatter(second_part, "tensor", scatter_dimension=1, tiled=True)
        norm_value, norm_back = jax.vjp(layer_norm, middle, norm_gain[1], model_bias[1])
        middle_from_norm, gain_two_grad, shift_two_grad = norm_back(second_grad)
        cot_float = cot_local.astype(jnp.float32)
        middle_grad = cot_float + middle_from_norm
        branch_grad = middle_grad.astype(jnp.bfloat16)
        branch_rows = lax.all_gather(branch_grad, "tensor", axis=1, tiled=True)
        outlet_block_grad = jnp.einsum(
            "isc,isd->cd", attended, branch_rows, preferred_element_type=jnp.float32
        )
        attended_grad = jnp.einsum(
            "isd,cd->isc", branch_rows, outlet_block, preferred_element_type=jnp.float32
        )
        attended_grad = attended_grad.astype(jnp.bfloat16).reshape(
            images, seq_len, local_heads, HEAD_DIM
        )
        attention = attend_weights(queries, keys_all, live_keys)
        attention_low = attention.astype(jnp.bfloat16)
        values_grad = jnp.einsum(
            "ihqk,iqhe->ikhe", attention_low, attended_grad, preferred_element_type=jnp.float32
        )
        attention_grad = jnp.einsum(
            "iqhe,ikhe->ihqk", attended_grad, values, preferred_element_type=jnp.float32
        )
        score_grad = attention * (
            attention_grad - jnp.sum(attention_grad * attention, axis=-1, keepdims=True)
        )
        score_grad = score_grad.astype(jnp.bfloat16)
        queries_grad = jnp.einsum(
            "ihqk,ikhe->iqhe", score_grad, keys_all, preferred_element_type=jnp.float32
        ) * HEAD_DIM ** (-0.5)
        keys_grad = jnp.einsum(
            "ihqk,iqhe->ikhe", score_grad, queries, preferred_element_type=jnp.float32
        ) * HEAD_DIM ** (-0.5)
        mixed_grad = jnp.stack([queries_grad, keys_grad, values_grad], axis=3).astype(jnp.bfloat16)
        mixed_sums = jnp.sum(mixed_grad.astype(jnp.float32), axis=(0, 1))
        mixed_bias_grad = mixed_bias_grad + jnp.stack(
            [mixed_sums[:, 0].reshape(head_cols), mixed_sums[:, 2].reshape(head_cols)]
        )
        mixed_grad = mixed_grad.reshape(images, seq_len, 3 * head_cols)
        intake_block_grad = jnp.einsum(
            "isr,isd->rd", mixed_grad, first_norm, preferred_element_type=jnp.float32
        )
        first_part = jnp.einsum(
            "isr,rd->isd", mixed_grad, intake_block, preferred_element_type=jnp.float32
        )
        first_grad = lax.psum_scatter(first_part, "tensor", scatter_dimension=1, tiled=True)
        first_value, first_back = jax.vjp(layer_norm, token_rows, norm_gain[0], model_bias[0])
        token_from_norm, gain_one_grad, shift_one_grad = first_back(first_grad)
        token_grads.append(middle_grad + token_from_norm)
        gain_grad = gain_grad + jnp.stack([gain_one_grad, gain_two_grad])
        bias_grad = bias_grad + jnp.stack(
            [
                shift_one_grad,
                shift_two_grad,
                jnp.sum(branch_grad.astype(jnp.float32), axis=(0, 1)),
                jnp.sum(cot_float, axis=(0, 1)),
            ]
        )
        block_grads = (intake_block_grad, outlet_block_grad, expand_block_grad, shrink_block_grad)
        totals = tuple((total + block_one for total, block_one in zip(totals, block_grads)))
    shards = reduce_blocks(totals)
    head_full = lax.dynamic_update_slice_in_dim(
        jnp.zeros((2, model_width), jnp.float32), mixed_bias_grad, head_start, 1
    )
    hidden_full = lax.dynamic_update_slice_in_dim(
        jnp.zeros(expand_bias.shape, jnp.float32), hidden_bias_grad, hidden_start, 0
    )
    gain_total, bias_total, head_total, hidden_total = lax.psum(
        (gain_grad, bias_grad, head_full, hidden_full), ("dp", "tensor")
    )
    moments = (intake_moment, outlet_moment, expand_moment, shrink_moment)
    moments_new = [muon_decay * moment + gradient for gradient, moment in zip(shards, moments)]
    updates = [gradient + muon_decay * moment for gradient, moment in zip(shards, moments_new)]
    rows_max = max((update.shape[0] for update in updates))
    padded = jnp.stack(
        [jnp.pad(update, ((0, rows_max - update.shape[0]), (0, 0))) for update in updates]
    )
    spread = lax.all_to_all(padded, "tensor", split_axis=0, concat_axis=0, tiled=True)
    own_matrix = spread.reshape(tensor_size * rows_max, model_width)
    raw_gram = gram_whole(own_matrix)
    measure = jnp.sqrt(jnp.trace(raw_gram)) + frob_eps
    scaled = own_matrix / measure
    gram = raw_gram / (measure * measure)
    for step in range(NS_STEPS):
        if step > 0:
            gram = gram_whole(scaled)
        scaled = newton_step(scaled, gram)
    returned = lax.all_to_all(
        scaled.reshape(tensor_size, rows_max, model_width),
        "tensor",
        split_axis=0,
        concat_axis=0,
        tiled=True,
    )
    rows_scale = lax.axis_size("dp") * tensor_size
    masters_new = [
        weight
        - muon_rates[position_one]
        * (weight.shape[0] * rows_scale / weight.shape[1]) ** 0.5
        * returned[position_one, : weight.shape[0]]
        for position_one, weight in enumerate(masters)
    ]
    head_bias_change, head_first_new, head_second_new = adam_step(
        head_total, head_first, head_second
    )
    expand_bias_change, expand_first_new, expand_second_new = adam_step(
        hidden_total, expand_first, expand_second
    )
    norm_gain_change, gain_first_new, gain_second_new = adam_step(
        gain_total, gain_first, gain_second
    )
    model_bias_change, bias_first_new, bias_second_new = adam_step(
        bias_total, bias_first, bias_second
    )
    output = jnp.stack(outputs)
    token_grad = jnp.stack(token_grads)
    return (
        output,
        token_grad,
        shards[0],
        shards[1],
        shards[2],
        shards[3],
        head_total,
        hidden_total,
        gain_total,
        bias_total,
        moments_new[0],
        moments_new[1],
        moments_new[2],
        moments_new[3],
        masters_new[0],
        masters_new[1],
        masters_new[2],
        masters_new[3],
        masters_new[0].astype(jnp.bfloat16),
        masters_new[1].astype(jnp.bfloat16),
        masters_new[2].astype(jnp.bfloat16),
        masters_new[3].astype(jnp.bfloat16),
        head_bias_change,
        expand_bias_change,
        norm_gain_change,
        model_bias_change,
        head_first_new,
        head_second_new,
        expand_first_new,
        expand_second_new,
        gain_first_new,
        gain_second_new,
        bias_first_new,
        bias_second_new,
    )


MESH = pl.DeviceIdType.MESH
BF = jnp.bfloat16
F32 = jnp.float32
VMEM_LIMIT = 60 * 1024 * 1024


def place():
    d = lax.axis_index("dp")
    z = lax.axis_index("tensor")
    y, x, c = d // 4, (d // 2) % 2, d % 2
    return d, z, y, x, c


def partners(d, z, y, x, c):
    core = (d + 1 - 2 * c, z)
    xn = (d + 2 - 4 * x, z)
    yn = (d + 4 - 8 * y, z)
    zn = [(d, (z + k) % 4) for k in range(1, 4)]
    return core, xn, yn, zn


def greet(others):
    barrier = pltpu.get_barrier_semaphore()
    for other in others:
        pl.semaphore_signal(barrier, inc=1, device_id=other, device_id_type=MESH)
    pl.semaphore_wait(barrier, len(others))


def push(src, dst, sems, to):
    return pltpu.make_async_remote_copy(
        src_ref=src, dst_ref=dst, send_sem=sems[0], recv_sem=sems[1], device_id=to, device_id_type=MESH
    )


LINK = 93.5e3


OPT = dict(lagz=2.0, rate=86e3, lat=1.5, full=3.0, work=1.0, brate=93.5e3, blat=1.5, bone=3.0, bwork=1.3, bhop=3.0, bwin=3, bz=0.0, wait=10.0)


def live_keys(keep, z):
    count = keep.shape[1]
    row = keep[z // count, pl.ds(z % count, 1)]
    position = lax.broadcasted_iota(jnp.int32, row.shape, 1)
    return jnp.logical_or(row != 0, position < BUF)


def plan_forward(blocks, order, sizes, width, slots):
    done, events = [], []
    link = {"x": 0.0, "y": 0.0, "z": 0.0}
    now, at_z = 0.0, 2.0

    def carry(lane, start, rows):
        link[lane] = max(start, link[lane]) + rows * width * 4 / OPT["rate"]
        return link[lane] + OPT["lat"]

    for i, (m, k) in enumerate(order):
        if k == 0:
            events.append((0.1 * i, "one", i))
        elif m != 1:
            at_z += sizes[m] * width * 4 / OPT["rate"]
            events.append((at_z + OPT["lagz"] * k, "one", i))
    whole, loaded = {}, {}
    head = 0
    todo = list(range(len(blocks)))
    while events or todo:
        events.sort()
        if events and events[0][0] <= now:
            _, kind, i = events.pop(0)
            s = sizes[order[i][0]]
            if kind != "full":
                done.append((kind, i))
                now += 0.15
            if kind == "one" and order[i][0] == 1 and order[i][1] > 0:
                events.append((now + OPT["full"], "full", i))
            elif kind == "one":
                ready = max(carry("x", now, s / 2), carry("y", now, s / 2))
                events.append((ready, "two", i))
            elif kind == "two":
                ready = max(carry("x", now, s), carry("y", now, s))
                events.append((ready, "three", i))
            elif kind == "three":
                events.append((now + OPT["full"], "full", i))
                if order[i] == (1, 0):
                    for k in (1, 2, 3):
                        events.append((now + k * (16 * s * width / OPT["rate"] + 2.0) + OPT["wait"], "one", order.index((1, k))))
            else:
                whole[i] = True
            continue
        busy = sum(1 for j in loaded if j in todo)
        while head < len(blocks) and (blocks[head][2] is None or (blocks[head][2] in whole and busy < slots)):
            if blocks[head][2] is not None:
                done.append(("load", head))
                loaded[head] = now + 2.0
                busy += 1
            head += 1
        wait = None
        if todo:
            j = todo[0]
            if blocks[j][2] is None or j in loaded:
                if blocks[j][2] is None or loaded[j] <= now:
                    todo.pop(0)
                    done.append(("block", j))
                    now += blocks[j][1] * OPT["work"]
                    continue
                wait = loaded[j]
        times = [v for v in (wait, events[0][0] if events else None) if v is not None]
        now = max(now, min(times))
    return done


def forward_kernel(sizes, order, *refs):
    n = 4
    w = refs[:n]
    tok, cot = refs[n : n + 2]
    norm_gain, model_bias, head_bias, expand_bias, keep = refs[n + 2 : n + 7]
    refs = refs[n + 7 :]
    o_full = refs[:n]
    o_x, cot_all, output, o_active, o_slope, o_middle, o_mixed, o_attended, o_second, o_first = refs[n : n + 10]
    refs = refs[n + 10 :]
    full = refs[:n]
    xs, first, mixed, attended, acc, middle, second, active, slope, mixed_bias = refs[n : n + 10]
    z_s, z_r, loc, t_s, t_r, p_s, p_r, w_l, out_l, s_l = refs[n + 10 :]
    d, z, y, x, c = place()
    core, xn, yn, zn = partners(d, z, y, x, c)
    for m in range(n):
        full[m][z, y, x, c] = w[m][...].astype(BF)
    greet([core, xn, yn] + zn)
    held = []
    written = []
    inner = z * (3 - z) > 0
    seq, width = first.shape

    def start(copy):
        copy.start()
        held.append(copy)
        return copy

    def source(j):
        return (z, z + 1 - 2 * (z % 2), 2 - z // 2, 3 - 3 * (z // 2))[j]

    def along(m, j, go):
        slot = full[m].at[source(j), :, :, c] if m == 1 else full[m].at[source(j), y, x, c]
        if j == 0:

            @pl.when(z < 3)
            def _():
                go(push(slot, slot, (z_s.at[m, 0], z_r.at[m, z]), (d, z + 1)))

            @pl.when(z > 0)
            def _():
                go(push(slot, slot, (z_s.at[m, 1], z_r.at[m, z]), (d, z - 1)))

        else:
            beyond = 3 - z if j == 1 else 3 * (z - 1)

            @pl.when(inner)
            def _():
                go(push(slot, slot, (z_s.at[m, 1 + j], z_r.at[m, source(j)]), (d, beyond)))

    locals_ = []
    for i, (a, b) in enumerate(((tok, xs), (cot, cot_all))):
        copy = pltpu.make_async_copy(a.at[z], b.at[z], loc.at[i])
        copy.start()
        locals_.append(copy)

    def rows_push(i, a, b):
        for k in range(1, 4):
            to = source(k)
            start(push(a.at[to], b.at[z], (t_s.at[i, k - 1], t_r.at[i, z]), (d, to)))

    def rows_wait(i, b):
        locals_[i].wait()
        for k in range(1, 4):
            s = source(k)
            push(b.at[s], b.at[s], (t_s.at[i, k - 1], t_r.at[i, s]), core).wait_recv()

    def sem(i, stage):
        return (p_s.at[stage, i], p_r.at[stage, i])

    def one(i):
        m, k = order[i]
        h = sizes[m] // 2
        s = source(k)
        if k > 0:
            slot = full[m].at[s, :, :, c] if m == 1 else full[m].at[s, y, x, c]
            push(slot, slot, (z_s.at[m, 1 + k], z_r.at[m, s]), core).wait_recv()
            along(m, k, lambda copy: copy.start())
            if m == 1:
                start(push(slot, slot, sem(i, 4), core))
                return
        a = full[m].at[s, y, x, c, pl.ds(0, h)]
        b = full[m].at[s, y, x, c, pl.ds(h, h)]
        start(push(a, a, sem(i, 0), xn))
        start(push(b, b, sem(i, 1), yn))

    def two(i):
        m, k = order[i]
        h = sizes[m] // 2
        s = source(k)
        a = full[m].at[s, y, 1 - x, c, pl.ds(0, h)]
        push(a, a, sem(i, 0), xn).wait_recv()
        a = full[m].at[s, y, :, c, pl.ds(0, h)]
        start(push(a, a, sem(i, 2), yn))
        b = full[m].at[s, 1 - y, x, c, pl.ds(h, h)]
        push(b, b, sem(i, 1), yn).wait_recv()
        b = full[m].at[s, :, x, c, pl.ds(h, h)]
        start(push(b, b, sem(i, 3), xn))

    def three(i):
        m, k = order[i]
        h = sizes[m] // 2
        s = source(k)
        a = full[m].at[s, 1 - y, :, c, pl.ds(0, h)]
        push(a, a, sem(i, 2), yn).wait_recv()
        b = full[m].at[s, :, 1 - x, c, pl.ds(h, h)]
        push(b, b, sem(i, 3), xn).wait_recv()
        e = full[m].at[s, :, :, c]
        start(push(e, e, sem(i, 4), core))
        if m == 1:
            along(1, 0, lambda copy: copy.start())

    ndims = (((1,), (1,)), ((), ()))
    kept = []

    def load(m, k):
        i = order.index((m, k))
        e = full[m].at[source(k), :, :, 1 - c]
        push(e, e, sem(i, 4), core).wait_recv()
        copy = pltpu.make_async_copy(full[m].at[source(k)], o_full[m].at[source(k)], w_l.at[i])
        copy.start()
        kept.append(copy)

    def save(src, dst, i):
        copy = pltpu.make_async_copy(src, dst, out_l.at[i])
        copy.start()
        written.append(copy)

    chunk = seq // 4

    def norm_rows(index, v_of, dst):
        gain, shift = norm_gain[pl.ds(index, 1)], model_bias[pl.ds(index, 1)]

        def body(i, carry):
            at = pl.ds(pl.multiple_of(i * chunk, chunk), chunk)
            v = v_of(at, i)
            center = v - jnp.mean(v, axis=-1, keepdims=True)
            r = lax.rsqrt(jnp.mean(center * center, axis=-1, keepdims=True) + norm_eps)
            dst[at] = (center * r * gain + shift).astype(BF)
            return carry

        lax.fori_loop(0, seq // chunk, body, 0)

    def first_norm():
        rows_wait(0, xs)
        for h in range(width // HEAD_DIM):
            at, to = h * HEAD_DIM, 3 * h * HEAD_DIM
            mixed_bias[:, to : to + HEAD_DIM] = head_bias[0:1, at : at + HEAD_DIM]
            mixed_bias[:, to + HEAD_DIM : to + 2 * HEAD_DIM] = jnp.zeros((1, HEAD_DIM), F32)
            mixed_bias[:, to + 2 * HEAD_DIM : to + 3 * HEAD_DIM] = head_bias[1:2, at : at + HEAD_DIM]
        norm_rows(0, lambda at, i: xs[i].astype(F32), first)
        save(xs, o_x, 1)
        save(first, o_first, 0)

    def project(k):
        s = source(k)
        rows = 4 * sizes[0]

        def body(j, carry):
            at = pl.ds(pl.multiple_of(s * 2 * rows + j * rows, rows), rows)
            right = full[0][s, j].reshape(rows, width)
            g = lax.dot_general(first[...], right, ndims, preferred_element_type=F32)
            mixed[:, at] = (g + mixed_bias[:, at]).astype(BF)
            return carry

        lax.fori_loop(0, 2, body, 0)

    scale = HEAD_DIM ** (-0.5)

    def heads(k):
        s0 = source(k)
        mask = live_keys(keep, z)

        def body(j, carry):
            p = s0 * 2 + j
            at = pl.ds(pl.multiple_of(p * 6 * HEAD_DIM, 6 * HEAD_DIM), 6 * HEAD_DIM)
            both = mixed[:, at]
            parts = []
            for e in range(2):
                q, kk, v = (both[:, (3 * e + b) * HEAD_DIM : (3 * e + b + 1) * HEAD_DIM] for b in range(3))
                s = lax.dot_general(q, kk, ndims, preferred_element_type=F32) * scale
                s = jnp.where(mask, s, masked_score)
                s = jnp.exp(s - jnp.max(s, axis=-1, keepdims=True))
                pr = (s / jnp.sum(s, axis=-1, keepdims=True)).astype(BF)
                parts.append(jnp.dot(pr, v, preferred_element_type=F32).astype(BF))
            to = pl.ds(pl.multiple_of(p * 2 * HEAD_DIM, 2 * HEAD_DIM), 2 * HEAD_DIM)
            attended[:, to] = jnp.concatenate(parts, axis=1)
            return carry

        lax.fori_loop(0, 2, body, 0)

    def outlet_part(k):
        s = source(k)
        rows = 8 * sizes[1]
        at = pl.ds(pl.multiple_of(s * rows, rows), rows)
        right = full[1][s].reshape(rows, width)
        g = jnp.dot(attended[:, at], right, preferred_element_type=F32)
        if k == 0:
            acc[...] = g
        else:
            acc[...] += g

    def second_norm():
        bias = model_bias[pl.ds(2, 1)]

        def body(i, carry):
            at = pl.ds(pl.multiple_of(i * chunk, chunk), chunk)
            middle[at] = xs[i].astype(F32) + acc[at] + bias
            return carry

        lax.fori_loop(0, seq // chunk, body, 0)
        norm_rows(1, lambda at, i: middle[at], second)
        save(mixed, o_mixed, 4)
        save(attended, o_attended, 5)
        save(middle, o_middle, 6)
        save(second, o_second, 7)

    def slope_copy(k):
        s = source(k)
        hidden = 8 * sizes[2]
        at = pl.ds(pl.multiple_of(s * hidden, hidden), hidden)
        return pltpu.make_async_copy(slope.at[k % 2], o_slope.at[:, at], s_l.at[k % 2])

    def expand_part(k):
        s = source(k)
        if k >= 2:
            slope_copy(k - 2).wait()
        rows = 2 * sizes[2]

        def body(j, carry):
            at = pl.ds(pl.multiple_of(s * 4 * rows + j * rows, rows), rows)
            right = full[2][s, j // 2, j % 2].reshape(rows, width)
            hidden = lax.dot_general(second[...], right, ndims, preferred_element_type=F32)
            hidden = hidden + expand_bias[:, at]
            bell = 0.5 * (1.0 + lax.erf(hidden * (0.5**0.5)))
            active[:, at] = (hidden * bell).astype(BF)
            slope[k % 2, :, pl.ds(pl.multiple_of(j * rows, rows), rows)] = (
                bell + hidden * jnp.exp(-0.5 * hidden * hidden) * (0.5 / jnp.pi) ** 0.5
            )
            return carry

        lax.fori_loop(0, 4, body, 0)
        slope_copy(k).start()
        if k == 3:
            save(active, o_active, 8)

    def shrink_part(k):
        s = source(k)
        hidden = 8 * sizes[3]

        def body(j, carry):
            cols = pl.ds(pl.multiple_of(j * 256, 256), 256)
            left = active[:, pl.ds(pl.multiple_of(s * hidden, hidden), hidden)]
            right = full[3][s, :, :, :, :, cols].reshape(hidden, 256)
            g = jnp.dot(left, right, preferred_element_type=F32)
            if k == 0:
                acc[:, cols] = g
            else:
                acc[:, cols] += g
            return carry

        lax.fori_loop(0, width // 256, body, 0)

    def last():
        bias = model_bias[pl.ds(3, 1)]

        def body(i, carry):
            at = pl.ds(pl.multiple_of(i * chunk, chunk), chunk)
            output[at] = (middle[at] + acc[at] + bias).astype(BF)
            return carry

        lax.fori_loop(0, seq // chunk, body, 0)

    blocks = [("n1", 4.0, None)]
    work = [first_norm]
    needs = [None]

    def block(us, piece, fn):
        blocks.append((len(blocks), us, order.index(piece) if piece else None))
        needs.append(piece)
        work.append(fn)

    for k in range(4):
        block(1.6, (0, k), functools.partial(project, k))
        block(5.0, None, functools.partial(heads, k))
    for k in range(4):
        block(0.8, (1, k), functools.partial(outlet_part, k))
    block(2.5, None, second_norm)
    for k in range(4):
        block(4.5, (2, k), functools.partial(expand_part, k))
    for k in range(4):
        block(1.5, (3, k), functools.partial(shrink_part, k))
    block(1.0, None, last)

    go = lambda copy: copy.start()
    along(0, 0, go)
    rows_push(0, tok, xs)
    ones = 0
    along(2, 0, go)
    for kind, i in plan_forward(blocks, order, sizes, width, len(order)):
        if kind == "one":
            one(i)
            ones += 1
            if ones == 5:
                along(3, 0, go)
            if ones == len(order):
                rows_push(1, cot, cot_all)
        elif kind == "two":
            two(i)
        elif kind == "three":
            three(i)
        elif kind == "load":
            load(*needs[i])
        else:
            work[i]()
    rows_wait(1, cot_all)
    for k in (2, 3):
        slope_copy(k).wait()
    for copy in written + kept:
        copy.wait()
    for copy in held:
        copy.wait_send()
    for m in range(n):
        for j in range(4):
            along(m, j, lambda copy: copy.wait_send())


def forward_all(weights, tok, cot, norm_gain, model_bias, head_bias, expand_bias, keep):
    sizes = tuple(v.shape[0] for v in weights)
    width = weights[0].shape[1]
    seq = tok.shape[0] * tok.shape[1]
    hidden = expand_bias.shape[1]
    order = [(m, 0) for m in range(4)] + [(m, k) for m in range(4) for k in (1, 2, 3)]
    count = len(order)
    anyspace = pl.BlockSpec(memory_space=pl.ANY)
    vmem = pl.BlockSpec(memory_space=pltpu.VMEM)
    dma = pltpu.SemaphoreType.DMA
    shape = jax.ShapeDtypeStruct
    return pl.pallas_call(
        functools.partial(forward_kernel, sizes, order),
        out_shape=[shape((4, 2, 2, 2, s, width), BF) for s in sizes]
        + [
            shape(tok.shape, BF),
            shape(cot.shape, BF),
            shape((seq, width), BF),
            shape((seq, hidden), BF),
            shape((seq, hidden), F32),
            shape((seq, width), F32),
            shape((seq, 3 * width), BF),
            shape((seq, width), BF),
            shape((seq, width), BF),
            shape((seq, width), BF),
        ],
        in_specs=[vmem] * len(sizes) + [anyspace] * 2 + [vmem] * 5,
        out_specs=[anyspace] * (len(sizes) + 2) + [vmem] + [anyspace] * 7,
        scratch_shapes=[pltpu.VMEM((4, 2, 2, 2, s, width), BF) for s in sizes]
        + [
            pltpu.VMEM(tok.shape, BF),
            pltpu.VMEM((seq, width), BF),
            pltpu.VMEM((seq, 3 * width), BF),
            pltpu.VMEM((seq, width), BF),
            pltpu.VMEM((seq, width), F32),
            pltpu.VMEM((seq, width), F32),
            pltpu.VMEM((seq, width), BF),
            pltpu.VMEM((seq, hidden), BF),
            pltpu.VMEM((2, seq, 8 * sizes[2]), F32),
            pltpu.VMEM((1, 3 * width), F32),
            dma((4, 5)),
            dma((4, 4)),
            dma((2,)),
            dma((2, 3)),
            dma((2, 4)),
            dma((5, count)),
            dma((5, count)),
            dma((count,)),
            dma((9,)),
            dma((2,)),
        ],
        compiler_params=pltpu.CompilerParams(collective_id=1, has_side_effects=True, vmem_limit_bytes=VMEM_LIMIT),
    )(*weights, tok, cot, norm_gain, model_bias, head_bias, expand_bias, keep)


def add_rows(dst, src, lead, rows):
    step = 16

    def body(i, carry):
        j, r = i // (rows // step), (i % (rows // step)) * step
        at = pl.ds(pl.multiple_of(r, step), step)
        dst[j, at] = dst[j, at] + src[j, at]
        return carry

    lax.fori_loop(0, lead * (rows // step), body, 0)


PLANES = (1, 2, 0, 3)


def plan(blocks, sizes, order, free_after, width):
    todo = list(blocks)
    done = []
    events = []
    link = {"x": 0.0, "y": 0.0, "z": 0.0}
    now = 0.0
    finished = set()

    def carry(lane, start, rows):
        begin = max(start, link[lane])
        link[lane] = begin + rows * width * 2 * 2 / OPT["brate"]
        return link[lane] + OPT["blat"]

    def emit(step):
        nonlocal now
        kind, i = step[0], step[1]
        done.append(step)
        finished.add(step)
        s = sizes[order[i][0]]
        if kind == "one":
            now += s / 128 * 1.0
            ready = max(carry("y", now, s), carry("x", now, s))
            events.append((ready, ("two", i)))
        elif kind == "two":
            now += s / 128 * 0.6
            ready = max(carry("x", now, s / 2), carry("y", now, s / 2))
            events.append((ready, ("three", i)))
        elif kind == "three":
            now += s / 128 * 0.3
            ready = carry("z", now, s)
            events.append((ready + OPT["bz"], ("four", i)))
            events.append((ready + OPT["bz"] + 0.001, ("fourb", i)))
        elif kind == "four":
            finished.discard(step)
            now += 0.2
        elif kind == "fourb":
            now += 0.2

    def open_now():
        ones = sum(1 for v in finished if v[0] == "one")
        twos = sum(1 for v in finished if v[0] == "two")
        for v in events:
            if v[1][0] != "one" or ones - twos < OPT["bwin"]:
                return v
        return events[0]

    while todo or events:
        events.sort()
        if events and open_now()[0] <= now:
            event = open_now()
            events.remove(event)
            step = event[1]
            if step[0] == "fourb":
                events.append((now + OPT["bhop"], ("fourc", step[1])))
                continue
            emit(step)
            continue
        if todo:
            name, us, piece = todo[0]
            blocked = piece is not None and piece >= free_after and ("one", piece - free_after) not in finished
            if not blocked:
                todo.pop(0)
                done.append(("block", name))
                now += us * OPT["bwork"]
                if piece is not None:
                    done.append(("push", piece))
                    events.append((now + OPT["bone"], ("one", piece)))
                continue
        now = max(now, open_now()[0])
    return done


def backward_kernel(sizes, order, *refs):
    n = 4
    small_count = 16
    shrink, expand, outlet, intake, active, slope = refs[:6]
    inputs = refs[6:13]
    norm_gain, keep = refs[13:15]
    mom_f = refs[15:19]
    total, small_out, mom_all, token_grad = refs[19:23]
    refs = refs[23:]
    own, mid, end, far = (refs[i * n : i * n + n] for i in range(4))
    refs = refs[4 * n :]
    (made, act, slo, wbuf, obuf, hgrad, wide, mgrad, branch, agrad) = refs[:10]
    small, s_got, s_acc, s_z = refs[10:14]
    loc, c_s, c_r, p_s, p_r, f_s, f_r, q_s, q_r, m_s, m_r, w_l = refs[14:26]
    mom = refs[26:30]
    middle, mixed, attended, second, first, x_in, cot, in_l = refs[30:]
    held_in = (middle, mixed, attended, second, first, x_in, cot)
    d, z, y, x, c = place()
    unit = wbuf.shape[1]
    count_units = shrink.shape[0] // unit

    def load(u):
        at = pl.ds(u * unit, unit)
        return [
            pltpu.make_async_copy(shrink.at[at], wbuf.at[u % 2], w_l.at[0, u % 2]),
            pltpu.make_async_copy(expand.at[at], wbuf.at[2 + u % 2], w_l.at[1, u % 2]),
            pltpu.make_async_copy(slope.at[:, at], slo.at[u % 2], w_l.at[3, u % 2]),
        ]

    def load_active(u):
        return pltpu.make_async_copy(active.at[:, pl.ds(u * unit, unit)], act.at[u % 2], w_l.at[2, u % 2])


    fetches = [
        pltpu.make_async_copy(src, dst, in_l.at[i]) for i, (src, dst) in enumerate(zip(inputs, held_in))
    ]
    fetches[6].start()
    for u in (0, 1):
        load_active(u).start()
    for copy in load(0) + load(1):
        copy.start()
    for i in (3, 0, 2, 1, 4, 5):
        fetches[i].start()
    for m in range(n):
        mom[m][...] = mom_f[m][...].astype(BF)
    core, xn, yn, zn = partners(d, z, y, x, c)
    greet([core, xn, yn] + zn)
    seq, width = cot.shape
    held = []
    top = max(sizes)

    def start(copy):
        copy.start()
        held.append(copy)

    def sem(i, stage):
        return (p_s.at[stage, i], p_r.at[stage, i])

    slots = made.shape[0]

    def core_push(i):
        m, k = order[i]
        return push(
            made.at[i % slots, :, :, 1 - c, pl.ds(0, sizes[m])], own[m].at[k], (c_s.at[i], c_r.at[i]), core
        )

    def one(i):
        m, k = order[i]
        s, h = sizes[m], sizes[m] // 2
        core_push(i).wait_recv()
        for j in range(2):
            for l in range(2):
                add_rows(own[m].at[k, j, pl.ds(l, 1)], made.at[i % slots, j, l, pl.ds(c, 1)], 1, s)
        start(push(own[m].at[k, 1 - y, :, pl.ds(0, h)], mid[m].at[k, 0], sem(i, 0), yn))
        start(push(own[m].at[k, :, 1 - x, pl.ds(h, h)], mid[m].at[k, 1], sem(i, 1), xn))

    def two(i):
        m, k = order[i]
        h = sizes[m] // 2
        push(mid[m].at[k, 0], mid[m].at[k, 0], sem(i, 0), yn).wait_recv()
        add_rows(own[m].at[k, y, :, pl.ds(0, h)], mid[m].at[k, 0], 2, h)
        start(push(own[m].at[k, y, 1 - x, pl.ds(0, h)], end[m].at[k, pl.ds(0, h)], sem(i, 2), xn))
        push(mid[m].at[k, 1], mid[m].at[k, 1], sem(i, 1), xn).wait_recv()
        add_rows(own[m].at[k, :, x, pl.ds(h, h)], mid[m].at[k, 1], 2, h)
        start(push(own[m].at[k, 1 - y, x, pl.ds(h, h)], end[m].at[k, pl.ds(h, h)], sem(i, 3), yn))

    def hop(i, p, go):
        m, k = order[i]
        side, to = (0, p + 1) if p < PLANES[m] else (1, p - 1)
        at = side if PLANES[m] in (1, 2) else 0
        go(push(own[m].at[k, y, x], far[m].at[at, k], (f_s.at[m, k], f_r.at[m, k, side]), (d, to)))

    def came(m, k, side):
        slot = far[m].at[side if PLANES[m] in (1, 2) else 0, k]
        push(slot, slot, (f_s.at[m, k], f_r.at[m, k, side]), core).wait_recv()

    def three(i):
        m, k = order[i]
        s, h = sizes[m], sizes[m] // 2
        push(end[m].at[k, pl.ds(0, h)], end[m].at[k, pl.ds(0, h)], sem(i, 2), xn).wait_recv()
        push(end[m].at[k, pl.ds(h, h)], end[m].at[k, pl.ds(h, h)], sem(i, 3), yn).wait_recv()
        add_rows(own[m].at[k, pl.ds(y, 1), x], end[m].at[pl.ds(k, 1)], 1, s)
        for p in (0, 3):
            if p != PLANES[m]:

                @pl.when(z == p)
                def _(p=p):
                    hop(i, p, lambda copy: copy.start())

    def four(i, far_hop):
        m, k = order[i]
        for p in (1, 2):
            below = p < PLANES[m]
            if p == PLANES[m] or far_hop != (p if below else 3 - p):
                continue

            @pl.when(z == p)
            def _(p=p, below=below):
                side = 0 if below else 1
                came(m, k, side)
                at = side if PLANES[m] in (1, 2) else 0
                add_rows(own[m].at[k, pl.ds(y, 1), x], far[m].at[at, pl.ds(k, 1)], 1, sizes[m])
                hop(i, p, lambda copy: copy.start())

    def five(i):
        m, k = order[i]
        s, p = sizes[m], PLANES[m]
        sides = [v for v in (0, 1) if p != 3 * v]

        @pl.when(z == p)
        def _():
            for side in sides:
                came(m, k, side)

            def body(r, carry):
                at = pl.ds(pl.multiple_of(r * 16, 16), 16)
                acc = own[m][k, y, x, at].astype(F32)
                for side in range(len(sides)):
                    acc = acc + far[m][side, k, at].astype(F32)
                total[k, at] = acc
                return carry

            lax.fori_loop(0, s // 16, body, 0)
            if s < total.shape[1]:
                total[k, pl.ds(s, total.shape[1] - s)] = jnp.zeros((total.shape[1] - s, width), F32)

    def small_step(stage):
        to = (core, xn, yn)
        if stage > 0:
            here = s_got.at[stage - 1]
            push(here, here, (q_s.at[stage - 1], q_r.at[stage - 1]), to[stage - 1]).wait_recv()
            s_acc[stage] = s_acc[stage - 1] + s_got[stage - 1]
        else:
            s_acc[0] = small[...]
        if stage < 3:
            start(push(s_acc.at[stage], s_got.at[stage], (q_s.at[stage], q_r.at[stage]), to[stage]))
        else:
            s_z[z] = s_acc[3]
            for k in range(1, 4):
                start(push(s_acc.at[3], s_z.at[z], (q_s.at[2 + k], q_r.at[2 + k]), zn[k - 1]))

    def moments(first):
        for t in range(n):
            p = PLANES[t]
            here = mom_all.at[z, pl.ds(0, sizes[t])]

            @pl.when(z == p)
            def _(t=t, p=p, here=here):
                copy = pltpu.make_async_copy(mom[t], here, loc.at[0])
                if first:
                    copy.start()
                else:
                    copy.wait()
                    for k in range(1, 4):
                        s = (p + k) % 4
                        there = mom_all.at[s, pl.ds(0, sizes[t])]
                        push(mom[t], there, (m_s.at[t], m_r.at[s]), (d, s)).wait_recv()

            @pl.when(z != p)
            def _(t=t, p=p, here=here):
                copy = push(mom[t], here, (m_s.at[t], m_r.at[z]), (d, p))
                if first:
                    copy.start()
                else:
                    copy.wait_send()

    def load_outlet():
        return pltpu.make_async_copy(outlet, obuf, loc.at[1])

    def load_intake(v):
        return pltpu.make_async_copy(intake.at[pl.ds(v * unit, unit)], wbuf.at[v % 4], w_l.at[4, v % 4])

    tdims = (((0,), (0,)), ((), ()))
    ndims = (((1,), (1,)), ((), ()))

    def shrink_rows(k):
        if k == 0:
            fetches[6].wait()
        i = 2 * k
        for half in (0, 1):
            u = 2 * k + half
            load_active(u).wait()

            def body(j, carry, half=half, u=u):
                cols = pl.ds(pl.multiple_of(j * 2 * top, 2 * top), 2 * top)
                g = lax.dot_general(act[u % 2, :, cols], cot[...], tdims, preferred_element_type=F32)
                made[i % slots, half, j] = g.astype(BF).reshape(2, top, width)
                return carry

            lax.fori_loop(0, unit // (2 * top), body, 0)
            if u + 2 < count_units:
                load_active(u + 2).start()

    def mlp_back(u):
        k, half = u // 2, u % 2
        for copy in load(u):
            copy.wait()

        def grad(j, carry):
            rows = pl.ds(pl.multiple_of(j * 256, 256), 256)
            to = pl.ds(pl.multiple_of(j * 256 + half * unit, 256), 256)
            g = lax.dot_general(cot[...], wbuf[u % 2, rows], ndims, preferred_element_type=F32)
            hg = (g * slo[u % 2, :, rows]).astype(BF)
            hgrad[:, to] = hg
            small[pl.ds(2 + k, 1), to] = jnp.sum(hg.astype(F32), axis=0, keepdims=True)
            return carry

        lax.fori_loop(0, unit // 256, grad, 0)

        def back(j, carry):
            cols = pl.ds(pl.multiple_of(j * 256, 256), 256)
            g = jnp.dot(hgrad[:, pl.ds(half * unit, unit)], wbuf[2 + u % 2, :, cols], preferred_element_type=F32)
            if u == 0:
                wide[:, cols] = g
            else:
                wide[:, cols] += g
            return carry

        lax.fori_loop(0, width // 256, back, 0)
        if u + 2 < count_units:
            for copy in load(u + 2):
                copy.start()

    def mlp_two(k):
        i = 2 * k + 1
        if k == 0:
            fetches[3].wait()

        def body(j, carry):
            cols = pl.ds(pl.multiple_of(j * 2 * top, 2 * top), 2 * top)
            g = lax.dot_general(hgrad[:, cols], second[...], tdims, preferred_element_type=F32)
            made[i % slots, j // 2, j % 2] = g.astype(BF).reshape(2, top, width)
            return carry

        lax.fori_loop(0, 4, body, 0)

    chunk = 64

    def norm_block(index, v_of, extra):
        gain = norm_gain[pl.ds(index, 1)]

        def body(i, carry):
            at = pl.ds(pl.multiple_of(i * chunk, chunk), chunk)
            v = v_of(at)
            center = v - jnp.mean(v, axis=-1, keepdims=True)
            r = lax.rsqrt(jnp.mean(center * center, axis=-1, keepdims=True) + norm_eps)
            nrm = center * r
            w = wide[at]
            u = w * gain
            down = r * (u - jnp.mean(u, axis=-1, keepdims=True) - nrm * jnp.mean(u * nrm, axis=-1, keepdims=True))
            sums = extra(at, down)
            new = [jnp.sum(w * nrm, axis=0, keepdims=True), jnp.sum(w, axis=0, keepdims=True)] + sums
            return tuple(a + b for a, b in zip(carry, new))

        zero = jnp.zeros((1, width), F32)
        out = lax.fori_loop(0, seq // chunk, body, (zero,) * (4 if index else 2))
        small[pl.ds(6 + index, 1)] = out[0]
        small[pl.ds(8 + index, 1)] = out[1]
        if index:
            small[pl.ds(10, 1)] = out[2]
            small[pl.ds(11, 1)] = out[3]

    def second_norm_back():
        fetches[0].wait()
        load_outlet().start()
        for v in range(4):
            load_intake(v).start()

        def extra(at, down):
            g = cot[at].astype(F32)
            m = g + down
            mgrad[at] = m
            low = m.astype(BF)
            branch[at] = low
            return [jnp.sum(low.astype(F32), axis=0, keepdims=True), jnp.sum(g, axis=0, keepdims=True)]

        norm_block(1, lambda at: middle[at], extra)

    def outlet_piece(k):
        i = 12 + k
        if k == 0:
            fetches[2].wait()
        cols = pl.ds(k * 8 * sizes[1], 8 * sizes[1])
        g = lax.dot_general(attended[:, cols], branch[...], tdims, preferred_element_type=F32)
        made[i % slots, :, :, :, pl.ds(0, sizes[1])] = g.astype(BF).reshape(2, 2, 2, sizes[1], width)

    def attended_back():
        load_outlet().wait()

        def body(j, carry):
            rows = pl.ds(pl.multiple_of(j * 256, 256), 256)
            g = lax.dot_general(branch[...], obuf[rows], ndims, preferred_element_type=F32)
            agrad[:, rows] = g.astype(BF)
            return carry

        lax.fori_loop(0, width // 256, body, 0)

    scale = HEAD_DIM ** (-0.5)

    def heads(first_pair, pairs):
        if first_pair == 0:
            fetches[1].wait()
        mask = live_keys(keep, z)

        def body(p, carry):
            at = pl.ds(pl.multiple_of(p * 6 * HEAD_DIM, 6 * HEAD_DIM), 6 * HEAD_DIM)
            both = mixed[:, at]
            ag_both = agrad[:, pl.ds(pl.multiple_of(p * 2 * HEAD_DIM, 2 * HEAD_DIM), 2 * HEAD_DIM)]
            parts, sums = [], []
            for e in range(2):
                q, k, v = (both[:, (3 * e + b) * HEAD_DIM : (3 * e + b + 1) * HEAD_DIM] for b in range(3))
                ag = ag_both[:, e * HEAD_DIM : (e + 1) * HEAD_DIM]
                s = lax.dot_general(q, k, ndims, preferred_element_type=F32) * scale
                s = jnp.where(mask, s, masked_score)
                s = jnp.exp(s - jnp.max(s, axis=-1, keepdims=True))
                pr = s / jnp.sum(s, axis=-1, keepdims=True)
                vg = lax.dot_general(pr.astype(BF), ag, tdims, preferred_element_type=F32)
                dp = lax.dot_general(ag, v, ndims, preferred_element_type=F32)
                ds = (pr * (dp - jnp.sum(dp * pr, axis=-1, keepdims=True))).astype(BF)
                qg = jnp.dot(ds, k, preferred_element_type=F32) * scale
                kg = lax.dot_general(ds, q, tdims, preferred_element_type=F32) * scale
                parts += [qg.astype(BF), kg.astype(BF), vg.astype(BF)]
                sums.append((jnp.sum(parts[-3].astype(F32), 0, keepdims=True), jnp.sum(parts[-1].astype(F32), 0, keepdims=True)))
            mixed[:, at] = jnp.concatenate(parts, axis=1)
            to = pl.ds(pl.multiple_of(p * 2 * HEAD_DIM, 2 * HEAD_DIM), 2 * HEAD_DIM)
            small[pl.ds(0, 1), to] = jnp.concatenate([sums[0][0], sums[1][0]], axis=1)
            small[pl.ds(1, 1), to] = jnp.concatenate([sums[0][1], sums[1][1]], axis=1)
            return carry

        lax.fori_loop(first_pair, first_pair + pairs, body, 0)

    def intake_piece(k):
        i = 8 + k
        if k == 0:
            fetches[4].wait()
        rows = 4 * sizes[0]

        def body(j, carry):
            cols = pl.ds(pl.multiple_of((2 * k + j) * rows, rows), rows)
            g = lax.dot_general(mixed[:, cols], first[...], tdims, preferred_element_type=F32)
            made[i % slots, j, :, :, pl.ds(0, sizes[0])] = g.astype(BF).reshape(2, 2, sizes[0], width)
            return carry

        lax.fori_loop(0, 2, body, 0)

    def first_back(v):
        load_intake(v).wait()

        def body(j, carry):
            cols = pl.ds(pl.multiple_of(j * 256, 256), 256)
            g = jnp.dot(mixed[:, pl.ds(v * unit, unit)], wbuf[v % 4, :, cols], preferred_element_type=F32)
            if v == 0:
                wide[:, cols] = g
            else:
                wide[:, cols] += g
            return carry

        lax.fori_loop(0, width // 256, body, 0)
        if v + 4 < intake.shape[0] // unit:
            load_intake(v + 4).start()

    def first_norm_back():
        fetches[5].wait()

        def extra(at, down):
            token_grad[at] = (mgrad[at] + down).astype(BF)
            return []

        norm_block(0, lambda at: x_in[at].astype(F32), extra)

    work = {}
    blocks = []

    def block(name, us, piece, fn):
        work[name] = fn
        blocks.append((name, us, piece))

    for k in range(4):
        block(("a", k), 2.0, 2 * k, functools.partial(shrink_rows, k))
        block(("m", 2 * k), 2.0, None, functools.partial(mlp_back, 2 * k))
        block(("m", 2 * k + 1), 2.0, None, functools.partial(mlp_back, 2 * k + 1))
        block(("e", k), 1.5, 2 * k + 1, functools.partial(mlp_two, k))
    block("n2", 3.0, None, second_norm_back)
    block("ab", 1.5, None, attended_back)
    for k in range(4):
        block(("h", k), 7.0, None, functools.partial(heads, 2 * k, 2))
        block(("i", k), 1.2, 8 + k, functools.partial(intake_piece, k))
    for k in range(4):
        block(("o", k), 0.5, 12 + k, functools.partial(outlet_piece, k))
    for v in range(intake.shape[0] // unit):
        block(("f", v), 0.8, None, functools.partial(first_back, v))
    block("n1", 3.0, None, first_norm_back)
    for stage in range(4):
        block(("s", stage), 2.0, None, functools.partial(small_step, stage))

    small[pl.ds(12, 4)] = jnp.zeros((4, width), F32)
    steps = plan(blocks, sizes, order, slots, width)
    pushed = {}
    stage = 1
    for step in steps:
        kind = step[0]
        if kind == "block":
            name = step[1]
            piece = {b[0]: b[2] for b in blocks}[name]
            if piece is not None and piece - slots in pushed:
                pushed.pop(piece - slots).wait_send()
            work[name]()
            if name == ("m", 1):
                moments(True)
        elif kind == "push":
            pushed[step[1]] = core_push(step[1])
            pushed[step[1]].start()
        elif kind == "one":
            one(step[1])
        elif kind == "two":
            two(step[1])
        elif kind == "three":
            three(step[1])
        elif kind == "four":
            four(step[1], 1)
        elif kind == "fourc":
            four(step[1], 2)
    for i in range(len(order)):
        five(i)
    for k in range(1, 4):
        slot = s_z.at[(z + 4 - k) % 4]
        push(slot, slot, (q_s.at[2 + k], q_r.at[2 + k]), zn[k - 1]).wait_recv()
    small_out[...] = s_z[0] + s_z[1] + s_z[2] + s_z[3]
    moments(False)
    for copy in pushed.values():
        copy.wait_send()
    for copy in held:
        copy.wait_send()
    for i in range(len(order)):
        for p in range(4):
            if p != PLANES[order[i][0]]:

                @pl.when(z == p)
                def _(i=i, p=p):
                    hop(i, p, lambda copy: copy.wait_send())


def backward_all(weights, saved, norm_gain, keep, moms, sizes):
    intake, outlet, expand, shrink = weights
    active, slope, middle, mixed, attended, second, first, x, cot = saved
    seq, width = cot.shape
    top = max(sizes)
    order = []
    for k in range(4):
        order += [(3, k), (2, k)]
    order += [(0, k) for k in range(4)] + [(1, k) for k in range(4)]
    count = len(order)
    anyspace = pl.BlockSpec(memory_space=pl.ANY)
    vmem = pl.BlockSpec(memory_space=pltpu.VMEM)
    dma = pltpu.SemaphoreType.DMA
    unit = 512
    return pl.pallas_call(
        functools.partial(backward_kernel, sizes, order),
        out_shape=[
            jax.ShapeDtypeStruct((4, top, width), F32),
            jax.ShapeDtypeStruct((16, width), F32),
            jax.ShapeDtypeStruct((4, top, width), BF),
            jax.ShapeDtypeStruct((seq, width), BF),
        ],
        in_specs=[anyspace] * 13 + [vmem] * 6,
        out_specs=[vmem, vmem, anyspace, vmem],
        scratch_shapes=[pltpu.VMEM((4, 2, 2, s, width), BF) for s in sizes]
        + [pltpu.VMEM((4, 2, 2, s // 2, width), BF) for s in sizes]
        + [pltpu.VMEM((4, s, width), BF) for s in sizes]
        + [pltpu.VMEM((2 if p in (1, 2) else 1, 4, s, width), BF) for s, p in zip(sizes, PLANES)]
        + [
            pltpu.VMEM((3, 2, 2, 2, top, width), BF),
            pltpu.VMEM((2, seq, unit), BF),
            pltpu.VMEM((2, seq, unit), F32),
            pltpu.VMEM((4, unit, width), BF),
            pltpu.VMEM((width, width), BF),
            pltpu.VMEM((seq, width), BF),
            pltpu.VMEM((seq, width), F32),
            pltpu.VMEM((seq, width), F32),
            pltpu.VMEM((seq, width), BF),
            pltpu.VMEM((seq, width), BF),
            pltpu.VMEM((16, width), F32),
            pltpu.VMEM((3, 16, width), F32),
            pltpu.VMEM((4, 16, width), F32),
            pltpu.VMEM((4, 16, width), F32),
            dma((2,)),
            dma((count,)),
            dma((count,)),
            dma((4, count)),
            dma((4, count)),
            dma((4, 4)),
            dma((4, 4, 2)),
            dma((6,)),
            dma((6,)),
            dma((4,)),
            dma((4,)),
            dma((5, 4)),
        ]
        + [pltpu.VMEM((s, width), BF) for s in sizes]
        + [pltpu.VMEM(v.shape, v.dtype) for v in saved[2:]]
        + [dma((7,))],
        compiler_params=pltpu.CompilerParams(collective_id=2, has_side_effects=True, vmem_limit_bytes=VMEM_LIMIT),
    )(shrink, expand, outlet, intake, active, slope, middle, mixed, attended, second, first, x, cot, norm_gain, keep, *moms)


def split(v):
    hi = v.astype(BF)
    return hi, (v - hi.astype(F32)).astype(BF)


def dot(a, b):
    return jnp.dot(a, b, preferred_element_type=F32)


def muon_kernel(sizes, *refs):
    n = len(sizes)
    total, mom, outp, tokg = refs[:4]
    rows_out = refs[4 : 4 + n]
    grads = refs[4 + n : 4 + 2 * n]
    outp_all, tokg_all = refs[4 + 2 * n : 6 + 2 * n]
    refs = refs[6 + 2 * n :]
    low_g, uh, ul, pack, r_core, r_one, r_two, gathered, gf, gh, low, b, tf, xf, xh = refs[:15]
    g_s, g_r, a_s, a_r, o_s, o_r, s_s, s_r, loc = refs[15:]
    d, z, y, x, c = place()
    core, xn, yn, zn = partners(d, z, y, x, c)
    greet([core, xn, yn] + zn)
    held = []

    def start(copy):
        copy.start()
        held.append(copy)

    top, width = total.shape[1:]
    count = 4 * top
    block = width // 4
    height = 0
    for t in range(n):
        height = jnp.where(z == PLANES[t], sizes[t], height)
    per = top // 16

    def make(i, carry):
        k, r = i // per, (i % per) * 16
        at = pl.ds(pl.multiple_of(r, 16), 16)
        g = total[k, at]
        low_g[k, at] = g.astype(BF)
        u = g + muon_decay * (muon_decay * mom[k, at].astype(F32) + g)
        row = lax.broadcasted_iota(jnp.int32, u.shape, 0) + r
        u = jnp.where(row < height, u, 0.0)
        to = pl.ds(pl.multiple_of(i * 16, 16), 16)
        uh[to], ul[to] = split(u)
        return carry

    lax.fori_loop(0, 4 * per, make, 0)

    def back_home(src, dst, sems, local, first):
        for t in range(n):
            s, p = sizes[t], PLANES[t]

            @pl.when(z == p)
            def _(t=t, s=s, p=p):
                own = pltpu.make_async_copy(src.at[p, pl.ds(0, s)], dst[t], loc.at[local])
                away = [
                    push(src.at[(p + k) % 4, pl.ds(0, s)], dst[t], (sems[0].at[k], sems[1].at[t]), (d, (p + k) % 4))
                    for k in range(1, 4)
                ]
                if first:
                    for copy in away:
                        copy.start()
                    own.start()
                else:
                    own.wait()
                    for copy in away:
                        copy.wait_send()

            if not first:

                @pl.when(z != p)
                def _(t=t, p=p):
                    push(dst[t], dst[t], (sems[0].at[0], sems[1].at[t]), (d, p)).wait_recv()

    back_home(low_g, grads, (g_s, g_r), 0, True)
    for i, (a, e) in enumerate(((outp, outp_all), (tokg, tokg_all))):
        pltpu.make_async_copy(a.at[z], e.at[z], loc.at[1 + i]).start()
        for k in range(1, 4):
            start(push(a.at[(z + k) % 4], e.at[z], (o_s.at[i, k - 1], o_r.at[i, k - 1]), zn[k - 1]))

    places = {0: (0, 0), 3: (0, 4 * block), 1: (1, 0), 2: (1, 3 * block)}
    tdims = (((0,), (0,)), ((), ()))

    def product(half):
        for r, (h, col) in places.items():
            if h != half:
                continue
            mine = slice(r * block, (r + 1) * block)
            rest = slice(r * block, width)
            acc = lax.dot_general(uh[:, mine], uh[:, rest], tdims, preferred_element_type=F32)
            acc = acc + lax.dot_general(uh[:, mine], ul[:, rest], tdims, preferred_element_type=F32)
            acc = acc + lax.dot_general(ul[:, mine], uh[:, rest], tdims, preferred_element_type=F32)
            pack[half, :, col : col + width - r * block] = acc

    def sem(i):
        return (a_s.at[i], a_r.at[i])

    for v in (0, 1):

        @pl.when(c == v)
        def _(v=v):
            product(1 - v)
            push(pack.at[1 - v], r_core, sem(0), core).start()
            product(v)

    def add(dst, r0, src, rows, into=None):
        def body(i, carry):
            at = pl.ds(pl.multiple_of(r0 + i * 8, 8), 8)
            v = dst[at] + src[pl.ds(pl.multiple_of(i * 8, 8), 8)]
            (dst if into is None else into)[at] = v
            return carry

        lax.fori_loop(0, rows // 8, body, 0)

    def rows(ref, r, size):
        return ref.at[pl.ds(pl.multiple_of(r, 32), size)]

    half, quarter, eighth = block // 2, block // 4, block // 8
    push(r_core, r_core, sem(0), core).wait_recv()
    mine, whole = pack.at[c], gathered.at[c]
    add(mine, 0, r_core, block)
    base_a, base_b = 0, half
    start(push(rows(mine, base_a + (1 - y) * quarter, quarter), r_one.at[0], sem(1), yn))
    start(push(rows(mine, base_b + (1 - x) * quarter, quarter), r_one.at[1], sem(2), xn))
    push(r_one.at[0], r_one.at[0], sem(1), yn).wait_recv()
    mine_a = base_a + y * quarter
    add(mine, mine_a, r_one.at[0], quarter)
    start(push(rows(mine, mine_a + (1 - x) * eighth, eighth), r_two.at[0], sem(3), xn))
    push(r_one.at[1], r_one.at[1], sem(2), xn).wait_recv()
    mine_b = base_b + x * quarter
    add(mine, mine_b, r_one.at[1], quarter)
    start(push(rows(mine, mine_b + (1 - y) * eighth, eighth), r_two.at[1], sem(4), yn))
    push(r_two.at[0], r_two.at[0], sem(3), xn).wait_recv()
    own_a = mine_a + x * eighth
    add(mine, own_a, r_two.at[0], eighth, whole)
    start(push(rows(whole, own_a, eighth), rows(whole, own_a, eighth), sem(5), xn))
    push(r_two.at[1], r_two.at[1], sem(4), yn).wait_recv()
    own_b = mine_b + y * eighth
    add(mine, own_b, r_two.at[1], eighth, whole)
    start(push(rows(whole, own_b, eighth), rows(whole, own_b, eighth), sem(6), yn))
    got = rows(whole, mine_a + (1 - x) * eighth, eighth)
    push(got, got, sem(5), xn).wait_recv()
    start(push(rows(whole, mine_a, quarter), rows(whole, mine_a, quarter), sem(7), yn))
    got = rows(whole, mine_b + (1 - y) * eighth, eighth)
    push(got, got, sem(6), yn).wait_recv()
    start(push(rows(whole, mine_b, quarter), rows(whole, mine_b, quarter), sem(8), xn))
    start(push(rows(whole, mine_a, quarter), rows(whole, mine_a, quarter), sem(9), core))
    start(push(rows(whole, mine_b, quarter), rows(whole, mine_b, quarter), sem(10), core))
    other_a = base_a + (1 - y) * quarter
    got = rows(whole, other_a, quarter)
    push(got, got, sem(7), yn).wait_recv()
    start(push(got, got, sem(11), core))
    other_b = base_b + (1 - x) * quarter
    got = rows(whole, other_b, quarter)
    push(got, got, sem(8), xn).wait_recv()
    start(push(got, got, sem(12), core))
    beside = gathered.at[1 - c]
    for r, i in ((mine_a, 9), (mine_b, 10), (other_a, 11), (other_b, 12)):
        got = rows(beside, r, quarter)
        push(got, got, sem(i), core).wait_recv()

    eye = lax.broadcasted_iota(jnp.int32, (block, block), 0) == lax.broadcasted_iota(jnp.int32, (block, block), 1)
    trace = jnp.zeros((1, 1), F32)
    for r, (h, col) in places.items():
        v = jnp.where(eye, gathered[h, :, col : col + block], 0.0)
        trace = trace + jnp.sum(jnp.sum(v, axis=1, keepdims=True), axis=0, keepdims=True)
    inverse = 1.0 / (jnp.sqrt(trace) + frob_eps)
    squared = inverse * inverse
    for r, (h, col) in places.items():
        for k in range(r, 4):
            v = gathered[h, :, col + (k - r) * block : col + (k - r + 1) * block] * squared
            a, e = slice(r * block, (r + 1) * block), slice(k * block, (k + 1) * block)
            gf[a, e] = v
            gh[a, e] = v.astype(BF)
            if k > r:
                v = v.T
                gf[e, a] = v
                gh[e, a] = v.astype(BF)

    step = 64

    def scale_x(i, carry):
        at = pl.ds(pl.multiple_of(i * step, step), step)
        v = (uh[at].astype(F32) + ul[at].astype(F32)) * inverse
        xf[at] = v
        xh[at] = v.astype(BF)
        return carry

    lax.fori_loop(0, count // step, scale_x, 0)

    def iterate(shift, last):
        level = coef_a + coef_b * shift + coef_c * shift * shift
        slope = coef_b + 2.0 * coef_c * shift
        if last:

            def lower(i, carry):
                at = pl.ds(pl.multiple_of(i * step, step), step)
                g = gf[at]
                row = lax.broadcasted_iota(jnp.int32, g.shape, 0) + i * step
                col = lax.broadcasted_iota(jnp.int32, g.shape, 1)
                g = g - jnp.where(row == col, shift, 0.0)
                gf[at] = g
                low[at] = g.astype(BF)
                return carry

            lax.fori_loop(0, width // step, lower, 0)
            b[...] = (slope * gf[...] + coef_c * dot(low[...], low[...])).astype(BF)
            xh[...] = (level * xf[...] + dot(xh[...], b[...])).astype(BF)
            return
        b[...] = (slope * gf[...] + coef_c * dot(gh[...], gh[...])).astype(BF)
        v = level * xf[...] + dot(xh[...], b[...])
        t = level * gf[...] + dot(gh[...], b[...])
        xf[...] = v
        xh[...] = v.astype(BF)
        tf[...] = t
        low[...] = t.astype(BF)
        g = level * tf[...] + dot(b[...], low[...])
        gf[...] = g
        gh[...] = g.astype(BF)

    def middle(i, carry):
        iterate(0.0, False)
        return carry

    lax.fori_loop(0, NS_STEPS - 1, middle, 0)
    iterate(0.8, True)

    back_home(xh.reshape(4, top, width), rows_out, (s_s, s_r), 3, True)

    for v in (0, 1):

        @pl.when(c == v)
        def _(v=v):
            push(pack.at[1 - v], r_core, sem(0), core).wait_send()

    for i, (a, e) in enumerate(((outp, outp_all), (tokg, tokg_all))):
        pltpu.make_async_copy(a.at[z], e.at[z], loc.at[1 + i]).wait()
        for k in range(1, 4):
            slot = e.at[(z + 4 - k) % 4]
            push(slot, slot, (o_s.at[i, k - 1], o_r.at[i, k - 1]), zn[k - 1]).wait_recv()
    back_home(low_g, grads, (g_s, g_r), 0, False)
    for copy in held:
        copy.wait_send()
    back_home(xh.reshape(4, top, width), rows_out, (s_s, s_r), 3, False)


def muon_all(total, mom, outp, tokg, sizes):
    top, width = total.shape[1:]
    count, block = 4 * top, width // 4
    anyspace = pl.BlockSpec(memory_space=pl.ANY)
    vmem = pl.BlockSpec(memory_space=pltpu.VMEM)
    dma = pltpu.SemaphoreType.DMA
    wide = block * 5
    return pl.pallas_call(
        functools.partial(muon_kernel, sizes),
        out_shape=[jax.ShapeDtypeStruct((s, width), BF) for s in sizes] * 2
        + [jax.ShapeDtypeStruct(outp.shape, outp.dtype), jax.ShapeDtypeStruct(tokg.shape, tokg.dtype)],
        in_specs=[vmem, vmem, anyspace, anyspace],
        out_specs=[anyspace] * (2 * len(sizes) + 2),
        scratch_shapes=[
            pltpu.VMEM((4, top, width), BF),
            pltpu.VMEM((count, width), BF),
            pltpu.VMEM((count, width), BF),
            pltpu.VMEM((2, block, wide), F32),
            pltpu.VMEM((block, wide), F32),
            pltpu.VMEM((2, block // 4, wide), F32),
            pltpu.VMEM((2, block // 8, wide), F32),
            pltpu.VMEM((2, block, wide), F32),
            pltpu.VMEM((width, width), F32),
            pltpu.VMEM((width, width), BF),
            pltpu.VMEM((width, width), BF),
            pltpu.VMEM((width, width), BF),
            pltpu.VMEM((width, width), F32),
            pltpu.VMEM((count, width), F32),
            pltpu.VMEM((count, width), BF),
            dma((4,)),
            dma((4,)),
            dma((13,)),
            dma((13,)),
            dma((2, 3)),
            dma((2, 3)),
            dma((4,)),
            dma((4,)),
            dma((4,)),
        ],
        compiler_params=pltpu.CompilerParams(collective_id=3, has_side_effects=True, vmem_limit_bytes=VMEM_LIMIT),
    )(total, mom, outp, tokg)


def finish_kernel(factors, *refs):
    n = len(factors)
    big = 4 * n + 2
    sources, small = refs[:big], refs[big]
    state = refs[big + 1 : big + 7]
    targets = refs[big + 7 : 2 * big + 7]
    vectors = refs[2 * big + 7 : 2 * big + 7 + 2 * len(state)]
    refs = refs[2 * big + 7 + 2 * len(state) :]
    got, made, in_sem, out_sem = refs[:big], refs[big : 2 * big], refs[2 * big], refs[2 * big + 1]
    outp, tokg = got[:2]
    grads, rows, masters, moments = (got[2 + i * n : 2 + i * n + n] for i in range(4))
    output, token_grad = made[:2]
    shards, moments_new, masters_new, copies = (made[2 + i * n : 2 + i * n + n] for i in range(4))
    loads = [pltpu.make_async_copy(a, b, in_sem.at[i]) for i, (a, b) in enumerate(zip(sources, got))]
    stores = [pltpu.make_async_copy(a, b, out_sem.at[i]) for i, (a, b) in enumerate(zip(made, targets))]
    for copy in loads:
        copy.start()
    step = 16

    def over(rows, body):
        def one(i, carry):
            body(pl.ds(pl.multiple_of(i * step, step), step))
            return carry

        lax.fori_loop(0, rows // step, one, 0)

    for i, (src, dst) in enumerate(((outp, output), (tokg, token_grad))):
        loads[i].wait()
        for k in range(src.shape[0]):

            def body(at, src=src, dst=dst, k=k):
                dst[k, at] = src[k, at].astype(F32)

            over(src.shape[1], body)
        stores[i].start()
    for m in range(n):
        for i in range(4):
            loads[2 + i * n + m].wait()

        def body(at, m=m):
            g = grads[m][at].astype(F32)
            shards[m][at] = g
            moments_new[m][at] = muon_decay * moments[m][at] + g
            new = masters[m][at] - factors[m] * rows[m][at].astype(F32)
            masters_new[m][at] = new
            copies[m][at] = new.astype(BF)

        over(grads[m].shape[0], body)
        for i in range(4):
            stores[2 + i * n + m].start()
    width = small.shape[1]
    at = 0
    for i, (lo, hi) in enumerate(((0, 2), (6, 8), (8, 12))):
        g = small[lo:hi]
        change, first, second = adam_step(g, state[2 * i][...], state[2 * i + 1][...])
        for value in (g, change, first, second):
            vectors[at][...] = value
            at += 1
    for copy in stores:
        copy.wait()


def finish(grads, rows, masters, moments, outp, tokg, small, state, factors):
    vmem = pl.BlockSpec(memory_space=pltpu.VMEM)
    anyspace = pl.BlockSpec(memory_space=pl.ANY)
    args = [outp, tokg, *grads, *rows, *masters, *moments, small, *state]
    sized = [jax.ShapeDtypeStruct(v.shape, F32) for v in masters]
    shapes = [jax.ShapeDtypeStruct(v.shape, F32) for v in (outp, tokg)] + sized * 3
    shapes += [jax.ShapeDtypeStruct(v.shape, BF) for v in masters]
    big = len(shapes)
    for v in state[::2]:
        shapes += [jax.ShapeDtypeStruct(v.shape, F32)] * 4
    return pl.pallas_call(
        functools.partial(finish_kernel, factors),
        out_shape=shapes,
        in_specs=[anyspace] * big + [vmem] * (len(args) - big),
        out_specs=[anyspace] * big + [vmem] * (len(shapes) - big),
        scratch_shapes=[pltpu.VMEM(v.shape, v.dtype) for v in args[:big]]
        + [pltpu.VMEM(v.shape, v.dtype) for v in shapes[:big]]
        + [pltpu.SemaphoreType.DMA((big,))] * 2,
        compiler_params=pltpu.CompilerParams(vmem_limit_bytes=VMEM_LIMIT),
        cost_estimate=pl.CostEstimate(flops=10**7, bytes_accessed=15 * 10**6, transcendentals=0),
    )(*args)


def per_device_fast(
    tokens,
    cotangent,
    keep_mask,
    intake,
    outlet,
    expand,
    shrink,
    intake_moment,
    outlet_moment,
    expand_moment,
    shrink_moment,
    head_bias,
    expand_bias,
    norm_gain,
    model_bias,
    head_first,
    head_second,
    expand_first,
    expand_second,
    gain_first,
    gain_second,
    bias_first,
    bias_second,
):
    shape = tokens.shape
    local, width = shape[2:]
    z = lax.axis_index("tensor")
    masters = (intake, outlet, expand, shrink)
    moments = (intake_moment, outlet_moment, expand_moment, shrink_moment)
    sizes = tuple(v.shape[0] for v in masters)
    made = forward_all(
        masters,
        tokens.reshape(-1, local, width),
        cotangent.reshape(-1, local, width),
        norm_gain,
        model_bias,
        head_bias,
        expand_bias[None],
        keep_mask,
    )
    whole = [v.reshape(-1, width) for v in made[:4]]
    x, cot = (v.reshape(-1, width) for v in made[4:6])
    out, saved = made[6], tuple(made[7:]) + (x, cot)
    total, small, mom, token_grad = backward_all(whole, saved, norm_gain, keep_mask, moments, sizes)
    made = muon_all(total, mom, out.reshape(-1, local, width), token_grad.reshape(-1, local, width), sizes)
    rows_scale = lax.axis_size("dp") * lax.axis_size("tensor")
    factors = [rate * (s * rows_scale / width) ** 0.5 for s, rate in zip(sizes, muon_rates)]
    state = (head_first, head_second, gain_first, gain_second, bias_first, bias_second)
    done = finish(made[4:8], made[:4], masters, moments, made[8], made[9], small, state, factors)
    output, token_grad = (v.reshape(shape) for v in done[:2])
    shards, moments_new, masters_new, copies = (tuple(done[2 + 4 * i : 6 + 4 * i]) for i in range(4))
    head, gain, bias = (done[18 + 4 * i : 22 + 4 * i] for i in range(3))
    hidden_total = small[2:6].reshape(expand_bias.shape)
    hidden = adam_step(hidden_total, expand_first, expand_second)
    return (
        (output, token_grad)
        + shards
        + (head[0], hidden_total, gain[0], bias[0])
        + moments_new
        + masters_new
        + copies
        + (head[1], hidden[0], gain[1], bias[1])
        + tuple(head[2:])
        + tuple(hidden[1:])
        + tuple(gain[2:])
        + tuple(bias[2:])
    )


def solution(mesh):
    placed = (
        P(None, "dp", "tensor", None),
        P(None, "dp", "tensor", None),
        P(None, "dp", None),
        P(("tensor", "dp"), None),
        P(("tensor", "dp"), None),
        P(("tensor", "dp"), None),
        P(("tensor", "dp"), None),
        P(("tensor", "dp"), None),
        P(("tensor", "dp"), None),
        P(("tensor", "dp"), None),
        P(("tensor", "dp"), None),
        P(),
        P(),
        P(),
        P(),
        P(),
        P(),
        P(),
        P(),
        P(),
        P(),
        P(),
        P(),
    )
    fast = mesh.shape["dp"] == 8 and mesh.shape["tensor"] == 4
    return jax.shard_map(
        per_device_fast if fast else per_device,
        mesh=mesh,
        in_specs=placed,
        out_specs=(
            P(None, "dp", "tensor", None),
            P(None, "dp", "tensor", None),
            P(("tensor", "dp"), None),
            P(("tensor", "dp"), None),
            P(("tensor", "dp"), None),
            P(("tensor", "dp"), None),
            P(),
            P(),
            P(),
            P(),
            P(("tensor", "dp"), None),
            P(("tensor", "dp"), None),
            P(("tensor", "dp"), None),
            P(("tensor", "dp"), None),
            P(("tensor", "dp"), None),
            P(("tensor", "dp"), None),
            P(("tensor", "dp"), None),
            P(("tensor", "dp"), None),
            P(("tensor", "dp"), None),
            P(("tensor", "dp"), None),
            P(("tensor", "dp"), None),
            P(("tensor", "dp"), None),
            P(),
            P(),
            P(),
            P(),
            P(),
            P(),
            P(),
            P(),
            P(),
            P(),
            P(),
            P(),
        ),
        check_vma=False,
    )
```
